32 devices in a mesh: dp: 4 (over y, x), expert: 4 (over z), tensor: 2 (over core).
Axes of the slice: x: 2, y: 2, z: 4, core: 2. Of those that a mesh axis runs over, the one named last changes fastest.
Arguments:
- tokens: bfloat16 [4096, 2048], P(('dp', 'expert')), may hold values from -6 to 6
- segments: int32 [4, 1024], P('dp', 'expert'), may hold values from 0 to 7, never falling along the last dimension, each value on 1 to 512 neighbouring positions
- routes: int32 [4096, 4], P(('dp', 'expert')), may hold values from 0 to 7, all different within a row; in each aligned block of 256 rows (0 to 255, 256 to 511, ...) at most 192 rows name the same one
- norm1_gain: bfloat16 [2048], replicated, may hold values from 0.5 to 1.5
- q_weight: bfloat16 [2048, 2048], P(None, 'tensor'), may hold values from -0.125 to 0.125
- k_weight: bfloat16 [2048, 2048], P(None, 'tensor'), may hold values from -0.125 to 0.125
- v_weight: bfloat16 [2048, 2048], P(None, 'tensor'), may hold values from -0.125 to 0.125
- o_weight: bfloat16 [2048, 2048], P(None, 'tensor'), may hold values from -0.5 to 0.5
- norm2_gain: bfloat16 [2048], replicated, may hold values from 0.5 to 1.5
- router_weight: bfloat16 [2048, 8], replicated, may hold values from -0.0625 to 0.0625
- shared_gate_vector: bfloat16 [2048], replicated, may hold values from -0.125 to 0.125
- shared_gate_weight: bfloat16 [2048, 5632], P(None, 'tensor'), may hold values from -0.125 to 0.125
- shared_up_weight: bfloat16 [2048, 5632], P(None, 'tensor'), may hold values from -0.125 to 0.125
- shared_down_weight: bfloat16 [2048, 5632], P(None, 'tensor'), may hold values from -0.25 to 0.25
- expert_gate_weight: bfloat16 [8, 2048, 1408], P('expert', None, 'tensor'), may hold values from -0.125 to 0.125
- expert_up_weight: bfloat16 [8, 2048, 1408], P('expert', None, 'tensor'), may hold values from -0.125 to 0.125
- expert_down_weight: bfloat16 [8, 2048, 1408], P('expert', None, 'tensor'), may hold values from -1 to 1
- out_grad: bfloat16 [4096, 2048], P(('dp', 'expert')), may hold values from -6 to 6
Outputs:
- layer_out: float32 [4096, 2048], P(('dp', 'expert'))
- input_grad: float32 [4096, 2048], P(('dp', 'expert'))
- rms_stats: float32 [2, 4096], P(None, ('dp', 'expert'))
- norm1_gain_grad: float32 [2048], P(('dp', 'expert'))
- q_weight_grad: float32 [2048, 2048], P(('dp', 'expert'), 'tensor')
- k_weight_grad: float32 [2048, 2048], P(('dp', 'expert'), 'tensor')
- v_weight_grad: float32 [2048, 2048], P(('dp', 'expert'), 'tensor')
- o_weight_grad: float32 [2048, 2048], P(('dp', 'expert'), 'tensor')
- norm2_gain_grad: float32 [2048], P(('dp', 'expert'))
- router_grad: float32 [2048, 8], P(('dp', 'expert'))
- shared_vector_grad: float32 [2048], P(('dp', 'expert'))
- shared_gate_grad: float32 [2048, 5632], P(('dp', 'expert'), 'tensor')
- shared_up_grad: float32 [2048, 5632], P(('dp', 'expert'), 'tensor')
- shared_down_grad: float32 [2048, 5632], P(('dp', 'expert'), 'tensor')
- expert_gate_grad: float32 [8, 2048, 1408], P('expert', 'dp', 'tensor')
- expert_up_grad: float32 [8, 2048, 1408], P('expert', 'dp', 'tensor')
- expert_down_grad: float32 [8, 2048, 1408], P('expert', 'dp', 'tensor')
The draws below stay inside these ranges and needn't reach their ends.
Inputs may be any that keep to these rules, and one draw needn't show every extreme that they name: `segments`: document numbers never fall along a sequence; each of the 8 documents of a sequence is present and holds 1 to 512 tokens, one exactly 512. `routes`: the 4 experts of a token differ. Among the 256 tokens of one index of dp and expert, no expert is named more than 192 times, a bound that some block reaches.
All inputs are finite; a program needn't handle non-finite values.
Results may differ from the reference program's by a relative error of at most 0.02.
Values may be sent and summed in bfloat16 or wider, within the bound.
A program may use at most 384 MiB of HBM per device.

```python
import math
import jax
import jax.numpy as jnp
import numpy as np
from jax import lax

D = 2048
H = 16
HD = 128
FFE = 1408
SH = 5632
TOP = 4
TOK_DEV = 256
DOCS = 8
EXPERTS = 8
SEQ = 1024
SEQS = 4
TOKENS = 4096
CAP = 192


def shard_levels(key, shape, shards, low, top_value):
    def one(axis_at, shards_of):
        steps = jax.random.uniform(jax.random.fold_in(jax.random.fold_in(key, 6), axis_at), (shards_of,), jnp.float32, low / len(shards), top_value / len(shards))
        return jnp.repeat(jnp.exp(steps), shape[axis_at] // shards_of).reshape((-1,) + (1,) * (len(shape) - axis_at - 1))

    level = one(*shards[0])
    for cut in shards[1:]:
        level = level * one(*cut)
    return level


def profile(number_of, total, reach, lean):
    portions = [(1 << 20) // math.isqrt(rank ** lean) + 1 for rank in range(2, number_of + 1)]
    rest, holding = total - reach - (number_of - 1), [1] * (number_of - 1)
    while rest > 0:
        candidates = [i for i in range(number_of - 1) if holding[i] < reach]
        pool, left = sum([portions[i] for i in candidates]), rest
        for i in candidates:
            more = min(reach - holding[i], max(1, left * portions[i] // pool), rest)
            holding[i] = holding[i] + more
            rest = rest - more
    return np.array([reach] + holding)


def uneven_parts(key, number_of, total, reach, lean):
    if number_of == 2:
        one = jax.random.randint(key, (), max(1, total - reach), min(reach, total - 1) + 1)
        return jnp.stack([one, total - one])
    tallies = jnp.asarray(profile(number_of, total, reach, lean), jnp.int32)
    pairs = (number_of - 1) // 2
    donor, sink = tallies[1:1 + 2 * pairs:2], tallies[2:2 + 2 * pairs:2]
    margin = jnp.minimum(donor - 1, reach - sink)
    passed = jax.random.randint(jax.random.fold_in(key, 1), (pairs,), 0, 1 << 20) % (margin + 1)
    tallies = tallies.at[1:1 + 2 * pairs:2].set(donor - passed).at[2:2 + 2 * pairs:2].set(sink + passed)
    return tallies[jax.random.permutation(jax.random.fold_in(key, 2), number_of)]


def assign_block(own_key, own, number, rows, number_of, top, reach, slope):
    sequence = jax.random.permutation(own_key, number_of)
    heavy_load, common = load_shares(number_of, rows * top, reach, slope, True), load_shares(number_of, rows * top, reach, slope, False)
    places = jnp.arange(number_of)

    def named(lengths, offset_by):
        used = int((lengths > 0).sum())
        fixed = max(1, used // 4)
        shifted = fixed + (places - fixed + offset_by * (used - fixed)) % max(1, number_of - fixed)
        return jnp.zeros((number_of,), jnp.int32).at[sequence[jnp.where(places < fixed, places, shifted)]].set(jnp.asarray(lengths, jnp.int32))

    lengths = jnp.where(number % 4 == 0, named(heavy_load, number // 4), named(common, number - number // 4 - 1))
    mixed = jax.random.permutation(jax.random.fold_in(own, 3), number_of)
    donor, receiver = mixed[0:number_of // 2 * 2:2], mixed[1:number_of // 2 * 2:2]
    margin = jnp.minimum(lengths[donor] - 1, reach - lengths[receiver]) // 2
    margin = jnp.where((donor == sequence[0]) | (receiver == sequence[0]) | (lengths[receiver] == 0), 0, jnp.maximum(margin, 0))
    shifted = jax.random.randint(jax.random.fold_in(own, 4), (number_of // 2,), 0, 1 << 20) % (margin + 1)
    lengths = lengths.at[donor].add(-shifted).at[receiver].add(shifted)
    items = jnp.searchsorted(jnp.cumsum(lengths), jnp.arange(rows * top), side="right").astype(jnp.int32)
    table = items.reshape(top, rows).T
    table = table[jax.random.permutation(jax.random.fold_in(own, 1), rows)]
    offset_by = jax.random.randint(jax.random.fold_in(own, 2), (rows, 1), 0, top)
    return jnp.take_along_axis(table, (jnp.arange(top)[None, :] + offset_by) % top, axis=1)


def load_shares(number_of, total, most, slope, full):
    weights = [(1 << 20) // math.isqrt(standing ** slope) + 1 for standing in range(1, number_of + 1)]
    largest = most if full else min(most, max(-(-total // number_of), total * weights[0] // sum(weights)))
    least = 1 if total - largest >= number_of - 1 else 0
    given, rest = [largest] + [least] * (number_of - 1), total - largest - least * (number_of - 1)
    while rest > 0:
        free = [i for i in range(1, number_of) if given[i] < largest] or [i for i in range(1, number_of) if given[i] < most]
        whole, remaining = sum([weights[i] for i in free]), rest
        for i in free:
            addition = min(most - given[i], max(1, remaining * weights[i] // whole), rest)
            given[i] = given[i] + addition
            rest = rest - addition
    return np.array(given)


def scatter_about(rng, extent, spread, limit, shards=(), kind=jnp.bfloat16):
    level = shard_levels(rng, extent, shards, -0.22, 0.18) if shards else 1.0
    values = jax.random.normal(rng, extent, jnp.float32) * spread * level
    return jnp.minimum(jnp.maximum(values, -limit), limit).astype(kind)


def setup_inputs(seed: int = 0) -> dict:
    key_of = jax.random.split(jax.random.key(seed), 19)
    tokens = scatter_about(key_of[0], (TOKENS, D), 1.0, 6.0, ((0, 16),))
    segments = jax.vmap(lambda own: jnp.searchsorted(jnp.cumsum(uneven_parts(own, DOCS, SEQ, SEQ // 2, 2)), jnp.arange(SEQ), side="right"))(jax.random.split(key_of[1], SEQS)).reshape((SEQS, SEQ)).astype(jnp.int32)
    routes_keys = jax.random.split(jax.random.fold_in(key_of[2], 1), TOKENS // TOK_DEV)
    routes_turns = jax.random.permutation(jax.random.fold_in(key_of[2], 3), TOKENS // TOK_DEV)
    routes = jax.vmap(lambda own, number: assign_block(jax.random.fold_in(key_of[2], 2), own, number, TOK_DEV, EXPERTS, TOP, CAP, 1))(routes_keys, routes_turns).reshape((TOKENS, TOP))
    norm1_gain = jnp.clip(1.0 + 0.1 * jax.random.normal(key_of[3], (D,), jnp.float32), 0.5, 1.5).astype(jnp.bfloat16)
    q_weight = scatter_about(key_of[4], (D, H * HD), D ** -0.5, 0.125, ((1, 2),))
    k_weight = scatter_about(key_of[5], (D, H * HD), D ** -0.5, 0.125, ((1, 2),))
    v_weight = scatter_about(key_of[6], (D, H * HD), D ** -0.5, 0.125, ((1, 2),))
    o_weight = scatter_about(key_of[7], (D, H * HD), (H * HD // 16) ** -0.5, 0.5, ((1, 2),))
    norm2_gain = jnp.clip(1.0 + 0.1 * jax.random.normal(key_of[8], (D,), jnp.float32), 0.5, 1.5).astype(jnp.bfloat16)
    router_weight = scatter_about(key_of[9], (D, EXPERTS), (4 * D) ** -0.5, 0.0625)
    shared_gate_vector = scatter_about(key_of[10], (D,), D ** -0.5, 0.125)
    shared_gate_weight = scatter_about(key_of[11], (D, SH), D ** -0.5, 0.125, ((1, 2),))
    shared_up_weight = scatter_about(key_of[12], (D, SH), D ** -0.5, 0.125, ((1, 2),))
    shared_down_weight = scatter_about(key_of[13], (D, SH), (SH // 9) ** -0.5, 0.25, ((1, 2),))
    expert_gate_weight = scatter_about(key_of[14], (EXPERTS, D, FFE), D ** -0.5, 0.125, ((0, 4), (2, 2)))
    expert_up_weight = scatter_about(key_of[15], (EXPERTS, D, FFE), D ** -0.5, 0.125, ((0, 4), (2, 2)))
    expert_down_weight = scatter_about(key_of[16], (EXPERTS, D, FFE), (max(FFE // 36, 1)) ** -0.5, 1.0, ((0, 4), (2, 2)))
    out_grad = scatter_about(key_of[17], (TOKENS, D), 1.0, 6.0, ((0, 16),))
    return dict(tokens=tokens, segments=segments, routes=routes, norm1_gain=norm1_gain, q_weight=q_weight, k_weight=k_weight, v_weight=v_weight, o_weight=o_weight, norm2_gain=norm2_gain, router_weight=router_weight, shared_gate_vector=shared_gate_vector, shared_gate_weight=shared_gate_weight, shared_up_weight=shared_up_weight, shared_down_weight=shared_down_weight, expert_gate_weight=expert_gate_weight, expert_up_weight=expert_up_weight, expert_down_weight=expert_down_weight, out_grad=out_grad)


epsilon = 1e-06
precise = lax.Precision.HIGHEST

@jax.custom_vjp
def low(v):
    return lax.optimization_barrier(v.astype(jnp.bfloat16)).astype(jnp.float32)

@jax.custom_vjp
def low_back(v):
    return v

def low_keep(v):
    return (low(v), None)

def low_pass(kept, grad):
    return (grad,)

def back_keep(v):
    return (v, None)

def back_low(kept, grad):
    return (low(grad),)
low.defvjp(low_keep, low_pass)
low_back.defvjp(back_keep, back_low)

def norm_apply(values, gain):
    inverse = lax.rsqrt(lax.optimization_barrier(jnp.mean(values * values, axis=-1, keepdims=True)) + epsilon)
    return (values * inverse * gain, inverse[:, 0])

def product(left, right):
    return jnp.dot(left, right, precision=precise)

def attend_one(queries, keys, values, labels):
    length = queries.shape[0]
    head_count = queries.shape[1] // HD
    query_heads = queries.reshape(length, head_count, HD)
    key_heads = keys.reshape(length, head_count, HD)
    value_heads = values.reshape(length, head_count, HD)
    scores = low_back(jnp.einsum('qhd,khd->hqk', query_heads, key_heads, precision=precise) * HD ** (-0.5))
    places = jnp.arange(length)
    allowed = (places[None, :] <= places[:, None]) & (labels[None, :] == labels[:, None])
    scores = jnp.where(allowed[None], scores, -jnp.inf)
    weights = low(jax.nn.softmax(scores, axis=-1))
    mixed = jnp.einsum('hqk,khd->qhd', weights, value_heads, precision=precise)
    return mixed.reshape(length, head_count * HD)

def expert_term(normed, gate_w, up_w, down_w):
    gate_pre = low_back(product(normed, gate_w))
    up_pre = low_back(product(normed, up_w))
    hidden = low(jax.nn.silu(gate_pre) * up_pre)
    return low_back(jnp.dot(hidden, down_w.T, precision=precise))

def layer_block_apply(input_rows, first_norm_gain, query_matrix, key_matrix, value_matrix, output_matrix, second_norm_gain, router_matrix, gate_vector_weight, shared_gate_matrix, shared_up_matrix, shared_down_matrix, expert_gate_matrix, expert_up_matrix, expert_down_matrix, segments, routes):
    normed_one, inverse_one = norm_apply(input_rows, first_norm_gain)
    normed_low = low(normed_one)
    queries = low_back(low(product(normed_low, query_matrix)))
    keys = low_back(low(product(normed_low, key_matrix)))
    values = low_back(low(product(normed_low, value_matrix)))

    def per_sequence(packed):
        return jax.checkpoint(attend_one)(packed[0], packed[1], packed[2], packed[3])
    mixed = lax.map(per_sequence, (queries.reshape(SEQS, SEQ, -1), keys.reshape(SEQS, SEQ, -1), values.reshape(SEQS, SEQ, -1), segments))
    mixed = low_back(low(mixed.reshape(TOKENS, -1)))
    residual_state = input_rows + low_back(jnp.dot(mixed, output_matrix.T, precision=precise))
    normed_two, inverse_two = norm_apply(residual_state, second_norm_gain)
    routed_in = low(normed_two)
    router_probs = jax.nn.softmax(product(routed_in, router_matrix), axis=-1)
    chosen = routes[:, :, None] == jnp.arange(EXPERTS)[None, None, :]
    expert_portions = lax.optimization_barrier(jnp.sum(jnp.where(chosen, router_probs[:, None, :], 0.0), axis=1))

    def expert_accumulate(total, packed):
        gate_w, up_w, down_w, expert_share = packed
        return (total + expert_share[:, None] * jax.checkpoint(expert_term)(routed_in, gate_w, up_w, down_w), None)
    routed_output, ignored_value = lax.scan(expert_accumulate, jnp.zeros_like(residual_state), (expert_gate_matrix, expert_up_matrix, expert_down_matrix, expert_portions.T))
    shared_gate_pre = low_back(product(routed_in, shared_gate_matrix))
    shared_up_pre = low_back(product(routed_in, shared_up_matrix))
    shared_hidden = low(jax.nn.silu(shared_gate_pre) * shared_up_pre)
    shared_out = low_back(jnp.dot(shared_hidden, shared_down_matrix.T, precision=precise))
    shared_sigma = jax.nn.sigmoid(product(routed_in, gate_vector_weight))
    branch = low_back(routed_output + shared_sigma[:, None] * shared_out)
    return (residual_state + branch, jnp.stack([inverse_one, inverse_two]))

def reference(tokens, segments, routes, norm1_gain, q_weight, k_weight, v_weight, o_weight, norm2_gain, router_weight, shared_gate_vector, shared_gate_weight, shared_up_weight, shared_down_weight, expert_gate_weight, expert_up_weight, expert_down_weight, out_grad):
    params = (norm1_gain, q_weight, k_weight, v_weight, o_weight, norm2_gain, router_weight, shared_gate_vector, shared_gate_weight, shared_up_weight, shared_down_weight, expert_gate_weight, expert_up_weight, expert_down_weight)
    full_params = tuple((item.astype(jnp.float32) for item in params))
    input_rows = tokens.astype(jnp.float32)

    def forward(layer_in, *weights):
        return layer_block_apply(layer_in, *weights, segments, routes)
    layer_out, pull_back, stats = jax.vjp(forward, input_rows, *full_params, has_aux=True)
    grads = pull_back(out_grad.astype(jnp.float32))
    return (layer_out, grads[0], stats, grads[1], grads[2], grads[3], grads[4], grads[5], grads[6], grads[7], grads[8], grads[9], grads[10], grads[11], grads[12], grads[13], grads[14])
```

```python
import jax
import jax.numpy as jnp
from jax import lax
from jax.sharding import PartitionSpec as P

HD = 128
SEQ_AXES = ("expert", "tensor")
epsilon = 1e-06
f32 = jnp.float32
bf16 = jnp.bfloat16


def norm_forward(values, gain):
    inverse = lax.rsqrt(jnp.mean(values * values, axis=-1, keepdims=True) + epsilon)
    return (values * inverse * gain, inverse)


def norm_backward(values, inverse, gain, upstream):
    scaled = upstream * gain
    gain_grad = jnp.sum(upstream * values * inverse, axis=0)
    inner = jnp.mean(scaled * values, axis=-1, keepdims=True)
    return (inverse * scaled - values * inverse * inverse * inverse * inner, gain_grad)


def cross_rows(left, right):
    return lax.dot_general(left, right, (((0,), (0,)), ((), ())), preferred_element_type=f32)


def cross_cols(left, right):
    return lax.dot_general(left, right, (((1,), (1,)), ((), ())), preferred_element_type=f32)


def dot(left, right):
    return jnp.dot(left, right, preferred_element_type=f32)


def two_parts(values):
    high = values.astype(bf16)
    return high, (values - high.astype(f32)).astype(bf16)


def gather(values):
    return lax.all_gather(values, SEQ_AXES, axis=0, tiled=True)


def scatter(values):
    return lax.psum_scatter(values.astype(bf16), SEQ_AXES, scatter_dimension=0, tiled=True).astype(f32)


def body(
    tokens, segments, routes, norm1_gain, q_weight, k_weight, v_weight, o_weight, norm2_gain,
    router_weight, shared_gate_vector, shared_gate_weight, shared_up_weight, shared_down_weight,
    expert_gate_weight, expert_up_weight, expert_down_weight, out_grad,
):
    nz = lax.axis_size("expert")
    nc = lax.axis_size("tensor")
    z = lax.axis_index("expert")
    c = lax.axis_index("tensor")
    rows, width = tokens.shape
    own_rows = rows // nc
    local_count, _, ffn = expert_gate_weight.shape
    expert_count = local_count * nz
    head_cols = q_weight.shape[1] // nz
    shared_cols = shared_gate_weight.shape[1] // nz
    heads = head_cols // HD
    seq = rows * nz
    scale = HD ** (-0.5)
    gain1 = norm1_gain.astype(f32)
    gain2 = norm2_gain.astype(f32)

    def own(values):
        return lax.dynamic_slice_in_dim(values, c * own_rows, own_rows, 0)

    def head_slice(values):
        return lax.dynamic_slice_in_dim(values, z * head_cols, head_cols, 1)

    def shared_slice(values):
        return lax.dynamic_slice_in_dim(values, z * shared_cols, shared_cols, 1)

    x_all_rows = tokens.astype(f32)
    inverse_one_rows = lax.rsqrt(jnp.mean(x_all_rows * x_all_rows, axis=-1) + epsilon)
    x = own(tokens).astype(f32)
    n1_own, inv1 = norm_forward(x, gain1)
    n1 = gather(n1_own.astype(bf16))
    dy = gather(own(out_grad))
    all_routes = lax.all_gather(routes, "expert", axis=0, tiled=True)
    labels = lax.all_gather(segments, "expert", axis=1, tiled=True)[0]

    wq, wk, wv, wo = head_slice(q_weight), head_slice(k_weight), head_slice(v_weight), head_slice(o_weight)
    q = dot(n1, wq).astype(bf16).reshape(seq, heads, HD)
    k = dot(n1, wk).astype(bf16).reshape(seq, heads, HD)
    v = dot(n1, wv).astype(bf16).reshape(seq, heads, HD)
    pos = jnp.arange(seq)
    allowed = (pos[None, :] <= pos[:, None]) & (labels[None, :] == labels[:, None])

    def masked_scores():
        raw = jnp.einsum("qhd,khd->hqk", q, k, preferred_element_type=f32) * scale
        return jnp.where(allowed[None], raw, -jnp.inf)

    scores = masked_scores()
    top = jnp.max(scores, axis=-1, keepdims=True)
    expd = jnp.exp(scores - top)
    total = jnp.sum(expd, axis=-1, keepdims=True)
    log_total = top + jnp.log(total)
    p_low = (expd / total).astype(bf16)
    o = jnp.einsum("hqk,khd->qhd", p_low, v, preferred_element_type=f32).reshape(seq, head_cols).astype(bf16)
    h = x + scatter(cross_cols(o, wo))
    n2_own, inv2 = norm_forward(h, gain2)
    n2 = gather(n2_own.astype(bf16))

    probs = jax.nn.softmax(dot(n2, router_weight), axis=-1)
    chosen = jnp.any(all_routes[:, :, None] == jnp.arange(expert_count)[None, None, :], axis=1)
    gates = jnp.where(chosen, probs, 0.0)
    sigma = jax.nn.sigmoid(dot(n2, shared_gate_vector))

    branch = None
    d_n2 = None
    grads = []
    d_gate_parts = []
    for index in range(local_count + 1):
        if index < local_count:
            w_gate, w_up, w_down = expert_gate_weight[index], expert_up_weight[index], expert_down_weight[index]
            gate = lax.dynamic_slice_in_dim(gates, z * local_count + index, 1, 1)
        else:
            w_gate, w_up, w_down = map(shared_slice, (shared_gate_weight, shared_up_weight, shared_down_weight))
            gate = sigma[:, None]
        a = dot(n2, w_gate)
        b = dot(n2, w_up)
        back = dot(dy, w_down)
        sig = jax.nn.sigmoid(a)
        act = a * sig
        u = act * b
        gu = (gate * u).astype(bf16)
        d_gate_parts.append(jnp.sum(u * back, axis=-1, keepdims=True))
        du = gate * back
        da = (du * b * (sig * (1.0 + a * (1.0 - sig)))).astype(bf16)
        db = (du * act).astype(bf16)
        part = cross_cols(gu, w_down)
        branch = part if branch is None else branch + part
        part = cross_cols(da, w_gate) + cross_cols(db, w_up)
        d_n2 = part if d_n2 is None else d_n2 + part
        grads.append((cross_rows(n2, da), cross_rows(n2, db), cross_rows(dy, gu)))

    d_expert = jnp.concatenate(d_gate_parts[:local_count], axis=1)
    d_probs = lax.dynamic_update_slice_in_dim(jnp.zeros_like(probs), d_expert, z * local_count, 1)
    d_probs = jnp.where(chosen, d_probs, 0.0)
    d_logits = probs * (d_probs - jnp.sum(probs * d_probs, axis=-1, keepdims=True))
    d_vector = d_gate_parts[local_count] * (sigma * (1.0 - sigma))[:, None]
    small = jnp.concatenate([d_logits, d_vector], axis=1)
    small_high, small_low = two_parts(small)
    small_weights = jnp.concatenate([router_weight, shared_gate_vector[:, None]], axis=1)
    d_n2 = d_n2 + cross_cols(small_high, small_weights)
    small_grad = cross_rows(n2, jnp.concatenate([small_high, small_low], axis=1))
    small_grad = small_grad[:, : expert_count + 1] + small_grad[:, expert_count + 1 :]

    d_n2_own = scatter(d_n2)
    branch_own = scatter(branch)
    upstream = own(out_grad).astype(f32)
    d_norm, grad_two = norm_backward(h, inv2, gain2, d_n2_own)
    dh = upstream + d_norm
    dhr = gather(dh.astype(bf16))
    d_o = dot(dhr, wo).astype(bf16).reshape(seq, heads, HD)
    grad_o = cross_rows(dhr, o)

    pf = jnp.exp(masked_scores() - log_total)
    pb = pf.astype(bf16)
    d_v = jnp.einsum("hqk,qhd->khd", pb, d_o, preferred_element_type=f32)
    dp = jnp.einsum("qhd,khd->hqk", d_o, v, preferred_element_type=f32)
    ds = (pf * (dp - jnp.sum(pf * dp, axis=-1, keepdims=True))).astype(bf16)
    d_q = jnp.einsum("hqk,khd->qhd", ds, k, preferred_element_type=f32) * scale
    d_k = jnp.einsum("hqk,qhd->khd", ds, q, preferred_element_type=f32) * scale
    d_q, d_k, d_v = (t.reshape(seq, head_cols).astype(bf16) for t in (d_q, d_k, d_v))
    grad_q, grad_k, grad_v = cross_rows(n1, d_q), cross_rows(n1, d_k), cross_rows(n1, d_v)
    d_n1 = cross_cols(d_q, wq) + cross_cols(d_k, wk) + cross_cols(d_v, wv)
    d_norm1, grad_one = norm_backward(x, inv1, gain1, scatter(d_n1))

    def pair(values):
        return lax.all_gather(values, "tensor", axis=0, tiled=True)

    layer_out = pair(h + branch_own)
    input_grad = pair(dh + d_norm1)
    inv2_rows = pair(inv2[:, 0])
    stats = jnp.stack([inverse_one_rows, inv2_rows])

    def over_dp(grad):
        return lax.psum_scatter(grad.astype(bf16), "dp", scatter_dimension=0, tiled=True)

    def over_all(grad):
        part = over_dp(grad)
        return lax.all_to_all(part, "expert", split_axis=0, concat_axis=1, tiled=True).astype(f32)

    small_all = jnp.concatenate([grad_one[:, None], grad_two[:, None], small_grad], axis=1)
    small_all = lax.psum_scatter(small_all, ("dp", "expert"), scatter_dimension=0, tiled=True)
    small_all = lax.psum(small_all, "tensor")
    g_one, g_two, g_router, g_vector = small_all[:, 0], small_all[:, 1], small_all[:, 2 : 2 + expert_count], small_all[:, 2 + expert_count]
    e_grads = [jnp.stack([over_dp(grads[i][j]) for i in range(local_count)]).astype(f32) for j in range(3)]
    s_grads = [over_all(grads[local_count][j]) for j in range(3)]
    g_q, g_k, g_v, g_o = (over_all(t) for t in (grad_q, grad_k, grad_v, grad_o))
    return (
        layer_out, input_grad, stats, g_one, g_q, g_k, g_v, g_o, g_two, g_router, g_vector,
        s_grads[0], s_grads[1], s_grads[2], e_grads[0], e_grads[1], e_grads[2],
    )


def solution(mesh):
    both = ("dp", "expert")
    cols = P(None, "tensor")
    placed = (
        P(both, None), P("dp", "expert"), P(both, None), P(), cols, cols, cols, cols, P(), P(), P(),
        cols, cols, cols, P("expert", None, "tensor"), P("expert", None, "tensor"),
        P("expert", None, "tensor"), P(both, None),
    )
    split = P(both, "tensor")
    experts = P("expert", "dp", "tensor")
    return jax.shard_map(
        body,
        mesh=mesh,
        in_specs=placed,
        out_specs=(
            P(both, None), P(both, None), P(None, both), P(both), split, split, split, split, P(both),
            P(both, None), P(both), split, split, split, experts, experts, experts,
        ),
        check_vma=False,
    )
```

```python
import functools

import jax
import jax.numpy as jnp
from jax import lax
from jax.experimental import pallas as pl
from jax.experimental.pallas import tpu as pltpu
from jax.sharding import PartitionSpec as P

HD = 128
MESH = pl.DeviceIdType.MESH
PIECES = 2
STRIP = 16
epsilon = 1e-06
f32 = jnp.float32
bf16 = jnp.bfloat16
UP, DOWN = 0, 1


def here():
    return lax.axis_index("expert"), lax.axis_index("tensor")


def greet(nz):
    z, c = here()
    barrier = pltpu.get_barrier_semaphore()

    def tell(device):
        pl.semaphore_signal(barrier, inc=1, device_id=device, device_id_type=MESH)

    tell({"tensor": 1 - c})
    for d in range(1, nz):
        tell({"expert": lax.rem(z + d, nz)})
    pl.semaphore_wait(barrier, nz)


def remote(src, dst, send, recv, device):
    return pltpu.make_async_remote_copy(
        src_ref=src, dst_ref=dst, send_sem=send, recv_sem=recv, device_id=device, device_id_type=MESH
    )


def strips(rows, step):
    def one(i, carry):
        step(pl.ds(pl.multiple_of(i * STRIP, STRIP), STRIP))
        return carry

    lax.fori_loop(0, rows // STRIP, one, 0)


GATHER_SEMS = 4


def gather_sems(nz):
    return [pltpu.SemaphoreType.DMA((2, nz, PIECES))] * GATHER_SEMS + [pltpu.SemaphoreType.DMA]


def gather_rows(nz, own_ref, out_ref, z_send, z_recv, s_send, s_recv, local_sem):
    z, c = here()
    rows = own_ref.shape[0]
    piece = rows // PIECES

    def origin(way, d):
        return z - d if way == UP else z + d

    def inside(way, d):
        return z >= d if way == UP else z + d < nz

    def onward(way):
        return z < nz - 1 if way == UP else z > 0

    def place(block, core, p):
        return out_ref.at[pl.ds(pl.multiple_of((block * 2 + core) * rows + p * piece, piece), piece)]

    def source(way, d, p):
        return own_ref.at[pl.ds(p * piece, piece)] if d == 0 else place(origin(way, d), c, p)

    def along(way, d, p):
        device = {"expert": z + 1 if way == UP else z - 1}
        return remote(
            source(way, d, p), place(origin(way, d), c, p), z_send.at[way, d, p], z_recv.at[way, d, p], device
        )

    def across(way, d, p):
        return remote(
            source(way, d, p), place(origin(way, d), c, p), s_send.at[way, d, p], s_recv.at[way, d, p],
            {"tensor": 1 - c},
        )

    def arrived(way, d, p):
        dst = place(origin(way, d), c, p)
        remote(dst, dst, z_send.at[way, d - 1, p], z_recv.at[way, d - 1, p], {"tensor": 1 - c}).wait_recv()

    def crossed(way, d, p):
        dst = place(origin(way, d), 1 - c, p)
        remote(dst, dst, s_send.at[way, d, p], s_recv.at[way, d, p], {"tensor": 1 - c}).wait_recv()

    mine = pltpu.make_async_copy(
        own_ref, out_ref.at[pl.ds(pl.multiple_of((z * 2 + c) * rows, rows), rows)], local_sem
    )
    for p in range(PIECES):
        for way in (UP, DOWN):
            pl.when(onward(way))(lambda way=way, p=p: along(way, 0, p).start())
        across(UP, 0, p).start()
    mine.start()
    for d in range(1, nz):
        for p in range(PIECES):
            for way in (UP, DOWN):

                @pl.when(inside(way, d))
                def _(way=way, d=d, p=p):
                    arrived(way, d, p)
                    pl.when(onward(way))(lambda: along(way, d, p).start())
                    across(way, d, p).start()

    for p in range(PIECES):
        crossed(UP, 0, p)
        across(UP, 0, p).wait_send()
        for way in (UP, DOWN):
            pl.when(onward(way))(lambda way=way, p=p: along(way, 0, p).wait_send())
            for d in range(1, nz):

                @pl.when(inside(way, d))
                def _(way=way, d=d, p=p):
                    crossed(way, d, p)
                    across(way, d, p).wait_send()
                    pl.when(onward(way))(lambda: along(way, d, p).wait_send())

    mine.wait()


REDUCE_SCRATCH = 8


def reduce_scratch(nz, rows, width):
    return [
        pltpu.VMEM((2, nz, rows, width), bf16),
        pltpu.VMEM((2, nz, rows, width), bf16),
        pltpu.VMEM((2, nz, rows, width), bf16),
        pltpu.VMEM((rows, width), f32),
        pltpu.SemaphoreType.DMA((2, nz, PIECES)),
        pltpu.SemaphoreType.DMA((2, nz, PIECES)),
        pltpu.SemaphoreType.DMA((2, nz, PIECES)),
        pltpu.SemaphoreType.DMA((2, nz, PIECES)),
    ]


def reduce_rows(nz, part_ref, side, inbox, outbox, total, s_send, s_recv, z_send, z_recv):
    z, c = here()
    rows = total.shape[0]
    piece = rows // PIECES

    def target(way, d):
        return z + d if way == UP else z - d

    def inside(way, d):
        return z + d < nz if way == UP else z >= d

    def behind(way):
        return z > 0 if way == UP else z < nz - 1

    def cut(p):
        return pl.ds(p * piece, piece)

    def across(way, d, p):
        src = part_ref.at[pl.ds(pl.multiple_of((target(way, d) * 2 + 1 - c) * rows + p * piece, piece), piece)]
        return remote(
            src, side.at[way, d, cut(p)], s_send.at[way, d, p], s_recv.at[way, d, p], {"tensor": 1 - c}
        )

    def along(way, d, p):
        device = {"expert": z + 1 if way == UP else z - 1}
        return remote(
            outbox.at[way, d, cut(p)], inbox.at[way, d - 1, cut(p)], z_send.at[way, d, p], z_recv.at[way, d - 1, p],
            device,
        )

    def arrived(way, d, p):
        dst = inbox.at[way, d, cut(p)]
        remote(dst, dst, z_send.at[way, d, p], z_recv.at[way, d, p], {"tensor": 1 - c}).wait_recv()

    def mine(way, d, p, strip):
        base = (target(way, d) * 2 + c) * rows + p * piece
        own = part_ref[pl.ds(pl.multiple_of(base + strip.start, STRIP), STRIP), :].astype(f32)
        return own + side[way, d, pl.ds(pl.multiple_of(p * piece + strip.start, STRIP), STRIP), :].astype(f32)

    for d in range(nz - 1, 0, -1):
        for p in range(PIECES):
            for way in (UP, DOWN):
                pl.when(inside(way, d))(lambda way=way, d=d, p=p: across(way, d, p).start())
    for p in range(PIECES):
        across(UP, 0, p).start()

    for d in range(nz - 1, 0, -1):
        for p in range(PIECES):
            for way in (UP, DOWN):

                @pl.when(inside(way, d))
                def _(way=way, d=d, p=p):
                    across(way, d, p).wait_recv()

                    @pl.when(behind(way))
                    def _():
                        arrived(way, d, p)

                        def add(strip):
                            at = pl.ds(pl.multiple_of(p * piece + strip.start, STRIP), STRIP)
                            value = mine(way, d, p, strip) + inbox[way, d, at, :].astype(f32)
                            outbox[way, d, at, :] = value.astype(bf16)

                        strips(piece, add)

                    @pl.when(jnp.logical_not(behind(way)))
                    def _():
                        def add(strip):
                            at = pl.ds(pl.multiple_of(p * piece + strip.start, STRIP), STRIP)
                            outbox[way, d, at, :] = mine(way, d, p, strip).astype(bf16)

                        strips(piece, add)

                    along(way, d, p).start()

    for p in range(PIECES):
        across(UP, 0, p).wait_recv()

        def first(strip, p=p):
            at = pl.ds(pl.multiple_of(p * piece + strip.start, STRIP), STRIP)
            total[at, :] = mine(UP, 0, p, strip)

        strips(piece, first)
        for way in (UP, DOWN):

            @pl.when(behind(way))
            def _(way=way, p=p):
                arrived(way, 0, p)

                def add(strip):
                    at = pl.ds(pl.multiple_of(p * piece + strip.start, STRIP), STRIP)
                    total[at, :] += inbox[way, 0, at, :].astype(f32)

                strips(piece, add)

    for p in range(PIECES):
        across(UP, 0, p).wait_send()
        for way in (UP, DOWN):
            for d in range(1, nz):

                @pl.when(inside(way, d))
                def _(way=way, d=d, p=p):
                    across(way, d, p).wait_send()
                    along(way, d, p).wait_send()


COST = pl.CostEstimate(flops=2 * 10**10, bytes_accessed=10**8, transcendentals=0)


def params(name, **more):
    return pltpu.CompilerParams(
        collective_id=name, has_side_effects=True, vmem_limit_bytes=56 * 1024 * 1024, **more
    )


VMEM = pl.BlockSpec(memory_space=pltpu.VMEM)
ANY = pl.BlockSpec(memory_space=pl.ANY)


def norm_rows(values, gain):
    inverse = lax.rsqrt(jnp.mean(values * values, axis=-1, keepdims=True) + epsilon)
    return values * inverse * gain, inverse


def norm_back(values, gain, upstream):
    inverse = lax.rsqrt(jnp.mean(values * values, axis=-1, keepdims=True) + epsilon)
    scaled = upstream * gain
    inner = jnp.mean(scaled * values, axis=-1, keepdims=True)
    change = inverse * scaled - values * inverse * inverse * inverse * inner
    return change, upstream * values * inverse


def first_gather(nz, x, gain, marks, name):
    rows, width = x.shape

    def kernel(x_ref, gain_ref, marks_ref, out_ref, all_ref, own, m_send, m_recv, m_local, *sems):
        z, c = here()
        greet(nz)
        keep = pltpu.make_async_copy(marks_ref, all_ref.at[z], m_local)
        keep.start()

        def send(way, d):
            to = z + d if way == UP else z - d
            return remote(marks_ref, all_ref.at[z], m_send.at[way, d], m_recv.at[way, d], {"expert": to})

        def take(way, d):
            dst = all_ref.at[z - d if way == UP else z + d]
            remote(dst, dst, m_send.at[way, d], m_recv.at[way, d], {"tensor": 1 - c}).wait_recv()

        for d in range(1, nz):
            for way in (UP, DOWN):
                pl.when(z + d < nz if way == UP else z >= d)(lambda way=way, d=d: send(way, d).start())

        def step(at):
            normed, _ = norm_rows(x_ref[at, :].astype(f32), gain_ref[...])
            own[at, :] = normed.astype(bf16)

        strips(rows, step)
        gather_rows(nz, own, out_ref, *sems)
        keep.wait()
        for d in range(1, nz):
            for way in (UP, DOWN):
                pl.when(z + d < nz if way == UP else z >= d)(lambda way=way, d=d: send(way, d).wait_send())
                pl.when(z >= d if way == UP else z + d < nz)(lambda way=way, d=d: take(way, d))

    return pl.pallas_call(
        kernel,
        out_shape=[
            jax.ShapeDtypeStruct((nz * 2 * rows, width), bf16),
            jax.ShapeDtypeStruct((nz,) + marks.shape, jnp.int32),
        ],
        in_specs=[VMEM, VMEM, VMEM],
        out_specs=[ANY, ANY],
        scratch_shapes=[
            pltpu.VMEM((rows, width), bf16),
            pltpu.SemaphoreType.DMA((2, nz)),
            pltpu.SemaphoreType.DMA((2, nz)),
            pltpu.SemaphoreType.DMA,
        ]
        + gather_sems(nz),
        compiler_params=params(name),
    )(x, gain, marks)


def project_and_gather(nz, o, weight, x, gain, name):
    rows, width = x.shape
    full = 2 * rows
    cols = o.shape[1]

    def kernel(o_ref, w_ref, x_ref, gain_ref, n2_ref, h_ref, inv_ref, heads, acc, give, take, own, inv_own, a_send,
               a_recv, e_send, e_recv, i_sems, *sems):
        z, c = here()
        greet(nz)

        def inside(way, d):
            return z + d < nz if way == UP else z >= d

        def send(way, d):
            to = z + d if way == UP else z - d
            src = o_ref.at[pl.ds(pl.multiple_of(to * full, full), full)]
            return remote(src, heads.at[way, d], a_send.at[way, d], a_recv.at[way, d], {"expert": to})

        for d in range(nz - 1, 0, -1):
            for way in (UP, DOWN):
                pl.when(inside(way, d))(lambda way=way, d=d: send(way, d).start())

        tile = 512 if width % 512 == 0 else width

        def project(block, left, fresh):
            at = pl.ds(pl.multiple_of(block * cols, cols), cols)

            def one(i, carry):
                to = pl.ds(pl.multiple_of(i * tile, tile), tile)
                value = lax.dot_general(
                    left(), w_ref[to, at], (((1,), (1,)), ((), ())), preferred_element_type=f32
                )
                acc[:, to] = value if fresh else acc[:, to] + value
                return carry

            lax.fori_loop(0, width // tile, one, 0)

        project(z, lambda: o_ref[pl.ds(pl.multiple_of(z * full, full), full), :], True)
        for d in range(1, nz):
            for way in (UP, DOWN):
                @pl.when(z >= d if way == UP else z + d < nz)
                def _(way=way, d=d):
                    remote(
                        heads.at[way, d], heads.at[way, d], a_send.at[way, d], a_recv.at[way, d], {"tensor": 1 - c}
                    ).wait_recv()
                    project(z - d if way == UP else z + d, lambda: heads[way, d], False)

        def pack(at):
            give[at, :] = acc[pl.ds(pl.multiple_of((1 - c) * rows + at.start, STRIP), STRIP), :].astype(bf16)

        strips(rows, pack)
        swap = remote(give, take, e_send, e_recv, {"tensor": 1 - c})
        swap.start()
        swap.wait_recv()

        def norm(at):
            mixed = acc[pl.ds(pl.multiple_of(c * rows + at.start, STRIP), STRIP), :] + take[at, :].astype(f32)
            h = x_ref[at, :].astype(f32) + mixed
            normed, inverse = norm_rows(h, gain_ref[...])
            h_ref[at, :] = h
            own[at, :] = normed.astype(bf16)
            inv_own[at, :] = jnp.broadcast_to(inverse, (STRIP, 128))

        strips(rows, norm)
        spot = inv_ref.at[pl.ds(pl.multiple_of(c * rows, rows), rows)]
        keep = pltpu.make_async_copy(inv_own, spot, i_sems.at[0])
        pass_on = remote(inv_own, spot, i_sems.at[1], i_sems.at[2], {"tensor": 1 - c})
        keep.start()
        pass_on.start()
        gather_rows(nz, own, n2_ref, *sems)
        keep.wait()
        pass_on.wait()
        swap.wait_send()
        for d in range(1, nz):
            for way in (UP, DOWN):
                pl.when(inside(way, d))(lambda way=way, d=d: send(way, d).wait_send())

    return pl.pallas_call(
        kernel,
        out_shape=[
            jax.ShapeDtypeStruct((nz * full, width), bf16),
            jax.ShapeDtypeStruct((rows, width), f32),
            jax.ShapeDtypeStruct((full, 128), f32),
        ],
        in_specs=[VMEM] * 4,
        out_specs=[ANY, VMEM, ANY],
        scratch_shapes=[
            pltpu.VMEM((2, nz, full, cols), bf16),
            pltpu.VMEM((full, width), f32),
            pltpu.VMEM((rows, width), bf16),
            pltpu.VMEM((rows, width), bf16),
            pltpu.VMEM((rows, width), bf16),
            pltpu.VMEM((rows, 128), f32),
            pltpu.SemaphoreType.DMA((2, nz)),
            pltpu.SemaphoreType.DMA((2, nz)),
            pltpu.SemaphoreType.DMA,
            pltpu.SemaphoreType.DMA,
            pltpu.SemaphoreType.DMA((3,)),
        ]
        + gather_sems(nz),
        compiler_params=params(name),
    )(o, weight, x, gain)


def reduce_and_gather(nz, part, h, gain, upstream, name):
    rows, width = h.shape

    def kernel(part_ref, h_ref, gain_ref, up_ref, out_ref, dh_ref, gg_ref, own, *rest):
        scratch, sems = rest[:REDUCE_SCRATCH], rest[REDUCE_SCRATCH:]
        total = scratch[3]
        greet(nz)
        reduce_rows(nz, part_ref, *scratch)
        gg_ref[...] = jnp.zeros_like(gg_ref)

        def step(at):
            change, along = norm_back(h_ref[at, :], gain_ref[...], total[at, :])
            dh = up_ref[at, :].astype(f32) + change
            dh_ref[at, :] = dh
            own[at, :] = dh.astype(bf16)
            gg_ref[...] += along

        strips(rows, step)
        gather_rows(nz, own, out_ref, *sems)

    return pl.pallas_call(
        kernel,
        out_shape=[
            jax.ShapeDtypeStruct((nz * 2 * rows, width), bf16),
            jax.ShapeDtypeStruct((rows, width), f32),
            jax.ShapeDtypeStruct((STRIP, width), f32),
        ],
        in_specs=[VMEM] * 4,
        out_specs=[ANY, VMEM, VMEM],
        scratch_shapes=[pltpu.VMEM((rows, width), bf16)] + reduce_scratch(nz, rows, width) + gather_sems(nz),
        compiler_params=params(name),
    )(part, h, gain, upstream)


def swap_rows(nz, own, out_ref, sems):
    z, c = here()
    rows = own.shape[0]
    spot = out_ref.at[pl.ds(pl.multiple_of(c * rows, rows), rows)]
    keep = pltpu.make_async_copy(own, spot, sems.at[0])
    pass_on = remote(own, spot, sems.at[1], sems.at[2], {"tensor": 1 - c})
    keep.start()
    pass_on.start()
    keep.wait()
    pass_on.wait()


def reduce_input(nz, part, x, gain, dh, name):
    rows, width = x.shape

    def kernel(part_ref, x_ref, gain_ref, dh_ref, out_ref, gg_ref, own, sems, *scratch):
        total = scratch[3]
        greet(nz)
        reduce_rows(nz, part_ref, *scratch)
        gg_ref[...] = jnp.zeros_like(gg_ref)

        def step(at):
            change, along = norm_back(x_ref[at, :].astype(f32), gain_ref[...], total[at, :])
            own[at, :] = dh_ref[at, :] + change
            gg_ref[...] += along

        strips(rows, step)
        swap_rows(nz, own, out_ref, sems)

    return pl.pallas_call(
        kernel,
        out_shape=[
            jax.ShapeDtypeStruct((2 * rows, width), f32),
            jax.ShapeDtypeStruct((STRIP, width), f32),
        ],
        in_specs=[VMEM] * 4,
        out_specs=[ANY, VMEM],
        scratch_shapes=[pltpu.VMEM((rows, width), f32), pltpu.SemaphoreType.DMA((3,))] + reduce_scratch(nz, rows, width),
        compiler_params=params(name),
    )(part, x, gain, dh)


def reduce_output(nz, part, h, name):
    rows, width = h.shape

    def kernel(part_ref, h_ref, out_ref, own, sems, *scratch):
        total = scratch[3]
        greet(nz)
        reduce_rows(nz, part_ref, *scratch)

        def step(at):
            own[at, :] = h_ref[at, :] + total[at, :]

        strips(rows, step)
        swap_rows(nz, own, out_ref, sems)

    return pl.pallas_call(
        kernel,
        out_shape=jax.ShapeDtypeStruct((2 * rows, width), f32),
        in_specs=[VMEM] * 2,
        out_specs=ANY,
        scratch_shapes=[pltpu.VMEM((rows, width), f32), pltpu.SemaphoreType.DMA((3,))] + reduce_scratch(nz, rows, width),
        compiler_params=params(name),
    )(part, h)


def spread(nz, parts, splits, name):
    block = parts[0].shape[0] // nz
    count = len(parts)
    outs = [(i, s) for i in range(count) for s in range(splits[i])]

    def kernel(*refs):
        ins, outs_refs, rest = refs[:count], refs[count : count + len(outs)], refs[count + len(outs) :]
        boxes, send_sem, recv_sem = rest[:count], rest[count], rest[count + 1]
        z, c = here()
        greet(nz)

        def cut(i, to):
            return ins[i].at[pl.ds(pl.multiple_of(to * block, block), block)]

        def send(i, way, d):
            to = z + d if way == UP else z - d
            return remote(cut(i, to), boxes[i].at[z], send_sem.at[i, way, d], recv_sem.at[i, way, d], {"expert": to})

        def take(i, way, d):
            dst = boxes[i].at[z - d if way == UP else z + d]
            remote(dst, dst, send_sem.at[i, way, d], recv_sem.at[i, way, d], {"tensor": 1 - c}).wait_recv()

        for i in range(count):
            for d in range(nz - 1, 0, -1):
                for way in (UP, DOWN):
                    pl.when(z + d < nz if way == UP else z >= d)(lambda i=i, way=way, d=d: send(i, way, d).start())
        for i in range(count):
            boxes[i][z] = ins[i][pl.ds(pl.multiple_of(z * block, block), block), :]
        for i in range(count):
            for d in range(1, nz):
                for way in (UP, DOWN):
                    pl.when(z + d < nz if way == UP else z >= d)(lambda i=i, way=way, d=d: send(i, way, d).wait_send())
                    pl.when(z >= d if way == UP else z + d < nz)(lambda i=i, way=way, d=d: take(i, way, d))
            for j, (k, s) in enumerate(outs):
                if k == i:
                    cols = ins[i].shape[1] // splits[i]
                    for b in range(nz):
                        outs_refs[j][:, b * cols : (b + 1) * cols] = boxes[i][b, :, s * cols : (s + 1) * cols].astype(f32)

    return pl.pallas_call(
        kernel,
        out_shape=[
            jax.ShapeDtypeStruct((block, nz * parts[i].shape[1] // splits[i]), f32) for i, _ in outs
        ],
        in_specs=[VMEM] * count,
        out_specs=[VMEM] * len(outs),
        scratch_shapes=[pltpu.VMEM((nz, block, p.shape[1]), bf16) for p in parts]
        + [pltpu.SemaphoreType.DMA((count, 2, nz)), pltpu.SemaphoreType.DMA((count, 2, nz))],
        compiler_params=params(name),
    )(*parts)


TILE = 256
TALL = 512
LANES = 128


def nt_dot(left, right):
    return lax.dot_general(left, right, (((1,), (1,)), ((), ())), preferred_element_type=f32)


def nn_dot(left, right):
    return jnp.dot(left, right, preferred_element_type=f32)


def tiles(count, step, size=TILE):
    def one(i, carry):
        step(i, pl.ds(pl.multiple_of(i * size, size), size))
        return carry

    lax.fori_loop(0, count, one, 0)


def padded(columns):
    return -(-columns // LANES) * LANES


def window(columns, place):
    first = place * columns // LANES * LANES
    return first, place * columns - first


def window_width(columns, places):
    return max(padded(window(columns, i)[1] + columns) for i in range(places))


def hidden_layer(nz, n2, dy, gate, weights, index, groups):
    seq, width = n2.shape
    shared = index is None
    ffn = weights[0].shape[1] // nz if shared else weights[0].shape[1]
    held = window_width(ffn, nz) if shared else ffn
    kept = held if shared else padded(ffn)
    block = width // groups
    lane = min(block, TILE)
    per = TILE // lane
    count, slabs = seq // TILE, width // TILE
    strip = 32
    product = nn_dot if shared else nt_dot
    w_shape = (width, held) if shared else (held, width)

    def kernel(n2_hbm, dy_hbm, wg_hbm, wu_hbm, wd_hbm, gate_ref, grad_hbm, da_hbm, db_hbm, gu_hbm, dgate_ref,
               n2_ref, dy_ref, wg, wu, wd, a, b, back, da, db, gu, turned, slab, in_sem, out_sem, slab_sem):
        z = lax.axis_index("expert")
        first = pl.multiple_of(z * ffn // LANES * LANES, LANES)
        skip = z * ffn - first

        def pick(ref):
            return ref.at[:, pl.ds(first, held)] if shared else ref.at[index]

        loads = [
            pltpu.make_async_copy(src, dst, in_sem.at[i])
            for i, (src, dst) in enumerate(
                ((pick(wg_hbm), wg), (n2_hbm, n2_ref), (pick(wu_hbm), wu), (pick(wd_hbm), wd), (dy_hbm, dy_ref))
            )
        ]
        for load in loads:
            load.start()
        if kept > held:
            for ref in (da, db, gu):
                ref[:, held:] = jnp.zeros((seq, kept - held), bf16)
        loads[0].wait()
        loads[1].wait()

        def one(i, at):
            a[at, :] = product(n2_ref[at, :], wg[...])

        tiles(seq // TALL, one, TALL)
        loads[2].wait()

        def two(i, at):
            b[at, :] = product(n2_ref[at, :], wu[...])

        tiles(seq // TALL, two, TALL)
        loads[3].wait()
        loads[4].wait()

        def three(i, at):
            back[...] = product(dy_ref[at, :], wd[...])

            def point(j, carry):
                row = pl.ds(pl.multiple_of(i * TILE + j * strip, strip), strip)
                local = pl.ds(pl.multiple_of(j * strip, strip), strip)
                av, bv, kv, gv = a[row, :], b[row, :], back[local, :], gate_ref[row, :]
                sig = 1.0 / (1.0 + jnp.exp(-av))
                act = av * sig
                u = act * bv
                if shared:
                    column = lax.broadcasted_iota(jnp.int32, (strip, held), 1)
                    mine = jnp.logical_and(column >= skip, column < skip + ffn)
                    u, kv = jnp.where(mine, u, 0.0), jnp.where(mine, kv, 0.0)
                dgate_ref[row, :] = jnp.sum(u * kv, axis=-1, keepdims=True)
                gu[row, :held] = (gv * u).astype(bf16)
                du = gv * kv
                da[row, :held] = (du * bv * (sig + act * (1.0 - sig))).astype(bf16)
                db[row, :held] = (du * act).astype(bf16)
                return carry

            lax.fori_loop(0, TILE // strip, point, 0)
            for k, ref in enumerate((da, db, gu)):
                turned[k, :, at] = ref[at, :held].T

        tiles(count, three)
        saves = [
            pltpu.make_async_copy(src, dst, out_sem.at[i])
            for i, (src, dst) in enumerate(((da, da_hbm), (db, db_hbm), (gu, gu_hbm)))
        ]
        for save in saves:
            save.start()

        def leave(i):
            slot = lax.rem(i, 2)
            if per > 1:
                dst = grad_hbm.at[pl.ds(i * per, per)]
            else:
                many = block // TILE
                dst = grad_hbm.at[pl.ds(i // many, 1), :, pl.ds(pl.multiple_of(lax.rem(i, many) * TILE, TILE), TILE)]
            return pltpu.make_async_copy(slab.at[slot], dst, slab_sem.at[slot])

        def four(i, at):
            slot = lax.rem(i, 2)
            pl.when(i >= 2)(lambda: leave(i).wait())
            for k, right in enumerate((n2_ref, n2_ref, dy_ref)):
                value = nn_dot(turned[k], right[:, at]).astype(bf16)
                for j in range(per):
                    slab[slot, j, k * held : (k + 1) * held, :] = value[:, j * lane : (j + 1) * lane]
            leave(i).start()

        tiles(slabs, four)
        leave(slabs - 2).wait()
        leave(slabs - 1).wait()
        for save in saves:
            save.wait()

    hidden = jax.ShapeDtypeStruct((seq, kept), bf16)
    return pl.pallas_call(
        kernel,
        out_shape=[
            jax.ShapeDtypeStruct((groups, 3 * held, block), bf16), hidden, hidden, hidden,
            jax.ShapeDtypeStruct((seq, 1), f32),
        ],
        in_specs=[ANY] * 5 + [VMEM],
        out_specs=[ANY] * 4 + [VMEM],
        scratch_shapes=[
            pltpu.VMEM((seq, width), bf16), pltpu.VMEM((seq, width), bf16),
            pltpu.VMEM(w_shape, bf16), pltpu.VMEM(w_shape, bf16), pltpu.VMEM(w_shape, bf16),
            pltpu.VMEM((seq, held), f32), pltpu.VMEM((seq, held), f32), pltpu.VMEM((TILE, held), f32),
            pltpu.VMEM((seq, kept), bf16), pltpu.VMEM((seq, kept), bf16), pltpu.VMEM((seq, kept), bf16),
            pltpu.VMEM((3, held, seq), bf16),
            pltpu.VMEM((2, per, 3 * held, lane), bf16),
            pltpu.SemaphoreType.DMA((5,)), pltpu.SemaphoreType.DMA((3,)), pltpu.SemaphoreType.DMA((2,)),
        ],
        compiler_params=pltpu.CompilerParams(vmem_limit_bytes=58 * 1024 * 1024),
    )(n2, dy, *weights, gate)


def sum_products(nz, experts, shared, extra):
    seq, kept = experts[0][0].shape
    _, ffn, width = experts[0][1][0].shape
    held = shared[0][0].shape[1]
    own = shared[0][1].shape[1] // nz
    ne, ns = len(experts), len(shared)
    step = 512
    more = [] if extra is None else list(extra)

    def kernel(*refs):
        e_left, e_right = refs[:ne], refs[ne : 2 * ne]
        s_left, s_right = refs[2 * ne : 2 * ne + ns], refs[2 * ne + ns : 2 * (ne + ns)]
        base = 2 * (ne + ns)
        small = refs[base : base + len(more)]
        out_hbm, left, right, sleft, sright, out, l_sem, r_sem, o_sem = refs[base + len(more) :]
        first = pl.multiple_of(lax.axis_index("expert") * own // LANES * LANES, LANES)

        def lefts():
            for i in range(ne):
                yield pltpu.make_async_copy(e_left[i], left.at[:, pl.ds(i * kept, kept)], l_sem.at[i])
            for i in range(ns):
                yield pltpu.make_async_copy(s_left[i], sleft.at[:, pl.ds(i * held, held)], l_sem.at[ne + i])

        def rights(j):
            to = pl.ds(j * step, step)
            for i in range(ne):
                src = e_right[i].at[experts[i][1][1], :, to]
                yield pltpu.make_async_copy(src, right.at[j % 2, pl.ds(i * kept, ffn)], r_sem.at[j % 2, i])
            for i in range(ns):
                src = s_right[i].at[to, pl.ds(first, held)]
                yield pltpu.make_async_copy(src, sright.at[j % 2, :, pl.ds(i * held, held)], r_sem.at[j % 2, ne + i])

        for copy in (*rights(0), *lefts()):
            copy.start()
        if kept > ffn:
            for j in range(2):
                for i in range(ne):
                    right[j, i * kept + ffn : (i + 1) * kept, :] = jnp.zeros((kept - ffn, step), bf16)
        for j in range(width // step):
            for copy in rights(j):
                copy.wait()
            if j == 0:
                for copy in lefts():
                    copy.wait()
            if (j + 1) * step < width:
                for copy in rights(j + 1):
                    copy.start()

            def one(m, at, j=j):
                value = nn_dot(left[at, :], right[j % 2]) + nt_dot(sleft[at, :], sright[j % 2])
                if more:
                    value += nt_dot(small[0][at, :], small[1][j * step : (j + 1) * step, :])
                out[at, j * step : (j + 1) * step] = value.astype(bf16)

            tiles(seq // TALL, one, TALL)
            to = pl.ds(j * step, step)
            pltpu.make_async_copy(out.at[:, to], out_hbm.at[:, to], o_sem).start()
        pltpu.make_async_copy(out, out_hbm, o_sem).wait()

    return pl.pallas_call(
        kernel,
        out_shape=jax.ShapeDtypeStruct((seq, width), bf16),
        in_specs=[ANY] * (2 * (ne + ns)) + [VMEM] * len(more),
        out_specs=ANY,
        scratch_shapes=[
            pltpu.VMEM((seq, ne * kept), bf16), pltpu.VMEM((2, ne * kept, step), bf16),
            pltpu.VMEM((seq, ns * held), bf16), pltpu.VMEM((2, step, ns * held), bf16),
            pltpu.VMEM((seq, width), bf16),
            pltpu.SemaphoreType.DMA((ne + ns,)), pltpu.SemaphoreType.DMA((2, ne + ns)), pltpu.SemaphoreType.DMA,
        ],
        compiler_params=pltpu.CompilerParams(vmem_limit_bytes=58 * 1024 * 1024),
    )(
        *[left for left, _ in experts], *[right[0] for _, right in experts],
        *[left for left, _ in shared], *[right for _, right in shared], *more,
    )


def spread_turned(nz, part, columns, places, name):
    _, held, block = part.shape
    count = 3
    held //= count

    def kernel(in_ref, *rest):
        outs, box, send_sem, recv_sem = rest[:count], rest[count], rest[count + 1], rest[count + 2]
        z, c = here()
        greet(nz)

        def send(way, d):
            to = z + d if way == UP else z - d
            return remote(in_ref.at[to], box.at[z], send_sem.at[way, d], recv_sem.at[way, d], {"expert": to})

        def take(way, d):
            dst = box.at[z - d if way == UP else z + d]
            remote(dst, dst, send_sem.at[way, d], recv_sem.at[way, d], {"tensor": 1 - c}).wait_recv()

        for d in range(nz - 1, 0, -1):
            for way in (UP, DOWN):
                pl.when(z + d < nz if way == UP else z >= d)(lambda way=way, d=d: send(way, d).start())
        box[z] = in_ref[z]
        for d in range(1, nz):
            for way in (UP, DOWN):
                pl.when(z + d < nz if way == UP else z >= d)(lambda way=way, d=d: send(way, d).wait_send())
                pl.when(z >= d if way == UP else z + d < nz)(lambda way=way, d=d: take(way, d))
        for k in range(count):
            end = 0
            for b in range(nz):
                first, _ = window(columns, b)
                value = box[b, k * held : (k + 1) * held, :].astype(f32).T
                shared = max(end - first, 0)
                if shared:
                    outs[k][:, first:end] += value[:, :shared]
                last = min(first + held, nz * columns)
                outs[k][:, first + shared : last] = value[:, shared : last - first]
                end = last

    return pl.pallas_call(
        kernel,
        out_shape=[jax.ShapeDtypeStruct((block, nz * columns), f32)] * count,
        in_specs=[VMEM],
        out_specs=[VMEM] * count,
        scratch_shapes=[
            pltpu.VMEM(part.shape, bf16), pltpu.SemaphoreType.DMA((2, nz)), pltpu.SemaphoreType.DMA((2, nz)),
        ],
        compiler_params=params(name),
    )(part)


def sum_everywhere(nz, ndp, parts, name):
    n, rows, block = parts.shape

    def kernel(in_ref, out_ref, box, total, other, send_sem, recv_sem, swap_sem):
        z, c = here()
        me = lax.axis_index("dp") * nz + z
        barrier = pltpu.get_barrier_semaphore()

        def peer(k):
            at = lax.rem(me + k, n)
            return at, {"dp": at // nz, "expert": lax.rem(at, nz)}

        pl.semaphore_signal(barrier, inc=1, device_id={"tensor": 1 - c}, device_id_type=MESH)
        for k in range(1, n):
            pl.semaphore_signal(barrier, inc=1, device_id=peer(k)[1], device_id_type=MESH)
        pl.semaphore_wait(barrier, n)

        def send(k):
            at, device = peer(k)
            return remote(in_ref.at[at], box.at[k], send_sem.at[k], recv_sem.at[k], device)

        for k in range(1, n):
            send(k).start()
        total[...] = in_ref[me]
        for k in range(1, n):
            send(k).wait_recv()
            total[...] += box[k]
        swap = remote(total, other, swap_sem.at[0], swap_sem.at[1], {"tensor": 1 - c})
        swap.start()
        swap.wait_recv()
        out_ref[...] = total[...] + other[...]
        swap.wait_send()
        for k in range(1, n):
            send(k).wait_send()

    return pl.pallas_call(
        kernel,
        out_shape=jax.ShapeDtypeStruct((rows, block), f32),
        in_specs=[VMEM],
        out_specs=VMEM,
        scratch_shapes=[
            pltpu.VMEM((n, rows, block), f32), pltpu.VMEM((rows, block), f32), pltpu.VMEM((rows, block), f32),
            pltpu.SemaphoreType.DMA((n,)), pltpu.SemaphoreType.DMA((n,)), pltpu.SemaphoreType.DMA((2,)),
        ],
        compiler_params=params(name),
    )(parts)


SEQ_AXES = ("expert", "tensor")


def cross_rows(left, right):
    return lax.dot_general(left, right, (((0,), (0,)), ((), ())), preferred_element_type=f32)


def cross_cols(left, right):
    return lax.dot_general(left, right, (((1,), (1,)), ((), ())), preferred_element_type=f32)


def dot(left, right):
    return jnp.dot(left, right, preferred_element_type=f32)


def two_parts(values):
    high = values.astype(bf16)
    return high, (values - high.astype(f32)).astype(bf16)


def body(
    tokens, segments, routes, norm1_gain, q_weight, k_weight, v_weight, o_weight, norm2_gain,
    router_weight, shared_gate_vector, shared_gate_weight, shared_up_weight, shared_down_weight,
    expert_gate_weight, expert_up_weight, expert_down_weight, out_grad,
):
    nz = lax.axis_size("expert")
    nc = lax.axis_size("tensor")
    z = lax.axis_index("expert")
    c = lax.axis_index("tensor")
    rows, width = tokens.shape
    own_rows = rows // nc
    local_count, _, ffn = expert_gate_weight.shape
    expert_count = local_count * nz
    head_cols = q_weight.shape[1] // nz
    shared_cols = shared_gate_weight.shape[1] // nz
    heads = head_cols // HD
    seq = rows * nz
    scale = HD ** (-0.5)
    gain1 = norm1_gain.astype(f32)[None]
    gain2 = norm2_gain.astype(f32)[None]

    def own(values):
        return lax.dynamic_slice_in_dim(values, c * own_rows, own_rows, 0)

    def head_slice(values):
        return lax.dynamic_slice_in_dim(values, z * head_cols, head_cols, 1)

    x_all_rows = tokens.astype(f32)
    inverse_one_rows = lax.rsqrt(jnp.mean(x_all_rows * x_all_rows, axis=-1) + epsilon)
    x = own(tokens)
    marks = jnp.concatenate([segments, routes.T, jnp.zeros((7 - routes.shape[1], rows), jnp.int32)], axis=0)
    n1, all_marks = first_gather(nz, x, gain1, marks, 0)
    labels = all_marks[:, 0].reshape(seq)
    all_routes = jnp.transpose(all_marks[:, 1 : 1 + routes.shape[1]], (0, 2, 1)).reshape(seq, routes.shape[1])
    upstream = own(out_grad)
    upstream_later, _ = lax.optimization_barrier((upstream, n1))
    dy = lax.all_gather(upstream_later, SEQ_AXES, axis=0, tiled=True)

    wq, wk, wv, wo = head_slice(q_weight), head_slice(k_weight), head_slice(v_weight), head_slice(o_weight)
    q = dot(n1, wq).astype(bf16).reshape(seq, heads, HD)
    k = dot(n1, wk).astype(bf16).reshape(seq, heads, HD)
    v = dot(n1, wv).astype(bf16).reshape(seq, heads, HD)
    pos = jnp.arange(seq)
    allowed = (pos[None, :] <= pos[:, None]) & (labels[None, :] == labels[:, None])

    def masked_scores():
        raw = jnp.einsum("qhd,khd->hqk", q, k, preferred_element_type=f32) * scale
        return jnp.where(allowed[None], raw, -jnp.inf)

    scores = masked_scores()
    top = jnp.max(scores, axis=-1, keepdims=True)
    expd = jnp.exp(scores - top)
    total = jnp.sum(expd, axis=-1, keepdims=True)
    log_total = top + jnp.log(total)
    p_low = (expd / total).astype(bf16)
    o = jnp.einsum("hqk,khd->qhd", p_low, v, preferred_element_type=f32).reshape(seq, head_cols).astype(bf16)
    n2, h, inverse_two = project_and_gather(nz, o, o_weight, x, gain2, 1)

    probs = jax.nn.softmax(dot(n2, router_weight), axis=-1)
    chosen = jnp.any(all_routes[:, :, None] == jnp.arange(expert_count)[None, None, :], axis=1)
    gates = jnp.where(chosen, probs, 0.0)
    sigma = jax.nn.sigmoid(dot(n2, shared_gate_vector))

    turned = [jnp.swapaxes(w, 1, 2) for w in (expert_gate_weight, expert_up_weight, expert_down_weight)]
    shared_weights = (shared_gate_weight, shared_up_weight, shared_down_weight)
    ndp = lax.axis_size("dp")
    grads, d_a, d_b, g_u, d_gate = {}, {}, {}, {}, {}
    n2_now = n2
    for index in (local_count, *range(local_count)):
        if index < local_count:
            gate = lax.dynamic_slice_in_dim(gates, z * local_count + index, 1, 1)
            out = hidden_layer(nz, n2_now, dy, gate, turned, index, ndp)
        else:
            out = hidden_layer(nz, n2_now, dy, sigma[:, None], shared_weights, None, ndp * nz)
        grads[index], d_a[index], d_b[index], g_u[index], d_gate[index] = out
        n2_now, d_gate[index] = lax.optimization_barrier((n2_now, d_gate[index]))

    d_expert = jnp.concatenate([d_gate[i] for i in range(local_count)], axis=1)
    d_probs = lax.dynamic_update_slice_in_dim(jnp.zeros_like(probs), d_expert, z * local_count, 1)
    d_probs = jnp.where(chosen, d_probs, 0.0)
    d_logits = probs * (d_probs - jnp.sum(probs * d_probs, axis=-1, keepdims=True))
    d_vector = d_gate[local_count] * (sigma * (1.0 - sigma))[:, None]
    small = jnp.concatenate([d_logits, d_vector], axis=1)
    small_high, small_low = two_parts(small)
    small_weights = jnp.concatenate([router_weight, shared_gate_vector[:, None]], axis=1)
    fill = ((0, 0), (0, 128 - small.shape[1]))
    experts = range(local_count)
    d_n2 = sum_products(
        nz,
        [(d_a[i], (turned[0], i)) for i in experts] + [(d_b[i], (turned[1], i)) for i in experts],
        [(d_a[local_count], shared_gate_weight), (d_b[local_count], shared_up_weight)],
        (jnp.pad(small_high, fill), jnp.pad(small_weights, fill)),
    )
    small_grad = cross_rows(n2, jnp.concatenate([small_high, small_low], axis=1))
    small_grad = small_grad[:, : expert_count + 1] + small_grad[:, expert_count + 1 :]


    def over_dp(grad):
        rows = grad.reshape(-1, grad.shape[-1])
        return lax.psum_scatter(rows, "dp", scatter_dimension=0, tiled=True)

    shared_grads = grads[local_count]
    shared_part = over_dp(shared_grads).reshape((nz,) + shared_grads.shape[1:])
    expert_parts = [over_dp(grads[i]) for i in experts]
    d_n2_low, shared_part = lax.optimization_barrier((d_n2, shared_part))
    dhr, dh, grad_two = reduce_and_gather(nz, d_n2_low, h, gain2, upstream, 2)
    d_o = dot(dhr, wo).astype(bf16).reshape(seq, heads, HD)
    grad_o = cross_rows(dhr, o)

    pf = jnp.exp(masked_scores() - log_total)
    pb = pf.astype(bf16)
    d_v = jnp.einsum("hqk,qhd->khd", pb, d_o, preferred_element_type=f32)
    dp = jnp.einsum("qhd,khd->hqk", d_o, v, preferred_element_type=f32)
    ds = (pf * (dp - jnp.sum(pf * dp, axis=-1, keepdims=True))).astype(bf16)
    d_q = jnp.einsum("hqk,khd->qhd", ds, k, preferred_element_type=f32) * scale
    d_k = jnp.einsum("hqk,qhd->khd", ds, q, preferred_element_type=f32) * scale
    d_q, d_k, d_v = (t.reshape(seq, head_cols).astype(bf16) for t in (d_q, d_k, d_v))
    grad_attention = jnp.concatenate(
        [cross_rows(n1, jnp.concatenate([d_q, d_k, d_v], axis=1)).astype(bf16), grad_o.astype(bf16)], axis=1
    )
    attention_part = over_dp(grad_attention)
    d_n1 = (cross_cols(d_q, wq) + cross_cols(d_k, wk) + cross_cols(d_v, wv)).astype(bf16)
    d_n1, _, expert_parts[0] = lax.optimization_barrier((d_n1, grad_attention, expert_parts[0]))
    input_grad, grad_one = reduce_input(nz, d_n1, x, gain1, dh, 3)
    branch = sum_products(
        nz,
        [(g_u[i], (turned[2], i)) for i in experts],
        [(g_u[local_count], shared_down_weight)],
        None,
    )
    branch, _ = lax.optimization_barrier((branch, grad_one))
    layer_out = reduce_output(nz, branch, h, 4)
    stats = jnp.stack([inverse_one_rows, inverse_two[:, 0]])

    small_rows = jnp.concatenate(
        [
            jnp.sum(grad_one, axis=0)[None], jnp.sum(grad_two, axis=0)[None], small_grad.T,
            jnp.zeros((13 - expert_count, width), f32),
        ],
        axis=0,
    )
    count = ndp * nz
    small_all = sum_everywhere(nz, ndp, jnp.swapaxes(small_rows.reshape(16, count, width // count), 0, 1), 7)
    g_one, g_two, g_router, g_vector = small_all[0], small_all[1], small_all[2 : 2 + expert_count].T, small_all[2 + expert_count]
    s_gate, s_up, s_down = spread_turned(nz, shared_part, shared_cols, nz, 5)
    (g_q, g_k, g_v, g_o) = spread(nz, [attention_part], (4,), 6)

    def whole(k):
        stack = jnp.stack([t[k * ffn : (k + 1) * ffn] for t in expert_parts]).astype(f32)
        return jnp.swapaxes(stack, 1, 2)

    e_gate, e_up, e_down = whole(0), whole(1), whole(2)
    return (
        layer_out, input_grad, stats, g_one, g_q, g_k, g_v, g_o, g_two, g_router, g_vector,
        s_gate, s_up, s_down, e_gate, e_up, e_down,
    )


def solution(mesh):
    both = ("dp", "expert")
    cols = P(None, "tensor")
    placed = (
        P(both, None), P("dp", "expert"), P(both, None), P(), cols, cols, cols, cols, P(), P(), P(),
        cols, cols, cols, P("expert", None, "tensor"), P("expert", None, "tensor"),
        P("expert", None, "tensor"), P(both, None),
    )
    split = P(both, "tensor")
    experts = P("expert", "dp", "tensor")
    return jax.shard_map(
        body,
        mesh=mesh,
        in_specs=placed,
        out_specs=(
            P(both, None), P(both, None), P(None, both), P(both), split, split, split, split, P(both),
            P(both, None), P(both), split, split, split, experts, experts, experts,
        ),
        check_vma=False,
    )
```

```python
import functools

import jax
import jax.numpy as jnp
from jax import lax
from jax.experimental import pallas as pl
from jax.experimental.pallas import tpu as pltpu
from jax.sharding import PartitionSpec as P

HD = 128
MESH = pl.DeviceIdType.MESH
PIECES = 2
STRIP = 16
epsilon = 1e-06
f32 = jnp.float32
bf16 = jnp.bfloat16
UP, DOWN = 0, 1


def here():
    return lax.axis_index("expert"), lax.axis_index("tensor")


def greet(nz):
    z, c = here()
    barrier = pltpu.get_barrier_semaphore()

    def tell(device):
        pl.semaphore_signal(barrier, inc=1, device_id=device, device_id_type=MESH)

    tell({"tensor": 1 - c})
    for d in range(1, nz):
        tell({"expert": lax.rem(z + d, nz)})
    pl.semaphore_wait(barrier, nz)


def remote(src, dst, send, recv, device):
    return pltpu.make_async_remote_copy(
        src_ref=src, dst_ref=dst, send_sem=send, recv_sem=recv, device_id=device, device_id_type=MESH
    )


def strips(rows, step):
    def one(i, carry):
        step(pl.ds(pl.multiple_of(i * STRIP, STRIP), STRIP))
        return carry

    lax.fori_loop(0, rows // STRIP, one, 0)


GATHER_SEMS = 4


def gather_sems(nz):
    return [pltpu.SemaphoreType.DMA((2, nz, PIECES))] * GATHER_SEMS + [pltpu.SemaphoreType.DMA]


def gather_rows(nz, own_ref, out_ref, z_send, z_recv, s_send, s_recv, local_sem):
    z, c = here()
    rows = own_ref.shape[0]
    piece = rows // PIECES

    def origin(way, d):
        return z - d if way == UP else z + d

    def inside(way, d):
        return z >= d if way == UP else z + d < nz

    def onward(way):
        return z < nz - 1 if way == UP else z > 0

    def place(block, core, p):
        return out_ref.at[pl.ds(pl.multiple_of((block * 2 + core) * rows + p * piece, piece), piece)]

    def source(way, d, p):
        return own_ref.at[pl.ds(p * piece, piece)] if d == 0 else place(origin(way, d), c, p)

    def along(way, d, p):
        device = {"expert": z + 1 if way == UP else z - 1}
        return remote(
            source(way, d, p), place(origin(way, d), c, p), z_send.at[way, d, p], z_recv.at[way, d, p], device
        )

    def across(way, d, p):
        return remote(
            source(way, d, p), place(origin(way, d), c, p), s_send.at[way, d, p], s_recv.at[way, d, p],
            {"tensor": 1 - c},
        )

    def arrived(way, d, p):
        dst = place(origin(way, d), c, p)
        remote(dst, dst, z_send.at[way, d - 1, p], z_recv.at[way, d - 1, p], {"tensor": 1 - c}).wait_recv()

    def crossed(way, d, p):
        dst = place(origin(way, d), 1 - c, p)
        remote(dst, dst, s_send.at[way, d, p], s_recv.at[way, d, p], {"tensor": 1 - c}).wait_recv()

    mine = pltpu.make_async_copy(
        own_ref, out_ref.at[pl.ds(pl.multiple_of((z * 2 + c) * rows, rows), rows)], local_sem
    )
    for p in range(PIECES):
        for way in (UP, DOWN):
            pl.when(onward(way))(lambda way=way, p=p: along(way, 0, p).start())
        across(UP, 0, p).start()
    mine.start()
    for d in range(1, nz):
        for p in range(PIECES):
            for way in (UP, DOWN):

                @pl.when(inside(way, d))
                def _(way=way, d=d, p=p):
                    arrived(way, d, p)
                    pl.when(onward(way))(lambda: along(way, d, p).start())
                    across(way, d, p).start()

    for p in range(PIECES):
        crossed(UP, 0, p)
        across(UP, 0, p).wait_send()
        for way in (UP, DOWN):
            pl.when(onward(way))(lambda way=way, p=p: along(way, 0, p).wait_send())
            for d in range(1, nz):

                @pl.when(inside(way, d))
                def _(way=way, d=d, p=p):
                    crossed(way, d, p)
                    across(way, d, p).wait_send()
                    pl.when(onward(way))(lambda: along(way, d, p).wait_send())

    mine.wait()


REDUCE_SCRATCH = 8


def reduce_scratch(nz, rows, width):
    return [
        pltpu.VMEM((nz, rows, width), bf16),
        pltpu.VMEM((nz + 1, rows, width), bf16),
        pltpu.VMEM((nz, rows, width), bf16),
        pltpu.VMEM((rows, width), f32),
        pltpu.SemaphoreType.DMA((nz, PIECES)),
        pltpu.SemaphoreType.DMA((nz, PIECES)),
        pltpu.SemaphoreType.DMA((nz, PIECES)),
        pltpu.SemaphoreType.DMA((nz + 1, PIECES)),
    ]


def block_order(nz, z, s):
    down = 2 * z // nz
    far = jnp.maximum(z, nz - 1 - z)
    near = nz - 1 - far
    late = s - (far - near)
    distance = jnp.where(late < 0, far - s, near - late // 2)
    sign = (1 - 2 * down) * jnp.where(late < 0, 1, 1 - 2 * lax.rem(late + nz * 2, 2))
    return z + sign * distance


class Reducer:
    def __init__(self, nz, part, side, inbox, outbox, total, s_send, s_recv, z_send, z_recv):
        self.nz, self.part, self.side, self.inbox, self.outbox, self.total = nz, part, side, inbox, outbox, total
        self.s_send, self.s_recv, self.z_send, self.z_recv = s_send, s_recv, z_send, z_recv
        self.z, self.c = here()
        self.rows = total.shape[0]
        self.piece = self.rows // PIECES

    def block(self, s):
        return block_order(self.nz, self.z, s)

    def cut(self, p):
        return pl.ds(p * self.piece, self.piece)

    def across(self, block, p):
        start = (block * 2 + 1 - self.c) * self.rows + p * self.piece
        src = self.part.at[pl.ds(pl.multiple_of(start, self.piece), self.piece)]
        return remote(
            src, self.side.at[block, self.cut(p)], self.s_send.at[block, p], self.s_recv.at[block, p],
            {"tensor": 1 - self.c},
        )

    def along(self, block, p):
        up = block > self.z
        slot = jnp.where(block == self.z - 1, self.nz, block)
        return remote(
            self.outbox.at[block, self.cut(p)], self.inbox.at[slot, self.cut(p)], self.z_send.at[block, p],
            self.z_recv.at[slot, p], {"expert": self.z + jnp.where(up, 1, -1)},
        )

    def arrived(self, slot, p):
        dst = self.inbox.at[slot, self.cut(p)]
        remote(dst, dst, self.z_send.at[0, p], self.z_recv.at[slot, p], {"tensor": 1 - self.c}).wait_recv()

    def mine(self, block, at):
        base = (block * 2 + self.c) * self.rows
        own = self.part[pl.ds(pl.multiple_of(base + at.start, STRIP), STRIP), :].astype(f32)
        return own + self.side[block, at, :].astype(f32)

    def strips(self, p, step):
        def one(i, carry):
            step(pl.ds(pl.multiple_of(p * self.piece + i * STRIP, STRIP), STRIP))
            return carry

        lax.fori_loop(0, self.piece // STRIP, one, 0)

    def begin(self, s):
        for p in range(PIECES):
            self.across(self.block(s), p).start()

    def forward(self, s):
        block = self.block(s)
        behind = jnp.where(block > self.z, self.z, self.nz - 1 - self.z) > 0
        for p in range(PIECES):
            self.across(block, p).wait_recv()

            @pl.when(behind)
            def _(p=p):
                self.arrived(block, p)

                def add(at):
                    self.outbox[block, at, :] = (self.mine(block, at) + self.inbox[block, at, :].astype(f32)).astype(bf16)

                self.strips(p, add)

            @pl.when(jnp.logical_not(behind))
            def _(p=p):
                def keep(at):
                    self.outbox[block, at, :] = self.mine(block, at).astype(bf16)

                self.strips(p, keep)

            self.along(block, p).start()

    def finish(self):
        z, nz = self.z, self.nz
        for p in range(PIECES):
            self.across(z, p).wait_recv()

            def first(at):
                self.total[at, :] = self.mine(z, at)

            self.strips(p, first)
            for slot, some in ((z, z > 0), (nz, z < nz - 1)):

                @pl.when(some)
                def _(slot=slot, p=p):
                    self.arrived(slot, p)

                    def add(at):
                        self.total[at, :] += self.inbox[slot, at, :].astype(f32)

                    self.strips(p, add)

    def drain(self):
        def one(s, carry):
            block = self.block(s)
            for p in range(PIECES):
                self.across(block, p).wait_send()
                pl.when(s < self.nz - 1)(lambda p=p: self.along(block, p).wait_send())
            return carry

        lax.fori_loop(0, self.nz, one, 0)


def params(name, **more):
    return pltpu.CompilerParams(
        collective_id=name, has_side_effects=True, vmem_limit_bytes=56 * 1024 * 1024, **more
    )


VMEM = pl.BlockSpec(memory_space=pltpu.VMEM)
ANY = pl.BlockSpec(memory_space=pl.ANY)


def norm_rows(values, gain):
    inverse = lax.rsqrt(jnp.mean(values * values, axis=-1, keepdims=True) + epsilon)
    return values * inverse * gain, inverse


def norm_back(values, gain, upstream):
    inverse = lax.rsqrt(jnp.mean(values * values, axis=-1, keepdims=True) + epsilon)
    scaled = upstream * gain
    inner = jnp.mean(scaled * values, axis=-1, keepdims=True)
    change = inverse * scaled - values * inverse * inverse * inverse * inner
    return change, upstream * values * inverse


def first_gather(nz, x, gain, marks, name):
    rows, width = x.shape

    def kernel(x_ref, gain_ref, marks_ref, out_ref, all_ref, own, m_send, m_recv, m_local, *sems):
        z, c = here()
        greet(nz)
        keep = pltpu.make_async_copy(marks_ref, all_ref.at[z], m_local)
        keep.start()

        def send(way, d):
            to = z + d if way == UP else z - d
            return remote(marks_ref, all_ref.at[z], m_send.at[way, d], m_recv.at[way, d], {"expert": to})

        def take(way, d):
            dst = all_ref.at[z - d if way == UP else z + d]
            remote(dst, dst, m_send.at[way, d], m_recv.at[way, d], {"tensor": 1 - c}).wait_recv()

        for d in range(1, nz):
            for way in (UP, DOWN):
                pl.when(z + d < nz if way == UP else z >= d)(lambda way=way, d=d: send(way, d).start())

        def step(at):
            normed, _ = norm_rows(x_ref[at, :].astype(f32), gain_ref[...])
            own[at, :] = normed.astype(bf16)

        strips(rows, step)
        gather_rows(nz, own, out_ref, *sems)
        keep.wait()
        for d in range(1, nz):
            for way in (UP, DOWN):
                pl.when(z + d < nz if way == UP else z >= d)(lambda way=way, d=d: send(way, d).wait_send())
                pl.when(z >= d if way == UP else z + d < nz)(lambda way=way, d=d: take(way, d))

    return pl.pallas_call(
        kernel,
        out_shape=[
            jax.ShapeDtypeStruct((nz * 2 * rows, width), bf16),
            jax.ShapeDtypeStruct((nz,) + marks.shape, jnp.int32),
        ],
        in_specs=[VMEM, VMEM, VMEM],
        out_specs=[ANY, ANY],
        scratch_shapes=[
            pltpu.VMEM((rows, width), bf16),
            pltpu.SemaphoreType.DMA((2, nz)),
            pltpu.SemaphoreType.DMA((2, nz)),
            pltpu.SemaphoreType.DMA,
        ]
        + gather_sems(nz),
        compiler_params=params(name),
    )(x, gain, marks)


def project_and_gather(nz, o, weight, x, gain, name):
    rows, width = x.shape
    full = 2 * rows
    cols = o.shape[1]

    def kernel(o_ref, w_ref, x_ref, gain_ref, n2_ref, h_ref, inv_ref, heads, acc, give, take, own, inv_own, a_send,
               a_recv, e_send, e_recv, i_sems, *sems):
        z, c = here()
        greet(nz)

        def inside(way, d):
            return z + d < nz if way == UP else z >= d

        def send(way, d):
            to = z + d if way == UP else z - d
            src = o_ref.at[pl.ds(pl.multiple_of(to * full, full), full)]
            return remote(src, heads.at[way, d], a_send.at[way, d], a_recv.at[way, d], {"expert": to})

        for d in range(nz - 1, 0, -1):
            for way in (UP, DOWN):
                pl.when(inside(way, d))(lambda way=way, d=d: send(way, d).start())

        tile = 512 if width % 512 == 0 else width

        def project(block, left, fresh):
            at = pl.ds(pl.multiple_of(block * cols, cols), cols)

            def one(i, carry):
                to = pl.ds(pl.multiple_of(i * tile, tile), tile)
                value = lax.dot_general(
                    left(), w_ref[to, at], (((1,), (1,)), ((), ())), preferred_element_type=f32
                )
                acc[:, to] = value if fresh else acc[:, to] + value
                return carry

            lax.fori_loop(0, width // tile, one, 0)

        project(z, lambda: o_ref[pl.ds(pl.multiple_of(z * full, full), full), :], True)
        for d in range(1, nz):
            for way in (UP, DOWN):
                @pl.when(z >= d if way == UP else z + d < nz)
                def _(way=way, d=d):
                    remote(
                        heads.at[way, d], heads.at[way, d], a_send.at[way, d], a_recv.at[way, d], {"tensor": 1 - c}
                    ).wait_recv()
                    project(z - d if way == UP else z + d, lambda: heads[way, d], False)

        def pack(at):
            give[at, :] = acc[pl.ds(pl.multiple_of((1 - c) * rows + at.start, STRIP), STRIP), :].astype(bf16)

        strips(rows, pack)
        swap = remote(give, take, e_send, e_recv, {"tensor": 1 - c})
        swap.start()
        swap.wait_recv()

        def norm(at):
            mixed = acc[pl.ds(pl.multiple_of(c * rows + at.start, STRIP), STRIP), :] + take[at, :].astype(f32)
            h = x_ref[at, :].astype(f32) + mixed
            normed, inverse = norm_rows(h, gain_ref[...])
            h_ref[at, :] = h
            own[at, :] = normed.astype(bf16)
            inv_own[at, :] = jnp.broadcast_to(inverse, (STRIP, 128))

        strips(rows, norm)
        spot = inv_ref.at[pl.ds(pl.multiple_of(c * rows, rows), rows)]
        keep = pltpu.make_async_copy(inv_own, spot, i_sems.at[0])
        pass_on = remote(inv_own, spot, i_sems.at[1], i_sems.at[2], {"tensor": 1 - c})
        keep.start()
        pass_on.start()
        gather_rows(nz, own, n2_ref, *sems)
        keep.wait()
        pass_on.wait()
        swap.wait_send()
        for d in range(1, nz):
            for way in (UP, DOWN):
                pl.when(inside(way, d))(lambda way=way, d=d: send(way, d).wait_send())

    return pl.pallas_call(
        kernel,
        out_shape=[
            jax.ShapeDtypeStruct((nz * full, width), bf16),
            jax.ShapeDtypeStruct((rows, width), f32),
            jax.ShapeDtypeStruct((full, 128), f32),
        ],
        in_specs=[VMEM] * 4,
        out_specs=[ANY, VMEM, ANY],
        scratch_shapes=[
            pltpu.VMEM((2, nz, full, cols), bf16),
            pltpu.VMEM((full, width), f32),
            pltpu.VMEM((rows, width), bf16),
            pltpu.VMEM((rows, width), bf16),
            pltpu.VMEM((rows, width), bf16),
            pltpu.VMEM((rows, 128), f32),
            pltpu.SemaphoreType.DMA((2, nz)),
            pltpu.SemaphoreType.DMA((2, nz)),
            pltpu.SemaphoreType.DMA,
            pltpu.SemaphoreType.DMA,
            pltpu.SemaphoreType.DMA((3,)),
        ]
        + gather_sems(nz),
        compiler_params=params(name),
    )(o, weight, x, gain)


def swap_rows(nz, own, out_ref, sems):
    z, c = here()
    rows = own.shape[0]
    spot = out_ref.at[pl.ds(pl.multiple_of(c * rows, rows), rows)]
    keep = pltpu.make_async_copy(own, spot, sems.at[0])
    pass_on = remote(own, spot, sems.at[1], sems.at[2], {"tensor": 1 - c})
    keep.start()
    pass_on.start()
    keep.wait()
    pass_on.wait()


def spread(nz, parts, splits, name):
    block = parts[0].shape[0] // nz
    count = len(parts)
    outs = [(i, s) for i in range(count) for s in range(splits[i])]

    def kernel(*refs):
        ins, outs_refs, rest = refs[:count], refs[count : count + len(outs)], refs[count + len(outs) :]
        boxes, send_sem, recv_sem = rest[:count], rest[count], rest[count + 1]
        z, c = here()
        greet(nz)

        def cut(i, to):
            return ins[i].at[pl.ds(pl.multiple_of(to * block, block), block)]

        def send(i, way, d):
            to = z + d if way == UP else z - d
            return remote(cut(i, to), boxes[i].at[z], send_sem.at[i, way, d], recv_sem.at[i, way, d], {"expert": to})

        def take(i, way, d):
            dst = boxes[i].at[z - d if way == UP else z + d]
            remote(dst, dst, send_sem.at[i, way, d], recv_sem.at[i, way, d], {"tensor": 1 - c}).wait_recv()

        for i in range(count):
            for d in range(nz - 1, 0, -1):
                for way in (UP, DOWN):
                    pl.when(z + d < nz if way == UP else z >= d)(lambda i=i, way=way, d=d: send(i, way, d).start())
        for i in range(count):
            boxes[i][z] = ins[i][pl.ds(pl.multiple_of(z * block, block), block), :]
        for i in range(count):
            for d in range(1, nz):
                for way in (UP, DOWN):
                    pl.when(z + d < nz if way == UP else z >= d)(lambda i=i, way=way, d=d: send(i, way, d).wait_send())
                    pl.when(z >= d if way == UP else z + d < nz)(lambda i=i, way=way, d=d: take(i, way, d))
            for j, (k, s) in enumerate(outs):
                if k == i:
                    cols = ins[i].shape[1] // splits[i]
                    for b in range(nz):
                        outs_refs[j][:, b * cols : (b + 1) * cols] = boxes[i][b, :, s * cols : (s + 1) * cols].astype(f32)

    return pl.pallas_call(
        kernel,
        out_shape=[
            jax.ShapeDtypeStruct((block, nz * parts[i].shape[1] // splits[i]), f32) for i, _ in outs
        ],
        in_specs=[VMEM] * count,
        out_specs=[VMEM] * len(outs),
        scratch_shapes=[pltpu.VMEM((nz, block, p.shape[1]), bf16) for p in parts]
        + [pltpu.SemaphoreType.DMA((count, 2, nz)), pltpu.SemaphoreType.DMA((count, 2, nz))],
        compiler_params=params(name),
    )(*parts)


TILE = 256
TALL = 512
LANES = 128


def nt_dot(left, right):
    return lax.dot_general(left, right, (((1,), (1,)), ((), ())), preferred_element_type=f32)


def nn_dot(left, right):
    return jnp.dot(left, right, preferred_element_type=f32)


def tiles(count, step, size=TILE):
    def one(i, carry):
        step(i, pl.ds(pl.multiple_of(i * size, size), size))
        return carry

    lax.fori_loop(0, count, one, 0)


def padded(columns):
    return -(-columns // LANES) * LANES


def window(columns, place):
    first = place * columns // LANES * LANES
    return first, place * columns - first


def window_width(columns, places):
    return max(padded(window(columns, i)[1] + columns) for i in range(places))


def hidden_layer(nz, n2, dy, gate, weights, groups):
    seq, width = n2.shape
    shared = weights[0].ndim == 2
    experts = 1 if shared else weights[0].shape[0]
    buffers = min(experts, 2)
    ffn = weights[0].shape[1] // nz if shared else weights[0].shape[1]
    held = window_width(ffn, nz) if shared else ffn
    kept = held if shared else padded(ffn)
    block = width // groups
    lane = min(block, TILE)
    per = TILE // lane
    count, slabs = seq // TILE, width // TILE
    strip = 32
    product = nn_dot if shared else nt_dot
    w_shape = (width, held) if shared else (held, width)

    def kernel(n2_hbm, dy_hbm, wg_hbm, wu_hbm, wd_hbm, gate_ref, grad_hbm, da_hbm, db_hbm, gu_hbm, dgate_ref,
               n2_ref, dy_ref, wg, wu, wd, a, b, back, da, db, gu, turned, slab, in_sem, row_sem, out_sem, slab_sem):
        z = lax.axis_index("expert")
        first = pl.multiple_of(z * ffn // LANES * LANES, LANES)
        skip = z * ffn - first

        def pick(ref, e):
            return ref.at[:, pl.ds(first, held)] if shared else ref.at[e]

        def weight(i, e):
            slot = lax.rem(e, buffers)
            src, dst = ((wg_hbm, wg), (wu_hbm, wu), (wd_hbm, wd))[i]
            return pltpu.make_async_copy(pick(src, e), dst.at[slot], in_sem.at[i, slot])

        rows_in = [
            pltpu.make_async_copy(n2_hbm, n2_ref, row_sem.at[0]), pltpu.make_async_copy(dy_hbm, dy_ref, row_sem.at[1])
        ]
        weight(0, 0).start()
        rows_in[0].start()
        weight(1, 0).start()
        weight(2, 0).start()
        rows_in[1].start()
        if kept > held:
            for ref in (da, db, gu):
                ref[:, held:] = jnp.zeros((seq, kept - held), bf16)

        def expert(e, carry):
            slot = lax.rem(e, buffers)
            weight(0, e).wait()
            pl.when(e == 0)(rows_in[0].wait)

            def one(i, at):
                a[at, :] = product(n2_ref[at, :], wg[slot])

            tiles(seq // TALL, one, TALL)
            weight(1, e).wait()

            def two(i, at):
                b[at, :] = product(n2_ref[at, :], wu[slot])

            tiles(seq // TALL, two, TALL)
            weight(2, e).wait()
            pl.when(e == 0)(rows_in[1].wait)
            if experts > 1:

                @pl.when(e + 1 < experts)
                def _():
                    for i in range(3):
                        weight(i, e + 1).start()

            def three(i, at):
                back[...] = product(dy_ref[at, :], wd[slot])

                def point(j, carry):
                    row = pl.ds(pl.multiple_of(i * TILE + j * strip, strip), strip)
                    local = pl.ds(pl.multiple_of(j * strip, strip), strip)
                    av, bv, kv, gv = a[row, :], b[row, :], back[local, :], gate_ref[e, row, :]
                    sig = 1.0 / (1.0 + jnp.exp(-av))
                    act = av * sig
                    u = act * bv
                    if shared:
                        column = lax.broadcasted_iota(jnp.int32, (strip, held), 1)
                        mine = jnp.logical_and(column >= skip, column < skip + ffn)
                        u, kv = jnp.where(mine, u, 0.0), jnp.where(mine, kv, 0.0)
                    dgate_ref[e, row, :] = jnp.sum(u * kv, axis=-1, keepdims=True)
                    gu[row, :held] = (gv * u).astype(bf16)
                    du = gv * kv
                    da[row, :held] = (du * bv * (sig + act * (1.0 - sig))).astype(bf16)
                    db[row, :held] = (du * act).astype(bf16)
                    return carry

                lax.fori_loop(0, TILE // strip, point, 0)
                for k, ref in enumerate((da, db, gu)):
                    turned[k, :, at] = ref[at, :held].T

            tiles(count, three)
            saves = [
                pltpu.make_async_copy(src, dst.at[e], out_sem.at[i])
                for i, (src, dst) in enumerate(((da, da_hbm), (db, db_hbm), (gu, gu_hbm)))
            ]
            for save in saves:
                save.start()

            def leave(i):
                slot = lax.rem(i, 2)
                below = pl.ds(pl.multiple_of(e * 3 * held, 16), 3 * held)
                if per > 1:
                    dst = grad_hbm.at[pl.ds(i * per, per), below]
                else:
                    many = block // TILE
                    to = pl.ds(pl.multiple_of(lax.rem(i, many) * TILE, TILE), TILE)
                    dst = grad_hbm.at[pl.ds(i // many, 1), below, to]
                return pltpu.make_async_copy(slab.at[slot], dst, slab_sem.at[slot])

            def four(i, at):
                slot = lax.rem(i, 2)
                pl.when(i >= 2)(lambda: leave(i).wait())
                for k, right in enumerate((n2_ref, n2_ref, dy_ref)):
                    value = nn_dot(turned[k], right[:, at]).astype(bf16)
                    for j in range(per):
                        slab[slot, j, k * held : (k + 1) * held, :] = value[:, j * lane : (j + 1) * lane]
                leave(i).start()

            tiles(slabs, four)
            leave(slabs - 2).wait()
            leave(slabs - 1).wait()
            for save in saves:
                save.wait()
            return carry

        if experts == 1:
            expert(0, 0)
        else:
            lax.fori_loop(0, experts, expert, 0)

    hidden = jax.ShapeDtypeStruct((experts, seq, kept), bf16)
    return pl.pallas_call(
        kernel,
        out_shape=[
            jax.ShapeDtypeStruct((groups, experts * 3 * held, block), bf16), hidden, hidden, hidden,
            jax.ShapeDtypeStruct((experts, seq, 1), f32),
        ],
        in_specs=[ANY] * 5 + [VMEM],
        out_specs=[ANY] * 4 + [VMEM],
        scratch_shapes=[
            pltpu.VMEM((seq, width), bf16), pltpu.VMEM((seq, width), bf16),
            pltpu.VMEM((buffers,) + w_shape, bf16), pltpu.VMEM((buffers,) + w_shape, bf16), pltpu.VMEM((buffers,) + w_shape, bf16),
            pltpu.VMEM((seq, held), f32), pltpu.VMEM((seq, held), f32), pltpu.VMEM((TILE, held), f32),
            pltpu.VMEM((seq, kept), bf16), pltpu.VMEM((seq, kept), bf16), pltpu.VMEM((seq, kept), bf16),
            pltpu.VMEM((3, held, seq), bf16),
            pltpu.VMEM((2, per, 3 * held, lane), bf16),
            pltpu.SemaphoreType.DMA((3, buffers)), pltpu.SemaphoreType.DMA((2,)), pltpu.SemaphoreType.DMA((3,)),
            pltpu.SemaphoreType.DMA((2,)),
        ],
        compiler_params=pltpu.CompilerParams(vmem_limit_bytes=58 * 1024 * 1024),
    )(n2, dy, *weights, gate)


class Products:
    def __init__(self, nz, experts, shared, extra):
        self.nz, self.experts, self.shared = nz, experts, shared
        _, self.seq, self.kept = experts[0][0][0].shape
        _, self.ffn, self.width = experts[0][1][0].shape
        self.held = shared[0][0][0].shape[2]
        self.own = shared[0][1].shape[1] // nz
        self.more = [] if extra is None else list(extra)
        self.inputs = (
            [left[0] for left, _ in experts] + [right[0] for _, right in experts] + [left[0] for left, _ in shared]
            + [right for _, right in shared] + self.more
        )
        ne, ns = len(experts), len(shared)
        self.specs = [ANY] * (2 * (ne + ns)) + [VMEM] * len(self.more)
        self.scratch = [
            pltpu.VMEM((self.seq, ne * self.kept), bf16), pltpu.VMEM((ne * self.kept, self.width), bf16),
            pltpu.VMEM((self.seq, ns * self.held), bf16), pltpu.VMEM((self.width, ns * self.held), bf16),
            pltpu.SemaphoreType.DMA((2 * (ne + ns),)),
        ]
        self.step = 512 if self.width % 512 == 0 else self.width

    def bind(self, refs, scratch):
        ne, ns = len(self.experts), len(self.shared)
        self.refs = refs
        self.left, self.right, self.sleft, self.sright, self.sem = scratch
        first = pl.multiple_of(lax.axis_index("expert") * self.own // LANES * LANES, LANES)
        kept, held = self.kept, self.held
        pairs = []
        for i in range(ne):
            pairs.append((refs[ne + i].at[self.experts[i][1][1]], self.right.at[pl.ds(i * kept, self.ffn)]))
            pairs.append((refs[i].at[self.experts[i][0][1]], self.left.at[:, pl.ds(i * kept, kept)]))
        base = 2 * ne
        for i in range(ns):
            pairs.append((refs[base + ns + i].at[:, pl.ds(first, held)], self.sright.at[:, pl.ds(i * held, held)]))
            pairs.append((refs[base + i].at[self.shared[i][0][1]], self.sleft.at[:, pl.ds(i * held, held)]))
        self.loads = [pltpu.make_async_copy(src, dst, self.sem.at[i]) for i, (src, dst) in enumerate(pairs)]
        self.small = refs[2 * (ne + ns) :]

    def fetch(self):
        for load in self.loads:
            load.start()
        if self.kept > self.ffn:
            for i in range(len(self.experts)):
                self.right[i * self.kept + self.ffn : (i + 1) * self.kept, :] = jnp.zeros(
                    (self.kept - self.ffn, self.width), bf16
                )

    def wait(self):
        for load in self.loads:
            load.wait()

    def block(self, b, out):
        rows = self.seq // self.nz
        at = pl.ds(pl.multiple_of(b * rows, rows), rows)

        def one(j, carry):
            to = pl.ds(pl.multiple_of(j * self.step, self.step), self.step)
            value = nn_dot(self.left[at, :], self.right[:, to]) + nt_dot(self.sleft[at, :], self.sright[to, :])
            if self.more:
                value += nt_dot(self.small[0][at, :], self.small[1][to, :])
            out[at, to] = value.astype(bf16)
            return carry

        lax.fori_loop(0, self.width // self.step, one, 0)


def reduce_and_gather(nz, products, h, gain, upstream, name):
    rows, width = h.shape
    n_in, n_scratch = len(products.inputs), len(products.scratch)

    def kernel(*refs):
        p_refs, (h_ref, gain_ref, up_ref, out_ref, dh_ref, gg_ref) = refs[:n_in], refs[n_in : n_in + 6]
        rest = refs[n_in + 6 :]
        p_scratch, (part, own), rest = rest[:n_scratch], rest[n_scratch : n_scratch + 2], rest[n_scratch + 2 :]
        scratch, sems = rest[:REDUCE_SCRATCH], rest[REDUCE_SCRATCH:]
        total = scratch[3]
        products.bind(p_refs, p_scratch)
        products.fetch()
        greet(nz)
        reducer = Reducer(nz, part, *scratch)
        products.wait()

        def one(s, carry):
            products.block(reducer.block(s), part)
            reducer.begin(s)
            pl.when(s >= 1)(lambda: reducer.forward(s - 1))
            return carry

        lax.fori_loop(0, nz, one, 0)
        reducer.finish()
        gg_ref[...] = jnp.zeros_like(gg_ref)

        def step(at):
            change, along = norm_back(h_ref[at, :], gain_ref[...], total[at, :])
            dh = up_ref[at, :].astype(f32) + change
            dh_ref[at, :] = dh
            own[at, :] = dh.astype(bf16)
            gg_ref[...] += along

        strips(rows, step)
        gather_rows(nz, own, out_ref, *sems)
        reducer.drain()

    return pl.pallas_call(
        kernel,
        out_shape=[
            jax.ShapeDtypeStruct((nz * 2 * rows, width), bf16),
            jax.ShapeDtypeStruct((rows, width), f32),
            jax.ShapeDtypeStruct((STRIP, width), f32),
        ],
        in_specs=products.specs + [VMEM] * 3,
        out_specs=[ANY, VMEM, VMEM],
        scratch_shapes=products.scratch
        + [pltpu.VMEM((nz * 2 * rows, width), bf16), pltpu.VMEM((rows, width), bf16)]
        + reduce_scratch(nz, rows, width)
        + gather_sems(nz),
        compiler_params=params(name),
    )(*products.inputs, h, gain, upstream)


def reduce_last(nz, d_heads, weights, x, gain, dh, products, h, name):
    rows, width = x.shape
    n_in, n_scratch = len(products.inputs), len(products.scratch)

    def kernel(*refs):
        p_refs, (d_ref, w_ref, x_ref, gain_ref, dh_ref, h_ref, in_ref, out_ref, gg_ref) = (
            refs[:n_in], refs[n_in : n_in + 9],
        )
        rest = refs[n_in + 9 :]
        p_scratch, (d_part, b_part, own, sems), rest = (
            rest[:n_scratch], rest[n_scratch : n_scratch + 4], rest[n_scratch + 4 :],
        )
        d_scratch, b_scratch = rest[:REDUCE_SCRATCH], rest[REDUCE_SCRATCH:]
        d_total, b_total = d_scratch[3], b_scratch[3]
        products.bind(p_refs, p_scratch)
        products.fetch()
        greet(nz)
        z, c = here()
        first, second = Reducer(nz, d_part, *d_scratch), Reducer(nz, b_part, *b_scratch)
        step_cols = products.step

        def inner(block):
            at = pl.ds(pl.multiple_of(block * 2 * rows, 2 * rows), 2 * rows)

            def one(j, carry):
                to = pl.ds(pl.multiple_of(j * step_cols, step_cols), step_cols)
                d_part[at, to] = nt_dot(d_ref[at, :], w_ref[to, :]).astype(bf16)
                return carry

            lax.fori_loop(0, width // step_cols, one, 0)

        def one(s, carry):
            inner(first.block(s))
            first.begin(s)
            pl.when(s == 0)(products.wait)
            products.block(second.block(s), b_part)
            second.begin(s)

            @pl.when(s >= 1)
            def _():
                first.forward(s - 1)
                second.forward(s - 1)

            return carry

        lax.fori_loop(0, nz, one, 0)
        first.finish()
        gg_ref[...] = jnp.zeros_like(gg_ref)

        def step(at):
            change, along = norm_back(x_ref[at, :].astype(f32), gain_ref[...], d_total[at, :])
            own[0, at, :] = dh_ref[at, :] + change
            gg_ref[...] += along

        strips(rows, step)

        def leave(i, ref):
            spot = ref.at[pl.ds(pl.multiple_of(c * rows, rows), rows)]
            return (
                pltpu.make_async_copy(own.at[i], spot, sems.at[i, 0]),
                remote(own.at[i], spot, sems.at[i, 1], sems.at[i, 2], {"tensor": 1 - c}),
            )

        for copy in leave(0, in_ref):
            copy.start()
        second.finish()

        def last(at):
            own[1, at, :] = h_ref[at, :] + b_total[at, :]

        strips(rows, last)
        for copy in leave(1, out_ref):
            copy.start()
        first.drain()
        second.drain()
        for copy in (*leave(0, in_ref), *leave(1, out_ref)):
            copy.wait()

    return pl.pallas_call(
        kernel,
        out_shape=[
            jax.ShapeDtypeStruct((2 * rows, width), f32),
            jax.ShapeDtypeStruct((2 * rows, width), f32),
            jax.ShapeDtypeStruct((STRIP, width), f32),
        ],
        in_specs=products.specs + [VMEM] * 6,
        out_specs=[ANY, ANY, VMEM],
        scratch_shapes=products.scratch
        + [
            pltpu.VMEM((nz * 2 * rows, width), bf16), pltpu.VMEM((nz * 2 * rows, width), bf16),
            pltpu.VMEM((2, rows, width), f32), pltpu.SemaphoreType.DMA((2, 3)),
        ]
        + reduce_scratch(nz, rows, width) * 2,
        compiler_params=params(name),
    )(*products.inputs, d_heads, weights, x, gain, dh, h)


def assemble(nz, box, columns):
    _, held, block = box.shape
    count = 3
    held //= count

    def kernel(box_ref, *outs):
        for k in range(count):
            end = 0
            for b in range(nz):
                first, _ = window(columns, b)
                value = box_ref[b, k * held : (k + 1) * held, :].astype(f32).T
                shared = max(end - first, 0)
                if shared:
                    outs[k][:, first:end] += value[:, :shared]
                last = min(first + held, nz * columns)
                outs[k][:, first + shared : last] = value[:, shared : last - first]
                end = last

    return pl.pallas_call(
        kernel,
        out_shape=[jax.ShapeDtypeStruct((block, nz * columns), f32)] * count,
        in_specs=[VMEM],
        out_specs=[VMEM] * count,
        compiler_params=pltpu.CompilerParams(vmem_limit_bytes=40 * 1024 * 1024),
    )(box)


def sum_everywhere(nz, ndp, parts, name):
    n, rows, block = parts.shape

    def kernel(in_ref, out_ref, box, total, other, send_sem, recv_sem, swap_sem):
        z, c = here()
        me = lax.axis_index("dp") * nz + z
        barrier = pltpu.get_barrier_semaphore()

        def peer(k):
            at = lax.rem(me + k, n)
            return at, {"dp": at // nz, "expert": lax.rem(at, nz)}

        pl.semaphore_signal(barrier, inc=1, device_id={"tensor": 1 - c}, device_id_type=MESH)
        for k in range(1, n):
            pl.semaphore_signal(barrier, inc=1, device_id=peer(k)[1], device_id_type=MESH)
        pl.semaphore_wait(barrier, n)

        def send(k):
            at, device = peer(k)
            return remote(in_ref.at[at], box.at[k], send_sem.at[k], recv_sem.at[k], device)

        for k in range(1, n):
            send(k).start()
        total[...] = in_ref[me]
        for k in range(1, n):
            send(k).wait_recv()
            total[...] += box[k]
        swap = remote(total, other, swap_sem.at[0], swap_sem.at[1], {"tensor": 1 - c})
        swap.start()
        swap.wait_recv()
        out_ref[...] = total[...] + other[...]
        swap.wait_send()
        for k in range(1, n):
            send(k).wait_send()

    return pl.pallas_call(
        kernel,
        out_shape=jax.ShapeDtypeStruct((rows, block), f32),
        in_specs=[VMEM],
        out_specs=VMEM,
        scratch_shapes=[
            pltpu.VMEM((n, rows, block), f32), pltpu.VMEM((rows, block), f32), pltpu.VMEM((rows, block), f32),
            pltpu.SemaphoreType.DMA((n,)), pltpu.SemaphoreType.DMA((n,)), pltpu.SemaphoreType.DMA((2,)),
        ],
        compiler_params=params(name),
    )(parts)


SEQ_AXES = ("expert", "tensor")


def cross_rows(left, right):
    return lax.dot_general(left, right, (((0,), (0,)), ((), ())), preferred_element_type=f32)


def cross_cols(left, right):
    return lax.dot_general(left, right, (((1,), (1,)), ((), ())), preferred_element_type=f32)


def dot(left, right):
    return jnp.dot(left, right, preferred_element_type=f32)


def two_parts(values):
    high = values.astype(bf16)
    return high, (values - high.astype(f32)).astype(bf16)


def body(
    tokens, segments, routes, norm1_gain, q_weight, k_weight, v_weight, o_weight, norm2_gain,
    router_weight, shared_gate_vector, shared_gate_weight, shared_up_weight, shared_down_weight,
    expert_gate_weight, expert_up_weight, expert_down_weight, out_grad,
):
    nz = lax.axis_size("expert")
    nc = lax.axis_size("tensor")
    z = lax.axis_index("expert")
    c = lax.axis_index("tensor")
    rows, width = tokens.shape
    own_rows = rows // nc
    local_count, _, ffn = expert_gate_weight.shape
    expert_count = local_count * nz
    head_cols = q_weight.shape[1] // nz
    shared_cols = shared_gate_weight.shape[1] // nz
    heads = head_cols // HD
    seq = rows * nz
    scale = HD ** (-0.5)
    gain1 = norm1_gain.astype(f32)[None]
    gain2 = norm2_gain.astype(f32)[None]

    def own(values):
        return lax.dynamic_slice_in_dim(values, c * own_rows, own_rows, 0)

    def head_slice(values):
        return lax.dynamic_slice_in_dim(values, z * head_cols, head_cols, 1)

    x_all_rows = tokens.astype(f32)
    inverse_one_rows = lax.rsqrt(jnp.mean(x_all_rows * x_all_rows, axis=-1) + epsilon)
    x = own(tokens)
    marks = jnp.concatenate([segments, routes.T, jnp.zeros((7 - routes.shape[1], rows), jnp.int32)], axis=0)
    n1, all_marks = first_gather(nz, x, gain1, marks, 0)
    labels = all_marks[:, 0].reshape(seq)
    all_routes = jnp.transpose(all_marks[:, 1 : 1 + routes.shape[1]], (0, 2, 1)).reshape(seq, routes.shape[1])
    upstream = own(out_grad)
    upstream_later, _ = lax.optimization_barrier((upstream, n1))
    dy = lax.all_gather(upstream_later, SEQ_AXES, axis=0, tiled=True)

    wo = head_slice(o_weight)
    w_heads = jnp.concatenate([head_slice(q_weight), head_slice(k_weight), head_slice(v_weight)], axis=1)
    qkv = dot(n1, w_heads).astype(bf16)
    q, k, v = (qkv[:, i * head_cols : (i + 1) * head_cols].reshape(seq, heads, HD) for i in range(3))
    pos = jnp.arange(seq)
    allowed = (pos[None, :] <= pos[:, None]) & (labels[None, :] == labels[:, None])

    raw = jnp.einsum("qhd,khd->hqk", q, k, preferred_element_type=f32) * scale
    scores = jnp.where(allowed[None], raw, -jnp.inf)
    expd = jnp.exp(scores - jnp.max(scores, axis=-1, keepdims=True))
    p_low = (expd / jnp.sum(expd, axis=-1, keepdims=True)).astype(bf16)
    o = jnp.einsum("hqk,khd->qhd", p_low, v, preferred_element_type=f32).reshape(seq, head_cols).astype(bf16)
    n2, h, inverse_two = project_and_gather(nz, o, o_weight, x, gain2, 1)

    probs = jax.nn.softmax(dot(n2, router_weight), axis=-1)
    chosen = jnp.any(all_routes[:, :, None] == jnp.arange(expert_count)[None, None, :], axis=1)
    gates = jnp.where(chosen, probs, 0.0)
    sigma = jax.nn.sigmoid(dot(n2, shared_gate_vector))

    turned = [jnp.swapaxes(w, 1, 2) for w in (expert_gate_weight, expert_up_weight, expert_down_weight)]
    shared_weights = (shared_gate_weight, shared_up_weight, shared_down_weight)
    ndp = lax.axis_size("dp")
    grad_s, da_s, db_s, gu_s, dgate_s = hidden_layer(nz, n2, dy, sigma[None, :, None], shared_weights, ndp * nz)
    n2_now, dgate_s = lax.optimization_barrier((n2, dgate_s))
    gate = jnp.swapaxes(lax.dynamic_slice_in_dim(gates, z * local_count, local_count, 1), 0, 1)[:, :, None]
    grad_e, da_e, db_e, gu_e, dgate_e = hidden_layer(nz, n2_now, dy, gate, turned, ndp)

    d_expert = jnp.swapaxes(dgate_e[:, :, 0], 0, 1)
    d_probs = lax.dynamic_update_slice_in_dim(jnp.zeros_like(probs), d_expert, z * local_count, 1)
    d_probs = jnp.where(chosen, d_probs, 0.0)
    d_logits = probs * (d_probs - jnp.sum(probs * d_probs, axis=-1, keepdims=True))
    d_vector = dgate_s[0] * (sigma * (1.0 - sigma))[:, None]
    small = jnp.concatenate([d_logits, d_vector], axis=1)
    small_high, small_low = two_parts(small)
    small_weights = jnp.concatenate([router_weight, shared_gate_vector[:, None]], axis=1)
    fill = ((0, 0), (0, 128 - small.shape[1]))
    experts = range(local_count)
    d_n2 = Products(
        nz,
        [((da_e, i), (turned[0], i)) for i in experts] + [((db_e, i), (turned[1], i)) for i in experts],
        [((da_s, 0), shared_gate_weight), ((db_s, 0), shared_up_weight)],
        (jnp.pad(small_high, fill), jnp.pad(small_weights, fill)),
    )
    small_grad = cross_rows(n2, jnp.concatenate([small_high, small_low], axis=1))
    small_grad = small_grad[:, : expert_count + 1] + small_grad[:, expert_count + 1 :]


    def over_dp(grad):
        rows = grad.reshape(-1, grad.shape[-1])
        return lax.psum_scatter(rows, "dp", scatter_dimension=0, tiled=True)

    shared_part = over_dp(grad_s).reshape((nz,) + grad_s.shape[1:])
    expert_part = over_dp(grad_e).reshape(local_count, 3, ffn, -1)
    dhr, dh, grad_two = reduce_and_gather(nz, d_n2, h, gain2, upstream, 2)
    shared_part, dhr = lax.optimization_barrier((shared_part, dhr))
    shared_box = lax.all_to_all(shared_part, "expert", split_axis=0, concat_axis=0, tiled=True)
    d_o = dot(dhr, wo).astype(bf16).reshape(seq, heads, HD)
    grad_o = cross_rows(dhr, o)

    d_v = jnp.einsum("hqk,qhd->khd", p_low, d_o, preferred_element_type=f32)
    dp = jnp.einsum("qhd,khd->hqk", d_o, v, preferred_element_type=f32)
    mean = jnp.sum(d_o.astype(f32) * o.reshape(seq, heads, HD).astype(f32), axis=-1).T
    ds = (p_low.astype(f32) * (dp - mean[:, :, None])).astype(bf16)
    d_q = jnp.einsum("hqk,khd->qhd", ds, k, preferred_element_type=f32) * scale
    d_k = jnp.einsum("hqk,qhd->khd", ds, q, preferred_element_type=f32) * scale
    d_heads = jnp.concatenate([t.reshape(seq, head_cols).astype(bf16) for t in (d_q, d_k, d_v)], axis=1)
    grad_attention = jnp.concatenate(
        [cross_rows(n1, d_heads).astype(bf16), grad_o.astype(bf16)], axis=1
    )
    attention_part = over_dp(grad_attention)
    branch = Products(
        nz,
        [((gu_e, i), (turned[2], i)) for i in experts],
        [((gu_s, 0), shared_down_weight)],
        None,
    )
    dh_now, _ = lax.optimization_barrier((dh, grad_attention))
    input_grad, layer_out, grad_one = reduce_last(
        nz, d_heads, w_heads, x, gain1, dh_now, branch, h, 3
    )
    stats = jnp.stack([inverse_one_rows, inverse_two[:, 0]])

    small_rows = jnp.concatenate(
        [
            jnp.sum(grad_one, axis=0)[None], jnp.sum(grad_two, axis=0)[None], small_grad.T,
            jnp.zeros((13 - expert_count, width), f32),
        ],
        axis=0,
    )
    small_rows, expert_part = lax.optimization_barrier((small_rows, expert_part))
    count = ndp * nz
    small_all = sum_everywhere(nz, ndp, jnp.swapaxes(small_rows.reshape(16, count, width // count), 0, 1), 7)
    s_gate, s_up, s_down = assemble(nz, shared_box, shared_cols)
    attention_part, small_all = lax.optimization_barrier((attention_part, small_all))
    (g_q, g_k, g_v, g_o) = spread(nz, [attention_part], (4,), 6)

    g_one, g_two, g_router, g_vector = small_all[0], small_all[1], small_all[2 : 2 + expert_count].T, small_all[2 + expert_count]
    e_gate, e_up, e_down = (jnp.swapaxes(expert_part[:, k].astype(f32), 1, 2) for k in range(3))
    return (
        layer_out, input_grad, stats, g_one, g_q, g_k, g_v, g_o, g_two, g_router, g_vector,
        s_gate, s_up, s_down, e_gate, e_up, e_down,
    )


def solution(mesh):
    both = ("dp", "expert")
    cols = P(None, "tensor")
    placed = (
        P(both, None), P("dp", "expert"), P(both, None), P(), cols, cols, cols, cols, P(), P(), P(),
        cols, cols, cols, P("expert", None, "tensor"), P("expert", None, "tensor"),
        P("expert", None, "tensor"), P(both, None),
    )
    split = P(both, "tensor")
    experts = P("expert", "dp", "tensor")
    return jax.shard_map(
        body,
        mesh=mesh,
        in_specs=placed,
        out_specs=(
            P(both, None), P(both, None), P(None, both), P(both), split, split, split, split, P(both),
            P(both, None), P(both), split, split, split, experts, experts, experts,
        ),
        check_vma=False,
    )
```

```python
import functools

import jax
import jax.numpy as jnp
from jax import lax
from jax.experimental import pallas as pl
from jax.experimental.pallas import tpu as pltpu
from jax.sharding import PartitionSpec as P

HD = 128
MESH = pl.DeviceIdType.MESH
PIECES = 2
STRIP = 16
epsilon = 1e-06
f32 = jnp.float32
bf16 = jnp.bfloat16
UP, DOWN = 0, 1


def here():
    return lax.axis_index("expert"), lax.axis_index("tensor")


def greet(nz):
    z, c = here()
    barrier = pltpu.get_barrier_semaphore()

    def tell(device):
        pl.semaphore_signal(barrier, inc=1, device_id=device, device_id_type=MESH)

    tell({"tensor": 1 - c})
    for d in range(1, nz):
        tell({"expert": lax.rem(z + d, nz)})
    pl.semaphore_wait(barrier, nz)


def remote(src, dst, send, recv, device):
    return pltpu.make_async_remote_copy(
        src_ref=src, dst_ref=dst, send_sem=send, recv_sem=recv, device_id=device, device_id_type=MESH
    )


def strips(rows, step):
    def one(i, carry):
        step(pl.ds(pl.multiple_of(i * STRIP, STRIP), STRIP))
        return carry

    lax.fori_loop(0, rows // STRIP, one, 0)


GATHER_SEMS = 4


def gather_sems(nz):
    return [pltpu.SemaphoreType.DMA((2, nz, PIECES))] * GATHER_SEMS + [pltpu.SemaphoreType.DMA]


def gather_rows(nz, own_ref, out_ref, z_send, z_recv, s_send, s_recv, local_sem):
    z, c = here()
    rows = own_ref.shape[0]
    piece = rows // PIECES

    def origin(way, d):
        return z - d if way == UP else z + d

    def inside(way, d):
        return z >= d if way == UP else z + d < nz

    def onward(way):
        return z < nz - 1 if way == UP else z > 0

    def place(block, core, p):
        return out_ref.at[pl.ds(pl.multiple_of((block * 2 + core) * rows + p * piece, piece), piece)]

    def source(way, d, p):
        return own_ref.at[pl.ds(p * piece, piece)] if d == 0 else place(origin(way, d), c, p)

    def along(way, d, p):
        device = {"expert": z + 1 if way == UP else z - 1}
        return remote(
            source(way, d, p), place(origin(way, d), c, p), z_send.at[way, d, p], z_recv.at[way, d, p], device
        )

    def across(way, d, p):
        return remote(
            source(way, d, p), place(origin(way, d), c, p), s_send.at[way, d, p], s_recv.at[way, d, p],
            {"tensor": 1 - c},
        )

    def arrived(way, d, p):
        dst = place(origin(way, d), c, p)
        remote(dst, dst, z_send.at[way, d - 1, p], z_recv.at[way, d - 1, p], {"tensor": 1 - c}).wait_recv()

    def crossed(way, d, p):
        dst = place(origin(way, d), 1 - c, p)
        remote(dst, dst, s_send.at[way, d, p], s_recv.at[way, d, p], {"tensor": 1 - c}).wait_recv()

    mine = pltpu.make_async_copy(
        own_ref, out_ref.at[pl.ds(pl.multiple_of((z * 2 + c) * rows, rows), rows)], local_sem
    )
    for p in range(PIECES):
        for way in (UP, DOWN):
            pl.when(onward(way))(lambda way=way, p=p: along(way, 0, p).start())
        across(UP, 0, p).start()
    mine.start()
    for d in range(1, nz):
        for p in range(PIECES):
            for way in (UP, DOWN):

                @pl.when(inside(way, d))
                def _(way=way, d=d, p=p):
                    arrived(way, d, p)
                    pl.when(onward(way))(lambda: along(way, d, p).start())
                    across(way, d, p).start()

    for p in range(PIECES):
        crossed(UP, 0, p)
        across(UP, 0, p).wait_send()
        for way in (UP, DOWN):
            pl.when(onward(way))(lambda way=way, p=p: along(way, 0, p).wait_send())
            for d in range(1, nz):

                @pl.when(inside(way, d))
                def _(way=way, d=d, p=p):
                    crossed(way, d, p)
                    across(way, d, p).wait_send()
                    pl.when(onward(way))(lambda: along(way, d, p).wait_send())

    mine.wait()


REDUCE_SCRATCH = 8


def reduce_scratch(nz, rows, width):
    return [
        pltpu.VMEM((nz, rows, width), bf16),
        pltpu.VMEM((nz + 1, rows, width), bf16),
        pltpu.VMEM((nz, rows, width), bf16),
        pltpu.VMEM((rows, width), f32),
        pltpu.SemaphoreType.DMA((nz, PIECES)),
        pltpu.SemaphoreType.DMA((nz, PIECES)),
        pltpu.SemaphoreType.DMA((nz, PIECES)),
        pltpu.SemaphoreType.DMA((nz + 1, PIECES)),
    ]


def block_order(nz, z, s):
    down = 2 * z // nz
    far = jnp.maximum(z, nz - 1 - z)
    near = nz - 1 - far
    late = s - (far - near)
    distance = jnp.where(late < 0, far - s, near - late // 2)
    sign = (1 - 2 * down) * jnp.where(late < 0, 1, 1 - 2 * lax.rem(late + nz * 2, 2))
    return z + sign * distance


class Reducer:
    def __init__(self, nz, part, side, inbox, outbox, total, s_send, s_recv, z_send, z_recv):
        self.nz, self.part, self.side, self.inbox, self.outbox, self.total = nz, part, side, inbox, outbox, total
        self.s_send, self.s_recv, self.z_send, self.z_recv = s_send, s_recv, z_send, z_recv
        self.z, self.c = here()
        self.rows = total.shape[0]
        self.piece = self.rows // PIECES

    def block(self, s):
        return block_order(self.nz, self.z, s)

    def cut(self, p):
        return pl.ds(p * self.piece, self.piece)

    def across(self, block, p):
        start = (block * 2 + 1 - self.c) * self.rows + p * self.piece
        src = self.part.at[pl.ds(pl.multiple_of(start, self.piece), self.piece)]
        return remote(
            src, self.side.at[block, self.cut(p)], self.s_send.at[block, p], self.s_recv.at[block, p],
            {"tensor": 1 - self.c},
        )

    def along(self, block, p):
        up = block > self.z
        slot = jnp.where(block == self.z - 1, self.nz, block)
        return remote(
            self.outbox.at[block, self.cut(p)], self.inbox.at[slot, self.cut(p)], self.z_send.at[block, p],
            self.z_recv.at[slot, p], {"expert": self.z + jnp.where(up, 1, -1)},
        )

    def arrived(self, slot, p):
        dst = self.inbox.at[slot, self.cut(p)]
        remote(dst, dst, self.z_send.at[0, p], self.z_recv.at[slot, p], {"tensor": 1 - self.c}).wait_recv()

    def mine(self, block, at):
        base = (block * 2 + self.c) * self.rows
        own = self.part[pl.ds(pl.multiple_of(base + at.start, STRIP), STRIP), :].astype(f32)
        return own + self.side[block, at, :].astype(f32)

    def strips(self, p, step):
        def one(i, carry):
            step(pl.ds(pl.multiple_of(p * self.piece + i * STRIP, STRIP), STRIP))
            return carry

        lax.fori_loop(0, self.piece // STRIP, one, 0)

    def ends(self):
        return jnp.logical_or(self.z == 0, self.z == self.nz - 1)

    def begin(self, s):
        for p in range(PIECES):
            self.across(self.block(s), p).start()

    def forward(self, s):
        block = self.block(s)
        behind = jnp.where(block > self.z, self.z, self.nz - 1 - self.z) > 0
        for p in range(PIECES):
            self.across(block, p).wait_recv()

            @pl.when(behind)
            def _(p=p):
                self.arrived(block, p)

                def add(at):
                    self.outbox[block, at, :] = (self.mine(block, at) + self.inbox[block, at, :].astype(f32)).astype(bf16)

                self.strips(p, add)

            @pl.when(jnp.logical_not(behind))
            def _(p=p):
                def keep(at):
                    self.outbox[block, at, :] = self.mine(block, at).astype(bf16)

                self.strips(p, keep)

            self.along(block, p).start()

    def finish(self):
        z, nz = self.z, self.nz
        for p in range(PIECES):
            self.across(z, p).wait_recv()

            def first(at):
                self.total[at, :] = self.mine(z, at)

            self.strips(p, first)
            for slot, some in ((z, z > 0), (nz, z < nz - 1)):

                @pl.when(some)
                def _(slot=slot, p=p):
                    self.arrived(slot, p)

                    def add(at):
                        self.total[at, :] += self.inbox[slot, at, :].astype(f32)

                    self.strips(p, add)

    def drain(self):
        def one(s, carry):
            block = self.block(s)
            for p in range(PIECES):
                self.across(block, p).wait_send()
                pl.when(s < self.nz - 1)(lambda p=p: self.along(block, p).wait_send())
            return carry

        lax.fori_loop(0, self.nz, one, 0)


def params(name, **more):
    return pltpu.CompilerParams(
        collective_id=name, has_side_effects=True, vmem_limit_bytes=56 * 1024 * 1024, **more
    )


VMEM = pl.BlockSpec(memory_space=pltpu.VMEM)
ANY = pl.BlockSpec(memory_space=pl.ANY)


def norm_rows(values, gain):
    inverse = lax.rsqrt(jnp.mean(values * values, axis=-1, keepdims=True) + epsilon)
    return values * inverse * gain, inverse


def norm_back(values, gain, upstream):
    inverse = lax.rsqrt(jnp.mean(values * values, axis=-1, keepdims=True) + epsilon)
    scaled = upstream * gain
    inner = jnp.mean(scaled * values, axis=-1, keepdims=True)
    change = inverse * scaled - values * inverse * inverse * inverse * inner
    return change, upstream * values * inverse


def first_gather(nz, x, gain, marks, name):
    rows, width = x.shape

    def kernel(x_ref, gain_ref, marks_ref, out_ref, all_ref, own, m_send, m_recv, m_local, *sems):
        z, c = here()
        greet(nz)
        keep = pltpu.make_async_copy(marks_ref, all_ref.at[z], m_local)
        keep.start()

        def send(way, d):
            to = z + d if way == UP else z - d
            return remote(marks_ref, all_ref.at[z], m_send.at[way, d], m_recv.at[way, d], {"expert": to})

        def take(way, d):
            dst = all_ref.at[z - d if way == UP else z + d]
            remote(dst, dst, m_send.at[way, d], m_recv.at[way, d], {"tensor": 1 - c}).wait_recv()

        for d in range(1, nz):
            for way in (UP, DOWN):
                pl.when(z + d < nz if way == UP else z >= d)(lambda way=way, d=d: send(way, d).start())

        def step(at):
            normed, _ = norm_rows(x_ref[at, :].astype(f32), gain_ref[...])
            own[at, :] = normed.astype(bf16)

        strips(rows, step)
        gather_rows(nz, own, out_ref, *sems)
        keep.wait()
        for d in range(1, nz):
            for way in (UP, DOWN):
                pl.when(z + d < nz if way == UP else z >= d)(lambda way=way, d=d: send(way, d).wait_send())
                pl.when(z >= d if way == UP else z + d < nz)(lambda way=way, d=d: take(way, d))

    return pl.pallas_call(
        kernel,
        out_shape=[
            jax.ShapeDtypeStruct((nz * 2 * rows, width), bf16),
            jax.ShapeDtypeStruct((nz,) + marks.shape, jnp.int32),
        ],
        in_specs=[VMEM, VMEM, VMEM],
        out_specs=[ANY, ANY],
        scratch_shapes=[
            pltpu.VMEM((rows, width), bf16),
            pltpu.SemaphoreType.DMA((2, nz)),
            pltpu.SemaphoreType.DMA((2, nz)),
            pltpu.SemaphoreType.DMA,
        ]
        + gather_sems(nz),
        compiler_params=params(name),
    )(x, gain, marks)


def project_and_gather(nz, o, weight, x, gain, name):
    rows, width = x.shape
    full = 2 * rows
    cols = o.shape[1]

    def kernel(o_ref, w_ref, x_ref, gain_ref, n2_ref, h_ref, inv_ref, heads, acc, give, take, own, inv_own, a_send,
               a_recv, e_send, e_recv, i_sems, *sems):
        z, c = here()
        greet(nz)

        def inside(way, d):
            return z + d < nz if way == UP else z >= d

        def send(way, d):
            to = z + d if way == UP else z - d
            src = o_ref.at[pl.ds(pl.multiple_of(to * full, full), full)]
            return remote(src, heads.at[way, d], a_send.at[way, d], a_recv.at[way, d], {"expert": to})

        for d in range(nz - 1, 0, -1):
            for way in (UP, DOWN):
                pl.when(inside(way, d))(lambda way=way, d=d: send(way, d).start())

        tile = 512 if width % 512 == 0 else width

        def project(block, left, fresh):
            at = pl.ds(pl.multiple_of(block * cols, cols), cols)

            def one(i, carry):
                to = pl.ds(pl.multiple_of(i * tile, tile), tile)
                value = lax.dot_general(
                    left(), w_ref[to, at], (((1,), (1,)), ((), ())), preferred_element_type=f32
                )
                acc[:, to] = value if fresh else acc[:, to] + value
                return carry

            lax.fori_loop(0, width // tile, one, 0)

        project(z, lambda: o_ref[pl.ds(pl.multiple_of(z * full, full), full), :], True)
        for d in range(1, nz):
            for way in (UP, DOWN):
                @pl.when(z >= d if way == UP else z + d < nz)
                def _(way=way, d=d):
                    remote(
                        heads.at[way, d], heads.at[way, d], a_send.at[way, d], a_recv.at[way, d], {"tensor": 1 - c}
                    ).wait_recv()
                    project(z - d if way == UP else z + d, lambda: heads[way, d], False)

        def pack(at):
            give[at, :] = acc[pl.ds(pl.multiple_of((1 - c) * rows + at.start, STRIP), STRIP), :].astype(bf16)

        strips(rows, pack)
        swap = remote(give, take, e_send, e_recv, {"tensor": 1 - c})
        swap.start()
        swap.wait_recv()

        def norm(at):
            mixed = acc[pl.ds(pl.multiple_of(c * rows + at.start, STRIP), STRIP), :] + take[at, :].astype(f32)
            h = x_ref[at, :].astype(f32) + mixed
            normed, inverse = norm_rows(h, gain_ref[...])
            h_ref[at, :] = h
            own[at, :] = normed.astype(bf16)
            inv_own[at, :] = jnp.broadcast_to(inverse, (STRIP, 128))

        strips(rows, norm)
        spot = inv_ref.at[pl.ds(pl.multiple_of(c * rows, rows), rows)]
        keep = pltpu.make_async_copy(inv_own, spot, i_sems.at[0])
        pass_on = remote(inv_own, spot, i_sems.at[1], i_sems.at[2], {"tensor": 1 - c})
        keep.start()
        pass_on.start()
        gather_rows(nz, own, n2_ref, *sems)
        keep.wait()
        pass_on.wait()
        swap.wait_send()
        for d in range(1, nz):
            for way in (UP, DOWN):
                pl.when(inside(way, d))(lambda way=way, d=d: send(way, d).wait_send())

    return pl.pallas_call(
        kernel,
        out_shape=[
            jax.ShapeDtypeStruct((nz * full, width), bf16),
            jax.ShapeDtypeStruct((rows, width), f32),
            jax.ShapeDtypeStruct((full, 128), f32),
        ],
        in_specs=[VMEM] * 4,
        out_specs=[ANY, VMEM, ANY],
        scratch_shapes=[
            pltpu.VMEM((2, nz, full, cols), bf16),
            pltpu.VMEM((full, width), f32),
            pltpu.VMEM((rows, width), bf16),
            pltpu.VMEM((rows, width), bf16),
            pltpu.VMEM((rows, width), bf16),
            pltpu.VMEM((rows, 128), f32),
            pltpu.SemaphoreType.DMA((2, nz)),
            pltpu.SemaphoreType.DMA((2, nz)),
            pltpu.SemaphoreType.DMA,
            pltpu.SemaphoreType.DMA,
            pltpu.SemaphoreType.DMA((3,)),
        ]
        + gather_sems(nz),
        compiler_params=params(name),
    )(o, weight, x, gain)


def swap_rows(nz, own, out_ref, sems):
    z, c = here()
    rows = own.shape[0]
    spot = out_ref.at[pl.ds(pl.multiple_of(c * rows, rows), rows)]
    keep = pltpu.make_async_copy(own, spot, sems.at[0])
    pass_on = remote(own, spot, sems.at[1], sems.at[2], {"tensor": 1 - c})
    keep.start()
    pass_on.start()
    keep.wait()
    pass_on.wait()


TILE = 256
TALL = 512
LANES = 128


def nt_dot(left, right):
    return lax.dot_general(left, right, (((1,), (1,)), ((), ())), preferred_element_type=f32)


def nn_dot(left, right):
    return jnp.dot(left, right, preferred_element_type=f32)


def tiles(count, step, size=TILE):
    def one(i, carry):
        step(i, pl.ds(pl.multiple_of(i * size, size), size))
        return carry

    lax.fori_loop(0, count, one, 0)


def padded(columns):
    return -(-columns // LANES) * LANES


def window(columns, place):
    first = place * columns // LANES * LANES
    return first, place * columns - first


def window_width(columns, places):
    return max(padded(window(columns, i)[1] + columns) for i in range(places))


def hidden_layer(nz, n2, dy, gate, weights, groups):
    seq, width = n2.shape
    shared = weights[0].ndim == 2
    experts = 1 if shared else weights[0].shape[0]
    buffers = min(experts, 2)
    ffn = weights[0].shape[1] // nz if shared else weights[0].shape[1]
    held = window_width(ffn, nz) if shared else ffn
    kept = held if shared else padded(ffn)
    block = width // groups
    lane = min(block, TILE)
    per = TILE // lane
    count, slabs = seq // TILE, width // TILE
    strip = 32
    product = nn_dot if shared else nt_dot
    w_shape = (width, held) if shared else (held, width)

    def kernel(n2_hbm, dy_hbm, wg_hbm, wu_hbm, wd_hbm, gate_ref, grad_hbm, da_hbm, db_hbm, gu_hbm, dgate_ref,
               n2_ref, dy_ref, wg, wu, wd, a, b, back, da, db, gu, turned, slab, in_sem, row_sem, out_sem, slab_sem):
        z = lax.axis_index("expert")
        first = pl.multiple_of(z * ffn // LANES * LANES, LANES)
        skip = z * ffn - first

        def pick(ref, e):
            return ref.at[:, pl.ds(first, held)] if shared else ref.at[e]

        def weight(i, e):
            slot = lax.rem(e, buffers)
            src, dst = ((wg_hbm, wg), (wu_hbm, wu), (wd_hbm, wd))[i]
            return pltpu.make_async_copy(pick(src, e), dst.at[slot], in_sem.at[i, slot])

        rows_in = [
            pltpu.make_async_copy(n2_hbm, n2_ref, row_sem.at[0]), pltpu.make_async_copy(dy_hbm, dy_ref, row_sem.at[1])
        ]
        weight(0, 0).start()
        rows_in[0].start()
        weight(1, 0).start()
        weight(2, 0).start()
        rows_in[1].start()
        if kept > held:
            for ref in (da, db, gu):
                ref[:, held:] = jnp.zeros((seq, kept - held), bf16)

        def expert(e, carry):
            slot = lax.rem(e, buffers)
            weight(0, e).wait()
            pl.when(e == 0)(rows_in[0].wait)

            def one(i, at):
                a[at, :] = product(n2_ref[at, :], wg[slot])

            tiles(seq // TALL, one, TALL)
            weight(1, e).wait()

            def two(i, at):
                b[at, :] = product(n2_ref[at, :], wu[slot])

            tiles(seq // TALL, two, TALL)
            weight(2, e).wait()
            pl.when(e == 0)(rows_in[1].wait)
            if experts > 1:

                @pl.when(e + 1 < experts)
                def _():
                    for i in range(3):
                        weight(i, e + 1).start()

            def three(i, at):
                back[...] = product(dy_ref[at, :], wd[slot])

                def point(j, carry):
                    row = pl.ds(pl.multiple_of(i * TILE + j * strip, strip), strip)
                    local = pl.ds(pl.multiple_of(j * strip, strip), strip)
                    av, bv, kv, gv = a[row, :], b[row, :], back[local, :], gate_ref[e, row, :]
                    sig = 1.0 / (1.0 + jnp.exp(-av))
                    act = av * sig
                    u = act * bv
                    if shared:
                        column = lax.broadcasted_iota(jnp.int32, (strip, held), 1)
                        mine = jnp.logical_and(column >= skip, column < skip + ffn)
                        u, kv = jnp.where(mine, u, 0.0), jnp.where(mine, kv, 0.0)
                    dgate_ref[e, row, :] = jnp.sum(u * kv, axis=-1, keepdims=True)
                    gu[row, :held] = (gv * u).astype(bf16)
                    du = gv * kv
                    da[row, :held] = (du * bv * (sig + act * (1.0 - sig))).astype(bf16)
                    db[row, :held] = (du * act).astype(bf16)
                    return carry

                lax.fori_loop(0, TILE // strip, point, 0)
                for k, ref in enumerate((da, db, gu)):
                    turned[k, :, at] = ref[at, :held].T

            tiles(count, three)
            saves = [
                pltpu.make_async_copy(src, dst.at[e], out_sem.at[i])
                for i, (src, dst) in enumerate(((da, da_hbm), (db, db_hbm), (gu, gu_hbm)))
            ]
            for save in saves:
                save.start()

            def leave(i):
                slot = lax.rem(i, 2)
                below = pl.ds(pl.multiple_of(e * 3 * ffn, 16), 3 * ffn)
                if per > 1:
                    dst = grad_hbm.at[pl.ds(i * per, per), below]
                else:
                    many = block // TILE
                    to = pl.ds(pl.multiple_of(lax.rem(i, many) * TILE, TILE), TILE)
                    dst = grad_hbm.at[pl.ds(i // many, 1), below, to]
                return pltpu.make_async_copy(slab.at[slot], dst, slab_sem.at[slot])

            def four(i, at):
                slot = lax.rem(i, 2)
                pl.when(i >= 2)(lambda: leave(i).wait())
                for k, right in enumerate((n2_ref, n2_ref, dy_ref)):
                    left = turned[k, pl.ds(pl.multiple_of(skip, 16), ffn), :] if shared else turned[k]
                    value = nn_dot(left, right[:, at]).astype(bf16)
                    for j in range(per):
                        slab[slot, j, k * ffn : (k + 1) * ffn, :] = value[:, j * lane : (j + 1) * lane]
                leave(i).start()

            tiles(slabs, four)
            leave(slabs - 2).wait()
            leave(slabs - 1).wait()
            for save in saves:
                save.wait()
            return carry

        if experts == 1:
            expert(0, 0)
        else:
            lax.fori_loop(0, experts, expert, 0)

    hidden = jax.ShapeDtypeStruct((experts, seq, kept), bf16)
    return pl.pallas_call(
        kernel,
        out_shape=[
            jax.ShapeDtypeStruct((groups, experts * 3 * ffn, block), bf16), hidden, hidden, hidden,
            jax.ShapeDtypeStruct((experts, seq, 1), f32),
        ],
        in_specs=[ANY] * 5 + [VMEM],
        out_specs=[ANY] * 4 + [VMEM],
        scratch_shapes=[
            pltpu.VMEM((seq, width), bf16), pltpu.VMEM((seq, width), bf16),
            pltpu.VMEM((buffers,) + w_shape, bf16), pltpu.VMEM((buffers,) + w_shape, bf16), pltpu.VMEM((buffers,) + w_shape, bf16),
            pltpu.VMEM((seq, held), f32), pltpu.VMEM((seq, held), f32), pltpu.VMEM((TILE, held), f32),
            pltpu.VMEM((seq, kept), bf16), pltpu.VMEM((seq, kept), bf16), pltpu.VMEM((seq, kept), bf16),
            pltpu.VMEM((3, held, seq), bf16),
            pltpu.VMEM((2, per, 3 * ffn, lane), bf16),
            pltpu.SemaphoreType.DMA((3, buffers)), pltpu.SemaphoreType.DMA((2,)), pltpu.SemaphoreType.DMA((3,)),
            pltpu.SemaphoreType.DMA((2,)),
        ],
        compiler_params=pltpu.CompilerParams(vmem_limit_bytes=58 * 1024 * 1024),
    )(n2, dy, *weights, gate)


PART = 512


class Products:
    def __init__(self, nz, experts, shared, extra):
        self.nz, self.experts, self.shared = nz, experts, shared
        _, self.seq, self.kept = experts[0][0][0].shape
        _, self.ffn, self.width = experts[0][1][0].shape
        self.held = shared[0][0][0].shape[2]
        self.own = shared[0][1].shape[1] // nz
        self.more = [] if extra is None else list(extra)
        self.inputs = (
            [left[0] for left, _ in experts] + [right[0] for _, right in experts] + [left[0] for left, _ in shared]
            + [right for _, right in shared] + self.more
        )
        ne, ns = len(experts), len(shared)
        self.specs = [ANY] * (2 * (ne + ns)) + [VMEM] * len(self.more)
        self.scratch = [
            pltpu.VMEM((self.seq, ne * self.kept), bf16), pltpu.VMEM((ne * self.kept, self.width), bf16),
            pltpu.VMEM((self.seq, ns * self.held), bf16), pltpu.VMEM((self.width, ns * self.held), bf16),
            pltpu.SemaphoreType.DMA((self.width // PART, ne + ns)), pltpu.SemaphoreType.DMA((nz, ne + ns)),
        ]

    def bind(self, refs, scratch):
        ne, ns = len(self.experts), len(self.shared)
        self.left, self.right, self.sleft, self.sright, self.r_sem, self.l_sem = scratch
        self.e_left, self.e_right = refs[:ne], refs[ne : 2 * ne]
        self.s_left, self.s_right = refs[2 * ne : 2 * ne + ns], refs[2 * ne + ns : 2 * (ne + ns)]
        self.small = refs[2 * (ne + ns) :]
        self.first = pl.multiple_of(lax.axis_index("expert") * self.own // LANES * LANES, LANES)

    def rights(self, j):
        to = pl.ds(pl.multiple_of(j * PART, PART), PART)
        for i, (_, (_, index)) in enumerate(self.experts):
            dst = self.right.at[pl.ds(i * self.kept, self.ffn), to]
            yield pltpu.make_async_copy(self.e_right[i].at[index, :, to], dst, self.r_sem.at[j, i])
        for i in range(len(self.shared)):
            src = self.s_right[i].at[to, pl.ds(self.first, self.held)]
            dst = self.sright.at[to, pl.ds(i * self.held, self.held)]
            yield pltpu.make_async_copy(src, dst, self.r_sem.at[j, len(self.experts) + i])

    def lefts(self, b):
        rows = self.seq // self.nz
        at = pl.ds(pl.multiple_of(b * rows, rows), rows)
        for i, ((_, index), _) in enumerate(self.experts):
            dst = self.left.at[at, pl.ds(i * self.kept, self.kept)]
            yield pltpu.make_async_copy(self.e_left[i].at[index, at], dst, self.l_sem.at[b, i])
        for i, ((_, index), _) in enumerate(self.shared):
            dst = self.sleft.at[at, pl.ds(i * self.held, self.held)]
            yield pltpu.make_async_copy(self.s_left[i].at[index, at], dst, self.l_sem.at[b, len(self.experts) + i])

    def fetch(self, order):
        for copy in self.lefts(order(0)):
            copy.start()
        for j in range(self.width // PART):
            for copy in self.rights(j):
                copy.start()
        for k in range(1, self.nz):
            for copy in self.lefts(order(k)):
                copy.start()
        if self.kept > self.ffn:
            for i in range(len(self.experts)):
                self.right[i * self.kept + self.ffn : (i + 1) * self.kept, :] = jnp.zeros(
                    (self.kept - self.ffn, self.width), bf16
                )

    def block(self, k, b, out, start, end):
        rows = self.seq // self.nz
        at = pl.ds(pl.multiple_of(b * rows, rows), rows)
        if start == 0:
            for copy in self.lefts(b):
                copy.wait()

        def one(j, carry):
            @pl.when(k == 0)
            def _():
                for copy in self.rights(j):
                    copy.wait()

            to = pl.ds(pl.multiple_of(j * PART, PART), PART)
            value = nn_dot(self.left[at, :], self.right[:, to]) + nt_dot(self.sleft[at, :], self.sright[to, :])
            if self.more:
                value += nt_dot(self.small[0][at, :], self.small[1][to, :])
            out[at, to] = value.astype(bf16)
            return carry

        lax.fori_loop(start, end, one, 0)


def reduce_and_gather(nz, products, h, gain, upstream, name):
    rows, width = h.shape
    n_in, n_scratch = len(products.inputs), len(products.scratch)

    def kernel(*refs):
        p_refs, (h_ref, gain_ref, up_ref, out_ref, dh_ref, gg_ref) = refs[:n_in], refs[n_in : n_in + 6]
        rest = refs[n_in + 6 :]
        p_scratch, (part, own), rest = rest[:n_scratch], rest[n_scratch : n_scratch + 2], rest[n_scratch + 2 :]
        scratch, sems = rest[:REDUCE_SCRATCH], rest[REDUCE_SCRATCH:]
        total = scratch[3]
        products.bind(p_refs, p_scratch)
        reducer = Reducer(nz, part, *scratch)
        products.fetch(reducer.block)
        greet(nz)
        ends = reducer.ends()

        def one(s, carry):
            products.block(s, reducer.block(s), part, 0, 1)
            pl.when(jnp.logical_and(ends, s >= 1))(lambda: reducer.forward(s - 1))
            products.block(s, reducer.block(s), part, 1, width // PART)
            reducer.begin(s)
            pl.when(jnp.logical_and(jnp.logical_not(ends), s >= 2))(lambda: reducer.forward(s - 2))
            return carry

        lax.fori_loop(0, nz, one, 0)
        pl.when(jnp.logical_not(ends))(lambda: reducer.forward(nz - 2))
        reducer.finish()
        gg_ref[...] = jnp.zeros_like(gg_ref)

        def step(at):
            change, along = norm_back(h_ref[at, :], gain_ref[...], total[at, :])
            dh = up_ref[at, :].astype(f32) + change
            dh_ref[at, :] = dh
            own[at, :] = dh.astype(bf16)
            gg_ref[...] += along

        strips(rows, step)
        gather_rows(nz, own, out_ref, *sems)
        reducer.drain()

    return pl.pallas_call(
        kernel,
        out_shape=[
            jax.ShapeDtypeStruct((nz * 2 * rows, width), bf16),
            jax.ShapeDtypeStruct((rows, width), f32),
            jax.ShapeDtypeStruct((STRIP, width), f32),
        ],
        in_specs=products.specs + [VMEM] * 3,
        out_specs=[ANY, VMEM, VMEM],
        scratch_shapes=products.scratch
        + [pltpu.VMEM((nz * 2 * rows, width), bf16), pltpu.VMEM((rows, width), bf16)]
        + reduce_scratch(nz, rows, width)
        + gather_sems(nz),
        compiler_params=params(name),
    )(*products.inputs, h, gain, upstream)


def reduce_last(nz, d_heads, weights, x, gain, dh, products, h, name):
    rows, width = x.shape
    n_in, n_scratch = len(products.inputs), len(products.scratch)

    def kernel(*refs):
        p_refs, (d_ref, w_ref, x_ref, gain_ref, dh_ref, h_ref, in_ref, out_ref, gg_ref) = (
            refs[:n_in], refs[n_in : n_in + 9],
        )
        rest = refs[n_in + 9 :]
        p_scratch, (d_part, b_part, own, sems), rest = (
            rest[:n_scratch], rest[n_scratch : n_scratch + 4], rest[n_scratch + 4 :],
        )
        d_scratch, b_scratch = rest[:REDUCE_SCRATCH], rest[REDUCE_SCRATCH:]
        d_total, b_total = d_scratch[3], b_scratch[3]
        products.bind(p_refs, p_scratch)
        first, second = Reducer(nz, d_part, *d_scratch), Reducer(nz, b_part, *b_scratch)
        products.fetch(second.block)
        greet(nz)
        z, c = here()
        ends = first.ends()
        middle = jnp.logical_not(ends)

        def inner(block):
            at = pl.ds(pl.multiple_of(block * 2 * rows, 2 * rows), 2 * rows)

            def one(j, carry):
                to = pl.ds(pl.multiple_of(j * PART, PART), PART)
                d_part[at, to] = nt_dot(d_ref[at, :], w_ref[to, :]).astype(bf16)
                return carry

            lax.fori_loop(0, width // PART, one, 0)

        def one(s, carry):
            inner(first.block(s))
            first.begin(s)
            pl.when(jnp.logical_and(ends, s >= 1))(lambda: first.forward(s - 1))
            return carry

        def two(s, carry):
            products.block(s, second.block(s), b_part, 0, width // PART)
            second.begin(s)

            @pl.when(s >= 1)
            def _():
                pl.when(ends)(lambda: second.forward(s - 1))
                pl.when(middle)(lambda: first.forward(s - 1))

            return carry

        def three(s, carry):
            pl.when(middle)(lambda: second.forward(s))
            return carry

        lax.fori_loop(0, nz, one, 0)
        lax.fori_loop(0, nz, two, 0)
        lax.fori_loop(0, nz - 1, three, 0)
        first.finish()
        gg_ref[...] = jnp.zeros_like(gg_ref)

        def step(at):
            change, along = norm_back(x_ref[at, :].astype(f32), gain_ref[...], d_total[at, :])
            own[0, at, :] = dh_ref[at, :] + change
            gg_ref[...] += along

        strips(rows, step)

        def leave(i, ref):
            spot = ref.at[pl.ds(pl.multiple_of(c * rows, rows), rows)]
            return (
                pltpu.make_async_copy(own.at[i], spot, sems.at[i, 0]),
                remote(own.at[i], spot, sems.at[i, 1], sems.at[i, 2], {"tensor": 1 - c}),
            )

        for copy in leave(0, in_ref):
            copy.start()
        second.finish()

        def last(at):
            own[1, at, :] = h_ref[at, :] + b_total[at, :]

        strips(rows, last)
        for copy in leave(1, out_ref):
            copy.start()
        first.drain()
        second.drain()
        for copy in (*leave(0, in_ref), *leave(1, out_ref)):
            copy.wait()

    return pl.pallas_call(
        kernel,
        out_shape=[
            jax.ShapeDtypeStruct((2 * rows, width), f32),
            jax.ShapeDtypeStruct((2 * rows, width), f32),
            jax.ShapeDtypeStruct((STRIP, width), f32),
        ],
        in_specs=products.specs + [VMEM] * 6,
        out_specs=[ANY, ANY, VMEM],
        scratch_shapes=products.scratch
        + [
            pltpu.VMEM((nz * 2 * rows, width), bf16), pltpu.VMEM((nz * 2 * rows, width), bf16),
            pltpu.VMEM((2, rows, width), f32), pltpu.SemaphoreType.DMA((2, 3)),
        ]
        + reduce_scratch(nz, rows, width) * 2,
        compiler_params=params(name),
    )(*products.inputs, d_heads, weights, x, gain, dh, h)


def assemble(nz, box, columns):
    block = box.shape[2]
    count = 3

    def kernel(box_ref, *outs):
        for k in range(count):
            for b in range(nz):
                value = box_ref[b, k * columns : (k + 1) * columns, :].astype(f32).T
                outs[k][:, b * columns : (b + 1) * columns] = value

    return pl.pallas_call(
        kernel,
        out_shape=[jax.ShapeDtypeStruct((block, nz * columns), f32)] * count,
        in_specs=[VMEM],
        out_specs=[VMEM] * count,
        compiler_params=pltpu.CompilerParams(vmem_limit_bytes=40 * 1024 * 1024),
    )(box)


def finish_gradients(nz, part, splits, small, experts, name):
    n, rows, lanes = small.shape
    block = part.shape[0] // nz
    cols = part.shape[1] // splits
    local, kinds, ffn, width = experts.shape

    def kernel(part_ref, small_ref, experts_ref, *rest):
        outs, (sum_ref,), e_outs = rest[:splits], rest[splits : splits + 1], rest[splits + 1 : splits + 1 + kinds]
        (box, s_box, total, other, wide, send_sem, recv_sem, s_send, s_recv, swap_sem, out_sem) = rest[splits + 1 + kinds :]
        z, c = here()
        me = lax.axis_index("dp") * nz + z
        barrier = pltpu.get_barrier_semaphore()

        def peer(k):
            at = lax.rem(me + k, n)
            return at, {"dp": at // nz, "expert": lax.rem(at, nz)}

        pl.semaphore_signal(barrier, inc=1, device_id={"tensor": 1 - c}, device_id_type=MESH)
        for k in range(1, n):
            pl.semaphore_signal(barrier, inc=1, device_id=peer(k)[1], device_id_type=MESH)
        pl.semaphore_wait(barrier, n)

        def send(way, d):
            to = z + d if way == UP else z - d
            src = part_ref.at[pl.ds(pl.multiple_of(to * block, block), block)]
            return remote(src, box.at[z], send_sem.at[way, d], recv_sem.at[way, d], {"expert": to})

        def take(way, d):
            dst = box.at[z - d if way == UP else z + d]
            remote(dst, dst, send_sem.at[way, d], recv_sem.at[way, d], {"tensor": 1 - c}).wait_recv()

        def send_small(k):
            at, device = peer(k)
            return remote(small_ref.at[at], s_box.at[k], s_send.at[k], s_recv.at[k], device)

        for k in range(1, n):
            send_small(k).start()
        for d in range(nz - 1, 0, -1):
            for way in (UP, DOWN):
                pl.when(z + d < nz if way == UP else z >= d)(lambda way=way, d=d: send(way, d).start())
        box[z] = part_ref[pl.ds(pl.multiple_of(z * block, block), block), :]
        leaves = [pltpu.make_async_copy(wide.at[i], e_outs[i], out_sem.at[i]) for i in range(kinds)]
        for i in range(kinds):
            for e in range(local):
                def widen(at, i=i, e=e):
                    wide[i, e, at, :] = experts_ref[e, i, at, :].astype(f32)

                strips(ffn, widen)
            leaves[i].start()
        total[...] = small_ref[me]
        for k in range(1, n):
            send_small(k).wait_recv()
            total[...] += s_box[k]
        swap = remote(total, other, swap_sem.at[0], swap_sem.at[1], {"tensor": 1 - c})
        swap.start()
        swap.wait_recv()
        sum_ref[...] = total[...] + other[...]
        for d in range(1, nz):
            for way in (UP, DOWN):
                pl.when(z >= d if way == UP else z + d < nz)(lambda way=way, d=d: take(way, d))
        for j in range(splits):
            for b in range(nz):
                outs[j][:, b * cols : (b + 1) * cols] = box[b, :, j * cols : (j + 1) * cols].astype(f32)
        swap.wait_send()
        for k in range(1, n):
            send_small(k).wait_send()
        for d in range(1, nz):
            for way in (UP, DOWN):
                pl.when(z + d < nz if way == UP else z >= d)(lambda way=way, d=d: send(way, d).wait_send())
        for leave in leaves:
            leave.wait()

    return pl.pallas_call(
        kernel,
        out_shape=[jax.ShapeDtypeStruct((block, nz * cols), f32)] * splits
        + [jax.ShapeDtypeStruct((rows, lanes), f32)]
        + [jax.ShapeDtypeStruct((local, ffn, width), f32)] * kinds,
        in_specs=[VMEM] * 3,
        out_specs=[VMEM] * (splits + 1) + [ANY] * kinds,
        scratch_shapes=[
            pltpu.VMEM((nz, block, part.shape[1]), bf16), pltpu.VMEM((n, rows, lanes), f32),
            pltpu.VMEM((rows, lanes), f32), pltpu.VMEM((rows, lanes), f32),
            pltpu.VMEM((kinds, local, ffn, width), f32),
            pltpu.SemaphoreType.DMA((2, nz)), pltpu.SemaphoreType.DMA((2, nz)),
            pltpu.SemaphoreType.DMA((n,)), pltpu.SemaphoreType.DMA((n,)), pltpu.SemaphoreType.DMA((2,)),
            pltpu.SemaphoreType.DMA((kinds,)),
        ],
        compiler_params=params(name),
    )(part, small, experts)


SEQ_AXES = ("expert", "tensor")


def cross_rows(left, right):
    return lax.dot_general(left, right, (((0,), (0,)), ((), ())), preferred_element_type=f32)


def cross_cols(left, right):
    return lax.dot_general(left, right, (((1,), (1,)), ((), ())), preferred_element_type=f32)


def dot(left, right):
    return jnp.dot(left, right, preferred_element_type=f32)


def two_parts(values):
    high = values.astype(bf16)
    return high, (values - high.astype(f32)).astype(bf16)


def body(
    tokens, segments, routes, norm1_gain, q_weight, k_weight, v_weight, o_weight, norm2_gain,
    router_weight, shared_gate_vector, shared_gate_weight, shared_up_weight, shared_down_weight,
    expert_gate_weight, expert_up_weight, expert_down_weight, out_grad,
):
    nz = lax.axis_size("expert")
    nc = lax.axis_size("tensor")
    z = lax.axis_index("expert")
    c = lax.axis_index("tensor")
    rows, width = tokens.shape
    own_rows = rows // nc
    local_count, _, ffn = expert_gate_weight.shape
    expert_count = local_count * nz
    head_cols = q_weight.shape[1] // nz
    shared_cols = shared_gate_weight.shape[1] // nz
    heads = head_cols // HD
    seq = rows * nz
    scale = HD ** (-0.5)
    gain1 = norm1_gain.astype(f32)[None]
    gain2 = norm2_gain.astype(f32)[None]

    def own(values):
        return lax.dynamic_slice_in_dim(values, c * own_rows, own_rows, 0)

    def head_slice(values):
        return lax.dynamic_slice_in_dim(values, z * head_cols, head_cols, 1)

    x_all_rows = tokens.astype(f32)
    inverse_one_rows = lax.rsqrt(jnp.mean(x_all_rows * x_all_rows, axis=-1) + epsilon)
    x = own(tokens)
    marks = jnp.concatenate([segments, routes.T, jnp.zeros((7 - routes.shape[1], rows), jnp.int32)], axis=0)
    n1, all_marks = first_gather(nz, x, gain1, marks, 0)
    labels = all_marks[:, 0].reshape(seq)
    all_routes = jnp.transpose(all_marks[:, 1 : 1 + routes.shape[1]], (0, 2, 1)).reshape(seq, routes.shape[1])
    upstream = own(out_grad)
    upstream_later, _ = lax.optimization_barrier((upstream, n1))
    dy = lax.all_gather(upstream_later, SEQ_AXES, axis=0, tiled=True)

    wo = head_slice(o_weight)
    w_heads = jnp.concatenate([head_slice(q_weight), head_slice(k_weight), head_slice(v_weight)], axis=1)
    qkv = dot(n1, w_heads).astype(bf16)
    q, k, v = (qkv[:, i * head_cols : (i + 1) * head_cols].reshape(seq, heads, HD) for i in range(3))
    pos = jnp.arange(seq)
    allowed = (pos[None, :] <= pos[:, None]) & (labels[None, :] == labels[:, None])

    raw = jnp.einsum("qhd,khd->hqk", q, k, preferred_element_type=f32) * scale
    scores = jnp.where(allowed[None], raw, -jnp.inf)
    expd = jnp.exp(scores - jnp.max(scores, axis=-1, keepdims=True))
    p_low = (expd / jnp.sum(expd, axis=-1, keepdims=True)).astype(bf16)
    o = jnp.einsum("hqk,khd->qhd", p_low, v, preferred_element_type=f32).reshape(seq, head_cols).astype(bf16)
    n2, h, inverse_two = project_and_gather(nz, o, o_weight, x, gain2, 1)

    probs = jax.nn.softmax(dot(n2, router_weight), axis=-1)
    chosen = jnp.any(all_routes[:, :, None] == jnp.arange(expert_count)[None, None, :], axis=1)
    gates = jnp.where(chosen, probs, 0.0)
    sigma = jax.nn.sigmoid(dot(n2, shared_gate_vector))

    turned = [jnp.swapaxes(w, 1, 2) for w in (expert_gate_weight, expert_up_weight, expert_down_weight)]
    shared_weights = (shared_gate_weight, shared_up_weight, shared_down_weight)
    ndp = lax.axis_size("dp")
    grad_s, da_s, db_s, gu_s, dgate_s = hidden_layer(nz, n2, dy, sigma[None, :, None], shared_weights, ndp * nz)
    n2_now, dgate_s = lax.optimization_barrier((n2, dgate_s))
    gate = jnp.swapaxes(lax.dynamic_slice_in_dim(gates, z * local_count, local_count, 1), 0, 1)[:, :, None]
    grad_e, da_e, db_e, gu_e, dgate_e = hidden_layer(nz, n2_now, dy, gate, turned, ndp)

    d_expert = jnp.swapaxes(dgate_e[:, :, 0], 0, 1)
    d_probs = lax.dynamic_update_slice_in_dim(jnp.zeros_like(probs), d_expert, z * local_count, 1)
    d_probs = jnp.where(chosen, d_probs, 0.0)
    d_logits = probs * (d_probs - jnp.sum(probs * d_probs, axis=-1, keepdims=True))
    d_vector = dgate_s[0] * (sigma * (1.0 - sigma))[:, None]
    small = jnp.concatenate([d_logits, d_vector], axis=1)
    small_high, small_low = two_parts(small)
    small_weights = jnp.concatenate([router_weight, shared_gate_vector[:, None]], axis=1)
    fill = ((0, 0), (0, 128 - small.shape[1]))
    experts = range(local_count)
    d_n2 = Products(
        nz,
        [((da_e, i), (turned[0], i)) for i in experts] + [((db_e, i), (turned[1], i)) for i in experts],
        [((da_s, 0), shared_gate_weight), ((db_s, 0), shared_up_weight)],
        (jnp.pad(small_high, fill), jnp.pad(small_weights, fill)),
    )
    small_grad = cross_rows(n2, jnp.concatenate([small_high, small_low], axis=1))
    small_grad = small_grad[:, : expert_count + 1] + small_grad[:, expert_count + 1 :]


    def over_dp(grad):
        rows = grad.reshape(-1, grad.shape[-1])
        return lax.psum_scatter(rows, "dp", scatter_dimension=0, tiled=True)

    shared_part = over_dp(grad_s).reshape((nz,) + grad_s.shape[1:])
    expert_part = over_dp(grad_e).reshape(local_count, 3, ffn, -1)
    dhr, dh, grad_two = reduce_and_gather(nz, d_n2, h, gain2, upstream, 2)
    shared_part, dhr = lax.optimization_barrier((shared_part, dhr))
    shared_box = lax.all_to_all(shared_part, "expert", split_axis=0, concat_axis=0, tiled=True)
    d_o = dot(dhr, wo).astype(bf16).reshape(seq, heads, HD)
    grad_o = cross_rows(dhr, o)

    d_v = jnp.einsum("hqk,qhd->khd", p_low, d_o, preferred_element_type=f32)
    dp = jnp.einsum("qhd,khd->hqk", d_o, v, preferred_element_type=f32)
    mean = jnp.sum(d_o.astype(f32) * o.reshape(seq, heads, HD).astype(f32), axis=-1).T
    ds = (p_low.astype(f32) * (dp - mean[:, :, None])).astype(bf16)
    d_q = jnp.einsum("hqk,khd->qhd", ds, k, preferred_element_type=f32) * scale
    d_k = jnp.einsum("hqk,qhd->khd", ds, q, preferred_element_type=f32) * scale
    d_heads = jnp.concatenate([t.reshape(seq, head_cols).astype(bf16) for t in (d_q, d_k, d_v)], axis=1)
    s_gate, s_up, s_down = assemble(nz, shared_box, shared_cols)
    d_heads, s_gate = lax.optimization_barrier((d_heads, s_gate))
    grad_attention = jnp.concatenate(
        [cross_rows(n1, d_heads).astype(bf16), grad_o.astype(bf16)], axis=1
    )
    attention_part = over_dp(grad_attention)
    branch = Products(
        nz,
        [((gu_e, i), (turned[2], i)) for i in experts],
        [((gu_s, 0), shared_down_weight)],
        None,
    )
    dh_now, _ = lax.optimization_barrier((dh, grad_attention))
    input_grad, layer_out, grad_one = reduce_last(
        nz, d_heads, w_heads, x, gain1, dh_now, branch, h, 3
    )
    stats = jnp.stack([inverse_one_rows, inverse_two[:, 0]])

    small_rows = jnp.concatenate(
        [
            jnp.sum(grad_one, axis=0)[None], jnp.sum(grad_two, axis=0)[None], small_grad.T,
            jnp.zeros((13 - expert_count, width), f32),
        ],
        axis=0,
    )
    small_rows, expert_part = lax.optimization_barrier((small_rows, expert_part))
    count = ndp * nz
    small_blocks = jnp.swapaxes(small_rows.reshape(16, count, width // count), 0, 1)
    g_q, g_k, g_v, g_o, small_all, *wide = finish_gradients(nz, attention_part, 4, small_blocks, expert_part, 6)
    e_gate, e_up, e_down = (jnp.swapaxes(t, 1, 2) for t in wide)
    g_one, g_two, g_router, g_vector = small_all[0], small_all[1], small_all[2 : 2 + expert_count].T, small_all[2 + expert_count]
    return (
        layer_out, input_grad, stats, g_one, g_q, g_k, g_v, g_o, g_two, g_router, g_vector,
        s_gate, s_up, s_down, e_gate, e_up, e_down,
    )


def solution(mesh):
    both = ("dp", "expert")
    cols = P(None, "tensor")
    placed = (
        P(both, None), P("dp", "expert"), P(both, None), P(), cols, cols, cols, cols, P(), P(), P(),
        cols, cols, cols, P("expert", None, "tensor"), P("expert", None, "tensor"),
        P("expert", None, "tensor"), P(both, None),
    )
    split = P(both, "tensor")
    experts = P("expert", "dp", "tensor")
    return jax.shard_map(
        body,
        mesh=mesh,
        in_specs=placed,
        out_specs=(
            P(both, None), P(both, None), P(None, both), P(both), split, split, split, split, P(both),
            P(both, None), P(both), split, split, split, experts, experts, experts,
        ),
        check_vma=False,
    )
```

```python
import functools

import jax
import jax.numpy as jnp
from jax import lax
from jax.experimental import pallas as pl
from jax.experimental.pallas import tpu as pltpu
from jax.sharding import PartitionSpec as P

HD = 128
MESH = pl.DeviceIdType.MESH
PIECES = 2
STRIP = 16
epsilon = 1e-06
f32 = jnp.float32
bf16 = jnp.bfloat16
UP, DOWN = 0, 1


def here():
    return lax.axis_index("expert"), lax.axis_index("tensor")


def greet(nz):
    z, c = here()
    barrier = pltpu.get_barrier_semaphore()

    def tell(device):
        pl.semaphore_signal(barrier, inc=1, device_id=device, device_id_type=MESH)

    tell({"tensor": 1 - c})
    for d in range(1, nz):
        tell({"expert": lax.rem(z + d, nz)})
    pl.semaphore_wait(barrier, nz)


def remote(src, dst, send, recv, device):
    return pltpu.make_async_remote_copy(
        src_ref=src, dst_ref=dst, send_sem=send, recv_sem=recv, device_id=device, device_id_type=MESH
    )


def strips(rows, step):
    def one(i, carry):
        step(pl.ds(pl.multiple_of(i * STRIP, STRIP), STRIP))
        return carry

    lax.fori_loop(0, rows // STRIP, one, 0)


GATHER_SEMS = 4


def gather_sems(nz):
    return [pltpu.SemaphoreType.DMA((2, nz, PIECES))] * GATHER_SEMS + [pltpu.SemaphoreType.DMA]


class Gather:
    def __init__(self, nz, own, out, z_send, z_recv, s_send, s_recv, local_sem):
        self.nz, self.own, self.out = nz, own, out
        self.z_send, self.z_recv, self.s_send, self.s_recv, self.local_sem = z_send, z_recv, s_send, s_recv, local_sem
        self.z, self.c = here()
        self.rows = own.shape[0]
        self.piece = self.rows // PIECES

    def origin(self, way, d):
        return self.z - d if way == UP else self.z + d

    def inside(self, way, d):
        return self.z >= d if way == UP else self.z + d < self.nz

    def onward(self, way):
        return self.z < self.nz - 1 if way == UP else self.z > 0

    def place(self, block, core, p):
        start = (block * 2 + core) * self.rows + p * self.piece
        return self.out.at[pl.ds(pl.multiple_of(start, self.piece), self.piece)]

    def source(self, way, d, p):
        if d == 0:
            return self.own.at[pl.ds(p * self.piece, self.piece)]
        return self.place(self.origin(way, d), self.c, p)

    def along(self, way, d, p):
        device = {"expert": self.z + 1 if way == UP else self.z - 1}
        dst = self.place(self.origin(way, d), self.c, p)
        return remote(self.source(way, d, p), dst, self.z_send.at[way, d, p], self.z_recv.at[way, d, p], device)

    def across(self, way, d, p):
        dst = self.place(self.origin(way, d), self.c, p)
        return remote(
            self.source(way, d, p), dst, self.s_send.at[way, d, p], self.s_recv.at[way, d, p], {"tensor": 1 - self.c}
        )

    def arrived(self, way, d, p):
        dst = self.place(self.origin(way, d), self.c, p)
        remote(dst, dst, self.z_send.at[way, d - 1, p], self.z_recv.at[way, d - 1, p], {"tensor": 1 - self.c}).wait_recv()

    def crossed(self, way, d, p):
        dst = self.place(self.origin(way, d), 1 - self.c, p)
        remote(dst, dst, self.s_send.at[way, d, p], self.s_recv.at[way, d, p], {"tensor": 1 - self.c}).wait_recv()

    def mine(self):
        dst = self.out.at[pl.ds(pl.multiple_of((self.z * 2 + self.c) * self.rows, self.rows), self.rows)]
        return pltpu.make_async_copy(self.own, dst, self.local_sem)

    def start_along(self, way):
        @pl.when(self.onward(way))
        def _():
            for p in range(PIECES):
                self.along(way, 0, p).start()

    def start_across(self):
        for p in range(PIECES):
            self.across(UP, 0, p).start()
        self.mine().start()

    def event(self, d, p):
        for way in (UP, DOWN):

            @pl.when(self.inside(way, d))
            def _(way=way):
                self.arrived(way, d, p)
                pl.when(self.onward(way))(lambda: self.along(way, d, p).start())
                self.across(way, d, p).start()

    def finish(self):
        for p in range(PIECES):
            self.crossed(UP, 0, p)
            self.across(UP, 0, p).wait_send()
            for way in (UP, DOWN):
                pl.when(self.onward(way))(lambda way=way, p=p: self.along(way, 0, p).wait_send())
                for d in range(1, self.nz):

                    @pl.when(self.inside(way, d))
                    def _(way=way, d=d, p=p):
                        self.crossed(way, d, p)
                        self.across(way, d, p).wait_send()
                        pl.when(self.onward(way))(lambda: self.along(way, d, p).wait_send())

        self.mine().wait()


def gather_rows(nz, own, out, *sems):
    gather = Gather(nz, own, out, *sems)
    gather.start_along(UP)
    gather.start_along(DOWN)
    gather.start_across()
    for d in range(1, nz):
        for p in range(PIECES):
            gather.event(d, p)
    gather.finish()


REDUCE_SCRATCH = 8


def reduce_scratch(nz, rows, width):
    return [
        pltpu.VMEM((nz, rows, width), bf16),
        pltpu.VMEM((nz + 1, rows, width), bf16),
        pltpu.VMEM((nz, rows, width), bf16),
        pltpu.VMEM((rows, width), f32),
        pltpu.SemaphoreType.DMA((nz, PIECES)),
        pltpu.SemaphoreType.DMA((nz, PIECES)),
        pltpu.SemaphoreType.DMA((nz, PIECES)),
        pltpu.SemaphoreType.DMA((nz + 1, PIECES)),
    ]


def block_order(nz, z, s):
    down = 2 * z // nz
    far = jnp.maximum(z, nz - 1 - z)
    near = nz - 1 - far
    late = s - (far - near)
    distance = jnp.where(late < 0, far - s, near - late // 2)
    sign = (1 - 2 * down) * jnp.where(late < 0, 1, 1 - 2 * lax.rem(late + nz * 2, 2))
    return z + sign * distance


class Reducer:
    def __init__(self, nz, part, side, inbox, outbox, total, s_send, s_recv, z_send, z_recv):
        self.nz, self.part, self.side, self.inbox, self.outbox, self.total = nz, part, side, inbox, outbox, total
        self.s_send, self.s_recv, self.z_send, self.z_recv = s_send, s_recv, z_send, z_recv
        self.z, self.c = here()
        self.rows = total.shape[0]
        self.piece = self.rows // PIECES

    def block(self, s):
        return block_order(self.nz, self.z, s)

    def cut(self, p):
        return pl.ds(p * self.piece, self.piece)

    def across(self, block, p):
        start = (block * 2 + 1 - self.c) * self.rows + p * self.piece
        src = self.part.at[pl.ds(pl.multiple_of(start, self.piece), self.piece)]
        return remote(
            src, self.side.at[block, self.cut(p)], self.s_send.at[block, p], self.s_recv.at[block, p],
            {"tensor": 1 - self.c},
        )

    def along(self, block, p):
        up = block > self.z
        slot = jnp.where(block == self.z - 1, self.nz, block)
        return remote(
            self.outbox.at[block, self.cut(p)], self.inbox.at[slot, self.cut(p)], self.z_send.at[block, p],
            self.z_recv.at[slot, p], {"expert": self.z + jnp.where(up, 1, -1)},
        )

    def arrived(self, slot, p):
        dst = self.inbox.at[slot, self.cut(p)]
        remote(dst, dst, self.z_send.at[0, p], self.z_recv.at[slot, p], {"tensor": 1 - self.c}).wait_recv()

    def mine(self, block, at):
        base = (block * 2 + self.c) * self.rows
        own = self.part[pl.ds(pl.multiple_of(base + at.start, STRIP), STRIP), :].astype(f32)
        return own + self.side[block, at, :].astype(f32)

    def strips(self, p, step):
        def one(i, carry):
            step(pl.ds(pl.multiple_of(p * self.piece + i * STRIP, STRIP), STRIP))
            return carry

        lax.fori_loop(0, self.piece // STRIP, one, 0)

    def ends(self):
        return jnp.logical_or(self.z == 0, self.z == self.nz - 1)

    def begin(self, s):
        for p in range(PIECES):
            self.across(self.block(s), p).start()

    def forward(self, s):
        block = self.block(s)
        behind = jnp.where(block > self.z, self.z, self.nz - 1 - self.z) > 0
        for p in range(PIECES):
            self.across(block, p).wait_recv()

            @pl.when(behind)
            def _(p=p):
                self.arrived(block, p)

                def add(at):
                    self.outbox[block, at, :] = (self.mine(block, at) + self.inbox[block, at, :].astype(f32)).astype(bf16)

                self.strips(p, add)

            @pl.when(jnp.logical_not(behind))
            def _(p=p):
                def keep(at):
                    self.outbox[block, at, :] = self.mine(block, at).astype(bf16)

                self.strips(p, keep)

            self.along(block, p).start()

    def finish(self):
        z, nz = self.z, self.nz
        for p in range(PIECES):
            self.across(z, p).wait_recv()

            def first(at):
                self.total[at, :] = self.mine(z, at)

            self.strips(p, first)
            for slot, some in ((z, z > 0), (nz, z < nz - 1)):

                @pl.when(some)
                def _(slot=slot, p=p):
                    self.arrived(slot, p)

                    def add(at):
                        self.total[at, :] += self.inbox[slot, at, :].astype(f32)

                    self.strips(p, add)

    def drain(self):
        def one(s, carry):
            block = self.block(s)
            for p in range(PIECES):
                self.across(block, p).wait_send()
                pl.when(s < self.nz - 1)(lambda p=p: self.along(block, p).wait_send())
            return carry

        lax.fori_loop(0, self.nz, one, 0)


def params(name, **more):
    return pltpu.CompilerParams(
        collective_id=name, has_side_effects=True, vmem_limit_bytes=56 * 1024 * 1024, **more
    )


VMEM = pl.BlockSpec(memory_space=pltpu.VMEM)
ANY = pl.BlockSpec(memory_space=pl.ANY)


def norm_rows(values, gain):
    inverse = lax.rsqrt(jnp.mean(values * values, axis=-1, keepdims=True) + epsilon)
    return values * inverse * gain, inverse


def norm_back(values, gain, upstream):
    inverse = lax.rsqrt(jnp.mean(values * values, axis=-1, keepdims=True) + epsilon)
    scaled = upstream * gain
    inner = jnp.mean(scaled * values, axis=-1, keepdims=True)
    change = inverse * scaled - values * inverse * inverse * inverse * inner
    return change, upstream * values * inverse


def attend(nz, x, gain, upstream, marks, weights, out_weight, gain2, name):
    rows, width = x.shape
    seq = nz * 2 * rows
    cols = weights[0].shape[1] // nz
    heads = cols // HD
    full = 2 * rows
    strip = 32
    scale = HD ** (-0.5)

    def kernel(x_ref, gain_ref, up_ref, marks_ref, gain2_ref, wq_hbm, wk_hbm, wv_hbm, wo_hbm, n1_ref, dy_ref, all_ref, qkv_ref,
               p_ref, o_ref, n2_ref, h_ref, inv_ref, own, w, scores, seg_q, seg_k, heads_in, acc, give, take_in, own2, inv_own, wo,
               w_sem, m_send, m_recv, m_local, a_send, a_recv, e_send, e_recv, i_sems, *sems):
        z, c = here()
        at = pl.ds(pl.multiple_of(z * cols, cols), cols)
        loads = [
            pltpu.make_async_copy(src.at[:, at], w.at[:, pl.ds(i * cols, cols)], w_sem.at[i])
            for i, src in enumerate((wq_hbm, wk_hbm, wv_hbm))
        ]
        loads.append(pltpu.make_async_copy(wo_hbm, wo, w_sem.at[3]))
        for load in loads:
            load.start()

        def step(strip_at):
            normed, _ = norm_rows(x_ref[strip_at, :].astype(f32), gain_ref[...])
            own[strip_at, :] = normed.astype(bf16)

        strips(rows, step)
        greet(nz)
        n1 = Gather(nz, own, n1_ref, *sems[:5])
        dy = Gather(nz, up_ref, dy_ref, *sems[5:10])
        n2 = Gather(nz, own2, n2_ref, *sems[10:])
        n1.start_along(UP)
        n1.start_along(DOWN)
        n1.start_across()
        keep = pltpu.make_async_copy(marks_ref, all_ref.at[z], m_local)
        keep.start()

        def send(way, d):
            to = z + d if way == UP else z - d
            return remote(marks_ref, all_ref.at[z], m_send.at[way, d], m_recv.at[way, d], {"expert": to})

        def take(way, d):
            dst = all_ref.at[z - d if way == UP else z + d]
            remote(dst, dst, m_send.at[way, d], m_recv.at[way, d], {"tensor": 1 - c}).wait_recv()

        for d in range(1, nz):
            for way in (UP, DOWN):
                pl.when(z + d < nz if way == UP else z >= d)(lambda way=way, d=d: send(way, d).start())

        def follow(d):
            pl.when(z == d)(lambda: dy.start_along(UP))
            pl.when(nz - 1 - z == d)(lambda: dy.start_along(DOWN))

        follow(0)
        for d in range(1, nz):
            for p in range(PIECES):
                n1.event(d, p)
            follow(d)
        dy.start_across()
        keep.wait()
        for d in range(1, nz):
            for way in (UP, DOWN):
                pl.when(z + d < nz if way == UP else z >= d)(lambda way=way, d=d: send(way, d).wait_send())
                pl.when(z >= d if way == UP else z + d < nz)(lambda way=way, d=d: take(way, d))
        n1.finish()
        for load in loads:
            load.wait()

        def project(first, last):
            def one(i, carry):
                to = pl.ds(pl.multiple_of(i * full, full), full)
                qkv_ref[to, :] = jnp.dot(n1_ref[to, :], w[...], preferred_element_type=f32).astype(bf16)
                return carry

            lax.fori_loop(first, last, one, 0)

        def label():
            for b in range(nz):
                some = all_ref[b].astype(f32)
                seg_q[b * full : (b + 1) * full, :] = some.T[:, :1]
                seg_k[:, b * full : (b + 1) * full] = some[:1, :]

        def head(i):
            length = (i + 1) * full

            def one(h, carry):
                def part(k):
                    return pl.ds(pl.multiple_of(k * cols + h * HD, HD), HD)

                base = i * full
                scores[:, :length] = lax.dot_general(
                    qkv_ref[base : base + full, part(0)], qkv_ref[:length, part(1)], (((1,), (1,)), ((), ())),
                    preferred_element_type=f32,
                )

                def soften(j, inner):
                    local = pl.ds(pl.multiple_of(j * strip, strip), strip)
                    row = pl.ds(pl.multiple_of(base + j * strip, strip), strip)
                    place_q = base + j * strip + lax.broadcasted_iota(jnp.int32, (strip, length), 0)
                    place_k = lax.broadcasted_iota(jnp.int32, (strip, length), 1)
                    allowed = jnp.logical_and(place_k <= place_q, seg_k[:, :length] == seg_q[row, :])
                    value = jnp.where(allowed, scores[local, :length] * scale, -jnp.inf)
                    value = jnp.exp(value - jnp.max(value, axis=-1, keepdims=True))
                    share = 1.0 / jnp.sum(value, axis=-1, keepdims=True)
                    p_ref[h, row, :length] = (value * share).astype(bf16)
                    return inner

                lax.fori_loop(0, full // strip, soften, 0)
                if length < seq:
                    p_ref[h, base : base + full, length:] = jnp.zeros((full, seq - length), bf16)
                o_ref[base : base + full, pl.ds(pl.multiple_of(h * HD, HD), HD)] = jnp.dot(
                    p_ref[h, base : base + full, :length], qkv_ref[:length, part(2)], preferred_element_type=f32
                ).astype(bf16)
                return carry

            lax.fori_loop(0, heads, one, 0)

        works = [label] + [functools.partial(head, i) for i in range(nz)]
        left_events = [(d, p) for d in range(1, nz) for p in range(PIECES)]

        def events(count=None):
            for _ in range(len(left_events) if count is None else count):
                dy.event(*left_events.pop(0))

        project(0, 2)
        events(1)
        project(2, nz)
        events(1)
        for work in works:
            work()
            if len(left_events) > 2:
                events(1)

        def inside(way, d):
            return z + d < nz if way == UP else z >= d

        def send_heads(way, d):
            to = z + d if way == UP else z - d
            src = o_ref.at[pl.ds(pl.multiple_of(to * full, full), full)]
            return remote(src, heads_in.at[way, d], a_send.at[way, d], a_recv.at[way, d], {"expert": to})

        for d in range(nz - 1, 0, -1):
            for way in (UP, DOWN):
                pl.when(inside(way, d))(lambda way=way, d=d: send_heads(way, d).start())

        tile = 512 if width % 512 == 0 else width

        def put(block, left, fresh):
            at = pl.ds(pl.multiple_of(block * cols, cols), cols)

            def one(i, carry):
                to = pl.ds(pl.multiple_of(i * tile, tile), tile)
                value = lax.dot_general(
                    left(), wo[to, at], (((1,), (1,)), ((), ())), preferred_element_type=f32
                )
                acc[:, to] = value if fresh else acc[:, to] + value
                return carry

            lax.fori_loop(0, width // tile, one, 0)

        put(z, lambda: o_ref[pl.ds(pl.multiple_of(z * full, full), full), :], True)
        events()
        for d in range(1, nz):
            for way in (UP, DOWN):
                @pl.when(z >= d if way == UP else z + d < nz)
                def _(way=way, d=d):
                    remote(
                        heads_in.at[way, d], heads_in.at[way, d], a_send.at[way, d], a_recv.at[way, d], {"tensor": 1 - c}
                    ).wait_recv()
                    put(z - d if way == UP else z + d, lambda: heads_in[way, d], False)

        def pack(at):
            give[at, :] = acc[pl.ds(pl.multiple_of((1 - c) * rows + at.start, STRIP), STRIP), :].astype(bf16)

        strips(rows, pack)
        swap = remote(give, take_in, e_send, e_recv, {"tensor": 1 - c})
        swap.start()
        swap.wait_recv()

        def norm_two(at):
            mixed = acc[pl.ds(pl.multiple_of(c * rows + at.start, STRIP), STRIP), :] + take_in[at, :].astype(f32)
            h = x_ref[at, :].astype(f32) + mixed
            normed, inverse = norm_rows(h, gain2_ref[...])
            h_ref[at, :] = h
            own2[at, :] = normed.astype(bf16)
            inv_own[at, :] = jnp.broadcast_to(inverse, (STRIP, 128))

        strips(rows, norm_two)
        spot = inv_ref.at[pl.ds(pl.multiple_of(c * rows, rows), rows)]
        keep_inv = pltpu.make_async_copy(inv_own, spot, i_sems.at[0])
        pass_on = remote(inv_own, spot, i_sems.at[1], i_sems.at[2], {"tensor": 1 - c})
        keep_inv.start()
        pass_on.start()
        n2.start_along(UP)
        n2.start_along(DOWN)
        n2.start_across()
        for d in range(1, nz):
            for p in range(PIECES):
                n2.event(d, p)
        n2.finish()
        dy.finish()
        keep_inv.wait()
        pass_on.wait()
        swap.wait_send()
        for d in range(1, nz):
            for way in (UP, DOWN):
                pl.when(inside(way, d))(lambda way=way, d=d: send_heads(way, d).wait_send())

    return pl.pallas_call(
        kernel,
        out_shape=[
            jax.ShapeDtypeStruct((seq, width), bf16),
            jax.ShapeDtypeStruct((seq, width), bf16),
            jax.ShapeDtypeStruct((nz,) + marks.shape, jnp.int32),
            jax.ShapeDtypeStruct((seq, 3 * cols), bf16),
            jax.ShapeDtypeStruct((heads, seq, seq), bf16),
            jax.ShapeDtypeStruct((seq, cols), bf16),
            jax.ShapeDtypeStruct((seq, width), bf16),
            jax.ShapeDtypeStruct((rows, width), f32),
            jax.ShapeDtypeStruct((full, 128), f32),
        ],
        in_specs=[VMEM] * 5 + [ANY] * 4,
        out_specs=[VMEM, ANY, VMEM, VMEM, VMEM, VMEM, ANY, VMEM, ANY],
        scratch_shapes=[
            pltpu.VMEM((rows, width), bf16), pltpu.VMEM((width, 3 * cols), bf16), pltpu.VMEM((full, seq), f32),
            pltpu.VMEM((seq, 1), f32), pltpu.VMEM((1, seq), f32),
            pltpu.VMEM((2, nz, full, cols), bf16),
            pltpu.VMEM((full, width), f32),
            pltpu.VMEM((rows, width), bf16),
            pltpu.VMEM((rows, width), bf16),
            pltpu.VMEM((rows, width), bf16),
            pltpu.VMEM((rows, 128), f32),
            pltpu.VMEM(out_weight.shape, bf16),
            pltpu.SemaphoreType.DMA((4,)),
            pltpu.SemaphoreType.DMA((2, nz)), pltpu.SemaphoreType.DMA((2, nz)), pltpu.SemaphoreType.DMA,
            pltpu.SemaphoreType.DMA((2, nz)),
            pltpu.SemaphoreType.DMA((2, nz)),
            pltpu.SemaphoreType.DMA,
            pltpu.SemaphoreType.DMA,
            pltpu.SemaphoreType.DMA((3,)),
        ]
        + gather_sems(nz) * 3,
        compiler_params=params(name),
    )(x, gain, upstream, marks, gain2, *weights, out_weight)


def swap_rows(nz, own, out_ref, sems):
    z, c = here()
    rows = own.shape[0]
    spot = out_ref.at[pl.ds(pl.multiple_of(c * rows, rows), rows)]
    keep = pltpu.make_async_copy(own, spot, sems.at[0])
    pass_on = remote(own, spot, sems.at[1], sems.at[2], {"tensor": 1 - c})
    keep.start()
    pass_on.start()
    keep.wait()
    pass_on.wait()


TILE = 256
TALL = 512
LANES = 128


def nt_dot(left, right):
    return lax.dot_general(left, right, (((1,), (1,)), ((), ())), preferred_element_type=f32)


def nn_dot(left, right):
    return jnp.dot(left, right, preferred_element_type=f32)


def tiles(count, step, size=TILE):
    def one(i, carry):
        step(i, pl.ds(pl.multiple_of(i * size, size), size))
        return carry

    lax.fori_loop(0, count, one, 0)


def padded(columns):
    return -(-columns // LANES) * LANES


def window(columns, place):
    first = place * columns // LANES * LANES
    return first, place * columns - first


def window_width(columns, places):
    return max(padded(window(columns, i)[1] + columns) for i in range(places))


def hidden_layer(nz, n2, dy, gate, weights, groups):
    seq, width = n2.shape
    shared = weights[0].ndim == 2
    experts = 1 if shared else weights[0].shape[0]
    buffers = min(experts, 2)
    ffn = weights[0].shape[1] // nz if shared else weights[0].shape[1]
    held = window_width(ffn, nz) if shared else ffn
    kept = held if shared else padded(ffn)
    block = width // groups
    lane = min(block, TILE)
    per = TILE // lane
    count, slabs = seq // TILE, width // TILE
    strip = 32
    product = nn_dot if shared else nt_dot
    w_shape = (width, held) if shared else (held, width)

    def kernel(n2_hbm, dy_hbm, wg_hbm, wu_hbm, wd_hbm, gate_ref, grad_hbm, da_hbm, db_hbm, gu_hbm, dgate_ref,
               n2_ref, dy_ref, wg, wu, wd, a, b, back, da, db, gu, turned, slab, in_sem, row_sem, out_sem, slab_sem):
        z = lax.axis_index("expert")
        first = pl.multiple_of(z * ffn // LANES * LANES, LANES)
        skip = z * ffn - first

        def pick(ref, e):
            return ref.at[:, pl.ds(first, held)] if shared else ref.at[e]

        def weight(i, e):
            slot = lax.rem(e, buffers)
            src, dst = ((wg_hbm, wg), (wu_hbm, wu), (wd_hbm, wd))[i]
            return pltpu.make_async_copy(pick(src, e), dst.at[slot], in_sem.at[i, slot])

        rows_in = [
            pltpu.make_async_copy(n2_hbm, n2_ref, row_sem.at[0]), pltpu.make_async_copy(dy_hbm, dy_ref, row_sem.at[1])
        ]
        weight(0, 0).start()
        rows_in[0].start()
        weight(1, 0).start()
        weight(2, 0).start()
        rows_in[1].start()
        if kept > held:
            for ref in (da, db, gu):
                ref[:, held:] = jnp.zeros((seq, kept - held), bf16)

        def expert(e, carry):
            slot = lax.rem(e, buffers)
            weight(0, e).wait()
            pl.when(e == 0)(rows_in[0].wait)

            def one(i, at):
                a[at, :] = product(n2_ref[at, :], wg[slot])

            tiles(seq // TALL, one, TALL)
            weight(1, e).wait()

            def two(i, at):
                b[at, :] = product(n2_ref[at, :], wu[slot])

            tiles(seq // TALL, two, TALL)
            weight(2, e).wait()
            pl.when(e == 0)(rows_in[1].wait)
            if experts > 1:

                @pl.when(e + 1 < experts)
                def _():
                    for i in range(3):
                        weight(i, e + 1).start()

            def three(i, at):
                back[...] = product(dy_ref[at, :], wd[slot])

                def point(j, carry):
                    row = pl.ds(pl.multiple_of(i * TILE + j * strip, strip), strip)
                    local = pl.ds(pl.multiple_of(j * strip, strip), strip)
                    av, bv, kv, gv = a[row, :], b[row, :], back[local, :], gate_ref[e, row, :]
                    sig = 1.0 / (1.0 + jnp.exp(-av))
                    act = av * sig
                    u = act * bv
                    if shared:
                        column = lax.broadcasted_iota(jnp.int32, (strip, held), 1)
                        mine = jnp.logical_and(column >= skip, column < skip + ffn)
                        u, kv = jnp.where(mine, u, 0.0), jnp.where(mine, kv, 0.0)
                    dgate_ref[e, row, :] = jnp.sum(u * kv, axis=-1, keepdims=True)
                    gu[row, :held] = (gv * u).astype(bf16)
                    du = gv * kv
                    da[row, :held] = (du * bv * (sig + act * (1.0 - sig))).astype(bf16)
                    db[row, :held] = (du * act).astype(bf16)
                    return carry

                lax.fori_loop(0, TILE // strip, point, 0)
                for k, ref in enumerate((da, db, gu)):
                    turned[k, :, at] = ref[at, :held].T

            tiles(count, three)
            saves = [
                pltpu.make_async_copy(src, dst.at[e], out_sem.at[i])
                for i, (src, dst) in enumerate(((da, da_hbm), (db, db_hbm), (gu, gu_hbm)))
            ]
            for save in saves:
                save.start()

            def leave(i):
                slot = lax.rem(i, 2)
                below = pl.ds(pl.multiple_of(e * 3 * ffn, 16), 3 * ffn)
                if per > 1:
                    dst = grad_hbm.at[pl.ds(i * per, per), below]
                else:
                    many = block // TILE
                    to = pl.ds(pl.multiple_of(lax.rem(i, many) * TILE, TILE), TILE)
                    dst = grad_hbm.at[pl.ds(i // many, 1), below, to]
                return pltpu.make_async_copy(slab.at[slot], dst, slab_sem.at[slot])

            def four(i, at):
                slot = lax.rem(i, 2)
                pl.when(i >= 2)(lambda: leave(i).wait())
                for k, right in enumerate((n2_ref, n2_ref, dy_ref)):
                    left = turned[k, pl.ds(pl.multiple_of(skip, 16), ffn), :] if shared else turned[k]
                    value = nn_dot(left, right[:, at]).astype(bf16)
                    for j in range(per):
                        slab[slot, j, k * ffn : (k + 1) * ffn, :] = value[:, j * lane : (j + 1) * lane]
                leave(i).start()

            tiles(slabs, four)
            leave(slabs - 2).wait()
            leave(slabs - 1).wait()
            for save in saves:
                save.wait()
            return carry

        if experts == 1:
            expert(0, 0)
        else:
            lax.fori_loop(0, experts, expert, 0)

    hidden = jax.ShapeDtypeStruct((experts, seq, kept), bf16)
    return pl.pallas_call(
        kernel,
        out_shape=[
            jax.ShapeDtypeStruct((groups, experts * 3 * ffn, block), bf16), hidden, hidden, hidden,
            jax.ShapeDtypeStruct((experts, seq, 1), f32),
        ],
        in_specs=[ANY] * 5 + [VMEM],
        out_specs=[ANY] * 4 + [VMEM],
        scratch_shapes=[
            pltpu.VMEM((seq, width), bf16), pltpu.VMEM((seq, width), bf16),
            pltpu.VMEM((buffers,) + w_shape, bf16), pltpu.VMEM((buffers,) + w_shape, bf16), pltpu.VMEM((buffers,) + w_shape, bf16),
            pltpu.VMEM((seq, held), f32), pltpu.VMEM((seq, held), f32), pltpu.VMEM((TILE, held), f32),
            pltpu.VMEM((seq, kept), bf16), pltpu.VMEM((seq, kept), bf16), pltpu.VMEM((seq, kept), bf16),
            pltpu.VMEM((3, held, seq), bf16),
            pltpu.VMEM((2, per, 3 * ffn, lane), bf16),
            pltpu.SemaphoreType.DMA((3, buffers)), pltpu.SemaphoreType.DMA((2,)), pltpu.SemaphoreType.DMA((3,)),
            pltpu.SemaphoreType.DMA((2,)),
        ],
        compiler_params=pltpu.CompilerParams(vmem_limit_bytes=58 * 1024 * 1024),
    )(n2, dy, *weights, gate)


PART = 512


class Products:
    def __init__(self, nz, experts, shared, extra):
        self.nz, self.experts, self.shared = nz, experts, shared
        _, self.seq, self.kept = experts[0][0][0].shape
        _, self.ffn, self.width = experts[0][1][0].shape
        self.held = shared[0][0][0].shape[2]
        self.own = shared[0][1].shape[1] // nz
        self.more = [] if extra is None else list(extra)
        self.inputs = (
            [left[0] for left, _ in experts] + [right[0] for _, right in experts] + [left[0] for left, _ in shared]
            + [right for _, right in shared] + self.more
        )
        ne, ns = len(experts), len(shared)
        self.specs = [ANY] * (2 * (ne + ns)) + [VMEM] * len(self.more)
        self.scratch = [
            pltpu.VMEM((self.seq, ne * self.kept), bf16), pltpu.VMEM((ne * self.kept, self.width), bf16),
            pltpu.VMEM((self.seq, ns * self.held), bf16), pltpu.VMEM((self.width, ns * self.held), bf16),
            pltpu.SemaphoreType.DMA((self.width // PART, ne + ns)), pltpu.SemaphoreType.DMA((nz, ne + ns)),
        ]

    def bind(self, refs, scratch):
        ne, ns = len(self.experts), len(self.shared)
        self.left, self.right, self.sleft, self.sright, self.r_sem, self.l_sem = scratch
        self.e_left, self.e_right = refs[:ne], refs[ne : 2 * ne]
        self.s_left, self.s_right = refs[2 * ne : 2 * ne + ns], refs[2 * ne + ns : 2 * (ne + ns)]
        self.small = refs[2 * (ne + ns) :]
        self.first = pl.multiple_of(lax.axis_index("expert") * self.own // LANES * LANES, LANES)

    def rights(self, j):
        to = pl.ds(pl.multiple_of(j * PART, PART), PART)
        for i, (_, (_, index)) in enumerate(self.experts):
            dst = self.right.at[pl.ds(i * self.kept, self.ffn), to]
            yield pltpu.make_async_copy(self.e_right[i].at[index, :, to], dst, self.r_sem.at[j, i])
        for i in range(len(self.shared)):
            src = self.s_right[i].at[to, pl.ds(self.first, self.held)]
            dst = self.sright.at[to, pl.ds(i * self.held, self.held)]
            yield pltpu.make_async_copy(src, dst, self.r_sem.at[j, len(self.experts) + i])

    def lefts(self, b):
        rows = self.seq // self.nz
        at = pl.ds(pl.multiple_of(b * rows, rows), rows)
        for i, ((_, index), _) in enumerate(self.experts):
            dst = self.left.at[at, pl.ds(i * self.kept, self.kept)]
            yield pltpu.make_async_copy(self.e_left[i].at[index, at], dst, self.l_sem.at[b, i])
        for i, ((_, index), _) in enumerate(self.shared):
            dst = self.sleft.at[at, pl.ds(i * self.held, self.held)]
            yield pltpu.make_async_copy(self.s_left[i].at[index, at], dst, self.l_sem.at[b, len(self.experts) + i])

    def fetch(self, order):
        for copy in self.lefts(order(0)):
            copy.start()
        for j in range(self.width // PART):
            for copy in self.rights(j):
                copy.start()
        for k in range(1, self.nz):
            for copy in self.lefts(order(k)):
                copy.start()
        if self.kept > self.ffn:
            for i in range(len(self.experts)):
                self.right[i * self.kept + self.ffn : (i + 1) * self.kept, :] = jnp.zeros(
                    (self.kept - self.ffn, self.width), bf16
                )

    def block(self, k, b, out, start, end):
        rows = self.seq // self.nz
        at = pl.ds(pl.multiple_of(b * rows, rows), rows)
        if start == 0:
            for copy in self.lefts(b):
                copy.wait()

        def one(j, carry):
            @pl.when(k == 0)
            def _():
                for copy in self.rights(j):
                    copy.wait()

            to = pl.ds(pl.multiple_of(j * PART, PART), PART)
            value = nn_dot(self.left[at, :], self.right[:, to]) + nt_dot(self.sleft[at, :], self.sright[to, :])
            if self.more:
                value += nt_dot(self.small[0][at, :], self.small[1][to, :])
            out[at, to] = value.astype(bf16)
            return carry

        lax.fori_loop(start, end, one, 0)


def reduce_and_gather(nz, products, h, gain, upstream, name):
    rows, width = h.shape
    n_in, n_scratch = len(products.inputs), len(products.scratch)

    def kernel(*refs):
        p_refs, (h_ref, gain_ref, up_ref, out_ref, dh_ref, gg_ref) = refs[:n_in], refs[n_in : n_in + 6]
        rest = refs[n_in + 6 :]
        p_scratch, (part, own), rest = rest[:n_scratch], rest[n_scratch : n_scratch + 2], rest[n_scratch + 2 :]
        scratch, sems = rest[:REDUCE_SCRATCH], rest[REDUCE_SCRATCH:]
        total = scratch[3]
        products.bind(p_refs, p_scratch)
        reducer = Reducer(nz, part, *scratch)
        products.fetch(reducer.block)
        greet(nz)
        ends = reducer.ends()

        def one(s, carry):
            products.block(s, reducer.block(s), part, 0, 1)
            pl.when(jnp.logical_and(ends, s >= 1))(lambda: reducer.forward(s - 1))
            products.block(s, reducer.block(s), part, 1, width // PART)
            reducer.begin(s)
            pl.when(jnp.logical_and(jnp.logical_not(ends), s >= 2))(lambda: reducer.forward(s - 2))
            return carry

        lax.fori_loop(0, nz, one, 0)
        pl.when(jnp.logical_not(ends))(lambda: reducer.forward(nz - 2))
        reducer.finish()
        gg_ref[...] = jnp.zeros_like(gg_ref)

        def step(at):
            change, along = norm_back(h_ref[at, :], gain_ref[...], total[at, :])
            dh = up_ref[at, :].astype(f32) + change
            dh_ref[at, :] = dh
            own[at, :] = dh.astype(bf16)
            gg_ref[...] += along

        strips(rows, step)
        gather_rows(nz, own, out_ref, *sems)
        reducer.drain()

    return pl.pallas_call(
        kernel,
        out_shape=[
            jax.ShapeDtypeStruct((nz * 2 * rows, width), bf16),
            jax.ShapeDtypeStruct((rows, width), f32),
            jax.ShapeDtypeStruct((STRIP, width), f32),
        ],
        in_specs=products.specs + [VMEM] * 3,
        out_specs=[ANY, VMEM, VMEM],
        scratch_shapes=products.scratch
        + [pltpu.VMEM((nz * 2 * rows, width), bf16), pltpu.VMEM((rows, width), bf16)]
        + reduce_scratch(nz, rows, width)
        + gather_sems(nz),
        compiler_params=params(name),
    )(*products.inputs, h, gain, upstream)


def reduce_last(nz, d_heads, weights, x, gain, dh, products, h, name):
    rows, width = x.shape
    n_in, n_scratch = len(products.inputs), len(products.scratch)

    def kernel(*refs):
        p_refs, (d_ref, w_ref, x_ref, gain_ref, dh_ref, h_ref, in_ref, out_ref, gg_ref) = (
            refs[:n_in], refs[n_in : n_in + 9],
        )
        rest = refs[n_in + 9 :]
        p_scratch, (d_part, b_part, own, sems), rest = (
            rest[:n_scratch], rest[n_scratch : n_scratch + 4], rest[n_scratch + 4 :],
        )
        d_scratch, b_scratch = rest[:REDUCE_SCRATCH], rest[REDUCE_SCRATCH:]
        d_total, b_total = d_scratch[3], b_scratch[3]
        products.bind(p_refs, p_scratch)
        first, second = Reducer(nz, d_part, *d_scratch), Reducer(nz, b_part, *b_scratch)
        products.fetch(second.block)
        greet(nz)
        z, c = here()
        ends = first.ends()
        middle = jnp.logical_not(ends)

        def inner(block):
            at = pl.ds(pl.multiple_of(block * 2 * rows, 2 * rows), 2 * rows)

            def one(j, carry):
                to = pl.ds(pl.multiple_of(j * PART, PART), PART)
                d_part[at, to] = nt_dot(d_ref[at, :], w_ref[to, :]).astype(bf16)
                return carry

            lax.fori_loop(0, width // PART, one, 0)

        def one(s, carry):
            inner(first.block(s))
            first.begin(s)
            pl.when(jnp.logical_and(ends, s >= 1))(lambda: first.forward(s - 1))
            return carry

        def two(s, carry):
            products.block(s, second.block(s), b_part, 0, width // PART)
            second.begin(s)

            @pl.when(s >= 1)
            def _():
                pl.when(ends)(lambda: second.forward(s - 1))
                pl.when(middle)(lambda: first.forward(s - 1))

            return carry

        def three(s, carry):
            pl.when(middle)(lambda: second.forward(s))
            return carry

        lax.fori_loop(0, nz, one, 0)
        lax.fori_loop(0, nz, two, 0)
        lax.fori_loop(0, nz - 1, three, 0)
        first.finish()
        gg_ref[...] = jnp.zeros_like(gg_ref)

        def step(at):
            change, along = norm_back(x_ref[at, :].astype(f32), gain_ref[...], d_total[at, :])
            own[0, at, :] = dh_ref[at, :] + change
            gg_ref[...] += along

        strips(rows, step)

        def leave(i, ref):
            spot = ref.at[pl.ds(pl.multiple_of(c * rows, rows), rows)]
            return (
                pltpu.make_async_copy(own.at[i], spot, sems.at[i, 0]),
                remote(own.at[i], spot, sems.at[i, 1], sems.at[i, 2], {"tensor": 1 - c}),
            )

        for copy in leave(0, in_ref):
            copy.start()
        second.finish()

        def last(at):
            own[1, at, :] = h_ref[at, :] + b_total[at, :]

        strips(rows, last)
        for copy in leave(1, out_ref):
            copy.start()
        first.drain()
        second.drain()
        for copy in (*leave(0, in_ref), *leave(1, out_ref)):
            copy.wait()

    return pl.pallas_call(
        kernel,
        out_shape=[
            jax.ShapeDtypeStruct((2 * rows, width), f32),
            jax.ShapeDtypeStruct((2 * rows, width), f32),
            jax.ShapeDtypeStruct((STRIP, width), f32),
        ],
        in_specs=products.specs + [VMEM] * 6,
        out_specs=[ANY, ANY, VMEM],
        scratch_shapes=products.scratch
        + [
            pltpu.VMEM((nz * 2 * rows, width), bf16), pltpu.VMEM((nz * 2 * rows, width), bf16),
            pltpu.VMEM((2, rows, width), f32), pltpu.SemaphoreType.DMA((2, 3)),
        ]
        + reduce_scratch(nz, rows, width) * 2,
        compiler_params=params(name),
    )(*products.inputs, d_heads, weights, x, gain, dh, h)


def assemble(nz, box, columns):
    block = box.shape[2]
    count = 3

    def kernel(box_ref, *outs):
        for k in range(count):
            for b in range(nz):
                value = box_ref[b, k * columns : (k + 1) * columns, :].astype(f32).T
                outs[k][:, b * columns : (b + 1) * columns] = value

    return pl.pallas_call(
        kernel,
        out_shape=[jax.ShapeDtypeStruct((block, nz * columns), f32)] * count,
        in_specs=[VMEM],
        out_specs=[VMEM] * count,
        compiler_params=pltpu.CompilerParams(vmem_limit_bytes=40 * 1024 * 1024),
    )(box)


def finish_gradients(nz, part, splits, small, experts, name):
    n, rows, lanes = small.shape
    block = part.shape[0] // nz
    cols = part.shape[1] // splits
    local, kinds, ffn, width = experts.shape

    def kernel(part_ref, small_ref, experts_ref, *rest):
        outs, (sum_ref,), e_outs = rest[:splits], rest[splits : splits + 1], rest[splits + 1 : splits + 1 + kinds]
        (box, s_box, total, other, wide, send_sem, recv_sem, s_send, s_recv, swap_sem, out_sem) = rest[splits + 1 + kinds :]
        z, c = here()
        me = lax.axis_index("dp") * nz + z
        barrier = pltpu.get_barrier_semaphore()

        def peer(k):
            at = lax.rem(me + k, n)
            return at, {"dp": at // nz, "expert": lax.rem(at, nz)}

        pl.semaphore_signal(barrier, inc=1, device_id={"tensor": 1 - c}, device_id_type=MESH)
        for k in range(1, n):
            pl.semaphore_signal(barrier, inc=1, device_id=peer(k)[1], device_id_type=MESH)
        pl.semaphore_wait(barrier, n)

        def send(way, d):
            to = z + d if way == UP else z - d
            src = part_ref.at[pl.ds(pl.multiple_of(to * block, block), block)]
            return remote(src, box.at[z], send_sem.at[way, d], recv_sem.at[way, d], {"expert": to})

        def take(way, d):
            dst = box.at[z - d if way == UP else z + d]
            remote(dst, dst, send_sem.at[way, d], recv_sem.at[way, d], {"tensor": 1 - c}).wait_recv()

        def send_small(k):
            at, device = peer(k)
            return remote(small_ref.at[at], s_box.at[k], s_send.at[k], s_recv.at[k], device)

        for k in range(1, n):
            send_small(k).start()
        for d in range(nz - 1, 0, -1):
            for way in (UP, DOWN):
                pl.when(z + d < nz if way == UP else z >= d)(lambda way=way, d=d: send(way, d).start())
        box[z] = part_ref[pl.ds(pl.multiple_of(z * block, block), block), :]
        leaves = [pltpu.make_async_copy(wide.at[i], e_outs[i], out_sem.at[i]) for i in range(kinds)]
        for i in range(kinds):
            for e in range(local):
                def widen(at, i=i, e=e):
                    wide[i, e, at, :] = experts_ref[e, i, at, :].astype(f32)

                strips(ffn, widen)
            leaves[i].start()
        total[...] = small_ref[me]
        for k in range(1, n):
            send_small(k).wait_recv()
            total[...] += s_box[k]
        swap = remote(total, other, swap_sem.at[0], swap_sem.at[1], {"tensor": 1 - c})
        swap.start()
        swap.wait_recv()
        sum_ref[...] = total[...] + other[...]
        for d in range(1, nz):
            for way in (UP, DOWN):
                pl.when(z >= d if way == UP else z + d < nz)(lambda way=way, d=d: take(way, d))
        for j in range(splits):
            for b in range(nz):
                outs[j][:, b * cols : (b + 1) * cols] = box[b, :, j * cols : (j + 1) * cols].astype(f32)
        swap.wait_send()
        for k in range(1, n):
            send_small(k).wait_send()
        for d in range(1, nz):
            for way in (UP, DOWN):
                pl.when(z + d < nz if way == UP else z >= d)(lambda way=way, d=d: send(way, d).wait_send())
        for leave in leaves:
            leave.wait()

    return pl.pallas_call(
        kernel,
        out_shape=[jax.ShapeDtypeStruct((block, nz * cols), f32)] * splits
        + [jax.ShapeDtypeStruct((rows, lanes), f32)]
        + [jax.ShapeDtypeStruct((local, ffn, width), f32)] * kinds,
        in_specs=[VMEM] * 3,
        out_specs=[VMEM] * (splits + 1) + [ANY] * kinds,
        scratch_shapes=[
            pltpu.VMEM((nz, block, part.shape[1]), bf16), pltpu.VMEM((n, rows, lanes), f32),
            pltpu.VMEM((rows, lanes), f32), pltpu.VMEM((rows, lanes), f32),
            pltpu.VMEM((kinds, local, ffn, width), f32),
            pltpu.SemaphoreType.DMA((2, nz)), pltpu.SemaphoreType.DMA((2, nz)),
            pltpu.SemaphoreType.DMA((n,)), pltpu.SemaphoreType.DMA((n,)), pltpu.SemaphoreType.DMA((2,)),
            pltpu.SemaphoreType.DMA((kinds,)),
        ],
        compiler_params=params(name),
    )(part, small, experts)


def cross_rows(left, right):
    return lax.dot_general(left, right, (((0,), (0,)), ((), ())), preferred_element_type=f32)


def cross_cols(left, right):
    return lax.dot_general(left, right, (((1,), (1,)), ((), ())), preferred_element_type=f32)


def dot(left, right):
    return jnp.dot(left, right, preferred_element_type=f32)


def two_parts(values):
    high = values.astype(bf16)
    return high, (values - high.astype(f32)).astype(bf16)


def body(
    tokens, segments, routes, norm1_gain, q_weight, k_weight, v_weight, o_weight, norm2_gain,
    router_weight, shared_gate_vector, shared_gate_weight, shared_up_weight, shared_down_weight,
    expert_gate_weight, expert_up_weight, expert_down_weight, out_grad,
):
    nz = lax.axis_size("expert")
    nc = lax.axis_size("tensor")
    z = lax.axis_index("expert")
    c = lax.axis_index("tensor")
    rows, width = tokens.shape
    own_rows = rows // nc
    local_count, _, ffn = expert_gate_weight.shape
    expert_count = local_count * nz
    head_cols = q_weight.shape[1] // nz
    shared_cols = shared_gate_weight.shape[1] // nz
    heads = head_cols // HD
    seq = rows * nz
    scale = HD ** (-0.5)
    gain1 = norm1_gain.astype(f32)[None]
    gain2 = norm2_gain.astype(f32)[None]

    def own(values):
        return lax.dynamic_slice_in_dim(values, c * own_rows, own_rows, 0)

    def head_slice(values):
        return lax.dynamic_slice_in_dim(values, z * head_cols, head_cols, 1)

    x_all_rows = tokens.astype(f32)
    inverse_one_rows = lax.rsqrt(jnp.mean(x_all_rows * x_all_rows, axis=-1) + epsilon)
    x = own(tokens)
    marks = jnp.concatenate([segments, routes.T, jnp.zeros((7 - routes.shape[1], rows), jnp.int32)], axis=0)
    upstream = own(out_grad)
    n1, dy, all_marks, qkv, p_low, o, n2, h, inverse_two = attend(
        nz, x, gain1, upstream, marks, (q_weight, k_weight, v_weight), o_weight, gain2, 0
    )
    all_routes = jnp.transpose(all_marks[:, 1 : 1 + routes.shape[1]], (0, 2, 1)).reshape(seq, routes.shape[1])
    wo = head_slice(o_weight)
    w_heads = jnp.concatenate([head_slice(q_weight), head_slice(k_weight), head_slice(v_weight)], axis=1)
    q, k, v = (qkv[:, i * head_cols : (i + 1) * head_cols].reshape(seq, heads, HD) for i in range(3))
    probs = jax.nn.softmax(dot(n2, router_weight), axis=-1)
    chosen = jnp.any(all_routes[:, :, None] == jnp.arange(expert_count)[None, None, :], axis=1)
    gates = jnp.where(chosen, probs, 0.0)
    sigma = jax.nn.sigmoid(dot(n2, shared_gate_vector))

    turned = [jnp.swapaxes(w, 1, 2) for w in (expert_gate_weight, expert_up_weight, expert_down_weight)]
    shared_weights = (shared_gate_weight, shared_up_weight, shared_down_weight)
    ndp = lax.axis_size("dp")
    grad_s, da_s, db_s, gu_s, dgate_s = hidden_layer(nz, n2, dy, sigma[None, :, None], shared_weights, ndp * nz)
    n2_now, dgate_s = lax.optimization_barrier((n2, dgate_s))
    gate = jnp.swapaxes(lax.dynamic_slice_in_dim(gates, z * local_count, local_count, 1), 0, 1)[:, :, None]
    grad_e, da_e, db_e, gu_e, dgate_e = hidden_layer(nz, n2_now, dy, gate, turned, ndp)

    d_expert = jnp.swapaxes(dgate_e[:, :, 0], 0, 1)
    d_probs = lax.dynamic_update_slice_in_dim(jnp.zeros_like(probs), d_expert, z * local_count, 1)
    d_probs = jnp.where(chosen, d_probs, 0.0)
    d_logits = probs * (d_probs - jnp.sum(probs * d_probs, axis=-1, keepdims=True))
    d_vector = dgate_s[0] * (sigma * (1.0 - sigma))[:, None]
    small = jnp.concatenate([d_logits, d_vector], axis=1)
    small_high, small_low = two_parts(small)
    small_weights = jnp.concatenate([router_weight, shared_gate_vector[:, None]], axis=1)
    fill = ((0, 0), (0, 128 - small.shape[1]))
    experts = range(local_count)
    d_n2 = Products(
        nz,
        [((da_e, i), (turned[0], i)) for i in experts] + [((db_e, i), (turned[1], i)) for i in experts],
        [((da_s, 0), shared_gate_weight), ((db_s, 0), shared_up_weight)],
        (jnp.pad(small_high, fill), jnp.pad(small_weights, fill)),
    )
    small_grad = cross_rows(n2, jnp.concatenate([small_high, small_low], axis=1))
    small_grad = small_grad[:, : expert_count + 1] + small_grad[:, expert_count + 1 :]


    def over_dp(grad):
        rows = grad.reshape(-1, grad.shape[-1])
        return lax.psum_scatter(rows, "dp", scatter_dimension=0, tiled=True)

    shared_part = over_dp(grad_s).reshape((nz,) + grad_s.shape[1:])
    expert_part = over_dp(grad_e).reshape(local_count, 3, ffn, -1)
    dhr, dh, grad_two = reduce_and_gather(nz, d_n2, h, gain2, upstream, 2)
    shared_part, dhr = lax.optimization_barrier((shared_part, dhr))
    shared_box = lax.all_to_all(shared_part, "expert", split_axis=0, concat_axis=0, tiled=True)
    d_o = dot(dhr, wo).astype(bf16).reshape(seq, heads, HD)
    grad_o = cross_rows(dhr, o)

    d_v = jnp.einsum("hqk,qhd->khd", p_low, d_o, preferred_element_type=f32)
    dp = jnp.einsum("qhd,khd->hqk", d_o, v, preferred_element_type=f32)
    mean = jnp.sum(d_o.astype(f32) * o.reshape(seq, heads, HD).astype(f32), axis=-1).T
    ds = (p_low.astype(f32) * (dp - mean[:, :, None])).astype(bf16)
    d_q = jnp.einsum("hqk,khd->qhd", ds, k, preferred_element_type=f32) * scale
    d_k = jnp.einsum("hqk,qhd->khd", ds, q, preferred_element_type=f32) * scale
    d_heads = jnp.concatenate([t.reshape(seq, head_cols).astype(bf16) for t in (d_q, d_k, d_v)], axis=1)
    s_gate, s_up, s_down = assemble(nz, shared_box, shared_cols)
    d_heads, s_gate = lax.optimization_barrier((d_heads, s_gate))
    grad_attention = jnp.concatenate(
        [cross_rows(n1, d_heads).astype(bf16), grad_o.astype(bf16)], axis=1
    )
    attention_part = over_dp(grad_attention)
    branch = Products(
        nz,
        [((gu_e, i), (turned[2], i)) for i in experts],
        [((gu_s, 0), shared_down_weight)],
        None,
    )
    dh_now, _ = lax.optimization_barrier((dh, grad_attention))
    input_grad, layer_out, grad_one = reduce_last(
        nz, d_heads, w_heads, x, gain1, dh_now, branch, h, 3
    )
    stats = jnp.stack([inverse_one_rows, inverse_two[:, 0]])

    small_rows = jnp.concatenate(
        [
            jnp.sum(grad_one, axis=0)[None], jnp.sum(grad_two, axis=0)[None], small_grad.T,
            jnp.zeros((13 - expert_count, width), f32),
        ],
        axis=0,
    )
    small_rows, expert_part = lax.optimization_barrier((small_rows, expert_part))
    count = ndp * nz
    small_blocks = jnp.swapaxes(small_rows.reshape(16, count, width // count), 0, 1)
    g_q, g_k, g_v, g_o, small_all, *wide = finish_gradients(nz, attention_part, 4, small_blocks, expert_part, 6)
    e_gate, e_up, e_down = (jnp.swapaxes(t, 1, 2) for t in wide)
    g_one, g_two, g_router, g_vector = small_all[0], small_all[1], small_all[2 : 2 + expert_count].T, small_all[2 + expert_count]
    return (
        layer_out, input_grad, stats, g_one, g_q, g_k, g_v, g_o, g_two, g_router, g_vector,
        s_gate, s_up, s_down, e_gate, e_up, e_down,
    )


def solution(mesh):
    both = ("dp", "expert")
    cols = P(None, "tensor")
    placed = (
        P(both, None), P("dp", "expert"), P(both, None), P(), cols, cols, cols, cols, P(), P(), P(),
        cols, cols, cols, P("expert", None, "tensor"), P("expert", None, "tensor"),
        P("expert", None, "tensor"), P(both, None),
    )
    split = P(both, "tensor")
    experts = P("expert", "dp", "tensor")
    return jax.shard_map(
        body,
        mesh=mesh,
        in_specs=placed,
        out_specs=(
            P(both, None), P(both, None), P(None, both), P(both), split, split, split, split, P(both),
            P(both, None), P(both), split, split, split, experts, experts, experts,
        ),
        check_vma=False,
    )
```

```python
import functools

import jax
import jax.numpy as jnp
from jax import lax
from jax.experimental import pallas as pl
from jax.experimental.pallas import tpu as pltpu
from jax.sharding import PartitionSpec as P

HD = 128
MESH = pl.DeviceIdType.MESH
PIECES = 2
STRIP = 16
epsilon = 1e-06
f32 = jnp.float32
bf16 = jnp.bfloat16
UP, DOWN = 0, 1


def here():
    return lax.axis_index("expert"), lax.axis_index("tensor")


def greet(nz):
    z, c = here()
    barrier = pltpu.get_barrier_semaphore()

    def tell(device):
        pl.semaphore_signal(barrier, inc=1, device_id=device, device_id_type=MESH)

    tell({"tensor": 1 - c})
    for d in range(1, nz):
        tell({"expert": lax.rem(z + d, nz)})
    pl.semaphore_wait(barrier, nz)


def remote(src, dst, send, recv, device):
    return pltpu.make_async_remote_copy(
        src_ref=src, dst_ref=dst, send_sem=send, recv_sem=recv, device_id=device, device_id_type=MESH
    )


def strips(rows, step):
    def one(i, carry):
        step(pl.ds(pl.multiple_of(i * STRIP, STRIP), STRIP))
        return carry

    lax.fori_loop(0, rows // STRIP, one, 0)


GATHER_SEMS = 4


def gather_sems(nz):
    return [pltpu.SemaphoreType.DMA((2, nz, PIECES))] * GATHER_SEMS + [pltpu.SemaphoreType.DMA]


class Gather:
    def __init__(self, nz, own, out, z_send, z_recv, s_send, s_recv, local_sem):
        self.nz, self.own, self.out = nz, own, out
        self.z_send, self.z_recv, self.s_send, self.s_recv, self.local_sem = z_send, z_recv, s_send, s_recv, local_sem
        self.z, self.c = here()
        self.rows = own.shape[0]
        self.piece = self.rows // PIECES

    def origin(self, way, d):
        return self.z - d if way == UP else self.z + d

    def inside(self, way, d):
        return self.z >= d if way == UP else self.z + d < self.nz

    def onward(self, way):
        return self.z < self.nz - 1 if way == UP else self.z > 0

    def place(self, block, core, p):
        start = (block * 2 + core) * self.rows + p * self.piece
        return self.out.at[pl.ds(pl.multiple_of(start, self.piece), self.piece)]

    def source(self, way, d, p):
        if d == 0:
            return self.own.at[pl.ds(p * self.piece, self.piece)]
        return self.place(self.origin(way, d), self.c, p)

    def along(self, way, d, p):
        device = {"expert": self.z + 1 if way == UP else self.z - 1}
        dst = self.place(self.origin(way, d), self.c, p)
        return remote(self.source(way, d, p), dst, self.z_send.at[way, d, p], self.z_recv.at[way, d, p], device)

    def across(self, way, d, p):
        dst = self.place(self.origin(way, d), self.c, p)
        return remote(
            self.source(way, d, p), dst, self.s_send.at[way, d, p], self.s_recv.at[way, d, p], {"tensor": 1 - self.c}
        )

    def arrived(self, way, d, p):
        dst = self.place(self.origin(way, d), self.c, p)
        remote(dst, dst, self.z_send.at[way, d - 1, p], self.z_recv.at[way, d - 1, p], {"tensor": 1 - self.c}).wait_recv()

    def crossed(self, way, d, p):
        dst = self.place(self.origin(way, d), 1 - self.c, p)
        remote(dst, dst, self.s_send.at[way, d, p], self.s_recv.at[way, d, p], {"tensor": 1 - self.c}).wait_recv()

    def mine(self):
        dst = self.out.at[pl.ds(pl.multiple_of((self.z * 2 + self.c) * self.rows, self.rows), self.rows)]
        return pltpu.make_async_copy(self.own, dst, self.local_sem)

    def start_along(self, way):
        @pl.when(self.onward(way))
        def _():
            for p in range(PIECES):
                self.along(way, 0, p).start()

    def start_across(self):
        for p in range(PIECES):
            self.across(UP, 0, p).start()
        self.mine().start()

    def event(self, d, p):
        for way in (UP, DOWN):

            @pl.when(self.inside(way, d))
            def _(way=way):
                self.arrived(way, d, p)
                pl.when(self.onward(way))(lambda: self.along(way, d, p).start())
                self.across(way, d, p).start()

    def settle(self, way, d):
        for p in range(PIECES):
            self.crossed(way, d, p)
        if d == 0:
            self.mine().wait()

    def settle_all(self):
        self.settle(UP, 0)
        for d in range(1, self.nz):
            for way in (UP, DOWN):
                pl.when(self.inside(way, d))(functools.partial(self.settle, way, d))

    def finish(self):
        for p in range(PIECES):
            self.across(UP, 0, p).wait_send()
            for way in (UP, DOWN):
                pl.when(self.onward(way))(lambda way=way, p=p: self.along(way, 0, p).wait_send())
                for d in range(1, self.nz):

                    @pl.when(self.inside(way, d))
                    def _(way=way, d=d, p=p):
                        self.across(way, d, p).wait_send()
                        pl.when(self.onward(way))(lambda: self.along(way, d, p).wait_send())


def gather_rows(nz, own, out, *sems):
    gather = Gather(nz, own, out, *sems)
    gather.start_along(UP)
    gather.start_along(DOWN)
    gather.start_across()
    for d in range(1, nz):
        for p in range(PIECES):
            gather.event(d, p)
    gather.settle_all()
    gather.finish()


REDUCE_SCRATCH = 8


def reduce_scratch(nz, rows, width):
    return [
        pltpu.VMEM((nz, rows, width), bf16),
        pltpu.VMEM((nz + 1, rows, width), bf16),
        pltpu.VMEM((nz, rows, width), bf16),
        pltpu.VMEM((rows, width), f32),
        pltpu.SemaphoreType.DMA((nz, PIECES)),
        pltpu.SemaphoreType.DMA((nz, PIECES)),
        pltpu.SemaphoreType.DMA((nz, PIECES)),
        pltpu.SemaphoreType.DMA((nz + 1, PIECES)),
    ]


def block_order(nz, z, s):
    down = 2 * z // nz
    far = jnp.maximum(z, nz - 1 - z)
    near = nz - 1 - far
    late = s - (far - near)
    distance = jnp.where(late < 0, far - s, near - late // 2)
    sign = (1 - 2 * down) * jnp.where(late < 0, 1, 1 - 2 * lax.rem(late + nz * 2, 2))
    return z + sign * distance


class Reducer:
    def __init__(self, nz, part, side, inbox, outbox, total, s_send, s_recv, z_send, z_recv):
        self.nz, self.part, self.side, self.inbox, self.outbox, self.total = nz, part, side, inbox, outbox, total
        self.s_send, self.s_recv, self.z_send, self.z_recv = s_send, s_recv, z_send, z_recv
        self.z, self.c = here()
        self.rows = total.shape[0]
        self.piece = self.rows // PIECES

    def block(self, s):
        return block_order(self.nz, self.z, s)

    def cut(self, p):
        return pl.ds(p * self.piece, self.piece)

    def across(self, block, p):
        start = (block * 2 + 1 - self.c) * self.rows + p * self.piece
        src = self.part.at[pl.ds(pl.multiple_of(start, self.piece), self.piece)]
        return remote(
            src, self.side.at[block, self.cut(p)], self.s_send.at[block, p], self.s_recv.at[block, p],
            {"tensor": 1 - self.c},
        )

    def along(self, block, p):
        up = block > self.z
        slot = jnp.where(block == self.z - 1, self.nz, block)
        return remote(
            self.outbox.at[block, self.cut(p)], self.inbox.at[slot, self.cut(p)], self.z_send.at[block, p],
            self.z_recv.at[slot, p], {"expert": self.z + jnp.where(up, 1, -1)},
        )

    def arrived(self, slot, p):
        dst = self.inbox.at[slot, self.cut(p)]
        remote(dst, dst, self.z_send.at[0, p], self.z_recv.at[slot, p], {"tensor": 1 - self.c}).wait_recv()

    def mine(self, block, at):
        base = (block * 2 + self.c) * self.rows
        own = self.part[pl.ds(pl.multiple_of(base + at.start, STRIP), STRIP), :].astype(f32)
        return own + self.side[block, at, :].astype(f32)

    def strips(self, p, step):
        def one(i, carry):
            step(pl.ds(pl.multiple_of(p * self.piece + i * STRIP, STRIP), STRIP))
            return carry

        lax.fori_loop(0, self.piece // STRIP, one, 0)

    def ends(self):
        return jnp.logical_or(self.z == 0, self.z == self.nz - 1)

    def begin(self, s):
        for p in range(PIECES):
            self.across(self.block(s), p).start()

    def forward(self, s):
        block = self.block(s)
        behind = jnp.where(block > self.z, self.z, self.nz - 1 - self.z) > 0
        for p in range(PIECES):
            self.across(block, p).wait_recv()

            @pl.when(behind)
            def _(p=p):
                self.arrived(block, p)

                def add(at):
                    self.outbox[block, at, :] = (self.mine(block, at) + self.inbox[block, at, :].astype(f32)).astype(bf16)

                self.strips(p, add)

            @pl.when(jnp.logical_not(behind))
            def _(p=p):
                def keep(at):
                    self.outbox[block, at, :] = self.mine(block, at).astype(bf16)

                self.strips(p, keep)

            self.along(block, p).start()

    def finish(self):
        z, nz = self.z, self.nz
        for p in range(PIECES):
            self.across(z, p).wait_recv()

            def first(at):
                self.total[at, :] = self.mine(z, at)

            self.strips(p, first)
            for slot, some in ((z, z > 0), (nz, z < nz - 1)):

                @pl.when(some)
                def _(slot=slot, p=p):
                    self.arrived(slot, p)

                    def add(at):
                        self.total[at, :] += self.inbox[slot, at, :].astype(f32)

                    self.strips(p, add)

    def drain(self):
        def one(s, carry):
            block = self.block(s)
            for p in range(PIECES):
                self.across(block, p).wait_send()
                pl.when(s < self.nz - 1)(lambda p=p: self.along(block, p).wait_send())
            return carry

        lax.fori_loop(0, self.nz, one, 0)


def params(name, **more):
    return pltpu.CompilerParams(
        collective_id=name, has_side_effects=True, vmem_limit_bytes=56 * 1024 * 1024, **more
    )


VMEM = pl.BlockSpec(memory_space=pltpu.VMEM)
ANY = pl.BlockSpec(memory_space=pl.ANY)


def norm_rows(values, gain):
    inverse = lax.rsqrt(jnp.mean(values * values, axis=-1, keepdims=True) + epsilon)
    return values * inverse * gain, inverse


def norm_back(values, gain, upstream):
    inverse = lax.rsqrt(jnp.mean(values * values, axis=-1, keepdims=True) + epsilon)
    scaled = upstream * gain
    inner = jnp.mean(scaled * values, axis=-1, keepdims=True)
    change = inverse * scaled - values * inverse * inverse * inverse * inner
    return change, upstream * values * inverse


def swap_rows(nz, own, out_ref, sems):
    z, c = here()
    rows = own.shape[0]
    spot = out_ref.at[pl.ds(pl.multiple_of(c * rows, rows), rows)]
    keep = pltpu.make_async_copy(own, spot, sems.at[0])
    pass_on = remote(own, spot, sems.at[1], sems.at[2], {"tensor": 1 - c})
    keep.start()
    pass_on.start()
    keep.wait()
    pass_on.wait()


TILE = 256
TALL = 512
LANES = 128


def nt_dot(left, right):
    return lax.dot_general(left, right, (((1,), (1,)), ((), ())), preferred_element_type=f32)


def tn_dot(left, right):
    return lax.dot_general(left, right, (((0,), (0,)), ((), ())), preferred_element_type=f32)


def nn_dot(left, right):
    return jnp.dot(left, right, preferred_element_type=f32)


def tiles(count, step, size=TILE):
    def one(i, carry):
        step(i, pl.ds(pl.multiple_of(i * size, size), size))
        return carry

    lax.fori_loop(0, count, one, 0)


def padded(columns):
    return -(-columns // LANES) * LANES


def window(columns, place):
    first = place * columns // LANES * LANES
    return first, place * columns - first


def window_width(columns, places):
    return max(padded(window(columns, i)[1] + columns) for i in range(places))


def hidden_layer(nz, n2, dy, gate, weights, groups):
    seq, width = n2.shape
    experts = weights[0].shape[0]
    buffers = min(experts, 2)
    held = weights[0].shape[1]
    ffn, kept = held, padded(held)
    block = width // groups
    lane = min(block, TILE)
    per = TILE // lane
    count, slabs = seq // TILE, width // TILE
    strip = 32
    w_shape = (held, width)

    def kernel(n2_hbm, dy_hbm, wg_hbm, wu_hbm, wd_hbm, gate_ref, grad_hbm, da_hbm, db_hbm, gu_hbm, dgate_ref,
               n2_ref, dy_ref, wg, wu, wd, a, b, back, da, db, gu, turned, slab, in_sem, row_sem, out_sem, slab_sem):
        z = lax.axis_index("expert")
        def weight(i, e):
            slot = lax.rem(e, buffers)
            src, dst = ((wg_hbm, wg), (wu_hbm, wu), (wd_hbm, wd))[i]
            return pltpu.make_async_copy(src.at[e], dst.at[slot], in_sem.at[i, slot])

        rows_in = [
            pltpu.make_async_copy(n2_hbm, n2_ref, row_sem.at[0]), pltpu.make_async_copy(dy_hbm, dy_ref, row_sem.at[1])
        ]
        weight(0, 0).start()
        rows_in[0].start()
        weight(1, 0).start()
        weight(2, 0).start()
        rows_in[1].start()
        if kept > held:
            for ref in (da, db, gu):
                ref[:, held:] = jnp.zeros((seq, kept - held), bf16)

        def expert(e, carry):
            slot = lax.rem(e, buffers)
            weight(0, e).wait()
            pl.when(e == 0)(rows_in[0].wait)

            def one(i, at):
                a[at, :] = nt_dot(n2_ref[at, :], wg[slot])

            tiles(seq // TALL, one, TALL)
            weight(1, e).wait()

            def two(i, at):
                b[at, :] = nt_dot(n2_ref[at, :], wu[slot])

            tiles(seq // TALL, two, TALL)
            weight(2, e).wait()
            pl.when(e == 0)(rows_in[1].wait)
            if experts > 1:

                @pl.when(e + 1 < experts)
                def _():
                    for i in range(3):
                        weight(i, e + 1).start()

            def three(i, at):
                back[...] = nt_dot(dy_ref[at, :], wd[slot])

                def point(j, carry):
                    row = pl.ds(pl.multiple_of(i * TILE + j * strip, strip), strip)
                    local = pl.ds(pl.multiple_of(j * strip, strip), strip)
                    av, bv, kv = a[row, :], b[row, :], back[local, :]
                    here_now = lax.broadcasted_iota(jnp.int32, (strip, gate.shape[1]), 1) == z * experts + e
                    gv = jnp.sum(jnp.where(here_now, gate_ref[row, :], 0.0), axis=-1, keepdims=True)
                    sig = 1.0 / (1.0 + jnp.exp(-av))
                    act = av * sig
                    u = act * bv
                    dgate_ref[row, :] += jnp.where(here_now, jnp.sum(u * kv, axis=-1, keepdims=True), 0.0)
                    gu[row, :held] = (gv * u).astype(bf16)
                    du = gv * kv
                    da[row, :held] = (du * bv * (sig + act * (1.0 - sig))).astype(bf16)
                    db[row, :held] = (du * act).astype(bf16)
                    return carry

                lax.fori_loop(0, TILE // strip, point, 0)
                for k, ref in enumerate((da, db, gu)):
                    turned[k, :, at] = ref[at, :held].T

            tiles(count, three)
            saves = [
                pltpu.make_async_copy(src, dst.at[e], out_sem.at[i])
                for i, (src, dst) in enumerate(((da, da_hbm), (db, db_hbm), (gu, gu_hbm)))
            ]
            for save in saves:
                save.start()

            def leave(i):
                slot = lax.rem(i, 2)
                below = pl.ds(pl.multiple_of(e * 3 * ffn, 16), 3 * ffn)
                if per > 1:
                    dst = grad_hbm.at[pl.ds(i * per, per), below]
                else:
                    many = block // TILE
                    to = pl.ds(pl.multiple_of(lax.rem(i, many) * TILE, TILE), TILE)
                    dst = grad_hbm.at[pl.ds(i // many, 1), below, to]
                return pltpu.make_async_copy(slab.at[slot], dst, slab_sem.at[slot])

            def four(i, at):
                slot = lax.rem(i, 2)
                pl.when(i >= 2)(lambda: leave(i).wait())
                for k, right in enumerate((n2_ref, n2_ref, dy_ref)):
                    value = nn_dot(turned[k], right[:, at]).astype(bf16)
                    for j in range(per):
                        slab[slot, j, k * ffn : (k + 1) * ffn, :] = value[:, j * lane : (j + 1) * lane]
                leave(i).start()

            tiles(slabs, four)
            leave(slabs - 2).wait()
            leave(slabs - 1).wait()
            for save in saves:
                save.wait()
            return carry

        dgate_ref[...] = jnp.zeros_like(dgate_ref)
        lax.fori_loop(0, experts, expert, 0)

    hidden = jax.ShapeDtypeStruct((experts, seq, kept), bf16)
    return pl.pallas_call(
        kernel,
        out_shape=[
            jax.ShapeDtypeStruct((groups, experts * 3 * ffn, block), bf16), hidden, hidden, hidden,
            jax.ShapeDtypeStruct(gate.shape, f32),
        ],
        in_specs=[ANY] * 5 + [VMEM],
        out_specs=[ANY] * 4 + [VMEM],
        scratch_shapes=[
            pltpu.VMEM((seq, width), bf16), pltpu.VMEM((seq, width), bf16),
            pltpu.VMEM((buffers,) + w_shape, bf16), pltpu.VMEM((buffers,) + w_shape, bf16), pltpu.VMEM((buffers,) + w_shape, bf16),
            pltpu.VMEM((seq, held), f32), pltpu.VMEM((seq, held), f32), pltpu.VMEM((TILE, held), f32),
            pltpu.VMEM((seq, kept), bf16), pltpu.VMEM((seq, kept), bf16), pltpu.VMEM((seq, kept), bf16),
            pltpu.VMEM((3, held, seq), bf16),
            pltpu.VMEM((2, per, 3 * ffn, lane), bf16),
            pltpu.SemaphoreType.DMA((3, buffers)), pltpu.SemaphoreType.DMA((2,)), pltpu.SemaphoreType.DMA((3,)),
            pltpu.SemaphoreType.DMA((2,)),
        ],
        compiler_params=pltpu.CompilerParams(vmem_limit_bytes=58 * 1024 * 1024),
    )(n2, dy, *weights, gate)


def forward_layer(nz, x, gain, upstream, marks, weights, out_weight, gain2, small, shared, groups, name):
    rows, width = x.shape
    seq = nz * 2 * rows
    cols = weights[0].shape[1] // nz
    heads = cols // HD
    full = 2 * rows
    strip = 32
    scale = HD ** (-0.5)
    ffn = shared[0].shape[1] // nz
    held = window_width(ffn, nz)
    block = width // groups
    lane = min(block, TILE)
    per = TILE // lane
    slabs = width // TILE
    gate_row = small.shape[0] - 1

    def kernel(x_ref, gain_ref, up_ref, marks_ref, gain2_ref, small_ref, wq_hbm, wk_hbm, wv_hbm, wo_hbm, wg_hbm, wu_hbm, wd_hbm,
               n1_hbm, dy_hbm, all_ref, qkv_hbm, p_hbm, o_hbm, n2_hbm, h_ref, inv_ref, logit_ref, grad_hbm, da_hbm, db_hbm,
               gu_hbm, dgate_ref,
               n1_ref, dy_ref, qkv_ref, p_ref, o_ref, n2_ref, own, w, scores, seg_q, seg_k, heads_in, acc, give, take_in, own2,
               inv_own, wo, wg, wu, wd, da, db, gu, turned, slab,
               w_sem, m_send, m_recv, m_local, a_send, a_recv, e_send, e_recv, i_sems, out_sem, slab_sem, *sems):
        z, c = here()
        at = pl.ds(pl.multiple_of(z * cols, cols), cols)
        loads = [
            pltpu.make_async_copy(src.at[:, at], w.at[:, pl.ds(i * cols, cols)], w_sem.at[i])
            for i, src in enumerate((wq_hbm, wk_hbm, wv_hbm))
        ]
        loads.append(pltpu.make_async_copy(wo_hbm, wo, w_sem.at[3]))
        first = pl.multiple_of(z * ffn // LANES * LANES, LANES)
        skip = z * ffn - first
        for i, (src, dst) in enumerate(((wg_hbm, wg), (wu_hbm, wu), (wd_hbm, wd))):
            loads.append(pltpu.make_async_copy(src.at[:, pl.ds(first, held)], dst, w_sem.at[4 + i]))
        saves = []

        def save(src, dst):
            saves.append(pltpu.make_async_copy(src, dst, out_sem.at[len(saves)]))
            saves[-1].start()

        for load in loads:
            load.start()

        def step(strip_at):
            normed, _ = norm_rows(x_ref[strip_at, :].astype(f32), gain_ref[...])
            own[strip_at, :] = normed.astype(bf16)

        strips(rows, step)
        greet(nz)
        n1 = Gather(nz, own, n1_ref, *sems[:5])
        dy = Gather(nz, up_ref, dy_ref, *sems[5:10])
        n2 = Gather(nz, own2, n2_ref, *sems[10:])
        n1.start_along(UP)
        n1.start_along(DOWN)
        n1.start_across()
        keep = pltpu.make_async_copy(marks_ref, all_ref.at[z], m_local)
        keep.start()

        def send(way, d):
            to = z + d if way == UP else z - d
            return remote(marks_ref, all_ref.at[z], m_send.at[way, d], m_recv.at[way, d], {"expert": to})

        def take(way, d):
            dst = all_ref.at[z - d if way == UP else z + d]
            remote(dst, dst, m_send.at[way, d], m_recv.at[way, d], {"tensor": 1 - c}).wait_recv()

        for d in range(1, nz):
            for way in (UP, DOWN):
                pl.when(z + d < nz if way == UP else z >= d)(lambda way=way, d=d: send(way, d).start())

        def follow(d):
            pl.when(z == d)(lambda: dy.start_along(UP))
            pl.when(nz - 1 - z == d)(lambda: dy.start_along(DOWN))

        follow(0)
        for d in range(1, nz):
            for p in range(PIECES):
                n1.event(d, p)
            follow(d)
        dy.start_across()
        keep.wait()
        for d in range(1, nz):
            for way in (UP, DOWN):
                pl.when(z + d < nz if way == UP else z >= d)(lambda way=way, d=d: send(way, d).wait_send())
                pl.when(z >= d if way == UP else z + d < nz)(lambda way=way, d=d: take(way, d))
        n1.settle_all()
        n1.finish()
        save(n1_ref, n1_hbm)
        for load in loads:
            load.wait()

        def project(first, last):
            def one(i, carry):
                to = pl.ds(pl.multiple_of(i * full, full), full)
                qkv_ref[to, :] = jnp.dot(n1_ref[to, :], w[...], preferred_element_type=f32).astype(bf16)
                return carry

            lax.fori_loop(first, last, one, 0)

        def label():
            for b in range(nz):
                some = all_ref[b].astype(f32)
                seg_q[b * full : (b + 1) * full, :] = some.T[:, :1]
                seg_k[:, b * full : (b + 1) * full] = some[:1, :]

        def head(i):
            length = (i + 1) * full

            def one(h, carry):
                def part(k):
                    return pl.ds(pl.multiple_of(k * cols + h * HD, HD), HD)

                base = i * full
                scores[:, :length] = lax.dot_general(
                    qkv_ref[base : base + full, part(0)], qkv_ref[:length, part(1)], (((1,), (1,)), ((), ())),
                    preferred_element_type=f32,
                )

                def soften(j, inner):
                    local = pl.ds(pl.multiple_of(j * strip, strip), strip)
                    row = pl.ds(pl.multiple_of(base + j * strip, strip), strip)
                    place_q = base + j * strip + lax.broadcasted_iota(jnp.int32, (strip, length), 0)
                    place_k = lax.broadcasted_iota(jnp.int32, (strip, length), 1)
                    allowed = jnp.logical_and(place_k <= place_q, seg_k[:, :length] == seg_q[row, :])
                    value = jnp.where(allowed, scores[local, :length] * scale, -jnp.inf)
                    value = jnp.exp(value - jnp.max(value, axis=-1, keepdims=True))
                    share = 1.0 / jnp.sum(value, axis=-1, keepdims=True)
                    p_ref[h, row, :length] = (value * share).astype(bf16)
                    return inner

                lax.fori_loop(0, full // strip, soften, 0)
                if length < seq:
                    p_ref[h, base : base + full, length:] = jnp.zeros((full, seq - length), bf16)
                o_ref[base : base + full, pl.ds(pl.multiple_of(h * HD, HD), HD)] = jnp.dot(
                    p_ref[h, base : base + full, :length], qkv_ref[:length, part(2)], preferred_element_type=f32
                ).astype(bf16)
                return carry

            lax.fori_loop(0, heads, one, 0)

        works = [label] + [functools.partial(head, i) for i in range(nz)]
        left_events = [(d, p) for d in range(1, nz) for p in range(PIECES)]

        def events(count=None):
            for _ in range(len(left_events) if count is None else count):
                dy.event(*left_events.pop(0))

        project(0, 2)
        events(1)
        project(2, nz)
        events(1)
        for work in works:
            work()
            if len(left_events) > 2:
                events(1)

        def inside(way, d):
            return z + d < nz if way == UP else z >= d

        def send_heads(way, d):
            to = z + d if way == UP else z - d
            src = o_ref.at[pl.ds(pl.multiple_of(to * full, full), full)]
            return remote(src, heads_in.at[way, d], a_send.at[way, d], a_recv.at[way, d], {"expert": to})

        for d in range(nz - 1, 0, -1):
            for way in (UP, DOWN):
                pl.when(inside(way, d))(lambda way=way, d=d: send_heads(way, d).start())

        save(qkv_ref, qkv_hbm)
        save(p_ref, p_hbm)
        save(o_ref, o_hbm)
        tile = 512 if width % 512 == 0 else width

        def put(block, left, fresh):
            at = pl.ds(pl.multiple_of(block * cols, cols), cols)

            def one(i, carry):
                to = pl.ds(pl.multiple_of(i * tile, tile), tile)
                value = lax.dot_general(
                    left(), wo[to, at], (((1,), (1,)), ((), ())), preferred_element_type=f32
                )
                acc[:, to] = value if fresh else acc[:, to] + value
                return carry

            lax.fori_loop(0, width // tile, one, 0)

        put(z, lambda: o_ref[pl.ds(pl.multiple_of(z * full, full), full), :], True)
        events()
        for d in range(1, nz):
            for way in (UP, DOWN):
                @pl.when(z >= d if way == UP else z + d < nz)
                def _(way=way, d=d):
                    remote(
                        heads_in.at[way, d], heads_in.at[way, d], a_send.at[way, d], a_recv.at[way, d], {"tensor": 1 - c}
                    ).wait_recv()
                    put(z - d if way == UP else z + d, lambda: heads_in[way, d], False)

        def pack(at):
            give[at, :] = acc[pl.ds(pl.multiple_of((1 - c) * rows + at.start, STRIP), STRIP), :].astype(bf16)

        strips(rows, pack)
        swap = remote(give, take_in, e_send, e_recv, {"tensor": 1 - c})
        swap.start()
        swap.wait_recv()

        def norm_two(at):
            mixed = acc[pl.ds(pl.multiple_of(c * rows + at.start, STRIP), STRIP), :] + take_in[at, :].astype(f32)
            h = x_ref[at, :].astype(f32) + mixed
            normed, inverse = norm_rows(h, gain2_ref[...])
            h_ref[at, :] = h
            own2[at, :] = normed.astype(bf16)
            inv_own[at, :] = jnp.broadcast_to(inverse, (STRIP, 128))

        strips(rows, norm_two)
        spot = inv_ref.at[pl.ds(pl.multiple_of(c * rows, rows), rows)]
        keep_inv = pltpu.make_async_copy(inv_own, spot, i_sems.at[0])
        pass_on = remote(inv_own, spot, i_sems.at[1], i_sems.at[2], {"tensor": 1 - c})
        keep_inv.start()
        pass_on.start()
        n2.start_along(UP)
        n2.start_along(DOWN)
        n2.start_across()
        dy.settle_all()
        dy.finish()
        save(dy_ref, dy_hbm)
        a, b, back = acc.at[:, pl.ds(0, held)], acc.at[:, pl.ds(held, held)], scores.at[:, pl.ds(0, held)]

        def hidden(index):
            at = pl.ds(pl.multiple_of(index * full, full), full)
            logit_ref[at, :] = nt_dot(n2_ref[at, :], small_ref[...])
            a[...] = nn_dot(n2_ref[at, :], wg[...])
            b[...] = nn_dot(n2_ref[at, :], wu[...])
            back[...] = nn_dot(dy_ref[at, :], wd[...])

            def point(j, carry):
                row = pl.ds(pl.multiple_of(index * full + j * strip, strip), strip)
                local = pl.ds(pl.multiple_of(j * strip, strip), strip)
                column = lax.broadcasted_iota(jnp.int32, (strip, held), 1)
                valid = jnp.logical_and(column >= skip, column < skip + ffn)
                av, bv = a[local, :], b[local, :]
                kv = jnp.where(valid, back[local, :], 0.0)
                gv = 1.0 / (1.0 + jnp.exp(-logit_ref[row, gate_row : gate_row + 1]))
                sig = 1.0 / (1.0 + jnp.exp(-av))
                act = av * sig
                u = jnp.where(valid, act * bv, 0.0)
                last = lax.broadcasted_iota(jnp.int32, (strip, small.shape[0]), 1) == gate_row
                dgate_ref[row, :] = jnp.where(last, jnp.sum(u * kv, axis=-1, keepdims=True), 0.0)
                gu[row, :] = (gv * u).astype(bf16)
                du = gv * kv
                da[row, :] = (du * bv * (sig + act * (1.0 - sig))).astype(bf16)
                db[row, :] = (du * act).astype(bf16)
                return carry

            lax.fori_loop(0, full // strip, point, 0)
            for k, ref in enumerate((da, db, gu)):
                turned[k, :, at] = ref[at, :].T

        def arrivals(d):
            for way in (UP, DOWN):

                @pl.when(n2.inside(way, d))
                def _(way=way):
                    n2.settle(way, d)

        def pair(d):
            def one(k, carry):
                index = z + (2 * k - 1) * d
                pl.when(jnp.logical_and(index >= 0, index < nz))(lambda: hidden(index))
                return carry

            arrivals(d)
            lax.fori_loop(0, 2, one, 0)

        n2.settle(UP, 0)
        hidden(z)
        for d in range(1, nz):
            for p in range(PIECES):
                n2.event(d, p)
            if d > 1:
                pair(d - 1)
        pair(nz - 1)
        n2.finish()
        save(n2_ref, n2_hbm)
        save(da, da_hbm.at[0])
        save(db, db_hbm.at[0])
        save(gu, gu_hbm.at[0])

        def leave(i):
            slot = lax.rem(i, 2)
            if per > 1:
                dst = grad_hbm.at[pl.ds(i * per, per)]
            else:
                many = block // TILE
                to = pl.ds(pl.multiple_of(lax.rem(i, many) * TILE, TILE), TILE)
                dst = grad_hbm.at[pl.ds(i // many, 1), :, to]
            return pltpu.make_async_copy(slab.at[slot], dst, slab_sem.at[slot])

        def four(i, at):
            slot = lax.rem(i, 2)
            pl.when(i >= 2)(lambda: leave(i).wait())
            for k, right in enumerate((n2_ref, n2_ref, dy_ref)):
                value = nn_dot(turned[k, pl.ds(pl.multiple_of(skip, 16), ffn), :], right[:, at]).astype(bf16)
                for j in range(per):
                    slab[slot, j, k * ffn : (k + 1) * ffn, :] = value[:, j * lane : (j + 1) * lane]
            leave(i).start()

        tiles(slabs, four)
        leave(slabs - 2).wait()
        leave(slabs - 1).wait()
        keep_inv.wait()
        pass_on.wait()
        swap.wait_send()
        for d in range(1, nz):
            for way in (UP, DOWN):
                pl.when(inside(way, d))(lambda way=way, d=d: send_heads(way, d).wait_send())
        for copy in saves:
            copy.wait()

    hidden_shape = jax.ShapeDtypeStruct((1, seq, held), bf16)
    return pl.pallas_call(
        kernel,
        out_shape=[
            jax.ShapeDtypeStruct((seq, width), bf16),
            jax.ShapeDtypeStruct((seq, width), bf16),
            jax.ShapeDtypeStruct((nz,) + marks.shape, jnp.int32),
            jax.ShapeDtypeStruct((seq, 3 * cols), bf16),
            jax.ShapeDtypeStruct((heads, seq, seq), bf16),
            jax.ShapeDtypeStruct((seq, cols), bf16),
            jax.ShapeDtypeStruct((seq, width), bf16),
            jax.ShapeDtypeStruct((rows, width), f32),
            jax.ShapeDtypeStruct((full, 128), f32),
            jax.ShapeDtypeStruct((seq, small.shape[0]), f32),
            jax.ShapeDtypeStruct((groups, 3 * ffn, block), bf16),
            hidden_shape, hidden_shape, hidden_shape,
            jax.ShapeDtypeStruct((seq, small.shape[0]), f32),
        ],
        in_specs=[VMEM] * 6 + [ANY] * 7,
        out_specs=[ANY, ANY, VMEM, ANY, ANY, ANY, ANY, VMEM, ANY, VMEM, ANY, ANY, ANY, ANY, VMEM],
        scratch_shapes=[
            pltpu.VMEM((seq, width), bf16), pltpu.VMEM((seq, width), bf16), pltpu.VMEM((seq, 3 * cols), bf16),
            pltpu.VMEM((heads, seq, seq), bf16), pltpu.VMEM((seq, cols), bf16), pltpu.VMEM((seq, width), bf16),
            pltpu.VMEM((rows, width), bf16), pltpu.VMEM((width, 3 * cols), bf16), pltpu.VMEM((full, seq), f32),
            pltpu.VMEM((seq, 1), f32), pltpu.VMEM((1, seq), f32),
            pltpu.VMEM((2, nz, full, cols), bf16),
            pltpu.VMEM((full, width), f32),
            pltpu.VMEM((rows, width), bf16), pltpu.VMEM((rows, width), bf16), pltpu.VMEM((rows, width), bf16),
            pltpu.VMEM((rows, 128), f32), pltpu.VMEM(out_weight.shape, bf16),
            pltpu.VMEM((width, held), bf16), pltpu.VMEM((width, held), bf16), pltpu.VMEM((width, held), bf16),
            pltpu.VMEM((seq, held), bf16), pltpu.VMEM((seq, held), bf16), pltpu.VMEM((seq, held), bf16),
            pltpu.VMEM((3, held, seq), bf16), pltpu.VMEM((2, per, 3 * ffn, lane), bf16),
            pltpu.SemaphoreType.DMA((7,)),
            pltpu.SemaphoreType.DMA((2, nz)), pltpu.SemaphoreType.DMA((2, nz)), pltpu.SemaphoreType.DMA,
            pltpu.SemaphoreType.DMA((2, nz)), pltpu.SemaphoreType.DMA((2, nz)),
            pltpu.SemaphoreType.DMA, pltpu.SemaphoreType.DMA, pltpu.SemaphoreType.DMA((3,)),
            pltpu.SemaphoreType.DMA((9,)), pltpu.SemaphoreType.DMA((2,)),
        ]
        + gather_sems(nz) * 3,
        compiler_params=pltpu.CompilerParams(
            collective_id=name, has_side_effects=True, vmem_limit_bytes=63 * 1024 * 1024
        ),
    )(x, gain, upstream, marks, gain2, small, *weights, out_weight, *shared)


def attention_back(nz, d_h, n1, qkv, probs, o, out_weight, groups, part, name):
    seq, width = d_h.shape
    heads = probs.shape[0]
    cols = o.shape[1]
    full = seq // nz
    block = width // groups
    lane = min(block, TILE)
    per = TILE // lane
    slabs = width // TILE
    strip = 32
    scale = HD ** (-0.5)

    def kernel(dh_hbm, n1_hbm, qkv_ref, p_ref, o_ref, wo_hbm, part_hbm, heads_ref, grad_hbm, box_hbm,
               b_send, b_recv, b_local, dh_ref, n1_ref, wo, d_o, scores, ds, dk, dv, turned, o_turned, slab, in_sem, slab_sem):
        z, c = here()
        at = pl.ds(pl.multiple_of(z * cols, cols), cols)
        loads = [
            pltpu.make_async_copy(wo_hbm.at[:, at], wo, in_sem.at[0]),
            pltpu.make_async_copy(dh_hbm, dh_ref, in_sem.at[1]),
            pltpu.make_async_copy(n1_hbm, n1_ref, in_sem.at[2]),
        ]
        for load in loads:
            load.start()
        greet(nz)
        keep = pltpu.make_async_copy(part_hbm.at[z], box_hbm.at[z], b_local)
        keep.start()

        def send(way, d):
            to = z + d if way == UP else z - d
            return remote(part_hbm.at[to], box_hbm.at[z], b_send.at[way, d], b_recv.at[way, d], {"expert": to})

        def take(way, d):
            dst = box_hbm.at[z - d if way == UP else z + d]
            remote(dst, dst, b_send.at[way, d], b_recv.at[way, d], {"tensor": 1 - c}).wait_recv()

        for d in range(nz - 1, 0, -1):
            for way in (UP, DOWN):
                pl.when(z + d < nz if way == UP else z >= d)(lambda way=way, d=d: send(way, d).start())
        o_turned[...] = o_ref[...].T
        loads[0].wait()
        loads[1].wait()

        def project(i, to):
            d_o[to, :] = nn_dot(dh_ref[to, :], wo[...]).astype(bf16)

        tiles(seq // TILE, project)

        def head(h, carry):
            def part(k):
                return pl.ds(pl.multiple_of(k * cols + h * HD, HD), HD)

            mine = part(0)
            for i in reversed(range(nz)):
                length = (i + 1) * full
                row = pl.ds(i * full, full)
                scores[:, :length] = nt_dot(d_o[row, mine], qkv_ref[:length, part(2)])

                def harden(j, inner, i=i, length=length):
                    local = pl.ds(pl.multiple_of(j * strip, strip), strip)
                    to = pl.ds(pl.multiple_of(i * full + j * strip, strip), strip)
                    mean = jnp.sum(
                        d_o[to, mine].astype(f32) * o_ref[to, mine].astype(f32), axis=-1, keepdims=True
                    )
                    value = p_ref[h, to, :length].astype(f32) * (scores[local, :length] - mean)
                    ds[local, :length] = value.astype(bf16)
                    return inner

                lax.fori_loop(0, full // strip, harden, 0)
                d_s = ds[:, :length]
                heads_ref[row, mine] = (nn_dot(d_s, qkv_ref[:length, part(1)]) * scale).astype(bf16)
                d_k = tn_dot(d_s, qkv_ref[row, mine])
                d_v = tn_dot(p_ref[h, row, :length], d_o[row, mine])
                if i == nz - 1:
                    dk[...], dv[...] = d_k, d_v
                else:
                    dk[:length, :] += d_k
                    dv[:length, :] += d_v
            heads_ref[:, part(1)] = (dk[...] * scale).astype(bf16)
            heads_ref[:, part(2)] = dv[...].astype(bf16)
            return carry

        lax.fori_loop(0, heads, head, 0)

        def turn(i, to):
            turned[:, to] = heads_ref[to, :].T

        tiles(seq // TILE, turn)
        loads[2].wait()

        def leave(i):
            slot = lax.rem(i, 2)
            if per > 1:
                dst = grad_hbm.at[pl.ds(i * per, per)]
            else:
                many = block // TILE
                to = pl.ds(pl.multiple_of(lax.rem(i, many) * TILE, TILE), TILE)
                dst = grad_hbm.at[pl.ds(i // many, 1), :, to]
            return pltpu.make_async_copy(slab.at[slot], dst, slab_sem.at[slot])

        def write(i, to):
            slot = lax.rem(i, 2)
            pl.when(i >= 2)(lambda: leave(i).wait())
            inner = nn_dot(turned[...], n1_ref[:, to]).astype(bf16)
            outer = nn_dot(o_turned[...], dh_ref[:, to]).astype(bf16)
            for j in range(per):
                slab[slot, j, : 3 * cols, :] = inner[:, j * lane : (j + 1) * lane]
                slab[slot, j, 3 * cols :, :] = outer[:, j * lane : (j + 1) * lane]
            leave(i).start()

        tiles(slabs, write)
        leave(slabs - 2).wait()
        leave(slabs - 1).wait()
        keep.wait()
        for d in range(1, nz):
            for way in (UP, DOWN):
                pl.when(z + d < nz if way == UP else z >= d)(lambda way=way, d=d: send(way, d).wait_send())
                pl.when(z >= d if way == UP else z + d < nz)(lambda way=way, d=d: take(way, d))

    return pl.pallas_call(
        kernel,
        out_shape=[
            jax.ShapeDtypeStruct((seq, 3 * cols), bf16),
            jax.ShapeDtypeStruct((groups, 4 * cols, block), bf16),
            jax.ShapeDtypeStruct(part.shape, bf16),
        ],
        in_specs=[ANY, ANY, VMEM, VMEM, VMEM, ANY, ANY],
        out_specs=[VMEM, ANY, ANY],
        scratch_shapes=[
            pltpu.SemaphoreType.DMA((2, nz)), pltpu.SemaphoreType.DMA((2, nz)), pltpu.SemaphoreType.DMA,
            pltpu.VMEM((seq, width), bf16), pltpu.VMEM((seq, width), bf16), pltpu.VMEM((width, cols), bf16),
            pltpu.VMEM((seq, cols), bf16), pltpu.VMEM((full, seq), f32), pltpu.VMEM((full, seq), bf16),
            pltpu.VMEM((seq, HD), f32), pltpu.VMEM((seq, HD), f32),
            pltpu.VMEM((3 * cols, seq), bf16), pltpu.VMEM((cols, seq), bf16), pltpu.VMEM((2, per, 4 * cols, lane), bf16),
            pltpu.SemaphoreType.DMA((3,)), pltpu.SemaphoreType.DMA((2,)),
        ],
        compiler_params=params(name),
    )(d_h, n1, qkv, probs, o, out_weight, part)


def finish_gradients(nz, part, splits, small, name):
    _, columns, block = part.shape
    cols = columns // splits
    n, rows, lanes = small.shape

    def kernel(in_ref, small_ref, *rest):
        outs, sum_ref, rest = rest[:splits], rest[splits], rest[splits + 1 :]
        box, s_box, total, other, send_sem, recv_sem, s_send, s_recv, swap_sem = rest
        z, c = here()
        me = lax.axis_index("dp") * nz + z
        barrier = pltpu.get_barrier_semaphore()

        def peer(k):
            at = lax.rem(me + k, n)
            return at, {"dp": at // nz, "expert": lax.rem(at, nz)}

        pl.semaphore_signal(barrier, inc=1, device_id={"tensor": 1 - c}, device_id_type=MESH)
        for k in range(1, n):
            pl.semaphore_signal(barrier, inc=1, device_id=peer(k)[1], device_id_type=MESH)
        pl.semaphore_wait(barrier, n)

        def send(way, d):
            to = z + d if way == UP else z - d
            return remote(in_ref.at[to], box.at[z], send_sem.at[way, d], recv_sem.at[way, d], {"expert": to})

        def take(way, d):
            dst = box.at[z - d if way == UP else z + d]
            remote(dst, dst, send_sem.at[way, d], recv_sem.at[way, d], {"tensor": 1 - c}).wait_recv()

        def send_small(k):
            at, device = peer(k)
            return remote(small_ref.at[at], s_box.at[k], s_send.at[k], s_recv.at[k], device)

        for k in range(1, n):
            send_small(k).start()
        for d in range(nz - 1, 0, -1):
            for way in (UP, DOWN):
                pl.when(z + d < nz if way == UP else z >= d)(lambda way=way, d=d: send(way, d).start())
        box[z] = in_ref[z]
        total[...] = small_ref[me]
        for k in range(1, n):
            send_small(k).wait_recv()
            total[...] += s_box[k]
        swap = remote(total, other, swap_sem.at[0], swap_sem.at[1], {"tensor": 1 - c})
        swap.start()
        swap.wait_recv()
        sum_ref[...] = total[...] + other[...]
        for d in range(1, nz):
            for way in (UP, DOWN):
                pl.when(z + d < nz if way == UP else z >= d)(lambda way=way, d=d: send(way, d).wait_send())
                pl.when(z >= d if way == UP else z + d < nz)(lambda way=way, d=d: take(way, d))
        for j in range(splits):
            for b in range(nz):
                value = box[b, j * cols : (j + 1) * cols, :].astype(f32).T
                outs[j][:, b * cols : (b + 1) * cols] = value
        swap.wait_send()
        for k in range(1, n):
            send_small(k).wait_send()

    return pl.pallas_call(
        kernel,
        out_shape=[jax.ShapeDtypeStruct((block, nz * cols), f32)] * splits + [jax.ShapeDtypeStruct((rows, lanes), f32)],
        in_specs=[VMEM] * 2,
        out_specs=[VMEM] * (splits + 1),
        scratch_shapes=[
            pltpu.VMEM(part.shape, bf16), pltpu.VMEM((n, rows, lanes), f32), pltpu.VMEM((rows, lanes), f32),
            pltpu.VMEM((rows, lanes), f32), pltpu.SemaphoreType.DMA((2, nz)), pltpu.SemaphoreType.DMA((2, nz)),
            pltpu.SemaphoreType.DMA((n,)), pltpu.SemaphoreType.DMA((n,)), pltpu.SemaphoreType.DMA((2,)),
        ],
        compiler_params=params(name),
    )(part, small)


PART = 512


class Products:
    def __init__(self, nz, experts, shared, extra):
        self.nz, self.experts, self.shared = nz, experts, shared
        _, self.seq, self.kept = experts[0][0][0].shape
        _, self.ffn, self.width = experts[0][1][0].shape
        self.held = shared[0][0][0].shape[2]
        self.own = shared[0][1].shape[1] // nz
        self.more = [] if extra is None else list(extra)
        self.inputs = (
            [left[0] for left, _ in experts] + [right[0] for _, right in experts] + [left[0] for left, _ in shared]
            + [right for _, right in shared] + self.more
        )
        ne, ns = len(experts), len(shared)
        self.specs = [ANY] * (2 * (ne + ns)) + [VMEM] * len(self.more)
        self.scratch = [
            pltpu.VMEM((self.seq, ne * self.kept), bf16), pltpu.VMEM((ne * self.kept, self.width), bf16),
            pltpu.VMEM((self.seq, ns * self.held), bf16), pltpu.VMEM((self.width, ns * self.held), bf16),
            pltpu.SemaphoreType.DMA((self.width // PART, ne + ns)), pltpu.SemaphoreType.DMA((nz, ne + ns)),
        ]

    def bind(self, refs, scratch):
        ne, ns = len(self.experts), len(self.shared)
        self.left, self.right, self.sleft, self.sright, self.r_sem, self.l_sem = scratch
        self.e_left, self.e_right = refs[:ne], refs[ne : 2 * ne]
        self.s_left, self.s_right = refs[2 * ne : 2 * ne + ns], refs[2 * ne + ns : 2 * (ne + ns)]
        self.small = refs[2 * (ne + ns) :]
        self.first = pl.multiple_of(lax.axis_index("expert") * self.own // LANES * LANES, LANES)

    def rights(self, j):
        to = pl.ds(pl.multiple_of(j * PART, PART), PART)
        for i, (_, (_, index)) in enumerate(self.experts):
            dst = self.right.at[pl.ds(i * self.kept, self.ffn), to]
            yield pltpu.make_async_copy(self.e_right[i].at[index, :, to], dst, self.r_sem.at[j, i])
        for i in range(len(self.shared)):
            src = self.s_right[i].at[to, pl.ds(self.first, self.held)]
            dst = self.sright.at[to, pl.ds(i * self.held, self.held)]
            yield pltpu.make_async_copy(src, dst, self.r_sem.at[j, len(self.experts) + i])

    def lefts(self, b):
        rows = self.seq // self.nz
        at = pl.ds(pl.multiple_of(b * rows, rows), rows)
        for i, ((_, index), _) in enumerate(self.experts):
            dst = self.left.at[at, pl.ds(i * self.kept, self.kept)]
            yield pltpu.make_async_copy(self.e_left[i].at[index, at], dst, self.l_sem.at[b, i])
        for i, ((_, index), _) in enumerate(self.shared):
            dst = self.sleft.at[at, pl.ds(i * self.held, self.held)]
            yield pltpu.make_async_copy(self.s_left[i].at[index, at], dst, self.l_sem.at[b, len(self.experts) + i])

    def fetch(self, order):
        for copy in self.lefts(order(0)):
            copy.start()
        for j in range(self.width // PART):
            for copy in self.rights(j):
                copy.start()
        for k in range(1, self.nz):
            for copy in self.lefts(order(k)):
                copy.start()
        if self.kept > self.ffn:
            for i in range(len(self.experts)):
                self.right[i * self.kept + self.ffn : (i + 1) * self.kept, :] = jnp.zeros(
                    (self.kept - self.ffn, self.width), bf16
                )

    def block(self, k, b, out, start, end):
        rows = self.seq // self.nz
        at = pl.ds(pl.multiple_of(b * rows, rows), rows)
        if start == 0:
            for copy in self.lefts(b):
                copy.wait()

        def one(j, carry):
            @pl.when(k == 0)
            def _():
                for copy in self.rights(j):
                    copy.wait()

            to = pl.ds(pl.multiple_of(j * PART, PART), PART)
            value = nn_dot(self.left[at, :], self.right[:, to]) + nt_dot(self.sleft[at, :], self.sright[to, :])
            if self.more:
                value += nt_dot(self.small[0][at, :], self.small[1][to, :])
            out[at, to] = value.astype(bf16)
            return carry

        lax.fori_loop(start, end, one, 0)


def reduce_and_gather(nz, products, h, gain, upstream, name):
    rows, width = h.shape
    n_in, n_scratch = len(products.inputs), len(products.scratch)

    def kernel(*refs):
        p_refs, (h_ref, gain_ref, up_ref, out_ref, dh_ref, gg_ref) = refs[:n_in], refs[n_in : n_in + 6]
        rest = refs[n_in + 6 :]
        p_scratch, (part, own), rest = rest[:n_scratch], rest[n_scratch : n_scratch + 2], rest[n_scratch + 2 :]
        scratch, sems = rest[:REDUCE_SCRATCH], rest[REDUCE_SCRATCH:]
        total = scratch[3]
        products.bind(p_refs, p_scratch)
        reducer = Reducer(nz, part, *scratch)
        products.fetch(reducer.block)
        greet(nz)
        ends = reducer.ends()

        def one(s, carry):
            products.block(s, reducer.block(s), part, 0, 1)
            pl.when(jnp.logical_and(ends, s >= 1))(lambda: reducer.forward(s - 1))
            products.block(s, reducer.block(s), part, 1, width // PART)
            reducer.begin(s)
            pl.when(jnp.logical_and(jnp.logical_not(ends), s >= 2))(lambda: reducer.forward(s - 2))
            return carry

        lax.fori_loop(0, nz, one, 0)
        pl.when(jnp.logical_not(ends))(lambda: reducer.forward(nz - 2))
        reducer.finish()
        gg_ref[...] = jnp.zeros_like(gg_ref)

        def step(at):
            change, along = norm_back(h_ref[at, :], gain_ref[...], total[at, :])
            dh = up_ref[at, :].astype(f32) + change
            dh_ref[at, :] = dh
            own[at, :] = dh.astype(bf16)
            gg_ref[...] += along

        strips(rows, step)
        gather_rows(nz, own, out_ref, *sems)
        reducer.drain()

    return pl.pallas_call(
        kernel,
        out_shape=[
            jax.ShapeDtypeStruct((nz * 2 * rows, width), bf16),
            jax.ShapeDtypeStruct((rows, width), f32),
            jax.ShapeDtypeStruct((STRIP, width), f32),
        ],
        in_specs=products.specs + [VMEM] * 3,
        out_specs=[ANY, VMEM, VMEM],
        scratch_shapes=products.scratch
        + [pltpu.VMEM((nz * 2 * rows, width), bf16), pltpu.VMEM((rows, width), bf16)]
        + reduce_scratch(nz, rows, width)
        + gather_sems(nz),
        compiler_params=params(name),
    )(*products.inputs, h, gain, upstream)


def reduce_last(nz, d_heads, weights, x, gain, dh, products, h, name):
    rows, width = x.shape
    cols = d_heads.shape[1] // 3
    n_in, n_scratch = len(products.inputs), len(products.scratch)

    def kernel(*refs):
        p_refs, (d_ref, wq_hbm, wk_hbm, wv_hbm, x_ref, gain_ref, dh_ref, h_ref, in_ref, out_ref, gg_ref) = (
            refs[:n_in], refs[n_in : n_in + 11],
        )
        rest = refs[n_in + 11 :]
        p_scratch, (d_part, b_part, own, sems, w_ref, w_sem), rest = (
            rest[:n_scratch], rest[n_scratch : n_scratch + 6], rest[n_scratch + 6 :],
        )
        mine = pl.ds(pl.multiple_of(lax.axis_index("expert") * cols, cols), cols)
        loads = [
            pltpu.make_async_copy(src.at[:, mine], w_ref.at[:, pl.ds(i * cols, cols)], w_sem.at[i])
            for i, src in enumerate((wq_hbm, wk_hbm, wv_hbm))
        ]
        for load in loads:
            load.start()
        d_scratch, b_scratch = rest[:REDUCE_SCRATCH], rest[REDUCE_SCRATCH:]
        d_total, b_total = d_scratch[3], b_scratch[3]
        products.bind(p_refs, p_scratch)
        first, second = Reducer(nz, d_part, *d_scratch), Reducer(nz, b_part, *b_scratch)
        greet(nz)
        z, c = here()
        ends = first.ends()
        middle = jnp.logical_not(ends)

        def inner(block):
            at = pl.ds(pl.multiple_of(block * 2 * rows, 2 * rows), 2 * rows)

            def one(j, carry):
                to = pl.ds(pl.multiple_of(j * PART, PART), PART)
                d_part[at, to] = nt_dot(d_ref[at, :], w_ref[to, :]).astype(bf16)
                return carry

            lax.fori_loop(0, width // PART, one, 0)

        def one(s, carry):
            inner(first.block(s))
            first.begin(s)
            pl.when(jnp.logical_and(ends, s >= 1))(lambda: first.forward(s - 1))
            return carry

        def two(s, carry):
            products.block(s, second.block(s), b_part, 0, width // PART)
            second.begin(s)

            @pl.when(s >= 1)
            def _():
                pl.when(ends)(lambda: second.forward(s - 1))
                pl.when(middle)(lambda: first.forward(s - 1))

            return carry

        def three(s, carry):
            pl.when(middle)(lambda: second.forward(s))
            return carry

        for load in loads:
            load.wait()
        products.fetch(second.block)
        lax.fori_loop(0, nz, one, 0)
        lax.fori_loop(0, nz, two, 0)
        lax.fori_loop(0, nz - 1, three, 0)
        first.finish()
        gg_ref[...] = jnp.zeros_like(gg_ref)

        def step(at):
            change, along = norm_back(x_ref[at, :].astype(f32), gain_ref[...], d_total[at, :])
            own[0, at, :] = dh_ref[at, :] + change
            gg_ref[...] += along

        strips(rows, step)

        def leave(i, ref):
            spot = ref.at[pl.ds(pl.multiple_of(c * rows, rows), rows)]
            return (
                pltpu.make_async_copy(own.at[i], spot, sems.at[i, 0]),
                remote(own.at[i], spot, sems.at[i, 1], sems.at[i, 2], {"tensor": 1 - c}),
            )

        for copy in leave(0, in_ref):
            copy.start()
        second.finish()

        def last(at):
            own[1, at, :] = h_ref[at, :] + b_total[at, :]

        strips(rows, last)
        for copy in leave(1, out_ref):
            copy.start()
        first.drain()
        second.drain()
        for copy in (*leave(0, in_ref), *leave(1, out_ref)):
            copy.wait()

    return pl.pallas_call(
        kernel,
        out_shape=[
            jax.ShapeDtypeStruct((2 * rows, width), f32),
            jax.ShapeDtypeStruct((2 * rows, width), f32),
            jax.ShapeDtypeStruct((STRIP, width), f32),
        ],
        in_specs=products.specs + [VMEM] + [ANY] * 3 + [VMEM] * 4,
        out_specs=[ANY, ANY, VMEM],
        scratch_shapes=products.scratch
        + [
            pltpu.VMEM((nz * 2 * rows, width), bf16), pltpu.VMEM((nz * 2 * rows, width), bf16),
            pltpu.VMEM((2, rows, width), f32), pltpu.SemaphoreType.DMA((2, 3)),
            pltpu.VMEM((width, 3 * cols), bf16), pltpu.SemaphoreType.DMA((3,)),
        ]
        + reduce_scratch(nz, rows, width) * 2,
        compiler_params=params(name),
    )(*products.inputs, d_heads, *weights, x, gain, dh, h)


def assemble(nz, box, columns):
    block = box.shape[2]
    count = 3

    def kernel(box_ref, *outs):
        for k in range(count):
            for b in range(nz):
                value = box_ref[b, k * columns : (k + 1) * columns, :].astype(f32).T
                outs[k][:, b * columns : (b + 1) * columns] = value

    return pl.pallas_call(
        kernel,
        out_shape=[jax.ShapeDtypeStruct((block, nz * columns), f32)] * count,
        in_specs=[VMEM],
        out_specs=[VMEM] * count,
        compiler_params=pltpu.CompilerParams(vmem_limit_bytes=40 * 1024 * 1024),
    )(box)


def cross_rows(left, right):
    return lax.dot_general(left, right, (((0,), (0,)), ((), ())), preferred_element_type=f32)


def cross_cols(left, right):
    return lax.dot_general(left, right, (((1,), (1,)), ((), ())), preferred_element_type=f32)


def dot(left, right):
    return jnp.dot(left, right, preferred_element_type=f32)


def two_parts(values):
    high = values.astype(bf16)
    return high, (values - high.astype(f32)).astype(bf16)


def body(
    tokens, segments, routes, norm1_gain, q_weight, k_weight, v_weight, o_weight, norm2_gain,
    router_weight, shared_gate_vector, shared_gate_weight, shared_up_weight, shared_down_weight,
    expert_gate_weight, expert_up_weight, expert_down_weight, out_grad,
):
    nz = lax.axis_size("expert")
    nc = lax.axis_size("tensor")
    z = lax.axis_index("expert")
    c = lax.axis_index("tensor")
    rows, width = tokens.shape
    own_rows = rows // nc
    local_count, _, ffn = expert_gate_weight.shape
    expert_count = local_count * nz
    head_cols = q_weight.shape[1] // nz
    shared_cols = shared_gate_weight.shape[1] // nz
    heads = head_cols // HD
    seq = rows * nz
    scale = HD ** (-0.5)
    gain1 = norm1_gain.astype(f32)[None]
    gain2 = norm2_gain.astype(f32)[None]

    def own(values):
        return lax.dynamic_slice_in_dim(values, c * own_rows, own_rows, 0)

    def head_slice(values):
        return lax.dynamic_slice_in_dim(values, z * head_cols, head_cols, 1)

    x_all_rows = tokens.astype(f32)
    inverse_one_rows = lax.rsqrt(jnp.mean(x_all_rows * x_all_rows, axis=-1) + epsilon)
    x = own(tokens)
    marks = jnp.concatenate([segments, routes.T, jnp.zeros((7 - routes.shape[1], rows), jnp.int32)], axis=0)
    upstream = own(out_grad)
    ndp = lax.axis_size("dp")
    small_rows_weight = jnp.concatenate([router_weight.T, shared_gate_vector[None]], axis=0)
    shared_weights = (shared_gate_weight, shared_up_weight, shared_down_weight)
    (
        n1, dy, all_marks, qkv, p_low, o, n2, h, inverse_two, logits, grad_s, da_s, db_s, gu_s, dgate_s,
    ) = forward_layer(
        nz, x, gain1, upstream, marks, (q_weight, k_weight, v_weight), o_weight, gain2, small_rows_weight, shared_weights,
        ndp * nz, 0,
    )
    all_routes = jnp.transpose(all_marks[:, 1 : 1 + routes.shape[1]], (0, 2, 1)).reshape(seq, routes.shape[1])

    probs = jax.nn.softmax(logits[:, :expert_count], axis=-1)
    chosen = jnp.any(all_routes[:, :, None] == jnp.arange(expert_count)[None, None, :], axis=1)
    gates = jnp.where(chosen, probs, 0.0)
    sigma = jax.nn.sigmoid(logits[:, expert_count:])

    turned = [jnp.swapaxes(w, 1, 2) for w in (expert_gate_weight, expert_up_weight, expert_down_weight)]
    grad_e, da_e, db_e, gu_e, dgate_e = hidden_layer(nz, n2, dy, gates, turned, ndp)

    d_probs = jnp.where(chosen, dgate_e, 0.0)
    d_logits = probs * (d_probs - jnp.sum(probs * d_probs, axis=-1, keepdims=True))
    d_vector = dgate_s[:, expert_count:] * (sigma * (1.0 - sigma))
    small = jnp.concatenate([d_logits, d_vector], axis=1)
    small_high, small_low = two_parts(small)
    small_weights = jnp.concatenate([router_weight, shared_gate_vector[:, None]], axis=1)
    fill = ((0, 0), (0, 128 - small.shape[1]))
    experts = range(local_count)
    d_n2 = Products(
        nz,
        [((da_e, i), (turned[0], i)) for i in experts] + [((db_e, i), (turned[1], i)) for i in experts],
        [((da_s, 0), shared_gate_weight), ((db_s, 0), shared_up_weight)],
        (jnp.pad(small_high, fill), jnp.pad(small_weights, fill)),
    )
    small_grad = cross_rows(n2, jnp.concatenate([small_high, small_low], axis=1))
    small_grad = small_grad[:, : expert_count + 1] + small_grad[:, expert_count + 1 :]


    def over_dp(grad):
        rows = grad.reshape(-1, grad.shape[-1])
        return lax.psum_scatter(rows, "dp", scatter_dimension=0, tiled=True)

    shared_part = over_dp(grad_s).reshape((nz,) + grad_s.shape[1:])
    expert_part = over_dp(grad_e).reshape(local_count, 3, ffn, -1)
    dhr, dh, grad_two = reduce_and_gather(nz, d_n2, h, gain2, upstream, 2)
    d_heads, grad_attention, shared_box = attention_back(
        nz, dhr, n1, qkv, p_low, o, o_weight, ndp * nz, shared_part, 1
    )
    attention_part = over_dp(grad_attention).reshape((nz,) + grad_attention.shape[1:])
    branch = Products(
        nz,
        [((gu_e, i), (turned[2], i)) for i in experts],
        [((gu_s, 0), shared_down_weight)],
        None,
    )
    dh_now, _ = lax.optimization_barrier((dh, grad_attention))
    input_grad, layer_out, grad_one = reduce_last(
        nz, d_heads, (q_weight, k_weight, v_weight), x, gain1, dh_now, branch, h, 3
    )
    stats = jnp.stack([inverse_one_rows, inverse_two[:, 0]])

    small_rows = jnp.concatenate(
        [
            jnp.sum(grad_one, axis=0)[None], jnp.sum(grad_two, axis=0)[None], small_grad.T,
            jnp.zeros((13 - expert_count, width), f32),
        ],
        axis=0,
    )
    small_rows, expert_part = lax.optimization_barrier((small_rows, expert_part))
    count = ndp * nz
    small_blocks = jnp.swapaxes(small_rows.reshape(16, count, width // count), 0, 1)
    s_gate, s_up, s_down = assemble(nz, shared_box, shared_cols)
    e_gate, e_up, e_down = (jnp.swapaxes(expert_part[:, k].astype(f32), 1, 2) for k in range(3))
    attention_part, small_blocks, e_gate, e_up, e_down, s_gate = lax.optimization_barrier(
        (attention_part, small_blocks, e_gate, e_up, e_down, s_gate)
    )
    g_q, g_k, g_v, g_o, small_all = finish_gradients(nz, attention_part, 4, small_blocks, 6)
    g_one, g_two, g_router, g_vector = small_all[0], small_all[1], small_all[2 : 2 + expert_count].T, small_all[2 + expert_count]
    return (
        layer_out, input_grad, stats, g_one, g_q, g_k, g_v, g_o, g_two, g_router, g_vector,
        s_gate, s_up, s_down, e_gate, e_up, e_down,
    )


def solution(mesh):
    both = ("dp", "expert")
    cols = P(None, "tensor")
    placed = (
        P(both, None), P("dp", "expert"), P(both, None), P(), cols, cols, cols, cols, P(), P(), P(),
        cols, cols, cols, P("expert", None, "tensor"), P("expert", None, "tensor"),
        P("expert", None, "tensor"), P(both, None),
    )
    split = P(both, "tensor")
    experts = P("expert", "dp", "tensor")
    return jax.shard_map(
        body,
        mesh=mesh,
        in_specs=placed,
        out_specs=(
            P(both, None), P(both, None), P(None, both), P(both), split, split, split, split, P(both),
            P(both, None), P(both), split, split, split, experts, experts, experts,
        ),
        check_vma=False,
    )
```

```python
import functools

import jax
import jax.numpy as jnp
from jax import lax
from jax.experimental import pallas as pl
from jax.experimental.pallas import tpu as pltpu
from jax.sharding import PartitionSpec as P

HD = 128
MESH = pl.DeviceIdType.MESH
PIECES = 2
STRIP = 16
epsilon = 1e-06
f32 = jnp.float32
bf16 = jnp.bfloat16
UP, DOWN = 0, 1


def here():
    return lax.axis_index("expert"), lax.axis_index("tensor")


def greet(nz):
    z, c = here()
    barrier = pltpu.get_barrier_semaphore()

    def tell(device):
        pl.semaphore_signal(barrier, inc=1, device_id=device, device_id_type=MESH)

    tell({"tensor": 1 - c})
    for d in range(1, nz):
        tell({"expert": lax.rem(z + d, nz)})
    pl.semaphore_wait(barrier, nz)


def remote(src, dst, send, recv, device):
    return pltpu.make_async_remote_copy(
        src_ref=src, dst_ref=dst, send_sem=send, recv_sem=recv, device_id=device, device_id_type=MESH
    )


def strips(rows, step):
    def one(i, carry):
        step(pl.ds(pl.multiple_of(i * STRIP, STRIP), STRIP))
        return carry

    lax.fori_loop(0, rows // STRIP, one, 0)


GATHER_SEMS = 4


def gather_sems(nz):
    return [pltpu.SemaphoreType.DMA((2, nz, PIECES))] * GATHER_SEMS + [pltpu.SemaphoreType.DMA]


class Gather:
    def __init__(self, nz, own, out, z_send, z_recv, s_send, s_recv, local_sem):
        self.nz, self.own, self.out = nz, own, out
        self.z_send, self.z_recv, self.s_send, self.s_recv, self.local_sem = z_send, z_recv, s_send, s_recv, local_sem
        self.z, self.c = here()
        self.rows = own.shape[0]
        self.piece = self.rows // PIECES

    def origin(self, way, d):
        return self.z - d if way == UP else self.z + d

    def inside(self, way, d):
        return self.z >= d if way == UP else self.z + d < self.nz

    def onward(self, way):
        return self.z < self.nz - 1 if way == UP else self.z > 0

    def place(self, block, core, p):
        start = (block * 2 + core) * self.rows + p * self.piece
        return self.out.at[pl.ds(pl.multiple_of(start, self.piece), self.piece)]

    def source(self, way, d, p):
        if d == 0:
            return self.own.at[pl.ds(p * self.piece, self.piece)]
        return self.place(self.origin(way, d), self.c, p)

    def along(self, way, d, p):
        device = {"expert": self.z + 1 if way == UP else self.z - 1}
        dst = self.place(self.origin(way, d), self.c, p)
        return remote(self.source(way, d, p), dst, self.z_send.at[way, d, p], self.z_recv.at[way, d, p], device)

    def across(self, way, d, p):
        dst = self.place(self.origin(way, d), self.c, p)
        return remote(
            self.source(way, d, p), dst, self.s_send.at[way, d, p], self.s_recv.at[way, d, p], {"tensor": 1 - self.c}
        )

    def arrived(self, way, d, p):
        dst = self.place(self.origin(way, d), self.c, p)
        remote(dst, dst, self.z_send.at[way, d - 1, p], self.z_recv.at[way, d - 1, p], {"tensor": 1 - self.c}).wait_recv()

    def crossed(self, way, d, p):
        dst = self.place(self.origin(way, d), 1 - self.c, p)
        remote(dst, dst, self.s_send.at[way, d, p], self.s_recv.at[way, d, p], {"tensor": 1 - self.c}).wait_recv()

    def mine(self):
        dst = self.out.at[pl.ds(pl.multiple_of((self.z * 2 + self.c) * self.rows, self.rows), self.rows)]
        return pltpu.make_async_copy(self.own, dst, self.local_sem)

    def start_along(self, way):
        @pl.when(self.onward(way))
        def _():
            for p in range(PIECES):
                self.along(way, 0, p).start()

    def start_across(self):
        for p in range(PIECES):
            self.across(UP, 0, p).start()
        self.mine().start()

    def event(self, d, p):
        for way in (UP, DOWN):

            @pl.when(self.inside(way, d))
            def _(way=way):
                self.arrived(way, d, p)
                pl.when(self.onward(way))(lambda: self.along(way, d, p).start())
                self.across(way, d, p).start()

    def settle(self, way, d):
        for p in range(PIECES):
            self.crossed(way, d, p)
        if d == 0:
            self.mine().wait()

    def settle_all(self):
        self.settle(UP, 0)
        for d in range(1, self.nz):
            for way in (UP, DOWN):
                pl.when(self.inside(way, d))(functools.partial(self.settle, way, d))

    def finish(self):
        for p in range(PIECES):
            self.across(UP, 0, p).wait_send()
            for way in (UP, DOWN):
                pl.when(self.onward(way))(lambda way=way, p=p: self.along(way, 0, p).wait_send())
                for d in range(1, self.nz):

                    @pl.when(self.inside(way, d))
                    def _(way=way, d=d, p=p):
                        self.across(way, d, p).wait_send()
                        pl.when(self.onward(way))(lambda: self.along(way, d, p).wait_send())


def gather_rows(nz, own, out, *sems):
    gather = Gather(nz, own, out, *sems)
    gather.start_along(UP)
    gather.start_along(DOWN)
    gather.start_across()
    for d in range(1, nz):
        for p in range(PIECES):
            gather.event(d, p)
    gather.settle_all()
    gather.finish()


REDUCE_SCRATCH = 8


def reduce_scratch(nz, rows, width):
    return [
        pltpu.VMEM((nz, rows, width), bf16),
        pltpu.VMEM((nz + 1, rows, width), bf16),
        pltpu.VMEM((nz, rows, width), bf16),
        pltpu.VMEM((rows, width), f32),
        pltpu.SemaphoreType.DMA((nz, PIECES)),
        pltpu.SemaphoreType.DMA((nz, PIECES)),
        pltpu.SemaphoreType.DMA((nz, PIECES)),
        pltpu.SemaphoreType.DMA((nz + 1, PIECES)),
    ]


def block_order(nz, z, s):
    down = 2 * z // nz
    far = jnp.maximum(z, nz - 1 - z)
    near = nz - 1 - far
    late = s - (far - near)
    distance = jnp.where(late < 0, far - s, near - late // 2)
    sign = (1 - 2 * down) * jnp.where(late < 0, 1, 1 - 2 * lax.rem(late + nz * 2, 2))
    return z + sign * distance


class Reducer:
    def __init__(self, nz, part, side, inbox, outbox, total, s_send, s_recv, z_send, z_recv):
        self.nz, self.part, self.side, self.inbox, self.outbox, self.total = nz, part, side, inbox, outbox, total
        self.s_send, self.s_recv, self.z_send, self.z_recv = s_send, s_recv, z_send, z_recv
        self.z, self.c = here()
        self.rows = total.shape[0]
        self.piece = self.rows // PIECES

    def block(self, s):
        return block_order(self.nz, self.z, s)

    def cut(self, p):
        return pl.ds(p * self.piece, self.piece)

    def across(self, block, p):
        start = (block * 2 + 1 - self.c) * self.rows + p * self.piece
        src = self.part.at[pl.ds(pl.multiple_of(start, self.piece), self.piece)]
        return remote(
            src, self.side.at[block, self.cut(p)], self.s_send.at[block, p], self.s_recv.at[block, p],
            {"tensor": 1 - self.c},
        )

    def along(self, block, p):
        up = block > self.z
        slot = jnp.where(block == self.z - 1, self.nz, block)
        return remote(
            self.outbox.at[block, self.cut(p)], self.inbox.at[slot, self.cut(p)], self.z_send.at[block, p],
            self.z_recv.at[slot, p], {"expert": self.z + jnp.where(up, 1, -1)},
        )

    def arrived(self, slot, p):
        dst = self.inbox.at[slot, self.cut(p)]
        remote(dst, dst, self.z_send.at[0, p], self.z_recv.at[slot, p], {"tensor": 1 - self.c}).wait_recv()

    def mine(self, block, at):
        base = (block * 2 + self.c) * self.rows
        own = self.part[pl.ds(pl.multiple_of(base + at.start, STRIP), STRIP), :].astype(f32)
        return own + self.side[block, at, :].astype(f32)

    def strips(self, p, step):
        def one(i, carry):
            step(pl.ds(pl.multiple_of(p * self.piece + i * STRIP, STRIP), STRIP))
            return carry

        lax.fori_loop(0, self.piece // STRIP, one, 0)

    def ends(self):
        return jnp.logical_or(self.z == 0, self.z == self.nz - 1)

    def begin(self, s):
        for p in range(PIECES):
            self.across(self.block(s), p).start()

    def forward(self, s):
        block = self.block(s)
        behind = jnp.where(block > self.z, self.z, self.nz - 1 - self.z) > 0
        for p in range(PIECES):
            self.across(block, p).wait_recv()

            @pl.when(behind)
            def _(p=p):
                self.arrived(block, p)

                def add(at):
                    self.outbox[block, at, :] = (self.mine(block, at) + self.inbox[block, at, :].astype(f32)).astype(bf16)

                self.strips(p, add)

            @pl.when(jnp.logical_not(behind))
            def _(p=p):
                def keep(at):
                    self.outbox[block, at, :] = self.mine(block, at).astype(bf16)

                self.strips(p, keep)

            self.along(block, p).start()

    def finish(self):
        z, nz = self.z, self.nz
        for p in range(PIECES):
            self.across(z, p).wait_recv()

            def first(at):
                self.total[at, :] = self.mine(z, at)

            self.strips(p, first)
            for slot, some in ((z, z > 0), (nz, z < nz - 1)):

                @pl.when(some)
                def _(slot=slot, p=p):
                    self.arrived(slot, p)

                    def add(at):
                        self.total[at, :] += self.inbox[slot, at, :].astype(f32)

                    self.strips(p, add)

    def drain(self):
        def one(s, carry):
            block = self.block(s)
            for p in range(PIECES):
                self.across(block, p).wait_send()
                pl.when(s < self.nz - 1)(lambda p=p: self.along(block, p).wait_send())
            return carry

        lax.fori_loop(0, self.nz, one, 0)


def params(name, room=56):
    return pltpu.CompilerParams(collective_id=name, has_side_effects=True, vmem_limit_bytes=room * 1024 * 1024)


VMEM = pl.BlockSpec(memory_space=pltpu.VMEM)
ANY = pl.BlockSpec(memory_space=pl.ANY)


def norm_rows(values, gain):
    inverse = lax.rsqrt(jnp.mean(values * values, axis=-1, keepdims=True) + epsilon)
    return values * inverse * gain, inverse


def norm_back(values, gain, upstream):
    inverse = lax.rsqrt(jnp.mean(values * values, axis=-1, keepdims=True) + epsilon)
    scaled = upstream * gain
    inner = jnp.mean(scaled * values, axis=-1, keepdims=True)
    change = inverse * scaled - values * inverse * inverse * inverse * inner
    return change, upstream * values * inverse


def swap_rows(nz, own, out_ref, sems):
    z, c = here()
    rows = own.shape[0]
    spot = out_ref.at[pl.ds(pl.multiple_of(c * rows, rows), rows)]
    keep = pltpu.make_async_copy(own, spot, sems.at[0])
    pass_on = remote(own, spot, sems.at[1], sems.at[2], {"tensor": 1 - c})
    keep.start()
    pass_on.start()
    keep.wait()
    pass_on.wait()


TILE = 256
TALL = 512
LANES = 128


def nt_dot(left, right):
    return lax.dot_general(left, right, (((1,), (1,)), ((), ())), preferred_element_type=f32)


def tn_dot(left, right):
    return lax.dot_general(left, right, (((0,), (0,)), ((), ())), preferred_element_type=f32)


def nn_dot(left, right):
    return jnp.dot(left, right, preferred_element_type=f32)


def tiles(count, step, size=TILE):
    def one(i, carry):
        step(i, pl.ds(pl.multiple_of(i * size, size), size))
        return carry

    lax.fori_loop(0, count, one, 0)


def padded(columns):
    return -(-columns // LANES) * LANES


def window(columns, place):
    first = place * columns // LANES * LANES
    return first, place * columns - first


def window_width(columns, places):
    return max(padded(window(columns, i)[1] + columns) for i in range(places))


def hidden_layer(nz, n2, dy, gate, weights, groups):
    seq, width = n2.shape
    experts = weights[0].shape[0]
    buffers = min(experts, 2)
    held = weights[0].shape[1]
    ffn, kept = held, padded(held)
    block = width // groups
    lane = min(block, TILE)
    per = TILE // lane
    count, slabs = seq // TILE, width // TILE
    strip = 32
    w_shape = (held, width)

    def kernel(n2_hbm, dy_hbm, wg_hbm, wu_hbm, wd_hbm, gate_ref, grad_hbm, da_hbm, db_hbm, gu_hbm, dgate_ref,
               n2_ref, dy_ref, wg, wu, wd, a, b, back, da, db, gu, turned, slab, in_sem, row_sem, out_sem, slab_sem):
        z = lax.axis_index("expert")
        def weight(i, e):
            slot = lax.rem(e, buffers)
            src, dst = ((wg_hbm, wg), (wu_hbm, wu), (wd_hbm, wd))[i]
            return pltpu.make_async_copy(src.at[e], dst.at[slot], in_sem.at[i, slot])

        rows_in = [
            pltpu.make_async_copy(n2_hbm, n2_ref, row_sem.at[0]), pltpu.make_async_copy(dy_hbm, dy_ref, row_sem.at[1])
        ]
        weight(0, 0).start()
        rows_in[0].start()
        weight(1, 0).start()
        weight(2, 0).start()
        rows_in[1].start()
        if kept > held:
            for ref in (da, db, gu):
                ref[:, held:] = jnp.zeros((seq, kept - held), bf16)

        def expert(e, carry):
            slot = lax.rem(e, buffers)
            weight(0, e).wait()
            pl.when(e == 0)(rows_in[0].wait)

            def one(i, at):
                a[at, :] = nt_dot(n2_ref[at, :], wg[slot])

            tiles(seq // TALL, one, TALL)
            weight(1, e).wait()

            def two(i, at):
                b[at, :] = nt_dot(n2_ref[at, :], wu[slot])

            tiles(seq // TALL, two, TALL)
            weight(2, e).wait()
            pl.when(e == 0)(rows_in[1].wait)
            if experts > 1:

                @pl.when(e + 1 < experts)
                def _():
                    for i in range(3):
                        weight(i, e + 1).start()

            def three(i, at):
                back[...] = nt_dot(dy_ref[at, :], wd[slot])

                def point(j, carry):
                    row = pl.ds(pl.multiple_of(i * TILE + j * strip, strip), strip)
                    local = pl.ds(pl.multiple_of(j * strip, strip), strip)
                    av, bv, kv = a[row, :], b[row, :], back[local, :]
                    here_now = lax.broadcasted_iota(jnp.int32, (strip, gate.shape[1]), 1) == z * experts + e
                    gv = jnp.sum(jnp.where(here_now, gate_ref[row, :], 0.0), axis=-1, keepdims=True)
                    sig = 1.0 / (1.0 + jnp.exp(-av))
                    act = av * sig
                    u = act * bv
                    dgate_ref[row, :] += jnp.where(here_now, jnp.sum(u * kv, axis=-1, keepdims=True), 0.0)
                    gu[row, :held] = (gv * u).astype(bf16)
                    du = gv * kv
                    da[row, :held] = (du * bv * (sig + act * (1.0 - sig))).astype(bf16)
                    db[row, :held] = (du * act).astype(bf16)
                    return carry

                lax.fori_loop(0, TILE // strip, point, 0)
                for k, ref in enumerate((da, db, gu)):
                    turned[k, :, at] = ref[at, :held].T

            tiles(count, three)
            saves = [
                pltpu.make_async_copy(src, dst.at[e], out_sem.at[i])
                for i, (src, dst) in enumerate(((da, da_hbm), (db, db_hbm), (gu, gu_hbm)))
            ]
            for save in saves:
                save.start()

            def leave(i):
                slot = lax.rem(i, 2)
                below = pl.ds(pl.multiple_of(e * 3 * ffn, 16), 3 * ffn)
                if per > 1:
                    dst = grad_hbm.at[pl.ds(i * per, per), below]
                else:
                    many = block // TILE
                    to = pl.ds(pl.multiple_of(lax.rem(i, many) * TILE, TILE), TILE)
                    dst = grad_hbm.at[pl.ds(i // many, 1), below, to]
                return pltpu.make_async_copy(slab.at[slot], dst, slab_sem.at[slot])

            def four(i, at):
                slot = lax.rem(i, 2)
                pl.when(i >= 2)(lambda: leave(i).wait())
                for k, right in enumerate((n2_ref, n2_ref, dy_ref)):
                    value = nn_dot(turned[k], right[:, at]).astype(bf16)
                    for j in range(per):
                        slab[slot, j, k * ffn : (k + 1) * ffn, :] = value[:, j * lane : (j + 1) * lane]
                leave(i).start()

            tiles(slabs, four)
            leave(slabs - 2).wait()
            leave(slabs - 1).wait()
            for save in saves:
                save.wait()
            return carry

        dgate_ref[...] = jnp.zeros_like(dgate_ref)
        lax.fori_loop(0, experts, expert, 0)

    hidden = jax.ShapeDtypeStruct((experts, seq, kept), bf16)
    return pl.pallas_call(
        kernel,
        out_shape=[
            jax.ShapeDtypeStruct((groups, experts * 3 * ffn, block), bf16), hidden, hidden, hidden,
            jax.ShapeDtypeStruct(gate.shape, f32),
        ],
        in_specs=[ANY] * 5 + [VMEM],
        out_specs=[ANY] * 4 + [VMEM],
        scratch_shapes=[
            pltpu.VMEM((seq, width), bf16), pltpu.VMEM((seq, width), bf16),
            pltpu.VMEM((buffers,) + w_shape, bf16), pltpu.VMEM((buffers,) + w_shape, bf16), pltpu.VMEM((buffers,) + w_shape, bf16),
            pltpu.VMEM((seq, held), f32), pltpu.VMEM((seq, held), f32), pltpu.VMEM((TILE, held), f32),
            pltpu.VMEM((seq, kept), bf16), pltpu.VMEM((seq, kept), bf16), pltpu.VMEM((seq, kept), bf16),
            pltpu.VMEM((3, held, seq), bf16),
            pltpu.VMEM((2, per, 3 * ffn, lane), bf16),
            pltpu.SemaphoreType.DMA((3, buffers)), pltpu.SemaphoreType.DMA((2,)), pltpu.SemaphoreType.DMA((3,)),
            pltpu.SemaphoreType.DMA((2,)),
        ],
        compiler_params=pltpu.CompilerParams(vmem_limit_bytes=58 * 1024 * 1024),
    )(n2, dy, *weights, gate)


def forward_layer(nz, x, gain, upstream, marks, weights, out_weight, gain2, small, shared, groups, name):
    rows, width = x.shape
    seq = nz * 2 * rows
    cols = weights[0].shape[1] // nz
    heads = cols // HD
    full = 2 * rows
    strip = 32
    scale = HD ** (-0.5)
    ffn = shared[0].shape[1] // nz
    held = window_width(ffn, nz)
    block = width // groups
    lane = min(block, TILE)
    per = TILE // lane
    slabs = width // TILE
    gate_row = small.shape[0] - 1

    def kernel(x_ref, gain_ref, up_ref, marks_ref, gain2_ref, small_ref, wq_hbm, wk_hbm, wv_hbm, wo_hbm, wg_hbm, wu_hbm, wd_hbm,
               n1_hbm, dy_hbm, all_ref, qkv_hbm, p_hbm, o_hbm, n2_hbm, h_ref, inv_ref, logit_ref, grad_hbm, da_hbm, db_hbm,
               gu_hbm, dgate_ref,
               n1_ref, dy_ref, qkv_ref, p_ref, o_ref, n2_ref, own, w, scores, seg_q, seg_k, heads_in, acc, give, take_in, own2,
               inv_own, wo, wg, wu, wd, da, db, gu, turned, slab,
               w_sem, m_send, m_recv, m_local, a_send, a_recv, e_send, e_recv, i_sems, out_sem, slab_sem, *sems):
        z, c = here()
        at = pl.ds(pl.multiple_of(z * cols, cols), cols)
        loads = [
            pltpu.make_async_copy(src.at[:, at], w.at[:, pl.ds(i * cols, cols)], w_sem.at[i])
            for i, src in enumerate((wq_hbm, wk_hbm, wv_hbm))
        ]
        loads.append(pltpu.make_async_copy(wo_hbm, wo, w_sem.at[3]))
        first = pl.multiple_of(z * ffn // LANES * LANES, LANES)
        skip = z * ffn - first
        for i, (src, dst) in enumerate(((wg_hbm, wg), (wu_hbm, wu), (wd_hbm, wd))):
            loads.append(pltpu.make_async_copy(src.at[:, pl.ds(first, held)], dst, w_sem.at[4 + i]))
        saves = []

        def save(src, dst):
            saves.append(pltpu.make_async_copy(src, dst, out_sem.at[len(saves)]))
            saves[-1].start()

        for load in loads:
            load.start()

        def step(strip_at):
            normed, _ = norm_rows(x_ref[strip_at, :].astype(f32), gain_ref[...])
            own[strip_at, :] = normed.astype(bf16)

        strips(rows, step)
        greet(nz)
        n1 = Gather(nz, own, n1_ref, *sems[:5])
        dy = Gather(nz, up_ref, dy_ref, *sems[5:10])
        n2 = Gather(nz, own2, n2_ref, *sems[10:])
        n1.start_along(UP)
        n1.start_along(DOWN)
        n1.start_across()
        keep = pltpu.make_async_copy(marks_ref, all_ref.at[z], m_local)
        keep.start()

        def send(way, d):
            to = z + d if way == UP else z - d
            return remote(marks_ref, all_ref.at[z], m_send.at[way, d], m_recv.at[way, d], {"expert": to})

        def take(way, d):
            dst = all_ref.at[z - d if way == UP else z + d]
            remote(dst, dst, m_send.at[way, d], m_recv.at[way, d], {"tensor": 1 - c}).wait_recv()

        for d in range(1, nz):
            for way in (UP, DOWN):
                pl.when(z + d < nz if way == UP else z >= d)(lambda way=way, d=d: send(way, d).start())

        def follow(d):
            pl.when(z == d)(lambda: dy.start_along(UP))
            pl.when(nz - 1 - z == d)(lambda: dy.start_along(DOWN))

        follow(0)
        for d in range(1, nz):
            for p in range(PIECES):
                n1.event(d, p)
            follow(d)
        dy.start_across()
        keep.wait()
        for d in range(1, nz):
            for way in (UP, DOWN):
                pl.when(z + d < nz if way == UP else z >= d)(lambda way=way, d=d: send(way, d).wait_send())
                pl.when(z >= d if way == UP else z + d < nz)(lambda way=way, d=d: take(way, d))
        n1.settle_all()
        n1.finish()
        save(n1_ref, n1_hbm)
        for load in loads:
            load.wait()

        def project(first, last):
            def one(i, carry):
                to = pl.ds(pl.multiple_of(i * full, full), full)
                qkv_ref[to, :] = jnp.dot(n1_ref[to, :], w[...], preferred_element_type=f32).astype(bf16)
                return carry

            lax.fori_loop(first, last, one, 0)

        def label():
            for b in range(nz):
                some = all_ref[b].astype(f32)
                seg_q[b * full : (b + 1) * full, :] = some.T[:, :1]
                seg_k[:, b * full : (b + 1) * full] = some[:1, :]

        def head(i):
            length = (i + 1) * full

            def one(h, carry):
                def part(k):
                    return pl.ds(pl.multiple_of(k * cols + h * HD, HD), HD)

                base = i * full
                scores[:, :length] = lax.dot_general(
                    qkv_ref[base : base + full, part(0)], qkv_ref[:length, part(1)], (((1,), (1,)), ((), ())),
                    preferred_element_type=f32,
                )

                def soften(j, inner):
                    local = pl.ds(pl.multiple_of(j * strip, strip), strip)
                    row = pl.ds(pl.multiple_of(base + j * strip, strip), strip)
                    place_q = base + j * strip + lax.broadcasted_iota(jnp.int32, (strip, length), 0)
                    place_k = lax.broadcasted_iota(jnp.int32, (strip, length), 1)
                    allowed = jnp.logical_and(place_k <= place_q, seg_k[:, :length] == seg_q[row, :])
                    value = jnp.where(allowed, scores[local, :length] * scale, -jnp.inf)
                    value = jnp.exp(value - jnp.max(value, axis=-1, keepdims=True))
                    share = 1.0 / jnp.sum(value, axis=-1, keepdims=True)
                    p_ref[h, row, :length] = (value * share).astype(bf16)
                    return inner

                lax.fori_loop(0, full // strip, soften, 0)
                if length < seq:
                    p_ref[h, base : base + full, length:] = jnp.zeros((full, seq - length), bf16)
                o_ref[base : base + full, pl.ds(pl.multiple_of(h * HD, HD), HD)] = jnp.dot(
                    p_ref[h, base : base + full, :length], qkv_ref[:length, part(2)], preferred_element_type=f32
                ).astype(bf16)
                return carry

            lax.fori_loop(0, heads, one, 0)

        works = [label] + [functools.partial(head, i) for i in range(nz)]
        left_events = [(d, p) for d in range(1, nz) for p in range(PIECES)]

        def events(count=None):
            for _ in range(len(left_events) if count is None else count):
                dy.event(*left_events.pop(0))

        project(0, 2)
        events(1)
        project(2, nz)
        events(1)
        for work in works:
            work()
            if len(left_events) > 2:
                events(1)

        def inside(way, d):
            return z + d < nz if way == UP else z >= d

        def send_heads(way, d):
            to = z + d if way == UP else z - d
            src = o_ref.at[pl.ds(pl.multiple_of(to * full, full), full)]
            return remote(src, heads_in.at[way, d], a_send.at[way, d], a_recv.at[way, d], {"expert": to})

        for d in range(nz - 1, 0, -1):
            for way in (UP, DOWN):
                pl.when(inside(way, d))(lambda way=way, d=d: send_heads(way, d).start())

        save(qkv_ref, qkv_hbm)
        save(p_ref, p_hbm)
        save(o_ref, o_hbm)
        tile = 512 if width % 512 == 0 else width

        def put(block, left, fresh):
            at = pl.ds(pl.multiple_of(block * cols, cols), cols)

            def one(i, carry):
                to = pl.ds(pl.multiple_of(i * tile, tile), tile)
                value = lax.dot_general(
                    left(), wo[to, at], (((1,), (1,)), ((), ())), preferred_element_type=f32
                )
                acc[:, to] = value if fresh else acc[:, to] + value
                return carry

            lax.fori_loop(0, width // tile, one, 0)

        put(z, lambda: o_ref[pl.ds(pl.multiple_of(z * full, full), full), :], True)
        events()
        for d in range(1, nz):
            for way in (UP, DOWN):
                @pl.when(z >= d if way == UP else z + d < nz)
                def _(way=way, d=d):
                    remote(
                        heads_in.at[way, d], heads_in.at[way, d], a_send.at[way, d], a_recv.at[way, d], {"tensor": 1 - c}
                    ).wait_recv()
                    put(z - d if way == UP else z + d, lambda: heads_in[way, d], False)

        def pack(at):
            give[at, :] = acc[pl.ds(pl.multiple_of((1 - c) * rows + at.start, STRIP), STRIP), :].astype(bf16)

        strips(rows, pack)
        swap = remote(give, take_in, e_send, e_recv, {"tensor": 1 - c})
        swap.start()
        swap.wait_recv()

        def norm_two(at):
            mixed = acc[pl.ds(pl.multiple_of(c * rows + at.start, STRIP), STRIP), :] + take_in[at, :].astype(f32)
            h = x_ref[at, :].astype(f32) + mixed
            normed, inverse = norm_rows(h, gain2_ref[...])
            h_ref[at, :] = h
            own2[at, :] = normed.astype(bf16)
            inv_own[at, :] = jnp.broadcast_to(inverse, (STRIP, 128))

        strips(rows, norm_two)
        spot = inv_ref.at[pl.ds(pl.multiple_of(c * rows, rows), rows)]
        keep_inv = pltpu.make_async_copy(inv_own, spot, i_sems.at[0])
        pass_on = remote(inv_own, spot, i_sems.at[1], i_sems.at[2], {"tensor": 1 - c})
        keep_inv.start()
        pass_on.start()
        n2.start_along(UP)
        n2.start_along(DOWN)
        n2.start_across()
        dy.settle_all()
        dy.finish()
        save(dy_ref, dy_hbm)
        a, b, back = acc.at[:, pl.ds(0, held)], acc.at[:, pl.ds(held, held)], scores.at[:, pl.ds(0, held)]

        def hidden(index):
            at = pl.ds(pl.multiple_of(index * full, full), full)
            logit_ref[at, :] = nt_dot(n2_ref[at, :], small_ref[...])
            a[...] = nn_dot(n2_ref[at, :], wg[...])
            b[...] = nn_dot(n2_ref[at, :], wu[...])
            back[...] = nn_dot(dy_ref[at, :], wd[...])

            def point(j, carry):
                row = pl.ds(pl.multiple_of(index * full + j * strip, strip), strip)
                local = pl.ds(pl.multiple_of(j * strip, strip), strip)
                column = lax.broadcasted_iota(jnp.int32, (strip, held), 1)
                valid = jnp.logical_and(column >= skip, column < skip + ffn)
                av, bv = a[local, :], b[local, :]
                kv = jnp.where(valid, back[local, :], 0.0)
                gv = 1.0 / (1.0 + jnp.exp(-logit_ref[row, gate_row : gate_row + 1]))
                sig = 1.0 / (1.0 + jnp.exp(-av))
                act = av * sig
                u = jnp.where(valid, act * bv, 0.0)
                last = lax.broadcasted_iota(jnp.int32, (strip, small.shape[0]), 1) == gate_row
                dgate_ref[row, :] = jnp.where(last, jnp.sum(u * kv, axis=-1, keepdims=True), 0.0)
                gu[row, :] = (gv * u).astype(bf16)
                du = gv * kv
                da[row, :] = (du * bv * (sig + act * (1.0 - sig))).astype(bf16)
                db[row, :] = (du * act).astype(bf16)
                return carry

            lax.fori_loop(0, full // strip, point, 0)
            for k, ref in enumerate((da, db, gu)):
                turned[k, :, at] = ref[at, :].T

        def arrivals(d):
            for way in (UP, DOWN):

                @pl.when(n2.inside(way, d))
                def _(way=way):
                    n2.settle(way, d)

        def pair(d):
            def one(k, carry):
                index = z + (2 * k - 1) * d
                pl.when(jnp.logical_and(index >= 0, index < nz))(lambda: hidden(index))
                return carry

            arrivals(d)
            lax.fori_loop(0, 2, one, 0)

        n2.settle(UP, 0)
        hidden(z)
        for d in range(1, nz):
            for p in range(PIECES):
                n2.event(d, p)
            if d > 1:
                pair(d - 1)
        pair(nz - 1)
        n2.finish()
        save(n2_ref, n2_hbm)
        save(da, da_hbm.at[0])
        save(db, db_hbm.at[0])
        save(gu, gu_hbm.at[0])

        def leave(i):
            slot = lax.rem(i, 2)
            if per > 1:
                dst = grad_hbm.at[pl.ds(i * per, per)]
            else:
                many = block // TILE
                to = pl.ds(pl.multiple_of(lax.rem(i, many) * TILE, TILE), TILE)
                dst = grad_hbm.at[pl.ds(i // many, 1), :, to]
            return pltpu.make_async_copy(slab.at[slot], dst, slab_sem.at[slot])

        def four(i, at):
            slot = lax.rem(i, 2)
            pl.when(i >= 2)(lambda: leave(i).wait())
            for k, right in enumerate((n2_ref, n2_ref, dy_ref)):
                value = nn_dot(turned[k, pl.ds(pl.multiple_of(skip, 16), ffn), :], right[:, at]).astype(bf16)
                for j in range(per):
                    slab[slot, j, k * ffn : (k + 1) * ffn, :] = value[:, j * lane : (j + 1) * lane]
            leave(i).start()

        tiles(slabs, four)
        leave(slabs - 2).wait()
        leave(slabs - 1).wait()
        keep_inv.wait()
        pass_on.wait()
        swap.wait_send()
        for d in range(1, nz):
            for way in (UP, DOWN):
                pl.when(inside(way, d))(lambda way=way, d=d: send_heads(way, d).wait_send())
        for copy in saves:
            copy.wait()

    hidden_shape = jax.ShapeDtypeStruct((1, seq, held), bf16)
    return pl.pallas_call(
        kernel,
        out_shape=[
            jax.ShapeDtypeStruct((seq, width), bf16),
            jax.ShapeDtypeStruct((seq, width), bf16),
            jax.ShapeDtypeStruct((nz,) + marks.shape, jnp.int32),
            jax.ShapeDtypeStruct((seq, 3 * cols), bf16),
            jax.ShapeDtypeStruct((heads, seq, seq), bf16),
            jax.ShapeDtypeStruct((seq, cols), bf16),
            jax.ShapeDtypeStruct((seq, width), bf16),
            jax.ShapeDtypeStruct((rows, width), f32),
            jax.ShapeDtypeStruct((full, 128), f32),
            jax.ShapeDtypeStruct((seq, small.shape[0]), f32),
            jax.ShapeDtypeStruct((groups, 3 * ffn, block), bf16),
            hidden_shape, hidden_shape, hidden_shape,
            jax.ShapeDtypeStruct((seq, small.shape[0]), f32),
        ],
        in_specs=[VMEM] * 6 + [ANY] * 7,
        out_specs=[ANY, ANY, VMEM, ANY, ANY, ANY, ANY, VMEM, ANY, VMEM, ANY, ANY, ANY, ANY, VMEM],
        scratch_shapes=[
            pltpu.VMEM((seq, width), bf16), pltpu.VMEM((seq, width), bf16), pltpu.VMEM((seq, 3 * cols), bf16),
            pltpu.VMEM((heads, seq, seq), bf16), pltpu.VMEM((seq, cols), bf16), pltpu.VMEM((seq, width), bf16),
            pltpu.VMEM((rows, width), bf16), pltpu.VMEM((width, 3 * cols), bf16), pltpu.VMEM((full, seq), f32),
            pltpu.VMEM((seq, 1), f32), pltpu.VMEM((1, seq), f32),
            pltpu.VMEM((2, nz, full, cols), bf16),
            pltpu.VMEM((full, width), f32),
            pltpu.VMEM((rows, width), bf16), pltpu.VMEM((rows, width), bf16), pltpu.VMEM((rows, width), bf16),
            pltpu.VMEM((rows, 128), f32), pltpu.VMEM(out_weight.shape, bf16),
            pltpu.VMEM((width, held), bf16), pltpu.VMEM((width, held), bf16), pltpu.VMEM((width, held), bf16),
            pltpu.VMEM((seq, held), bf16), pltpu.VMEM((seq, held), bf16), pltpu.VMEM((seq, held), bf16),
            pltpu.VMEM((3, held, seq), bf16), pltpu.VMEM((2, per, 3 * ffn, lane), bf16),
            pltpu.SemaphoreType.DMA((7,)),
            pltpu.SemaphoreType.DMA((2, nz)), pltpu.SemaphoreType.DMA((2, nz)), pltpu.SemaphoreType.DMA,
            pltpu.SemaphoreType.DMA((2, nz)), pltpu.SemaphoreType.DMA((2, nz)),
            pltpu.SemaphoreType.DMA, pltpu.SemaphoreType.DMA, pltpu.SemaphoreType.DMA((3,)),
            pltpu.SemaphoreType.DMA((9,)), pltpu.SemaphoreType.DMA((2,)),
        ]
        + gather_sems(nz) * 3,
        compiler_params=pltpu.CompilerParams(
            collective_id=name, has_side_effects=True, vmem_limit_bytes=63 * 1024 * 1024
        ),
    )(x, gain, upstream, marks, gain2, small, *weights, out_weight, *shared)


def attention_back(nz, d_h, n1, qkv, probs, o, out_weight, groups, part, name):
    seq, width = d_h.shape
    heads = probs.shape[0]
    cols = o.shape[1]
    full = seq // nz
    block = width // groups
    lane = min(block, TILE)
    per = TILE // lane
    slabs = width // TILE
    strip = 32
    scale = HD ** (-0.5)

    def kernel(dh_hbm, n1_hbm, qkv_ref, p_ref, o_ref, wo_hbm, part_hbm, heads_ref, grad_hbm, box_hbm,
               b_send, b_recv, b_local, dh_ref, n1_ref, wo, d_o, scores, ds, dk, dv, turned, o_turned, slab, in_sem, slab_sem):
        z, c = here()
        at = pl.ds(pl.multiple_of(z * cols, cols), cols)
        loads = [
            pltpu.make_async_copy(wo_hbm.at[:, at], wo, in_sem.at[0]),
            pltpu.make_async_copy(dh_hbm, dh_ref, in_sem.at[1]),
            pltpu.make_async_copy(n1_hbm, n1_ref, in_sem.at[2]),
        ]
        for load in loads:
            load.start()
        greet(nz)
        keep = pltpu.make_async_copy(part_hbm.at[z], box_hbm.at[z], b_local)
        keep.start()

        def send(way, d):
            to = z + d if way == UP else z - d
            return remote(part_hbm.at[to], box_hbm.at[z], b_send.at[way, d], b_recv.at[way, d], {"expert": to})

        def take(way, d):
            dst = box_hbm.at[z - d if way == UP else z + d]
            remote(dst, dst, b_send.at[way, d], b_recv.at[way, d], {"tensor": 1 - c}).wait_recv()

        for d in range(nz - 1, 0, -1):
            for way in (UP, DOWN):
                pl.when(z + d < nz if way == UP else z >= d)(lambda way=way, d=d: send(way, d).start())
        o_turned[...] = o_ref[...].T
        loads[0].wait()
        loads[1].wait()

        def project(i, to):
            d_o[to, :] = nn_dot(dh_ref[to, :], wo[...]).astype(bf16)

        tiles(seq // TILE, project)

        def head(h, carry):
            def part(k):
                return pl.ds(pl.multiple_of(k * cols + h * HD, HD), HD)

            mine = part(0)
            for i in reversed(range(nz)):
                length = (i + 1) * full
                row = pl.ds(i * full, full)
                scores[:, :length] = nt_dot(d_o[row, mine], qkv_ref[:length, part(2)])

                def harden(j, inner, i=i, length=length):
                    local = pl.ds(pl.multiple_of(j * strip, strip), strip)
                    to = pl.ds(pl.multiple_of(i * full + j * strip, strip), strip)
                    mean = jnp.sum(
                        d_o[to, mine].astype(f32) * o_ref[to, mine].astype(f32), axis=-1, keepdims=True
                    )
                    value = p_ref[h, to, :length].astype(f32) * (scores[local, :length] - mean)
                    ds[local, :length] = value.astype(bf16)
                    return inner

                lax.fori_loop(0, full // strip, harden, 0)
                d_s = ds[:, :length]
                heads_ref[row, mine] = (nn_dot(d_s, qkv_ref[:length, part(1)]) * scale).astype(bf16)
                d_k = tn_dot(d_s, qkv_ref[row, mine])
                d_v = tn_dot(p_ref[h, row, :length], d_o[row, mine])
                if i == nz - 1:
                    dk[...], dv[...] = d_k, d_v
                else:
                    dk[:length, :] += d_k
                    dv[:length, :] += d_v
            heads_ref[:, part(1)] = (dk[...] * scale).astype(bf16)
            heads_ref[:, part(2)] = dv[...].astype(bf16)
            return carry

        lax.fori_loop(0, heads, head, 0)

        def turn(i, to):
            turned[:, to] = heads_ref[to, :].T

        tiles(seq // TILE, turn)
        loads[2].wait()

        def leave(i):
            slot = lax.rem(i, 2)
            if per > 1:
                dst = grad_hbm.at[pl.ds(i * per, per)]
            else:
                many = block // TILE
                to = pl.ds(pl.multiple_of(lax.rem(i, many) * TILE, TILE), TILE)
                dst = grad_hbm.at[pl.ds(i // many, 1), :, to]
            return pltpu.make_async_copy(slab.at[slot], dst, slab_sem.at[slot])

        def write(i, to):
            slot = lax.rem(i, 2)
            pl.when(i >= 2)(lambda: leave(i).wait())
            inner = nn_dot(turned[...], n1_ref[:, to]).astype(bf16)
            outer = nn_dot(o_turned[...], dh_ref[:, to]).astype(bf16)
            for j in range(per):
                slab[slot, j, : 3 * cols, :] = inner[:, j * lane : (j + 1) * lane]
                slab[slot, j, 3 * cols :, :] = outer[:, j * lane : (j + 1) * lane]
            leave(i).start()

        tiles(slabs, write)
        leave(slabs - 2).wait()
        leave(slabs - 1).wait()
        keep.wait()
        for d in range(1, nz):
            for way in (UP, DOWN):
                pl.when(z + d < nz if way == UP else z >= d)(lambda way=way, d=d: send(way, d).wait_send())
                pl.when(z >= d if way == UP else z + d < nz)(lambda way=way, d=d: take(way, d))

    return pl.pallas_call(
        kernel,
        out_shape=[
            jax.ShapeDtypeStruct((seq, 3 * cols), bf16),
            jax.ShapeDtypeStruct((groups, 4 * cols, block), bf16),
            jax.ShapeDtypeStruct(part.shape, bf16),
        ],
        in_specs=[ANY, ANY, VMEM, VMEM, VMEM, ANY, ANY],
        out_specs=[VMEM, ANY, ANY],
        scratch_shapes=[
            pltpu.SemaphoreType.DMA((2, nz)), pltpu.SemaphoreType.DMA((2, nz)), pltpu.SemaphoreType.DMA,
            pltpu.VMEM((seq, width), bf16), pltpu.VMEM((seq, width), bf16), pltpu.VMEM((width, cols), bf16),
            pltpu.VMEM((seq, cols), bf16), pltpu.VMEM((full, seq), f32), pltpu.VMEM((full, seq), bf16),
            pltpu.VMEM((seq, HD), f32), pltpu.VMEM((seq, HD), f32),
            pltpu.VMEM((3 * cols, seq), bf16), pltpu.VMEM((cols, seq), bf16), pltpu.VMEM((2, per, 4 * cols, lane), bf16),
            pltpu.SemaphoreType.DMA((3,)), pltpu.SemaphoreType.DMA((2,)),
        ],
        compiler_params=params(name),
    )(d_h, n1, qkv, probs, o, out_weight, part)


def spread_turned(nz, part, splits, name):
    _, columns, block = part.shape
    cols = columns // splits

    def kernel(in_ref, *rest):
        outs, (box, send_sem, recv_sem) = rest[:splits], rest[splits:]
        z, c = here()
        greet(nz)

        def send(way, d):
            to = z + d if way == UP else z - d
            return remote(in_ref.at[to], box.at[z], send_sem.at[way, d], recv_sem.at[way, d], {"expert": to})

        def take(way, d):
            dst = box.at[z - d if way == UP else z + d]
            remote(dst, dst, send_sem.at[way, d], recv_sem.at[way, d], {"tensor": 1 - c}).wait_recv()

        for d in range(nz - 1, 0, -1):
            for way in (UP, DOWN):
                pl.when(z + d < nz if way == UP else z >= d)(lambda way=way, d=d: send(way, d).start())
        box[z] = in_ref[z]
        for d in range(1, nz):
            for way in (UP, DOWN):
                pl.when(z + d < nz if way == UP else z >= d)(lambda way=way, d=d: send(way, d).wait_send())
                pl.when(z >= d if way == UP else z + d < nz)(lambda way=way, d=d: take(way, d))
        for j in range(splits):
            for b in range(nz):
                value = box[b, j * cols : (j + 1) * cols, :].astype(f32).T
                outs[j][:, b * cols : (b + 1) * cols] = value

    return pl.pallas_call(
        kernel,
        out_shape=[jax.ShapeDtypeStruct((block, nz * cols), f32)] * splits,
        in_specs=[VMEM],
        out_specs=[VMEM] * splits,
        scratch_shapes=[
            pltpu.VMEM(part.shape, bf16), pltpu.SemaphoreType.DMA((2, nz)), pltpu.SemaphoreType.DMA((2, nz)),
        ],
        compiler_params=params(name),
    )(part)


PART = 512


class Products:
    def __init__(self, nz, experts, shared, extra):
        self.nz, self.experts, self.shared = nz, experts, shared
        _, self.seq, self.kept = experts[0][0][0].shape
        _, self.ffn, self.width = experts[0][1][0].shape
        self.held = shared[0][0][0].shape[2]
        self.own = shared[0][1].shape[1] // nz
        self.more = [] if extra is None else list(extra)
        self.inputs = (
            [left[0] for left, _ in experts] + [right[0] for _, right in experts] + [left[0] for left, _ in shared]
            + [right for _, right in shared] + self.more
        )
        ne, ns = len(experts), len(shared)
        self.specs = [ANY] * (2 * (ne + ns)) + [VMEM] * len(self.more)
        self.scratch = [
            pltpu.VMEM((self.seq, ne * self.kept), bf16), pltpu.VMEM((ne * self.kept, self.width), bf16),
            pltpu.VMEM((self.seq, ns * self.held), bf16), pltpu.VMEM((self.width, ns * self.held), bf16),
            pltpu.SemaphoreType.DMA((self.width // PART, ne + ns)), pltpu.SemaphoreType.DMA((nz, ne + ns)),
        ]

    def bind(self, refs, scratch):
        ne, ns = len(self.experts), len(self.shared)
        self.left, self.right, self.sleft, self.sright, self.r_sem, self.l_sem = scratch
        self.e_left, self.e_right = refs[:ne], refs[ne : 2 * ne]
        self.s_left, self.s_right = refs[2 * ne : 2 * ne + ns], refs[2 * ne + ns : 2 * (ne + ns)]
        self.small = refs[2 * (ne + ns) :]
        self.first = pl.multiple_of(lax.axis_index("expert") * self.own // LANES * LANES, LANES)

    def rights(self, j):
        to = pl.ds(pl.multiple_of(j * PART, PART), PART)
        for i, (_, (_, index)) in enumerate(self.experts):
            dst = self.right.at[pl.ds(i * self.kept, self.ffn), to]
            yield pltpu.make_async_copy(self.e_right[i].at[index, :, to], dst, self.r_sem.at[j, i])
        for i in range(len(self.shared)):
            src = self.s_right[i].at[to, pl.ds(self.first, self.held)]
            dst = self.sright.at[to, pl.ds(i * self.held, self.held)]
            yield pltpu.make_async_copy(src, dst, self.r_sem.at[j, len(self.experts) + i])

    def lefts(self, b):
        rows = self.seq // self.nz
        at = pl.ds(pl.multiple_of(b * rows, rows), rows)
        for i, ((_, index), _) in enumerate(self.experts):
            dst = self.left.at[at, pl.ds(i * self.kept, self.kept)]
            yield pltpu.make_async_copy(self.e_left[i].at[index, at], dst, self.l_sem.at[b, i])
        for i, ((_, index), _) in enumerate(self.shared):
            dst = self.sleft.at[at, pl.ds(i * self.held, self.held)]
            yield pltpu.make_async_copy(self.s_left[i].at[index, at], dst, self.l_sem.at[b, len(self.experts) + i])

    def fetch(self, order):
        for copy in self.lefts(order(0)):
            copy.start()
        for j in range(self.width // PART):
            for copy in self.rights(j):
                copy.start()
        for k in range(1, self.nz):
            for copy in self.lefts(order(k)):
                copy.start()
        if self.kept > self.ffn:
            for i in range(len(self.experts)):
                self.right[i * self.kept + self.ffn : (i + 1) * self.kept, :] = jnp.zeros(
                    (self.kept - self.ffn, self.width), bf16
                )

    def block(self, k, b, out, start, end):
        rows = self.seq // self.nz
        at = pl.ds(pl.multiple_of(b * rows, rows), rows)
        if start == 0:
            for copy in self.lefts(b):
                copy.wait()

        def one(j, carry):
            @pl.when(k == 0)
            def _():
                for copy in self.rights(j):
                    copy.wait()

            to = pl.ds(pl.multiple_of(j * PART, PART), PART)
            value = nn_dot(self.left[at, :], self.right[:, to]) + nt_dot(self.sleft[at, :], self.sright[to, :])
            if self.more:
                value += nt_dot(self.small[0][at, :], self.small[1][to, :])
            out[at, to] = value.astype(bf16)
            return carry

        lax.fori_loop(start, end, one, 0)


def reduce_and_gather(nz, products, h, gain, upstream, name):
    rows, width = h.shape
    n_in, n_scratch = len(products.inputs), len(products.scratch)

    def kernel(*refs):
        p_refs, (h_ref, gain_ref, up_ref, out_ref, dh_ref, gg_ref) = refs[:n_in], refs[n_in : n_in + 6]
        rest = refs[n_in + 6 :]
        p_scratch, (part, own), rest = rest[:n_scratch], rest[n_scratch : n_scratch + 2], rest[n_scratch + 2 :]
        scratch, sems = rest[:REDUCE_SCRATCH], rest[REDUCE_SCRATCH:]
        total = scratch[3]
        products.bind(p_refs, p_scratch)
        reducer = Reducer(nz, part, *scratch)
        products.fetch(reducer.block)
        greet(nz)
        ends = reducer.ends()

        def one(s, carry):
            products.block(s, reducer.block(s), part, 0, 1)
            pl.when(jnp.logical_and(ends, s >= 1))(lambda: reducer.forward(s - 1))
            products.block(s, reducer.block(s), part, 1, width // PART)
            reducer.begin(s)
            pl.when(jnp.logical_and(jnp.logical_not(ends), s >= 2))(lambda: reducer.forward(s - 2))
            return carry

        lax.fori_loop(0, nz, one, 0)
        pl.when(jnp.logical_not(ends))(lambda: reducer.forward(nz - 2))
        reducer.finish()
        gg_ref[...] = jnp.zeros_like(gg_ref)

        def step(at):
            change, along = norm_back(h_ref[at, :], gain_ref[...], total[at, :])
            dh = up_ref[at, :].astype(f32) + change
            dh_ref[at, :] = dh
            own[at, :] = dh.astype(bf16)
            gg_ref[...] += along

        strips(rows, step)
        gather_rows(nz, own, out_ref, *sems)
        reducer.drain()

    return pl.pallas_call(
        kernel,
        out_shape=[
            jax.ShapeDtypeStruct((nz * 2 * rows, width), bf16),
            jax.ShapeDtypeStruct((rows, width), f32),
            jax.ShapeDtypeStruct((STRIP, width), f32),
        ],
        in_specs=products.specs + [VMEM] * 3,
        out_specs=[ANY, VMEM, VMEM],
        scratch_shapes=products.scratch
        + [pltpu.VMEM((nz * 2 * rows, width), bf16), pltpu.VMEM((rows, width), bf16)]
        + reduce_scratch(nz, rows, width)
        + gather_sems(nz),
        compiler_params=params(name),
    )(*products.inputs, h, gain, upstream)


def reduce_last(nz, d_heads, weights, x, gain, dh, products, h, small, box, name):
    rows, width = x.shape
    cols = d_heads.shape[1] // 3
    n, small_rows, lanes = small.shape
    box_rows, block = box.shape[1] // 3, box.shape[2]
    n_in, n_scratch = len(products.inputs), len(products.scratch)

    def kernel(*refs):
        p_refs, (
            d_ref, wq_hbm, wk_hbm, wv_hbm, x_ref, gain_ref, dh_ref, h_ref, small_ref, box_ref, in_ref, out_ref, sum_ref, *turned,
        ) = refs[:n_in], refs[n_in : n_in + 16]
        gg_ref, s_out, s_box, s_total, s_other, s_send, s_recv, swap_sem = refs[n_in + 16 : n_in + 24]
        rest = refs[n_in + 24 :]
        p_scratch, (d_part, b_part, own, sems, w_ref, w_sem), rest = (
            rest[:n_scratch], rest[n_scratch : n_scratch + 6], rest[n_scratch + 6 :],
        )
        mine = pl.ds(pl.multiple_of(lax.axis_index("expert") * cols, cols), cols)
        loads = [
            pltpu.make_async_copy(src.at[:, mine], w_ref.at[:, pl.ds(i * cols, cols)], w_sem.at[i])
            for i, src in enumerate((wq_hbm, wk_hbm, wv_hbm))
        ]
        for load in loads:
            load.start()
        d_scratch, b_scratch = rest[:REDUCE_SCRATCH], rest[REDUCE_SCRATCH:]
        d_total, b_total = d_scratch[3], b_scratch[3]
        products.bind(p_refs, p_scratch)
        first, second = Reducer(nz, d_part, *d_scratch), Reducer(nz, b_part, *b_scratch)
        z, c = here()
        me = lax.axis_index("dp") * nz + z
        barrier = pltpu.get_barrier_semaphore()

        def peer(q):
            to = lax.rem(me + q, n)
            return to, {"dp": to // nz, "expert": lax.rem(to, nz)}

        pl.semaphore_signal(barrier, inc=1, device_id={"tensor": 1 - c}, device_id_type=MESH)
        for q in range(1, n):
            pl.semaphore_signal(barrier, inc=1, device_id=peer(q)[1], device_id_type=MESH)
        pl.semaphore_wait(barrier, n)

        def send_small(q):
            to, device = peer(q)
            return remote(s_out.at[to], s_box.at[q], s_send.at[q], s_recv.at[q], device)

        ends = first.ends()
        middle = jnp.logical_not(ends)

        def inner(block):
            at = pl.ds(pl.multiple_of(block * 2 * rows, 2 * rows), 2 * rows)

            def one(j, carry):
                to = pl.ds(pl.multiple_of(j * PART, PART), PART)
                d_part[at, to] = nt_dot(d_ref[at, :], w_ref[to, :]).astype(bf16)
                return carry

            lax.fori_loop(0, width // PART, one, 0)

        def one(s, carry):
            inner(first.block(s))
            first.begin(s)
            pl.when(jnp.logical_and(ends, s >= 1))(lambda: first.forward(s - 1))
            return carry

        def two(s, carry):
            products.block(s, second.block(s), b_part, 0, width // PART)
            second.begin(s)

            @pl.when(s >= 1)
            def _():
                pl.when(ends)(lambda: second.forward(s - 1))
                pl.when(middle)(lambda: first.forward(s - 1))

            return carry

        def three(s, carry):
            pl.when(middle)(lambda: second.forward(s))
            return carry

        for load in loads:
            load.wait()
        products.fetch(second.block)
        lax.fori_loop(0, nz, one, 0)
        lax.fori_loop(0, nz, two, 0)
        lax.fori_loop(0, nz - 1, three, 0)
        for i in range(3):
            for b in range(nz):
                value = box_ref[b, i * box_rows : (i + 1) * box_rows, :].astype(f32).T
                turned[i][:, b * box_rows : (b + 1) * box_rows] = value
        first.finish()
        gg_ref[...] = jnp.zeros_like(gg_ref)

        def step(at):
            change, along = norm_back(x_ref[at, :].astype(f32), gain_ref[...], d_total[at, :])
            own[0, at, :] = dh_ref[at, :] + change
            gg_ref[...] += along

        strips(rows, step)

        def leave(i, ref):
            spot = ref.at[pl.ds(pl.multiple_of(c * rows, rows), rows)]
            return (
                pltpu.make_async_copy(own.at[i], spot, sems.at[i, 0]),
                remote(own.at[i], spot, sems.at[i, 1], sems.at[i, 2], {"tensor": 1 - c}),
            )

        for copy in leave(0, in_ref):
            copy.start()
        first_row = jnp.sum(gg_ref[...], axis=0, keepdims=True)
        for q in range(n):
            s_out[q] = small_ref[q]
            s_out[q, :1, :] = first_row[:, q * lanes : (q + 1) * lanes]
        for q in range(1, n):
            send_small(q).start()
        second.finish()

        def last(at):
            own[1, at, :] = h_ref[at, :] + b_total[at, :]

        strips(rows, last)
        for copy in leave(1, out_ref):
            copy.start()
        s_total[...] = s_out[me]
        for q in range(1, n):
            send_small(q).wait_recv()
            s_total[...] += s_box[q]
        swap = remote(s_total, s_other, swap_sem.at[0], swap_sem.at[1], {"tensor": 1 - c})
        swap.start()
        first.drain()
        second.drain()
        swap.wait_recv()
        sum_ref[...] = s_total[...] + s_other[...]
        swap.wait_send()
        for q in range(1, n):
            send_small(q).wait_send()
        for copy in (*leave(0, in_ref), *leave(1, out_ref)):
            copy.wait()

    return pl.pallas_call(
        kernel,
        out_shape=[
            jax.ShapeDtypeStruct((2 * rows, width), f32),
            jax.ShapeDtypeStruct((2 * rows, width), f32),
            jax.ShapeDtypeStruct((small_rows, lanes), f32),
        ]
        + [jax.ShapeDtypeStruct((block, nz * box_rows), f32)] * 3,
        in_specs=products.specs + [VMEM] + [ANY] * 3 + [VMEM] * 6,
        out_specs=[ANY, ANY] + [VMEM] * 4,
        scratch_shapes=[
            pltpu.VMEM((STRIP, width), f32), pltpu.VMEM(small.shape, f32), pltpu.VMEM(small.shape, f32),
            pltpu.VMEM((small_rows, lanes), f32), pltpu.VMEM((small_rows, lanes), f32),
            pltpu.SemaphoreType.DMA((n,)), pltpu.SemaphoreType.DMA((n,)), pltpu.SemaphoreType.DMA((2,)),
        ]
        + products.scratch
        + [
            pltpu.VMEM((nz * 2 * rows, width), bf16), pltpu.VMEM((nz * 2 * rows, width), bf16),
            pltpu.VMEM((2, rows, width), f32), pltpu.SemaphoreType.DMA((2, 3)),
            pltpu.VMEM((width, 3 * cols), bf16), pltpu.SemaphoreType.DMA((3,)),
        ]
        + reduce_scratch(nz, rows, width) * 2,
        compiler_params=params(name, 60),
    )(*products.inputs, d_heads, *weights, x, gain, dh, h, small, box)


def cross_rows(left, right):
    return lax.dot_general(left, right, (((0,), (0,)), ((), ())), preferred_element_type=f32)


def cross_cols(left, right):
    return lax.dot_general(left, right, (((1,), (1,)), ((), ())), preferred_element_type=f32)


def dot(left, right):
    return jnp.dot(left, right, preferred_element_type=f32)


def two_parts(values):
    high = values.astype(bf16)
    return high, (values - high.astype(f32)).astype(bf16)


def body(
    tokens, segments, routes, norm1_gain, q_weight, k_weight, v_weight, o_weight, norm2_gain,
    router_weight, shared_gate_vector, shared_gate_weight, shared_up_weight, shared_down_weight,
    expert_gate_weight, expert_up_weight, expert_down_weight, out_grad,
):
    nz = lax.axis_size("expert")
    nc = lax.axis_size("tensor")
    z = lax.axis_index("expert")
    c = lax.axis_index("tensor")
    rows, width = tokens.shape
    own_rows = rows // nc
    local_count, _, ffn = expert_gate_weight.shape
    expert_count = local_count * nz
    head_cols = q_weight.shape[1] // nz
    shared_cols = shared_gate_weight.shape[1] // nz
    heads = head_cols // HD
    seq = rows * nz
    scale = HD ** (-0.5)
    gain1 = norm1_gain.astype(f32)[None]
    gain2 = norm2_gain.astype(f32)[None]

    def own(values):
        return lax.dynamic_slice_in_dim(values, c * own_rows, own_rows, 0)

    def head_slice(values):
        return lax.dynamic_slice_in_dim(values, z * head_cols, head_cols, 1)

    x_all_rows = tokens.astype(f32)
    inverse_one_rows = lax.rsqrt(jnp.mean(x_all_rows * x_all_rows, axis=-1) + epsilon)
    x = own(tokens)
    marks = jnp.concatenate([segments, routes.T, jnp.zeros((7 - routes.shape[1], rows), jnp.int32)], axis=0)
    upstream = own(out_grad)
    ndp = lax.axis_size("dp")
    small_rows_weight = jnp.concatenate([router_weight.T, shared_gate_vector[None]], axis=0)
    shared_weights = (shared_gate_weight, shared_up_weight, shared_down_weight)
    (
        n1, dy, all_marks, qkv, p_low, o, n2, h, inverse_two, logits, grad_s, da_s, db_s, gu_s, dgate_s,
    ) = forward_layer(
        nz, x, gain1, upstream, marks, (q_weight, k_weight, v_weight), o_weight, gain2, small_rows_weight, shared_weights,
        ndp * nz, 0,
    )
    all_routes = jnp.transpose(all_marks[:, 1 : 1 + routes.shape[1]], (0, 2, 1)).reshape(seq, routes.shape[1])

    probs = jax.nn.softmax(logits[:, :expert_count], axis=-1)
    chosen = jnp.any(all_routes[:, :, None] == jnp.arange(expert_count)[None, None, :], axis=1)
    gates = jnp.where(chosen, probs, 0.0)
    sigma = jax.nn.sigmoid(logits[:, expert_count:])

    turned = [jnp.swapaxes(w, 1, 2) for w in (expert_gate_weight, expert_up_weight, expert_down_weight)]
    grad_e, da_e, db_e, gu_e, dgate_e = hidden_layer(nz, n2, dy, gates, turned, ndp)

    d_probs = jnp.where(chosen, dgate_e, 0.0)
    d_logits = probs * (d_probs - jnp.sum(probs * d_probs, axis=-1, keepdims=True))
    d_vector = dgate_s[:, expert_count:] * (sigma * (1.0 - sigma))
    small = jnp.concatenate([d_logits, d_vector], axis=1)
    small_high, small_low = two_parts(small)
    small_weights = jnp.concatenate([router_weight, shared_gate_vector[:, None]], axis=1)
    fill = ((0, 0), (0, 128 - small.shape[1]))
    experts = range(local_count)
    d_n2 = Products(
        nz,
        [((da_e, i), (turned[0], i)) for i in experts] + [((db_e, i), (turned[1], i)) for i in experts],
        [((da_s, 0), shared_gate_weight), ((db_s, 0), shared_up_weight)],
        (jnp.pad(small_high, fill), jnp.pad(small_weights, fill)),
    )
    small_grad = cross_rows(n2, jnp.concatenate([small_high, small_low], axis=1))
    small_grad = small_grad[:, : expert_count + 1] + small_grad[:, expert_count + 1 :]


    def over_dp(grad):
        rows = grad.reshape(-1, grad.shape[-1])
        return lax.psum_scatter(rows, "dp", scatter_dimension=0, tiled=True)

    shared_part = over_dp(grad_s).reshape((nz,) + grad_s.shape[1:])
    expert_part = over_dp(grad_e).reshape(local_count, 3, ffn, -1)
    dhr, dh, grad_two = reduce_and_gather(nz, d_n2, h, gain2, upstream, 2)
    d_heads, grad_attention, shared_box = attention_back(
        nz, dhr, n1, qkv, p_low, o, o_weight, ndp * nz, shared_part, 1
    )
    attention_part = over_dp(grad_attention).reshape((nz,) + grad_attention.shape[1:])
    branch = Products(
        nz,
        [((gu_e, i), (turned[2], i)) for i in experts],
        [((gu_s, 0), shared_down_weight)],
        None,
    )
    dh_now, _ = lax.optimization_barrier((dh, grad_attention))
    small_rows = jnp.concatenate(
        [
            jnp.zeros((1, width), f32), jnp.sum(grad_two, axis=0)[None], small_grad.T,
            jnp.zeros((13 - expert_count, width), f32),
        ],
        axis=0,
    )
    count = ndp * nz
    small_blocks = jnp.swapaxes(small_rows.reshape(16, count, width // count), 0, 1)
    input_grad, layer_out, small_all, s_gate, s_up, s_down = reduce_last(
        nz, d_heads, (q_weight, k_weight, v_weight), x, gain1, dh_now, branch, h, small_blocks, shared_box, 3
    )
    stats = jnp.stack([inverse_one_rows, inverse_two[:, 0]])

    e_gate, e_up, e_down = (jnp.swapaxes(expert_part[:, k].astype(f32), 1, 2) for k in range(3))
    attention_part, e_gate, e_up, e_down, small_all = lax.optimization_barrier(
        (attention_part, e_gate, e_up, e_down, small_all)
    )
    g_q, g_k, g_v, g_o = spread_turned(nz, attention_part, 4, 6)
    g_one, g_two, g_router, g_vector = small_all[0], small_all[1], small_all[2 : 2 + expert_count].T, small_all[2 + expert_count]
    return (
        layer_out, input_grad, stats, g_one, g_q, g_k, g_v, g_o, g_two, g_router, g_vector,
        s_gate, s_up, s_down, e_gate, e_up, e_down,
    )


def solution(mesh):
    both = ("dp", "expert")
    cols = P(None, "tensor")
    placed = (
        P(both, None), P("dp", "expert"), P(both, None), P(), cols, cols, cols, cols, P(), P(), P(),
        cols, cols, cols, P("expert", None, "tensor"), P("expert", None, "tensor"),
        P("expert", None, "tensor"), P(both, None),
    )
    split = P(both, "tensor")
    experts = P("expert", "dp", "tensor")
    return jax.shard_map(
        body,
        mesh=mesh,
        in_specs=placed,
        out_specs=(
            P(both, None), P(both, None), P(None, both), P(both), split, split, split, split, P(both),
            P(both, None), P(both), split, split, split, experts, experts, experts,
        ),
        check_vma=False,
    )
```

```python
import functools

import jax
import jax.numpy as jnp
from jax import lax
from jax.experimental import pallas as pl
from jax.experimental.pallas import tpu as pltpu
from jax.sharding import PartitionSpec as P

HD = 128
MESH = pl.DeviceIdType.MESH
PIECES = 2
STRIP = 16
epsilon = 1e-06
f32 = jnp.float32
bf16 = jnp.bfloat16
UP, DOWN = 0, 1


def here():
    return lax.axis_index("expert"), lax.axis_index("tensor")


def greet(nz):
    z, c = here()
    barrier = pltpu.get_barrier_semaphore()

    def tell(device):
        pl.semaphore_signal(barrier, inc=1, device_id=device, device_id_type=MESH)

    tell({"tensor": 1 - c})
    for d in range(1, nz):
        tell({"expert": lax.rem(z + d, nz)})
    pl.semaphore_wait(barrier, nz)


def remote(src, dst, send, recv, device):
    return pltpu.make_async_remote_copy(
        src_ref=src, dst_ref=dst, send_sem=send, recv_sem=recv, device_id=device, device_id_type=MESH
    )


def strips(rows, step):
    def one(i, carry):
        step(pl.ds(pl.multiple_of(i * STRIP, STRIP), STRIP))
        return carry

    lax.fori_loop(0, rows // STRIP, one, 0)


GATHER_SEMS = 4


def gather_sems(nz):
    return [pltpu.SemaphoreType.DMA((2, nz, PIECES))] * GATHER_SEMS + [pltpu.SemaphoreType.DMA]


class Gather:
    def __init__(self, nz, own, out, z_send, z_recv, s_send, s_recv, local_sem):
        self.nz, self.own, self.out = nz, own, out
        self.z_send, self.z_recv, self.s_send, self.s_recv, self.local_sem = z_send, z_recv, s_send, s_recv, local_sem
        self.z, self.c = here()
        self.rows = own.shape[0]
        self.piece = self.rows // PIECES

    def origin(self, way, d):
        return self.z - d if way == UP else self.z + d

    def inside(self, way, d):
        return self.z >= d if way == UP else self.z + d < self.nz

    def onward(self, way):
        return self.z < self.nz - 1 if way == UP else self.z > 0

    def place(self, block, core, p):
        start = (block * 2 + core) * self.rows + p * self.piece
        return self.out.at[pl.ds(pl.multiple_of(start, self.piece), self.piece)]

    def source(self, way, d, p):
        if d == 0:
            return self.own.at[pl.ds(p * self.piece, self.piece)]
        return self.place(self.origin(way, d), self.c, p)

    def along(self, way, d, p):
        device = {"expert": self.z + 1 if way == UP else self.z - 1}
        dst = self.place(self.origin(way, d), self.c, p)
        return remote(self.source(way, d, p), dst, self.z_send.at[way, d, p], self.z_recv.at[way, d, p], device)

    def across(self, way, d, p):
        dst = self.place(self.origin(way, d), self.c, p)
        return remote(
            self.source(way, d, p), dst, self.s_send.at[way, d, p], self.s_recv.at[way, d, p], {"tensor": 1 - self.c}
        )

    def arrived(self, way, d, p):
        dst = self.place(self.origin(way, d), self.c, p)
        remote(dst, dst, self.z_send.at[way, d - 1, p], self.z_recv.at[way, d - 1, p], {"tensor": 1 - self.c}).wait_recv()

    def crossed(self, way, d, p):
        dst = self.place(self.origin(way, d), 1 - self.c, p)
        remote(dst, dst, self.s_send.at[way, d, p], self.s_recv.at[way, d, p], {"tensor": 1 - self.c}).wait_recv()

    def mine(self):
        dst = self.out.at[pl.ds(pl.multiple_of((self.z * 2 + self.c) * self.rows, self.rows), self.rows)]
        return pltpu.make_async_copy(self.own, dst, self.local_sem)

    def start_along(self, way):
        @pl.when(self.onward(way))
        def _():
            for p in range(PIECES):
                self.along(way, 0, p).start()

    def start_across(self):
        for p in range(PIECES):
            self.across(UP, 0, p).start()
        self.mine().start()

    def event(self, d, p):
        for way in (UP, DOWN):

            @pl.when(self.inside(way, d))
            def _(way=way):
                self.arrived(way, d, p)
                pl.when(self.onward(way))(lambda: self.along(way, d, p).start())
                self.across(way, d, p).start()

    def settle(self, way, d):
        for p in range(PIECES):
            self.crossed(way, d, p)
        if d == 0:
            self.mine().wait()

    def settle_all(self):
        self.settle(UP, 0)
        for d in range(1, self.nz):
            for way in (UP, DOWN):
                pl.when(self.inside(way, d))(functools.partial(self.settle, way, d))

    def finish(self):
        for p in range(PIECES):
            self.across(UP, 0, p).wait_send()
            for way in (UP, DOWN):
                pl.when(self.onward(way))(lambda way=way, p=p: self.along(way, 0, p).wait_send())
                for d in range(1, self.nz):

                    @pl.when(self.inside(way, d))
                    def _(way=way, d=d, p=p):
                        self.across(way, d, p).wait_send()
                        pl.when(self.onward(way))(lambda: self.along(way, d, p).wait_send())


def gather_rows(nz, own, out, *sems):
    gather = Gather(nz, own, out, *sems)
    gather.start_along(UP)
    gather.start_along(DOWN)
    gather.start_across()
    for d in range(1, nz):
        for p in range(PIECES):
            gather.event(d, p)
    gather.settle_all()
    gather.finish()


REDUCE_SCRATCH = 8


def reduce_scratch(nz, rows, width):
    return [
        pltpu.VMEM((nz, rows, width), bf16),
        pltpu.VMEM((nz + 1, rows, width), bf16),
        pltpu.VMEM((nz, rows, width), bf16),
        pltpu.VMEM((rows, width), f32),
        pltpu.SemaphoreType.DMA((nz, PIECES)),
        pltpu.SemaphoreType.DMA((nz, PIECES)),
        pltpu.SemaphoreType.DMA((nz, PIECES)),
        pltpu.SemaphoreType.DMA((nz + 1, PIECES)),
    ]


def block_order(nz, z, s):
    down = 2 * z // nz
    far = jnp.maximum(z, nz - 1 - z)
    near = nz - 1 - far
    late = s - (far - near)
    distance = jnp.where(late < 0, far - s, near - late // 2)
    sign = (1 - 2 * down) * jnp.where(late < 0, 1, 1 - 2 * lax.rem(late + nz * 2, 2))
    return z + sign * distance


class Reducer:
    def __init__(self, nz, part, side, inbox, outbox, total, s_send, s_recv, z_send, z_recv):
        self.nz, self.part, self.side, self.inbox, self.outbox, self.total = nz, part, side, inbox, outbox, total
        self.s_send, self.s_recv, self.z_send, self.z_recv = s_send, s_recv, z_send, z_recv
        self.z, self.c = here()
        self.rows = total.shape[0]
        self.piece = self.rows // PIECES

    def block(self, s):
        return block_order(self.nz, self.z, s)

    def cut(self, p):
        return pl.ds(p * self.piece, self.piece)

    def across(self, block, p):
        start = (block * 2 + 1 - self.c) * self.rows + p * self.piece
        src = self.part.at[pl.ds(pl.multiple_of(start, self.piece), self.piece)]
        return remote(
            src, self.side.at[block, self.cut(p)], self.s_send.at[block, p], self.s_recv.at[block, p],
            {"tensor": 1 - self.c},
        )

    def along(self, block, p):
        up = block > self.z
        slot = jnp.where(block == self.z - 1, self.nz, block)
        return remote(
            self.outbox.at[block, self.cut(p)], self.inbox.at[slot, self.cut(p)], self.z_send.at[block, p],
            self.z_recv.at[slot, p], {"expert": self.z + jnp.where(up, 1, -1)},
        )

    def arrived(self, slot, p):
        dst = self.inbox.at[slot, self.cut(p)]
        remote(dst, dst, self.z_send.at[0, p], self.z_recv.at[slot, p], {"tensor": 1 - self.c}).wait_recv()

    def mine(self, block, at):
        base = (block * 2 + self.c) * self.rows
        own = self.part[pl.ds(pl.multiple_of(base + at.start, STRIP), STRIP), :].astype(f32)
        return own + self.side[block, at, :].astype(f32)

    def strips(self, p, step):
        def one(i, carry):
            step(pl.ds(pl.multiple_of(p * self.piece + i * STRIP, STRIP), STRIP))
            return carry

        lax.fori_loop(0, self.piece // STRIP, one, 0)

    def ends(self):
        return jnp.logical_or(self.z == 0, self.z == self.nz - 1)

    def begin(self, s):
        for p in range(PIECES):
            self.across(self.block(s), p).start()

    def forward(self, s):
        block = self.block(s)
        behind = jnp.where(block > self.z, self.z, self.nz - 1 - self.z) > 0
        for p in range(PIECES):
            self.across(block, p).wait_recv()

            @pl.when(behind)
            def _(p=p):
                self.arrived(block, p)

                def add(at):
                    self.outbox[block, at, :] = (self.mine(block, at) + self.inbox[block, at, :].astype(f32)).astype(bf16)

                self.strips(p, add)

            @pl.when(jnp.logical_not(behind))
            def _(p=p):
                def keep(at):
                    self.outbox[block, at, :] = self.mine(block, at).astype(bf16)

                self.strips(p, keep)

            self.along(block, p).start()

    def finish(self):
        z, nz = self.z, self.nz
        for p in range(PIECES):
            self.across(z, p).wait_recv()

            def first(at):
                self.total[at, :] = self.mine(z, at)

            self.strips(p, first)
            for slot, some in ((z, z > 0), (nz, z < nz - 1)):

                @pl.when(some)
                def _(slot=slot, p=p):
                    self.arrived(slot, p)

                    def add(at):
                        self.total[at, :] += self.inbox[slot, at, :].astype(f32)

                    self.strips(p, add)

    def drain(self):
        def one(s, carry):
            block = self.block(s)
            for p in range(PIECES):
                self.across(block, p).wait_send()
                pl.when(s < self.nz - 1)(lambda p=p: self.along(block, p).wait_send())
            return carry

        lax.fori_loop(0, self.nz, one, 0)


def params(name, room=56):
    return pltpu.CompilerParams(collective_id=name, has_side_effects=True, vmem_limit_bytes=room * 1024 * 1024)


VMEM = pl.BlockSpec(memory_space=pltpu.VMEM)
ANY = pl.BlockSpec(memory_space=pl.ANY)


def norm_rows(values, gain):
    inverse = lax.rsqrt(jnp.mean(values * values, axis=-1, keepdims=True) + epsilon)
    return values * inverse * gain, inverse


def norm_back(values, gain, upstream):
    inverse = lax.rsqrt(jnp.mean(values * values, axis=-1, keepdims=True) + epsilon)
    scaled = upstream * gain
    inner = jnp.mean(scaled * values, axis=-1, keepdims=True)
    change = inverse * scaled - values * inverse * inverse * inverse * inner
    return change, upstream * values * inverse


def swap_rows(nz, own, out_ref, sems):
    z, c = here()
    rows = own.shape[0]
    spot = out_ref.at[pl.ds(pl.multiple_of(c * rows, rows), rows)]
    keep = pltpu.make_async_copy(own, spot, sems.at[0])
    pass_on = remote(own, spot, sems.at[1], sems.at[2], {"tensor": 1 - c})
    keep.start()
    pass_on.start()
    keep.wait()
    pass_on.wait()


TILE = 256
TALL = 512
LANES = 128


def nt_dot(left, right):
    return lax.dot_general(left, right, (((1,), (1,)), ((), ())), preferred_element_type=f32)


def tn_dot(left, right):
    return lax.dot_general(left, right, (((0,), (0,)), ((), ())), preferred_element_type=f32)


def nn_dot(left, right):
    return jnp.dot(left, right, preferred_element_type=f32)


def tiles(count, step, size=TILE):
    def one(i, carry):
        step(i, pl.ds(pl.multiple_of(i * size, size), size))
        return carry

    lax.fori_loop(0, count, one, 0)


def padded(columns):
    return -(-columns // LANES) * LANES


def window(columns, place):
    first = place * columns // LANES * LANES
    return first, place * columns - first


def window_width(columns, places):
    return max(padded(window(columns, i)[1] + columns) for i in range(places))


def hidden_layer(nz, n2, dy, gate, weights, groups):
    seq, width = n2.shape
    experts = weights[0].shape[0]
    buffers = min(experts, 2)
    held = weights[0].shape[1]
    ffn, kept = held, padded(held)
    block = width // groups
    lane = min(block, TILE)
    per = TILE // lane
    count, slabs = seq // TILE, width // TILE
    strip = 32
    w_shape = (held, width)

    def kernel(n2_hbm, dy_hbm, wg_hbm, wu_hbm, wd_hbm, gate_ref, grad_hbm, da_hbm, db_hbm, gu_hbm, dgate_ref,
               n2_ref, dy_ref, wg, wu, wd, a, b, back, da, db, gu, turned, slab, in_sem, row_sem, out_sem, slab_sem):
        z = lax.axis_index("expert")
        def weight(i, e):
            slot = lax.rem(e, buffers)
            src, dst = ((wg_hbm, wg), (wu_hbm, wu), (wd_hbm, wd))[i]
            return pltpu.make_async_copy(src.at[e], dst.at[slot], in_sem.at[i, slot])

        rows_in = [
            pltpu.make_async_copy(n2_hbm, n2_ref, row_sem.at[0]), pltpu.make_async_copy(dy_hbm, dy_ref, row_sem.at[1])
        ]
        weight(0, 0).start()
        rows_in[0].start()
        weight(1, 0).start()
        weight(2, 0).start()
        rows_in[1].start()
        if kept > held:
            for ref in (da, db, gu):
                ref[:, held:] = jnp.zeros((seq, kept - held), bf16)

        def expert(e, carry):
            slot = lax.rem(e, buffers)
            weight(0, e).wait()
            pl.when(e == 0)(rows_in[0].wait)

            def one(i, at):
                a[at, :] = nt_dot(n2_ref[at, :], wg[slot])

            tiles(seq // TALL, one, TALL)
            weight(1, e).wait()

            def two(i, at):
                b[at, :] = nt_dot(n2_ref[at, :], wu[slot])

            tiles(seq // TALL, two, TALL)
            weight(2, e).wait()
            pl.when(e == 0)(rows_in[1].wait)
            if experts > 1:

                @pl.when(e + 1 < experts)
                def _():
                    for i in range(3):
                        weight(i, e + 1).start()

            def three(i, at):
                back[...] = nt_dot(dy_ref[at, :], wd[slot])

                def point(j, carry):
                    row = pl.ds(pl.multiple_of(i * TILE + j * strip, strip), strip)
                    local = pl.ds(pl.multiple_of(j * strip, strip), strip)
                    av, bv, kv = a[row, :], b[row, :], back[local, :]
                    here_now = lax.broadcasted_iota(jnp.int32, (strip, gate.shape[1]), 1) == z * experts + e
                    gv = jnp.sum(jnp.where(here_now, gate_ref[row, :], 0.0), axis=-1, keepdims=True)
                    sig = 1.0 / (1.0 + jnp.exp(-av))
                    act = av * sig
                    u = act * bv
                    dgate_ref[row, :] += jnp.where(here_now, jnp.sum(u * kv, axis=-1, keepdims=True), 0.0)
                    gu[row, :held] = (gv * u).astype(bf16)
                    du = gv * kv
                    da[row, :held] = (du * bv * (sig + act * (1.0 - sig))).astype(bf16)
                    db[row, :held] = (du * act).astype(bf16)
                    return carry

                lax.fori_loop(0, TILE // strip, point, 0)
                for k, ref in enumerate((da, db, gu)):
                    turned[k, :, at] = ref[at, :held].T

            tiles(count, three)
            saves = [
                pltpu.make_async_copy(src, dst.at[e], out_sem.at[i])
                for i, (src, dst) in enumerate(((da, da_hbm), (db, db_hbm), (gu, gu_hbm)))
            ]
            for save in saves:
                save.start()

            def leave(i):
                slot = lax.rem(i, 2)
                below = pl.ds(pl.multiple_of(e * 3 * ffn, 16), 3 * ffn)
                if per > 1:
                    dst = grad_hbm.at[pl.ds(i * per, per), below]
                else:
                    many = block // TILE
                    to = pl.ds(pl.multiple_of(lax.rem(i, many) * TILE, TILE), TILE)
                    dst = grad_hbm.at[pl.ds(i // many, 1), below, to]
                return pltpu.make_async_copy(slab.at[slot], dst, slab_sem.at[slot])

            def four(i, at):
                slot = lax.rem(i, 2)
                pl.when(i >= 2)(lambda: leave(i).wait())
                for k, right in enumerate((n2_ref, n2_ref, dy_ref)):
                    value = nn_dot(turned[k], right[:, at]).astype(bf16)
                    for j in range(per):
                        slab[slot, j, k * ffn : (k + 1) * ffn, :] = value[:, j * lane : (j + 1) * lane]
                leave(i).start()

            tiles(slabs, four)
            leave(slabs - 2).wait()
            leave(slabs - 1).wait()
            for save in saves:
                save.wait()
            return carry

        dgate_ref[...] = jnp.zeros_like(dgate_ref)
        lax.fori_loop(0, experts, expert, 0)

    hidden = jax.ShapeDtypeStruct((experts, seq, kept), bf16)
    return pl.pallas_call(
        kernel,
        out_shape=[
            jax.ShapeDtypeStruct((groups, experts * 3 * ffn, block), bf16), hidden, hidden, hidden,
            jax.ShapeDtypeStruct(gate.shape, f32),
        ],
        in_specs=[ANY] * 5 + [VMEM],
        out_specs=[ANY] * 4 + [VMEM],
        scratch_shapes=[
            pltpu.VMEM((seq, width), bf16), pltpu.VMEM((seq, width), bf16),
            pltpu.VMEM((buffers,) + w_shape, bf16), pltpu.VMEM((buffers,) + w_shape, bf16), pltpu.VMEM((buffers,) + w_shape, bf16),
            pltpu.VMEM((seq, held), f32), pltpu.VMEM((seq, held), f32), pltpu.VMEM((TILE, held), f32),
            pltpu.VMEM((seq, kept), bf16), pltpu.VMEM((seq, kept), bf16), pltpu.VMEM((seq, kept), bf16),
            pltpu.VMEM((3, held, seq), bf16),
            pltpu.VMEM((2, per, 3 * ffn, lane), bf16),
            pltpu.SemaphoreType.DMA((3, buffers)), pltpu.SemaphoreType.DMA((2,)), pltpu.SemaphoreType.DMA((3,)),
            pltpu.SemaphoreType.DMA((2,)),
        ],
        compiler_params=pltpu.CompilerParams(vmem_limit_bytes=58 * 1024 * 1024),
    )(n2, dy, *weights, gate)


def forward_layer(nz, x, gain, upstream, marks, weights, out_weight, gain2, small, shared, groups, name):
    rows, width = x.shape
    seq = nz * 2 * rows
    cols = weights[0].shape[1] // nz
    heads = cols // HD
    full = 2 * rows
    strip = 32
    scale = HD ** (-0.5)
    ffn = shared[0].shape[1] // nz
    held = window_width(ffn, nz)
    block = width // groups
    lane = min(block, TILE)
    per = TILE // lane
    slabs = width // TILE
    gate_row = small.shape[0] - 1

    def kernel(x_ref, gain_ref, up_ref, marks_ref, gain2_ref, small_ref, wq_hbm, wk_hbm, wv_hbm, wo_hbm, wg_hbm, wu_hbm, wd_hbm,
               n1_hbm, dy_hbm, all_ref, qkv_hbm, p_hbm, o_hbm, n2_hbm, h_ref, inv_ref, logit_ref, grad_hbm, da_hbm, db_hbm,
               gu_hbm, dgate_ref,
               n1_ref, dy_ref, qkv_ref, p_ref, o_ref, n2_ref, own, w, scores, seg_q, seg_k, heads_in, acc, give, take_in, own2,
               inv_own, wo, wg, wu, wd, da, db, gu, turned, slab,
               w_sem, m_send, m_recv, m_local, a_send, a_recv, e_send, e_recv, i_sems, out_sem, slab_sem, *sems):
        z, c = here()
        at = pl.ds(pl.multiple_of(z * cols, cols), cols)
        loads = [
            pltpu.make_async_copy(src.at[:, at], w.at[:, pl.ds(i * cols, cols)], w_sem.at[i])
            for i, src in enumerate((wq_hbm, wk_hbm, wv_hbm))
        ]
        loads.append(pltpu.make_async_copy(wo_hbm, wo, w_sem.at[3]))
        first = pl.multiple_of(z * ffn // LANES * LANES, LANES)
        skip = z * ffn - first
        for i, (src, dst) in enumerate(((wg_hbm, wg), (wu_hbm, wu), (wd_hbm, wd))):
            loads.append(pltpu.make_async_copy(src.at[:, pl.ds(first, held)], dst, w_sem.at[4 + i]))
        saves = []

        def save(src, dst):
            saves.append(pltpu.make_async_copy(src, dst, out_sem.at[len(saves)]))
            saves[-1].start()

        for load in loads:
            load.start()

        def step(strip_at):
            normed, _ = norm_rows(x_ref[strip_at, :].astype(f32), gain_ref[...])
            own[strip_at, :] = normed.astype(bf16)

        strips(rows, step)
        greet(nz)
        n1 = Gather(nz, own, n1_ref, *sems[:5])
        dy = Gather(nz, up_ref, dy_ref, *sems[5:10])
        n2 = Gather(nz, own2, n2_ref, *sems[10:])
        n1.start_along(UP)
        n1.start_along(DOWN)
        n1.start_across()
        keep = pltpu.make_async_copy(marks_ref, all_ref.at[z], m_local)
        keep.start()

        def send(way, d):
            to = z + d if way == UP else z - d
            return remote(marks_ref, all_ref.at[z], m_send.at[way, d], m_recv.at[way, d], {"expert": to})

        def take(way, d):
            dst = all_ref.at[z - d if way == UP else z + d]
            remote(dst, dst, m_send.at[way, d], m_recv.at[way, d], {"tensor": 1 - c}).wait_recv()

        for d in range(1, nz):
            for way in (UP, DOWN):
                pl.when(z + d < nz if way == UP else z >= d)(lambda way=way, d=d: send(way, d).start())

        def follow(d):
            pl.when(z == d)(lambda: dy.start_along(UP))
            pl.when(nz - 1 - z == d)(lambda: dy.start_along(DOWN))

        follow(0)
        for d in range(1, nz):
            for p in range(PIECES):
                n1.event(d, p)
            follow(d)
        dy.start_across()
        keep.wait()
        for d in range(1, nz):
            for way in (UP, DOWN):
                pl.when(z + d < nz if way == UP else z >= d)(lambda way=way, d=d: send(way, d).wait_send())
                pl.when(z >= d if way == UP else z + d < nz)(lambda way=way, d=d: take(way, d))
        n1.settle_all()
        n1.finish()
        save(n1_ref, n1_hbm)
        for load in loads:
            load.wait()

        def project(first, last):
            def one(i, carry):
                to = pl.ds(pl.multiple_of(i * full, full), full)
                qkv_ref[to, :] = jnp.dot(n1_ref[to, :], w[...], preferred_element_type=f32).astype(bf16)
                return carry

            lax.fori_loop(first, last, one, 0)

        def label():
            for b in range(nz):
                some = all_ref[b].astype(f32)
                seg_q[b * full : (b + 1) * full, :] = some.T[:, :1]
                seg_k[:, b * full : (b + 1) * full] = some[:1, :]

        def head(i):
            length = (i + 1) * full

            def one(h, carry):
                def part(k):
                    return pl.ds(pl.multiple_of(k * cols + h * HD, HD), HD)

                base = i * full
                scores[:, :length] = lax.dot_general(
                    qkv_ref[base : base + full, part(0)], qkv_ref[:length, part(1)], (((1,), (1,)), ((), ())),
                    preferred_element_type=f32,
                )

                def soften(j, inner):
                    local = pl.ds(pl.multiple_of(j * strip, strip), strip)
                    row = pl.ds(pl.multiple_of(base + j * strip, strip), strip)
                    place_q = base + j * strip + lax.broadcasted_iota(jnp.int32, (strip, length), 0)
                    place_k = lax.broadcasted_iota(jnp.int32, (strip, length), 1)
                    allowed = jnp.logical_and(place_k <= place_q, seg_k[:, :length] == seg_q[row, :])
                    value = jnp.where(allowed, scores[local, :length] * scale, -jnp.inf)
                    value = jnp.exp(value - jnp.max(value, axis=-1, keepdims=True))
                    share = 1.0 / jnp.sum(value, axis=-1, keepdims=True)
                    p_ref[h, row, :length] = (value * share).astype(bf16)
                    return inner

                lax.fori_loop(0, full // strip, soften, 0)
                if length < seq:
                    p_ref[h, base : base + full, length:] = jnp.zeros((full, seq - length), bf16)
                o_ref[base : base + full, pl.ds(pl.multiple_of(h * HD, HD), HD)] = jnp.dot(
                    p_ref[h, base : base + full, :length], qkv_ref[:length, part(2)], preferred_element_type=f32
                ).astype(bf16)
                return carry

            lax.fori_loop(0, heads, one, 0)

        works = [label] + [functools.partial(head, i) for i in range(nz)]
        left_events = [(d, p) for d in range(1, nz) for p in range(PIECES)]

        def events(count=None):
            for _ in range(len(left_events) if count is None else count):
                dy.event(*left_events.pop(0))

        project(0, 2)
        events(1)
        project(2, nz)
        events(1)
        for work in works:
            work()
            if len(left_events) > 2:
                events(1)

        def inside(way, d):
            return z + d < nz if way == UP else z >= d

        def send_heads(way, d):
            to = z + d if way == UP else z - d
            src = o_ref.at[pl.ds(pl.multiple_of(to * full, full), full)]
            return remote(src, heads_in.at[way, d], a_send.at[way, d], a_recv.at[way, d], {"expert": to})

        for d in range(nz - 1, 0, -1):
            for way in (UP, DOWN):
                pl.when(inside(way, d))(lambda way=way, d=d: send_heads(way, d).start())

        save(qkv_ref, qkv_hbm)
        save(p_ref, p_hbm)
        save(o_ref, o_hbm)
        tile = 512 if width % 512 == 0 else width

        def put(block, left, fresh):
            at = pl.ds(pl.multiple_of(block * cols, cols), cols)

            def one(i, carry):
                to = pl.ds(pl.multiple_of(i * tile, tile), tile)
                value = lax.dot_general(
                    left(), wo[to, at], (((1,), (1,)), ((), ())), preferred_element_type=f32
                )
                acc[:, to] = value if fresh else acc[:, to] + value
                return carry

            lax.fori_loop(0, width // tile, one, 0)

        put(z, lambda: o_ref[pl.ds(pl.multiple_of(z * full, full), full), :], True)
        events()
        for d in range(1, nz):
            for way in (UP, DOWN):
                @pl.when(z >= d if way == UP else z + d < nz)
                def _(way=way, d=d):
                    remote(
                        heads_in.at[way, d], heads_in.at[way, d], a_send.at[way, d], a_recv.at[way, d], {"tensor": 1 - c}
                    ).wait_recv()
                    put(z - d if way == UP else z + d, lambda: heads_in[way, d], False)

        def pack(at):
            give[at, :] = acc[pl.ds(pl.multiple_of((1 - c) * rows + at.start, STRIP), STRIP), :].astype(bf16)

        strips(rows, pack)
        swap = remote(give, take_in, e_send, e_recv, {"tensor": 1 - c})
        swap.start()
        swap.wait_recv()

        def norm_two(at):
            mixed = acc[pl.ds(pl.multiple_of(c * rows + at.start, STRIP), STRIP), :] + take_in[at, :].astype(f32)
            h = x_ref[at, :].astype(f32) + mixed
            normed, inverse = norm_rows(h, gain2_ref[...])
            h_ref[at, :] = h
            own2[at, :] = normed.astype(bf16)
            inv_own[at, :] = jnp.broadcast_to(inverse, (STRIP, 128))

        strips(rows, norm_two)
        spot = inv_ref.at[pl.ds(pl.multiple_of(c * rows, rows), rows)]
        keep_inv = pltpu.make_async_copy(inv_own, spot, i_sems.at[0])
        pass_on = remote(inv_own, spot, i_sems.at[1], i_sems.at[2], {"tensor": 1 - c})
        keep_inv.start()
        pass_on.start()
        n2.start_along(UP)
        n2.start_along(DOWN)
        n2.start_across()
        dy.settle_all()
        dy.finish()
        save(dy_ref, dy_hbm)
        a, b, back = acc.at[:, pl.ds(0, held)], acc.at[:, pl.ds(held, held)], scores.at[:, pl.ds(0, held)]

        def hidden(index):
            at = pl.ds(pl.multiple_of(index * full, full), full)
            logit_ref[at, :] = nt_dot(n2_ref[at, :], small_ref[...])
            a[...] = nn_dot(n2_ref[at, :], wg[...])
            b[...] = nn_dot(n2_ref[at, :], wu[...])
            back[...] = nn_dot(dy_ref[at, :], wd[...])

            def point(j, carry):
                row = pl.ds(pl.multiple_of(index * full + j * strip, strip), strip)
                local = pl.ds(pl.multiple_of(j * strip, strip), strip)
                column = lax.broadcasted_iota(jnp.int32, (strip, held), 1)
                valid = jnp.logical_and(column >= skip, column < skip + ffn)
                av, bv = a[local, :], b[local, :]
                kv = jnp.where(valid, back[local, :], 0.0)
                gv = 1.0 / (1.0 + jnp.exp(-logit_ref[row, gate_row : gate_row + 1]))
                sig = 1.0 / (1.0 + jnp.exp(-av))
                act = av * sig
                u = jnp.where(valid, act * bv, 0.0)
                last = lax.broadcasted_iota(jnp.int32, (strip, small.shape[0]), 1) == gate_row
                dgate_ref[row, :] = jnp.where(last, jnp.sum(u * kv, axis=-1, keepdims=True), 0.0)
                gu[row, :] = (gv * u).astype(bf16)
                du = gv * kv
                da[row, :] = (du * bv * (sig + act * (1.0 - sig))).astype(bf16)
                db[row, :] = (du * act).astype(bf16)
                return carry

            lax.fori_loop(0, full // strip, point, 0)
            for k, ref in enumerate((da, db, gu)):
                turned[k, :, at] = ref[at, :].T

        def arrivals(d):
            for way in (UP, DOWN):

                @pl.when(n2.inside(way, d))
                def _(way=way):
                    n2.settle(way, d)

        def pair(d):
            def one(k, carry):
                index = z + (2 * k - 1) * d
                pl.when(jnp.logical_and(index >= 0, index < nz))(lambda: hidden(index))
                return carry

            arrivals(d)
            lax.fori_loop(0, 2, one, 0)

        n2.settle(UP, 0)
        hidden(z)
        for d in range(1, nz):
            for p in range(PIECES):
                n2.event(d, p)
            if d > 1:
                pair(d - 1)
        pair(nz - 1)
        n2.finish()
        save(n2_ref, n2_hbm)
        save(da, da_hbm.at[0])
        save(db, db_hbm.at[0])
        save(gu, gu_hbm.at[0])

        def leave(i):
            slot = lax.rem(i, 2)
            if per > 1:
                dst = grad_hbm.at[pl.ds(i * per, per)]
            else:
                many = block // TILE
                to = pl.ds(pl.multiple_of(lax.rem(i, many) * TILE, TILE), TILE)
                dst = grad_hbm.at[pl.ds(i // many, 1), :, to]
            return pltpu.make_async_copy(slab.at[slot], dst, slab_sem.at[slot])

        def four(i, at):
            slot = lax.rem(i, 2)
            pl.when(i >= 2)(lambda: leave(i).wait())
            for k, right in enumerate((n2_ref, n2_ref, dy_ref)):
                value = nn_dot(turned[k, pl.ds(pl.multiple_of(skip, 16), ffn), :], right[:, at]).astype(bf16)
                for j in range(per):
                    slab[slot, j, k * ffn : (k + 1) * ffn, :] = value[:, j * lane : (j + 1) * lane]
            leave(i).start()

        tiles(slabs, four)
        leave(slabs - 2).wait()
        leave(slabs - 1).wait()
        keep_inv.wait()
        pass_on.wait()
        swap.wait_send()
        for d in range(1, nz):
            for way in (UP, DOWN):
                pl.when(inside(way, d))(lambda way=way, d=d: send_heads(way, d).wait_send())
        for copy in saves:
            copy.wait()

    hidden_shape = jax.ShapeDtypeStruct((1, seq, held), bf16)
    return pl.pallas_call(
        kernel,
        out_shape=[
            jax.ShapeDtypeStruct((seq, width), bf16),
            jax.ShapeDtypeStruct((seq, width), bf16),
            jax.ShapeDtypeStruct((nz,) + marks.shape, jnp.int32),
            jax.ShapeDtypeStruct((seq, 3 * cols), bf16),
            jax.ShapeDtypeStruct((heads, seq, seq), bf16),
            jax.ShapeDtypeStruct((seq, cols), bf16),
            jax.ShapeDtypeStruct((seq, width), bf16),
            jax.ShapeDtypeStruct((rows, width), f32),
            jax.ShapeDtypeStruct((full, 128), f32),
            jax.ShapeDtypeStruct((seq, small.shape[0]), f32),
            jax.ShapeDtypeStruct((groups, 3 * ffn, block), bf16),
            hidden_shape, hidden_shape, hidden_shape,
            jax.ShapeDtypeStruct((seq, small.shape[0]), f32),
        ],
        in_specs=[VMEM] * 6 + [ANY] * 7,
        out_specs=[ANY, ANY, VMEM, ANY, ANY, ANY, ANY, VMEM, ANY, VMEM, ANY, ANY, ANY, ANY, VMEM],
        scratch_shapes=[
            pltpu.VMEM((seq, width), bf16), pltpu.VMEM((seq, width), bf16), pltpu.VMEM((seq, 3 * cols), bf16),
            pltpu.VMEM((heads, seq, seq), bf16), pltpu.VMEM((seq, cols), bf16), pltpu.VMEM((seq, width), bf16),
            pltpu.VMEM((rows, width), bf16), pltpu.VMEM((width, 3 * cols), bf16), pltpu.VMEM((full, seq), f32),
            pltpu.VMEM((seq, 1), f32), pltpu.VMEM((1, seq), f32),
            pltpu.VMEM((2, nz, full, cols), bf16),
            pltpu.VMEM((full, width), f32),
            pltpu.VMEM((rows, width), bf16), pltpu.VMEM((rows, width), bf16), pltpu.VMEM((rows, width), bf16),
            pltpu.VMEM((rows, 128), f32), pltpu.VMEM(out_weight.shape, bf16),
            pltpu.VMEM((width, held), bf16), pltpu.VMEM((width, held), bf16), pltpu.VMEM((width, held), bf16),
            pltpu.VMEM((seq, held), bf16), pltpu.VMEM((seq, held), bf16), pltpu.VMEM((seq, held), bf16),
            pltpu.VMEM((3, held, seq), bf16), pltpu.VMEM((2, per, 3 * ffn, lane), bf16),
            pltpu.SemaphoreType.DMA((7,)),
            pltpu.SemaphoreType.DMA((2, nz)), pltpu.SemaphoreType.DMA((2, nz)), pltpu.SemaphoreType.DMA,
            pltpu.SemaphoreType.DMA((2, nz)), pltpu.SemaphoreType.DMA((2, nz)),
            pltpu.SemaphoreType.DMA, pltpu.SemaphoreType.DMA, pltpu.SemaphoreType.DMA((3,)),
            pltpu.SemaphoreType.DMA((9,)), pltpu.SemaphoreType.DMA((2,)),
        ]
        + gather_sems(nz) * 3,
        compiler_params=pltpu.CompilerParams(
            collective_id=name, has_side_effects=True, vmem_limit_bytes=63 * 1024 * 1024
        ),
    )(x, gain, upstream, marks, gain2, small, *weights, out_weight, *shared)


def attention_back(nz, d_h, n1, qkv, probs, o, out_weight, groups, part, n2, small, name):
    seq, width = d_h.shape
    heads = probs.shape[0]
    cols = o.shape[1]
    full = seq // nz
    block = width // groups
    lane = min(block, TILE)
    per = TILE // lane
    slabs = width // TILE
    strip = 32
    scale = HD ** (-0.5)

    def kernel(dh_hbm, n1_hbm, qkv_ref, p_ref, o_ref, wo_hbm, part_hbm, n2_hbm, small_ref, heads_ref, grad_hbm, box_hbm,
               sum_ref, n2_ref, s_turned, b_send, b_recv, b_local, dh_ref, n1_ref, wo, d_o, scores, ds, dk, dv, turned, o_turned, slab, in_sem, slab_sem):
        z, c = here()
        at = pl.ds(pl.multiple_of(z * cols, cols), cols)
        loads = [
            pltpu.make_async_copy(wo_hbm.at[:, at], wo, in_sem.at[0]),
            pltpu.make_async_copy(dh_hbm, dh_ref, in_sem.at[1]),
            pltpu.make_async_copy(n1_hbm, n1_ref, in_sem.at[2]),
            pltpu.make_async_copy(n2_hbm, n2_ref, in_sem.at[3]),
        ]
        for load in loads:
            load.start()
        greet(nz)
        keep = pltpu.make_async_copy(part_hbm.at[z], box_hbm.at[z], b_local)
        keep.start()

        def send(way, d):
            to = z + d if way == UP else z - d
            return remote(part_hbm.at[to], box_hbm.at[z], b_send.at[way, d], b_recv.at[way, d], {"expert": to})

        def take(way, d):
            dst = box_hbm.at[z - d if way == UP else z + d]
            remote(dst, dst, b_send.at[way, d], b_recv.at[way, d], {"tensor": 1 - c}).wait_recv()

        for d in range(nz - 1, 0, -1):
            for way in (UP, DOWN):
                pl.when(z + d < nz if way == UP else z >= d)(lambda way=way, d=d: send(way, d).start())
        o_turned[...] = o_ref[...].T
        s_turned[...] = small_ref[...].T
        loads[0].wait()
        loads[1].wait()

        def project(i, to):
            d_o[to, :] = nn_dot(dh_ref[to, :], wo[...]).astype(bf16)

        tiles(seq // TILE, project)

        def head(h, carry):
            def part(k):
                return pl.ds(pl.multiple_of(k * cols + h * HD, HD), HD)

            mine = part(0)
            for i in reversed(range(nz)):
                length = (i + 1) * full
                row = pl.ds(i * full, full)
                scores[:, :length] = nt_dot(d_o[row, mine], qkv_ref[:length, part(2)])

                def harden(j, inner, i=i, length=length):
                    local = pl.ds(pl.multiple_of(j * strip, strip), strip)
                    to = pl.ds(pl.multiple_of(i * full + j * strip, strip), strip)
                    mean = jnp.sum(
                        d_o[to, mine].astype(f32) * o_ref[to, mine].astype(f32), axis=-1, keepdims=True
                    )
                    value = p_ref[h, to, :length].astype(f32) * (scores[local, :length] - mean)
                    ds[local, :length] = value.astype(bf16)
                    return inner

                lax.fori_loop(0, full // strip, harden, 0)
                d_s = ds[:, :length]
                heads_ref[row, mine] = (nn_dot(d_s, qkv_ref[:length, part(1)]) * scale).astype(bf16)
                d_k = tn_dot(d_s, qkv_ref[row, mine])
                d_v = tn_dot(p_ref[h, row, :length], d_o[row, mine])
                if i == nz - 1:
                    dk[...], dv[...] = d_k, d_v
                else:
                    dk[:length, :] += d_k
                    dv[:length, :] += d_v
            heads_ref[:, part(1)] = (dk[...] * scale).astype(bf16)
            heads_ref[:, part(2)] = dv[...].astype(bf16)
            return carry

        lax.fori_loop(0, heads, head, 0)

        def turn(i, to):
            turned[:, to] = heads_ref[to, :].T

        tiles(seq // TILE, turn)
        loads[2].wait()
        loads[3].wait()

        def leave(i):
            slot = lax.rem(i, 2)
            if per > 1:
                dst = grad_hbm.at[pl.ds(i * per, per)]
            else:
                many = block // TILE
                to = pl.ds(pl.multiple_of(lax.rem(i, many) * TILE, TILE), TILE)
                dst = grad_hbm.at[pl.ds(i // many, 1), :, to]
            return pltpu.make_async_copy(slab.at[slot], dst, slab_sem.at[slot])

        def write(i, to):
            slot = lax.rem(i, 2)
            pl.when(i >= 2)(lambda: leave(i).wait())
            inner = nn_dot(turned[...], n1_ref[:, to]).astype(bf16)
            outer = nn_dot(o_turned[...], dh_ref[:, to]).astype(bf16)
            both = nn_dot(s_turned[:32, :], n2_ref[:, to])
            sum_ref[:, to] = both[:16, :] + both[16:, :]
            for j in range(per):
                slab[slot, j, : 3 * cols, :] = inner[:, j * lane : (j + 1) * lane]
                slab[slot, j, 3 * cols :, :] = outer[:, j * lane : (j + 1) * lane]
            leave(i).start()

        tiles(slabs, write)
        leave(slabs - 2).wait()
        leave(slabs - 1).wait()
        keep.wait()
        for d in range(1, nz):
            for way in (UP, DOWN):
                pl.when(z + d < nz if way == UP else z >= d)(lambda way=way, d=d: send(way, d).wait_send())
                pl.when(z >= d if way == UP else z + d < nz)(lambda way=way, d=d: take(way, d))

    return pl.pallas_call(
        kernel,
        out_shape=[
            jax.ShapeDtypeStruct((seq, 3 * cols), bf16),
            jax.ShapeDtypeStruct((groups, 4 * cols, block), bf16),
            jax.ShapeDtypeStruct(part.shape, bf16),
            jax.ShapeDtypeStruct((16, width), f32),
        ],
        in_specs=[ANY, ANY, VMEM, VMEM, VMEM, ANY, ANY, ANY, VMEM],
        out_specs=[VMEM, ANY, ANY, VMEM],
        scratch_shapes=[
            pltpu.VMEM((seq, width), bf16), pltpu.VMEM((small.shape[1], seq), bf16),
            pltpu.SemaphoreType.DMA((2, nz)), pltpu.SemaphoreType.DMA((2, nz)), pltpu.SemaphoreType.DMA,
            pltpu.VMEM((seq, width), bf16), pltpu.VMEM((seq, width), bf16), pltpu.VMEM((width, cols), bf16),
            pltpu.VMEM((seq, cols), bf16), pltpu.VMEM((full, seq), f32), pltpu.VMEM((full, seq), bf16),
            pltpu.VMEM((seq, HD), f32), pltpu.VMEM((seq, HD), f32),
            pltpu.VMEM((3 * cols, seq), bf16), pltpu.VMEM((cols, seq), bf16), pltpu.VMEM((2, per, 4 * cols, lane), bf16),
            pltpu.SemaphoreType.DMA((4,)), pltpu.SemaphoreType.DMA((2,)),
        ],
        compiler_params=params(name),
    )(d_h, n1, qkv, probs, o, out_weight, part, n2, small)


def spread_turned(nz, part, splits, name):
    _, columns, block = part.shape
    cols = columns // splits

    def kernel(in_ref, *rest):
        outs, (box, send_sem, recv_sem) = rest[:splits], rest[splits:]
        z, c = here()
        greet(nz)

        def send(way, d):
            to = z + d if way == UP else z - d
            return remote(in_ref.at[to], box.at[z], send_sem.at[way, d], recv_sem.at[way, d], {"expert": to})

        def take(way, d):
            dst = box.at[z - d if way == UP else z + d]
            remote(dst, dst, send_sem.at[way, d], recv_sem.at[way, d], {"tensor": 1 - c}).wait_recv()

        for d in range(nz - 1, 0, -1):
            for way in (UP, DOWN):
                pl.when(z + d < nz if way == UP else z >= d)(lambda way=way, d=d: send(way, d).start())
        box[z] = in_ref[z]
        for d in range(1, nz):
            for way in (UP, DOWN):
                pl.when(z + d < nz if way == UP else z >= d)(lambda way=way, d=d: send(way, d).wait_send())
                pl.when(z >= d if way == UP else z + d < nz)(lambda way=way, d=d: take(way, d))
        for j in range(splits):
            for b in range(nz):
                value = box[b, j * cols : (j + 1) * cols, :].astype(f32).T
                outs[j][:, b * cols : (b + 1) * cols] = value

    return pl.pallas_call(
        kernel,
        out_shape=[jax.ShapeDtypeStruct((block, nz * cols), f32)] * splits,
        in_specs=[VMEM],
        out_specs=[VMEM] * splits,
        scratch_shapes=[
            pltpu.VMEM(part.shape, bf16), pltpu.SemaphoreType.DMA((2, nz)), pltpu.SemaphoreType.DMA((2, nz)),
        ],
        compiler_params=params(name),
    )(part)


PART = 512


class Products:
    def __init__(self, nz, experts, shared, extra):
        self.nz, self.experts, self.shared = nz, experts, shared
        _, self.seq, self.kept = experts[0][0][0].shape
        _, self.ffn, self.width = experts[0][1][0].shape
        self.held = shared[0][0][0].shape[2]
        self.own = shared[0][1].shape[1] // nz
        self.more = [] if extra is None else list(extra)
        self.inputs = (
            [left[0] for left, _ in experts] + [right[0] for _, right in experts] + [left[0] for left, _ in shared]
            + [right for _, right in shared] + self.more
        )
        ne, ns = len(experts), len(shared)
        self.specs = [ANY] * (2 * (ne + ns)) + [VMEM] * len(self.more)
        self.scratch = [
            pltpu.VMEM((self.seq, ne * self.kept), bf16), pltpu.VMEM((ne * self.kept, self.width), bf16),
            pltpu.VMEM((self.seq, ns * self.held), bf16), pltpu.VMEM((self.width, ns * self.held), bf16),
            pltpu.SemaphoreType.DMA((self.width // PART, ne + ns)), pltpu.SemaphoreType.DMA((nz, ne + ns)),
        ]

    def bind(self, refs, scratch):
        ne, ns = len(self.experts), len(self.shared)
        self.left, self.right, self.sleft, self.sright, self.r_sem, self.l_sem = scratch
        self.e_left, self.e_right = refs[:ne], refs[ne : 2 * ne]
        self.s_left, self.s_right = refs[2 * ne : 2 * ne + ns], refs[2 * ne + ns : 2 * (ne + ns)]
        self.small = refs[2 * (ne + ns) :]
        self.first = pl.multiple_of(lax.axis_index("expert") * self.own // LANES * LANES, LANES)

    def rights(self, j):
        to = pl.ds(pl.multiple_of(j * PART, PART), PART)
        for i, (_, (_, index)) in enumerate(self.experts):
            dst = self.right.at[pl.ds(i * self.kept, self.ffn), to]
            yield pltpu.make_async_copy(self.e_right[i].at[index, :, to], dst, self.r_sem.at[j, i])
        for i in range(len(self.shared)):
            src = self.s_right[i].at[to, pl.ds(self.first, self.held)]
            dst = self.sright.at[to, pl.ds(i * self.held, self.held)]
            yield pltpu.make_async_copy(src, dst, self.r_sem.at[j, len(self.experts) + i])

    def lefts(self, b):
        rows = self.seq // self.nz
        at = pl.ds(pl.multiple_of(b * rows, rows), rows)
        for i, ((_, index), _) in enumerate(self.experts):
            dst = self.left.at[at, pl.ds(i * self.kept, self.kept)]
            yield pltpu.make_async_copy(self.e_left[i].at[index, at], dst, self.l_sem.at[b, i])
        for i, ((_, index), _) in enumerate(self.shared):
            dst = self.sleft.at[at, pl.ds(i * self.held, self.held)]
            yield pltpu.make_async_copy(self.s_left[i].at[index, at], dst, self.l_sem.at[b, len(self.experts) + i])

    def fetch(self, order):
        for copy in self.lefts(order(0)):
            copy.start()
        for j in range(self.width // PART):
            for copy in self.rights(j):
                copy.start()
        for k in range(1, self.nz):
            for copy in self.lefts(order(k)):
                copy.start()
        if self.kept > self.ffn:
            for i in range(len(self.experts)):
                self.right[i * self.kept + self.ffn : (i + 1) * self.kept, :] = jnp.zeros(
                    (self.kept - self.ffn, self.width), bf16
                )

    def block(self, k, b, out, start, end):
        rows = self.seq // self.nz
        at = pl.ds(pl.multiple_of(b * rows, rows), rows)
        if start == 0:
            for copy in self.lefts(b):
                copy.wait()

        def one(j, carry):
            @pl.when(k == 0)
            def _():
                for copy in self.rights(j):
                    copy.wait()

            to = pl.ds(pl.multiple_of(j * PART, PART), PART)
            value = nn_dot(self.left[at, :], self.right[:, to]) + nt_dot(self.sleft[at, :], self.sright[to, :])
            if self.more:
                value += nt_dot(self.small[0][at, :], self.small[1][to, :])
            out[at, to] = value.astype(bf16)
            return carry

        lax.fori_loop(start, end, one, 0)


def reduce_and_gather(nz, products, h, gain, upstream, name):
    rows, width = h.shape
    n_in, n_scratch = len(products.inputs), len(products.scratch)

    def kernel(*refs):
        p_refs, (h_ref, gain_ref, up_ref, out_ref, dh_ref, gg_ref) = refs[:n_in], refs[n_in : n_in + 6]
        rest = refs[n_in + 6 :]
        p_scratch, (part, own), rest = rest[:n_scratch], rest[n_scratch : n_scratch + 2], rest[n_scratch + 2 :]
        scratch, sems = rest[:REDUCE_SCRATCH], rest[REDUCE_SCRATCH:]
        total = scratch[3]
        products.bind(p_refs, p_scratch)
        reducer = Reducer(nz, part, *scratch)
        products.fetch(reducer.block)
        greet(nz)
        ends = reducer.ends()

        def one(s, carry):
            products.block(s, reducer.block(s), part, 0, 1)
            pl.when(jnp.logical_and(ends, s >= 1))(lambda: reducer.forward(s - 1))
            products.block(s, reducer.block(s), part, 1, width // PART)
            reducer.begin(s)
            pl.when(jnp.logical_and(jnp.logical_not(ends), s >= 2))(lambda: reducer.forward(s - 2))
            return carry

        lax.fori_loop(0, nz, one, 0)
        pl.when(jnp.logical_not(ends))(lambda: reducer.forward(nz - 2))
        reducer.finish()
        gg_ref[...] = jnp.zeros_like(gg_ref)

        def step(at):
            change, along = norm_back(h_ref[at, :], gain_ref[...], total[at, :])
            dh = up_ref[at, :].astype(f32) + change
            dh_ref[at, :] = dh
            own[at, :] = dh.astype(bf16)
            gg_ref[...] += along

        strips(rows, step)
        gather_rows(nz, own, out_ref, *sems)
        reducer.drain()

    return pl.pallas_call(
        kernel,
        out_shape=[
            jax.ShapeDtypeStruct((nz * 2 * rows, width), bf16),
            jax.ShapeDtypeStruct((rows, width), f32),
            jax.ShapeDtypeStruct((STRIP, width), f32),
        ],
        in_specs=products.specs + [VMEM] * 3,
        out_specs=[ANY, VMEM, VMEM],
        scratch_shapes=products.scratch
        + [pltpu.VMEM((nz * 2 * rows, width), bf16), pltpu.VMEM((rows, width), bf16)]
        + reduce_scratch(nz, rows, width)
        + gather_sems(nz),
        compiler_params=params(name),
    )(*products.inputs, h, gain, upstream)


def reduce_last(nz, d_heads, weights, x, gain, dh, products, h, small, box, name):
    rows, width = x.shape
    cols = d_heads.shape[1] // 3
    n, small_rows, lanes = small.shape
    box_rows, block = box.shape[1] // 3, box.shape[2]
    n_in, n_scratch = len(products.inputs), len(products.scratch)

    def kernel(*refs):
        p_refs, (
            d_ref, wq_hbm, wk_hbm, wv_hbm, x_ref, gain_ref, dh_ref, h_ref, small_ref, box_ref, in_ref, out_ref, sum_ref, *turned,
        ) = refs[:n_in], refs[n_in : n_in + 16]
        gg_ref, s_out, s_box, s_total, s_other, s_send, s_recv, swap_sem = refs[n_in + 16 : n_in + 24]
        rest = refs[n_in + 24 :]
        p_scratch, (d_part, b_part, own, sems, w_ref, w_sem), rest = (
            rest[:n_scratch], rest[n_scratch : n_scratch + 6], rest[n_scratch + 6 :],
        )
        mine = pl.ds(pl.multiple_of(lax.axis_index("expert") * cols, cols), cols)
        loads = [
            pltpu.make_async_copy(src.at[:, mine], w_ref.at[:, pl.ds(i * cols, cols)], w_sem.at[i])
            for i, src in enumerate((wq_hbm, wk_hbm, wv_hbm))
        ]
        for load in loads:
            load.start()
        d_scratch, b_scratch = rest[:REDUCE_SCRATCH], rest[REDUCE_SCRATCH:]
        d_total, b_total = d_scratch[3], b_scratch[3]
        products.bind(p_refs, p_scratch)
        first, second = Reducer(nz, d_part, *d_scratch), Reducer(nz, b_part, *b_scratch)
        z, c = here()
        me = lax.axis_index("dp") * nz + z
        barrier = pltpu.get_barrier_semaphore()

        def peer(q):
            to = lax.rem(me + q, n)
            return to, {"dp": to // nz, "expert": lax.rem(to, nz)}

        pl.semaphore_signal(barrier, inc=1, device_id={"tensor": 1 - c}, device_id_type=MESH)
        for q in range(1, n):
            pl.semaphore_signal(barrier, inc=1, device_id=peer(q)[1], device_id_type=MESH)
        pl.semaphore_wait(barrier, n)

        def send_small(q):
            to, device = peer(q)
            return remote(s_out.at[to], s_box.at[q], s_send.at[q], s_recv.at[q], device)

        ends = first.ends()
        middle = jnp.logical_not(ends)

        def inner(block):
            at = pl.ds(pl.multiple_of(block * 2 * rows, 2 * rows), 2 * rows)

            def one(j, carry):
                to = pl.ds(pl.multiple_of(j * PART, PART), PART)
                d_part[at, to] = nt_dot(d_ref[at, :], w_ref[to, :]).astype(bf16)
                return carry

            lax.fori_loop(0, width // PART, one, 0)

        def one(s, carry):
            inner(first.block(s))
            first.begin(s)
            pl.when(jnp.logical_and(ends, s >= 1))(lambda: first.forward(s - 1))
            return carry

        def two(s, carry):
            products.block(s, second.block(s), b_part, 0, width // PART)
            second.begin(s)

            @pl.when(s >= 1)
            def _():
                pl.when(ends)(lambda: second.forward(s - 1))
                pl.when(middle)(lambda: first.forward(s - 1))

            return carry

        def three(s, carry):
            pl.when(middle)(lambda: second.forward(s))
            return carry

        for load in loads:
            load.wait()
        products.fetch(second.block)
        lax.fori_loop(0, nz, one, 0)
        lax.fori_loop(0, nz, two, 0)
        lax.fori_loop(0, nz - 1, three, 0)
        for i in range(3):
            for b in range(nz):
                value = box_ref[b, i * box_rows : (i + 1) * box_rows, :].astype(f32).T
                turned[i][:, b * box_rows : (b + 1) * box_rows] = value
        first.finish()
        gg_ref[...] = jnp.zeros_like(gg_ref)

        def step(at):
            change, along = norm_back(x_ref[at, :].astype(f32), gain_ref[...], d_total[at, :])
            own[0, at, :] = dh_ref[at, :] + change
            gg_ref[...] += along

        strips(rows, step)

        def leave(i, ref):
            spot = ref.at[pl.ds(pl.multiple_of(c * rows, rows), rows)]
            return (
                pltpu.make_async_copy(own.at[i], spot, sems.at[i, 0]),
                remote(own.at[i], spot, sems.at[i, 1], sems.at[i, 2], {"tensor": 1 - c}),
            )

        for copy in leave(0, in_ref):
            copy.start()
        first_row = jnp.sum(gg_ref[...], axis=0, keepdims=True)
        for q in range(n):
            s_out[q] = small_ref[q]
            s_out[q, :1, :] = first_row[:, q * lanes : (q + 1) * lanes]
        for q in range(1, n):
            send_small(q).start()
        s_total[...] = s_out[me]
        for q in range(1, n):
            send_small(q).wait_recv()
            s_total[...] += s_box[q]
        swap = remote(s_total, s_other, swap_sem.at[0], swap_sem.at[1], {"tensor": 1 - c})
        swap.start()
        second.finish()

        def last(at):
            own[1, at, :] = h_ref[at, :] + b_total[at, :]

        strips(rows, last)
        for copy in leave(1, out_ref):
            copy.start()
        first.drain()
        second.drain()
        swap.wait_recv()
        sum_ref[...] = s_total[...] + s_other[...]
        swap.wait_send()
        for q in range(1, n):
            send_small(q).wait_send()
        for copy in (*leave(0, in_ref), *leave(1, out_ref)):
            copy.wait()

    return pl.pallas_call(
        kernel,
        out_shape=[
            jax.ShapeDtypeStruct((2 * rows, width), f32),
            jax.ShapeDtypeStruct((2 * rows, width), f32),
            jax.ShapeDtypeStruct((small_rows, lanes), f32),
        ]
        + [jax.ShapeDtypeStruct((block, nz * box_rows), f32)] * 3,
        in_specs=products.specs + [VMEM] + [ANY] * 3 + [VMEM] * 6,
        out_specs=[ANY, ANY] + [VMEM] * 4,
        scratch_shapes=[
            pltpu.VMEM((STRIP, width), f32), pltpu.VMEM(small.shape, f32), pltpu.VMEM(small.shape, f32),
            pltpu.VMEM((small_rows, lanes), f32), pltpu.VMEM((small_rows, lanes), f32),
            pltpu.SemaphoreType.DMA((n,)), pltpu.SemaphoreType.DMA((n,)), pltpu.SemaphoreType.DMA((2,)),
        ]
        + products.scratch
        + [
            pltpu.VMEM((nz * 2 * rows, width), bf16), pltpu.VMEM((nz * 2 * rows, width), bf16),
            pltpu.VMEM((2, rows, width), f32), pltpu.SemaphoreType.DMA((2, 3)),
            pltpu.VMEM((width, 3 * cols), bf16), pltpu.SemaphoreType.DMA((3,)),
        ]
        + reduce_scratch(nz, rows, width) * 2,
        compiler_params=params(name, 60),
    )(*products.inputs, d_heads, *weights, x, gain, dh, h, small, box)


def cross_rows(left, right):
    return lax.dot_general(left, right, (((0,), (0,)), ((), ())), preferred_element_type=f32)


def cross_cols(left, right):
    return lax.dot_general(left, right, (((1,), (1,)), ((), ())), preferred_element_type=f32)


def dot(left, right):
    return jnp.dot(left, right, preferred_element_type=f32)


def two_parts(values):
    high = values.astype(bf16)
    return high, (values - high.astype(f32)).astype(bf16)


def body(
    tokens, segments, routes, norm1_gain, q_weight, k_weight, v_weight, o_weight, norm2_gain,
    router_weight, shared_gate_vector, shared_gate_weight, shared_up_weight, shared_down_weight,
    expert_gate_weight, expert_up_weight, expert_down_weight, out_grad,
):
    nz = lax.axis_size("expert")
    nc = lax.axis_size("tensor")
    z = lax.axis_index("expert")
    c = lax.axis_index("tensor")
    rows, width = tokens.shape
    own_rows = rows // nc
    local_count, _, ffn = expert_gate_weight.shape
    expert_count = local_count * nz
    head_cols = q_weight.shape[1] // nz
    shared_cols = shared_gate_weight.shape[1] // nz
    heads = head_cols // HD
    seq = rows * nz
    scale = HD ** (-0.5)
    gain1 = norm1_gain.astype(f32)[None]
    gain2 = norm2_gain.astype(f32)[None]

    def own(values):
        return lax.dynamic_slice_in_dim(values, c * own_rows, own_rows, 0)

    def head_slice(values):
        return lax.dynamic_slice_in_dim(values, z * head_cols, head_cols, 1)

    x_all_rows = tokens.astype(f32)
    inverse_one_rows = lax.rsqrt(jnp.mean(x_all_rows * x_all_rows, axis=-1) + epsilon)
    x = own(tokens)
    marks = jnp.concatenate([segments, routes.T, jnp.zeros((7 - routes.shape[1], rows), jnp.int32)], axis=0)
    upstream = own(out_grad)
    ndp = lax.axis_size("dp")
    small_rows_weight = jnp.concatenate([router_weight.T, shared_gate_vector[None]], axis=0)
    shared_weights = (shared_gate_weight, shared_up_weight, shared_down_weight)
    (
        n1, dy, all_marks, qkv, p_low, o, n2, h, inverse_two, logits, grad_s, da_s, db_s, gu_s, dgate_s,
    ) = forward_layer(
        nz, x, gain1, upstream, marks, (q_weight, k_weight, v_weight), o_weight, gain2, small_rows_weight, shared_weights,
        ndp * nz, 0,
    )
    all_routes = jnp.transpose(all_marks[:, 1 : 1 + routes.shape[1]], (0, 2, 1)).reshape(seq, routes.shape[1])

    probs = jax.nn.softmax(logits[:, :expert_count], axis=-1)
    chosen = jnp.any(all_routes[:, :, None] == jnp.arange(expert_count)[None, None, :], axis=1)
    gates = jnp.where(chosen, probs, 0.0)
    sigma = jax.nn.sigmoid(logits[:, expert_count:])

    turned = [jnp.swapaxes(w, 1, 2) for w in (expert_gate_weight, expert_up_weight, expert_down_weight)]
    grad_e, da_e, db_e, gu_e, dgate_e = hidden_layer(nz, n2, dy, gates, turned, ndp)

    d_probs = jnp.where(chosen, dgate_e, 0.0)
    d_logits = probs * (d_probs - jnp.sum(probs * d_probs, axis=-1, keepdims=True))
    d_vector = dgate_s[:, expert_count:] * (sigma * (1.0 - sigma))
    small = jnp.concatenate([d_logits, d_vector], axis=1)
    small_high, small_low = two_parts(small)
    small_weights = jnp.concatenate([router_weight, shared_gate_vector[:, None]], axis=1)
    fill = ((0, 0), (0, 128 - small.shape[1]))
    experts = range(local_count)
    d_n2 = Products(
        nz,
        [((da_e, i), (turned[0], i)) for i in experts] + [((db_e, i), (turned[1], i)) for i in experts],
        [((da_s, 0), shared_gate_weight), ((db_s, 0), shared_up_weight)],
        (jnp.pad(small_high, fill), jnp.pad(small_weights, fill)),
    )
    few = small.shape[1]
    mixed = jnp.pad(small_high, ((0, 0), (2, 126 - few))) + jnp.pad(small_low, ((0, 0), (18, 110 - few)))


    def over_dp(grad):
        rows = grad.reshape(-1, grad.shape[-1])
        return lax.psum_scatter(rows, "dp", scatter_dimension=0, tiled=True)

    shared_part = over_dp(grad_s).reshape((nz,) + grad_s.shape[1:])
    expert_part = over_dp(grad_e).reshape(local_count, 3, ffn, -1)
    dhr, dh, grad_two = reduce_and_gather(nz, d_n2, h, gain2, upstream, 2)
    d_heads, grad_attention, shared_box, small_grad = attention_back(
        nz, dhr, n1, qkv, p_low, o, o_weight, ndp * nz, shared_part, n2, mixed, 1
    )
    attention_part = over_dp(grad_attention).reshape((nz,) + grad_attention.shape[1:])
    branch = Products(
        nz,
        [((gu_e, i), (turned[2], i)) for i in experts],
        [((gu_s, 0), shared_down_weight)],
        None,
    )
    dh_now, _ = lax.optimization_barrier((dh, grad_attention))
    small_rows = small_grad + jnp.pad(jnp.sum(grad_two, axis=0)[None], ((1, 14), (0, 0)))
    count = ndp * nz
    small_blocks = jnp.swapaxes(small_rows.reshape(16, count, width // count), 0, 1)
    input_grad, layer_out, small_all, s_gate, s_up, s_down = reduce_last(
        nz, d_heads, (q_weight, k_weight, v_weight), x, gain1, dh_now, branch, h, small_blocks, shared_box, 3
    )
    stats = jnp.stack([inverse_one_rows, inverse_two[:, 0]])

    e_gate, e_up, e_down = (jnp.swapaxes(expert_part[:, k].astype(f32), 1, 2) for k in range(3))
    attention_part, e_gate, e_up, e_down, small_all = lax.optimization_barrier(
        (attention_part, e_gate, e_up, e_down, small_all)
    )
    g_q, g_k, g_v, g_o = spread_turned(nz, attention_part, 4, 6)
    g_one, g_two, g_router, g_vector = small_all[0], small_all[1], small_all[2 : 2 + expert_count].T, small_all[2 + expert_count]
    return (
        layer_out, input_grad, stats, g_one, g_q, g_k, g_v, g_o, g_two, g_router, g_vector,
        s_gate, s_up, s_down, e_gate, e_up, e_down,
    )


def solution(mesh):
    both = ("dp", "expert")
    cols = P(None, "tensor")
    placed = (
        P(both, None), P("dp", "expert"), P(both, None), P(), cols, cols, cols, cols, P(), P(), P(),
        cols, cols, cols, P("expert", None, "tensor"), P("expert", None, "tensor"),
        P("expert", None, "tensor"), P(both, None),
    )
    split = P(both, "tensor")
    experts = P("expert", "dp", "tensor")
    return jax.shard_map(
        body,
        mesh=mesh,
        in_specs=placed,
        out_specs=(
            P(both, None), P(both, None), P(None, both), P(both), split, split, split, split, P(both),
            P(both, None), P(both), split, split, split, experts, experts, experts,
        ),
        check_vma=False,
    )
```

```python
import functools

import jax
import jax.numpy as jnp
from jax import lax
from jax.experimental import pallas as pl
from jax.experimental.pallas import tpu as pltpu
from jax.sharding import PartitionSpec as P

HD = 128
MESH = pl.DeviceIdType.MESH
PIECES = 2
STRIP = 16
epsilon = 1e-06
f32 = jnp.float32
bf16 = jnp.bfloat16
UP, DOWN = 0, 1


def here():
    return lax.axis_index("expert"), lax.axis_index("tensor")


def greet(nz):
    z, c = here()
    barrier = pltpu.get_barrier_semaphore()

    def tell(device):
        pl.semaphore_signal(barrier, inc=1, device_id=device, device_id_type=MESH)

    tell({"tensor": 1 - c})
    for d in range(1, nz):
        tell({"expert": lax.rem(z + d, nz)})
    pl.semaphore_wait(barrier, nz)


def remote(src, dst, send, recv, device):
    return pltpu.make_async_remote_copy(
        src_ref=src, dst_ref=dst, send_sem=send, recv_sem=recv, device_id=device, device_id_type=MESH
    )


def strips(rows, step):
    def one(i, carry):
        step(pl.ds(pl.multiple_of(i * STRIP, STRIP), STRIP))
        return carry

    lax.fori_loop(0, rows // STRIP, one, 0)


GATHER_SEMS = 4


def gather_sems(nz):
    return [pltpu.SemaphoreType.DMA((2, nz, PIECES))] * GATHER_SEMS + [pltpu.SemaphoreType.DMA]


class Gather:
    def __init__(self, nz, own, out, z_send, z_recv, s_send, s_recv, local_sem):
        self.nz, self.own, self.out = nz, own, out
        self.z_send, self.z_recv, self.s_send, self.s_recv, self.local_sem = z_send, z_recv, s_send, s_recv, local_sem
        self.z, self.c = here()
        self.rows = own.shape[0]
        self.piece = self.rows // PIECES

    def origin(self, way, d):
        return self.z - d if way == UP else self.z + d

    def inside(self, way, d):
        return self.z >= d if way == UP else self.z + d < self.nz

    def onward(self, way):
        return self.z < self.nz - 1 if way == UP else self.z > 0

    def place(self, block, core, p):
        start = (block * 2 + core) * self.rows + p * self.piece
        return self.out.at[pl.ds(pl.multiple_of(start, self.piece), self.piece)]

    def source(self, way, d, p):
        if d == 0:
            return self.own.at[pl.ds(p * self.piece, self.piece)]
        return self.place(self.origin(way, d), self.c, p)

    def along(self, way, d, p):
        device = {"expert": self.z + 1 if way == UP else self.z - 1}
        dst = self.place(self.origin(way, d), self.c, p)
        return remote(self.source(way, d, p), dst, self.z_send.at[way, d, p], self.z_recv.at[way, d, p], device)

    def across(self, way, d, p):
        dst = self.place(self.origin(way, d), self.c, p)
        return remote(
            self.source(way, d, p), dst, self.s_send.at[way, d, p], self.s_recv.at[way, d, p], {"tensor": 1 - self.c}
        )

    def arrived(self, way, d, p):
        dst = self.place(self.origin(way, d), self.c, p)
        remote(dst, dst, self.z_send.at[way, d - 1, p], self.z_recv.at[way, d - 1, p], {"tensor": 1 - self.c}).wait_recv()

    def crossed(self, way, d, p):
        dst = self.place(self.origin(way, d), 1 - self.c, p)
        remote(dst, dst, self.s_send.at[way, d, p], self.s_recv.at[way, d, p], {"tensor": 1 - self.c}).wait_recv()

    def mine(self):
        dst = self.out.at[pl.ds(pl.multiple_of((self.z * 2 + self.c) * self.rows, self.rows), self.rows)]
        return pltpu.make_async_copy(self.own, dst, self.local_sem)

    def start_along(self, way):
        @pl.when(self.onward(way))
        def _():
            for p in range(PIECES):
                self.along(way, 0, p).start()

    def start_across(self):
        for p in range(PIECES):
            self.across(UP, 0, p).start()
        self.mine().start()

    def event(self, d, p):
        for way in (UP, DOWN):

            @pl.when(self.inside(way, d))
            def _(way=way):
                self.arrived(way, d, p)
                pl.when(self.onward(way))(lambda: self.along(way, d, p).start())
                self.across(way, d, p).start()

    def settle(self, way, d):
        for p in range(PIECES):
            self.crossed(way, d, p)
        if d == 0:
            self.mine().wait()

    def settle_all(self):
        self.settle(UP, 0)
        for d in range(1, self.nz):
            for way in (UP, DOWN):
                pl.when(self.inside(way, d))(functools.partial(self.settle, way, d))

    def finish(self):
        for p in range(PIECES):
            self.across(UP, 0, p).wait_send()
            for way in (UP, DOWN):
                pl.when(self.onward(way))(lambda way=way, p=p: self.along(way, 0, p).wait_send())
                for d in range(1, self.nz):

                    @pl.when(self.inside(way, d))
                    def _(way=way, d=d, p=p):
                        self.across(way, d, p).wait_send()
                        pl.when(self.onward(way))(lambda: self.along(way, d, p).wait_send())


def gather_rows(nz, own, out, *sems):
    gather = Gather(nz, own, out, *sems)
    gather.start_along(UP)
    gather.start_along(DOWN)
    gather.start_across()
    for d in range(1, nz):
        for p in range(PIECES):
            gather.event(d, p)
    gather.settle_all()
    gather.finish()


REDUCE_SCRATCH = 8


def reduce_scratch(nz, rows, width):
    return [
        pltpu.VMEM((nz, rows, width), bf16),
        pltpu.VMEM((nz + 1, rows, width), bf16),
        pltpu.VMEM((nz, rows, width), bf16),
        pltpu.VMEM((rows, width), f32),
        pltpu.SemaphoreType.DMA((nz, PIECES)),
        pltpu.SemaphoreType.DMA((nz, PIECES)),
        pltpu.SemaphoreType.DMA((nz, PIECES)),
        pltpu.SemaphoreType.DMA((nz + 1, PIECES)),
    ]


def block_order(nz, z, s):
    down = 2 * z // nz
    far = jnp.maximum(z, nz - 1 - z)
    near = nz - 1 - far
    late = s - (far - near)
    distance = jnp.where(late < 0, far - s, near - late // 2)
    sign = (1 - 2 * down) * jnp.where(late < 0, 1, 1 - 2 * lax.rem(late + nz * 2, 2))
    return z + sign * distance


class Reducer:
    def __init__(self, nz, part, side, inbox, outbox, total, s_send, s_recv, z_send, z_recv):
        self.nz, self.part, self.side, self.inbox, self.outbox, self.total = nz, part, side, inbox, outbox, total
        self.s_send, self.s_recv, self.z_send, self.z_recv = s_send, s_recv, z_send, z_recv
        self.z, self.c = here()
        self.rows = total.shape[0]
        self.piece = self.rows // PIECES

    def block(self, s):
        return block_order(self.nz, self.z, s)

    def cut(self, p):
        return pl.ds(p * self.piece, self.piece)

    def across(self, block, p):
        start = (block * 2 + 1 - self.c) * self.rows + p * self.piece
        src = self.part.at[pl.ds(pl.multiple_of(start, self.piece), self.piece)]
        return remote(
            src, self.side.at[block, self.cut(p)], self.s_send.at[block, p], self.s_recv.at[block, p],
            {"tensor": 1 - self.c},
        )

    def along(self, block, p):
        up = block > self.z
        slot = jnp.where(block == self.z - 1, self.nz, block)
        return remote(
            self.outbox.at[block, self.cut(p)], self.inbox.at[slot, self.cut(p)], self.z_send.at[block, p],
            self.z_recv.at[slot, p], {"expert": self.z + jnp.where(up, 1, -1)},
        )

    def arrived(self, slot, p):
        dst = self.inbox.at[slot, self.cut(p)]
        remote(dst, dst, self.z_send.at[0, p], self.z_recv.at[slot, p], {"tensor": 1 - self.c}).wait_recv()

    def mine(self, block, at):
        base = (block * 2 + self.c) * self.rows
        own = self.part[pl.ds(pl.multiple_of(base + at.start, STRIP), STRIP), :].astype(f32)
        return own + self.side[block, at, :].astype(f32)

    def strips(self, p, step):
        def one(i, carry):
            step(pl.ds(pl.multiple_of(p * self.piece + i * STRIP, STRIP), STRIP))
            return carry

        lax.fori_loop(0, self.piece // STRIP, one, 0)

    def ends(self):
        return jnp.logical_or(self.z == 0, self.z == self.nz - 1)

    def begin(self, s):
        for p in range(PIECES):
            self.across(self.block(s), p).start()

    def forward(self, s):
        block = self.block(s)
        behind = jnp.where(block > self.z, self.z, self.nz - 1 - self.z) > 0
        for p in range(PIECES):
            self.across(block, p).wait_recv()

            @pl.when(behind)
            def _(p=p):
                self.arrived(block, p)

                def add(at):
                    self.outbox[block, at, :] = (self.mine(block, at) + self.inbox[block, at, :].astype(f32)).astype(bf16)

                self.strips(p, add)

            @pl.when(jnp.logical_not(behind))
            def _(p=p):
                def keep(at):
                    self.outbox[block, at, :] = self.mine(block, at).astype(bf16)

                self.strips(p, keep)

            self.along(block, p).start()

    def finish(self):
        z, nz = self.z, self.nz
        for p in range(PIECES):
            self.across(z, p).wait_recv()

            def first(at):
                self.total[at, :] = self.mine(z, at)

            self.strips(p, first)
            for slot, some in ((z, z > 0), (nz, z < nz - 1)):

                @pl.when(some)
                def _(slot=slot, p=p):
                    self.arrived(slot, p)

                    def add(at):
                        self.total[at, :] += self.inbox[slot, at, :].astype(f32)

                    self.strips(p, add)

    def drain(self):
        def one(s, carry):
            block = self.block(s)
            for p in range(PIECES):
                self.across(block, p).wait_send()
                pl.when(s < self.nz - 1)(lambda p=p: self.along(block, p).wait_send())
            return carry

        lax.fori_loop(0, self.nz, one, 0)


def params(name, room=56):
    return pltpu.CompilerParams(collective_id=name, has_side_effects=True, vmem_limit_bytes=room * 1024 * 1024)


VMEM = pl.BlockSpec(memory_space=pltpu.VMEM)
ANY = pl.BlockSpec(memory_space=pl.ANY)


def norm_rows(values, gain):
    inverse = lax.rsqrt(jnp.mean(values * values, axis=-1, keepdims=True) + epsilon)
    return values * inverse * gain, inverse


def norm_back(values, gain, upstream):
    inverse = lax.rsqrt(jnp.mean(values * values, axis=-1, keepdims=True) + epsilon)
    scaled = upstream * gain
    inner = jnp.mean(scaled * values, axis=-1, keepdims=True)
    change = inverse * scaled - values * inverse * inverse * inverse * inner
    return change, upstream * values * inverse


def swap_rows(nz, own, out_ref, sems):
    z, c = here()
    rows = own.shape[0]
    spot = out_ref.at[pl.ds(pl.multiple_of(c * rows, rows), rows)]
    keep = pltpu.make_async_copy(own, spot, sems.at[0])
    pass_on = remote(own, spot, sems.at[1], sems.at[2], {"tensor": 1 - c})
    keep.start()
    pass_on.start()
    keep.wait()
    pass_on.wait()


TILE = 256
TALL = 512
LANES = 128


def nt_dot(left, right):
    return lax.dot_general(left, right, (((1,), (1,)), ((), ())), preferred_element_type=f32)


def tn_dot(left, right):
    return lax.dot_general(left, right, (((0,), (0,)), ((), ())), preferred_element_type=f32)


def nn_dot(left, right):
    return jnp.dot(left, right, preferred_element_type=f32)


def tiles(count, step, size=TILE):
    def one(i, carry):
        step(i, pl.ds(pl.multiple_of(i * size, size), size))
        return carry

    lax.fori_loop(0, count, one, 0)


def padded(columns):
    return -(-columns // LANES) * LANES


def window(columns, place):
    first = place * columns // LANES * LANES
    return first, place * columns - first


def window_width(columns, places):
    return max(padded(window(columns, i)[1] + columns) for i in range(places))


def hidden_layer(nz, n2, dy, gate, weights, groups):
    seq, width = n2.shape
    experts = weights[0].shape[0]
    buffers = min(experts, 2)
    held = weights[0].shape[1]
    ffn, kept = held, padded(held)
    block = width // groups
    lane = min(block, TILE)
    per = TILE // lane
    count, slabs = seq // TILE, width // TILE
    strip = 32
    w_shape = (held, width)

    def kernel(n2_hbm, dy_hbm, wg_hbm, wu_hbm, wd_hbm, gate_ref, grad_hbm, da_hbm, db_hbm, gu_hbm, dgate_ref,
               n2_ref, dy_ref, wg, wu, wd, a, b, back, da, db, gu, turned, slab, in_sem, row_sem, out_sem, slab_sem):
        z = lax.axis_index("expert")
        def weight(i, e):
            slot = lax.rem(e, buffers)
            src, dst = ((wg_hbm, wg), (wu_hbm, wu), (wd_hbm, wd))[i]
            return pltpu.make_async_copy(src.at[e], dst.at[slot], in_sem.at[i, slot])

        rows_in = [
            pltpu.make_async_copy(n2_hbm, n2_ref, row_sem.at[0]), pltpu.make_async_copy(dy_hbm, dy_ref, row_sem.at[1])
        ]
        weight(0, 0).start()
        rows_in[0].start()
        weight(1, 0).start()
        weight(2, 0).start()
        rows_in[1].start()
        if kept > held:
            for ref in (da, db, gu):
                ref[:, held:] = jnp.zeros((seq, kept - held), bf16)

        def expert(e, carry):
            slot = lax.rem(e, buffers)
            weight(0, e).wait()
            pl.when(e == 0)(rows_in[0].wait)

            def one(i, at):
                a[at, :] = nt_dot(n2_ref[at, :], wg[slot])

            tiles(seq // TALL, one, TALL)
            weight(1, e).wait()

            def two(i, at):
                b[at, :] = nt_dot(n2_ref[at, :], wu[slot])

            tiles(seq // TALL, two, TALL)
            weight(2, e).wait()
            pl.when(e == 0)(rows_in[1].wait)
            if experts > 1:

                @pl.when(e + 1 < experts)
                def _():
                    for i in range(3):
                        weight(i, e + 1).start()

            def three(i, at):
                back[...] = nt_dot(dy_ref[at, :], wd[slot])

                def point(j, carry):
                    row = pl.ds(pl.multiple_of(i * TILE + j * strip, strip), strip)
                    local = pl.ds(pl.multiple_of(j * strip, strip), strip)
                    av, bv, kv = a[row, :], b[row, :], back[local, :]
                    here_now = lax.broadcasted_iota(jnp.int32, (strip, gate.shape[1]), 1) == z * experts + e
                    gv = jnp.sum(jnp.where(here_now, gate_ref[row, :], 0.0), axis=-1, keepdims=True)
                    sig = 1.0 / (1.0 + jnp.exp(-av))
                    act = av * sig
                    u = act * bv
                    dgate_ref[row, :] += jnp.where(here_now, jnp.sum(u * kv, axis=-1, keepdims=True), 0.0)
                    gu[row, :held] = (gv * u).astype(bf16)
                    du = gv * kv
                    da[row, :held] = (du * bv * (sig + act * (1.0 - sig))).astype(bf16)
                    db[row, :held] = (du * act).astype(bf16)
                    return carry

                lax.fori_loop(0, TILE // strip, point, 0)
                for k, ref in enumerate((da, db, gu)):
                    turned[k, :, at] = ref[at, :held].T

            tiles(count, three)
            saves = [
                pltpu.make_async_copy(src, dst.at[e], out_sem.at[i])
                for i, (src, dst) in enumerate(((da, da_hbm), (db, db_hbm), (gu, gu_hbm)))
            ]
            for save in saves:
                save.start()

            def leave(i):
                slot = lax.rem(i, 2)
                below = pl.ds(pl.multiple_of(e * 3 * ffn, 16), 3 * ffn)
                if per > 1:
                    dst = grad_hbm.at[pl.ds(i * per, per), below]
                else:
                    many = block // TILE
                    to = pl.ds(pl.multiple_of(lax.rem(i, many) * TILE, TILE), TILE)
                    dst = grad_hbm.at[pl.ds(i // many, 1), below, to]
                return pltpu.make_async_copy(slab.at[slot], dst, slab_sem.at[slot])

            def four(i, at):
                slot = lax.rem(i, 2)
                pl.when(i >= 2)(lambda: leave(i).wait())
                for k, right in enumerate((n2_ref, n2_ref, dy_ref)):
                    value = nn_dot(turned[k], right[:, at]).astype(bf16)
                    for j in range(per):
                        slab[slot, j, k * ffn : (k + 1) * ffn, :] = value[:, j * lane : (j + 1) * lane]
                leave(i).start()

            tiles(slabs, four)
            leave(slabs - 2).wait()
            leave(slabs - 1).wait()
            for save in saves:
                save.wait()
            return carry

        dgate_ref[...] = jnp.zeros_like(dgate_ref)
        lax.fori_loop(0, experts, expert, 0)

    hidden = jax.ShapeDtypeStruct((experts, seq, kept), bf16)
    return pl.pallas_call(
        kernel,
        out_shape=[
            jax.ShapeDtypeStruct((groups, experts * 3 * ffn, block), bf16), hidden, hidden, hidden,
            jax.ShapeDtypeStruct(gate.shape, f32),
        ],
        in_specs=[ANY] * 5 + [VMEM],
        out_specs=[ANY] * 4 + [VMEM],
        scratch_shapes=[
            pltpu.VMEM((seq, width), bf16), pltpu.VMEM((seq, width), bf16),
            pltpu.VMEM((buffers,) + w_shape, bf16), pltpu.VMEM((buffers,) + w_shape, bf16), pltpu.VMEM((buffers,) + w_shape, bf16),
            pltpu.VMEM((seq, held), f32), pltpu.VMEM((seq, held), f32), pltpu.VMEM((TILE, held), f32),
            pltpu.VMEM((seq, kept), bf16), pltpu.VMEM((seq, kept), bf16), pltpu.VMEM((seq, kept), bf16),
            pltpu.VMEM((3, held, seq), bf16),
            pltpu.VMEM((2, per, 3 * ffn, lane), bf16),
            pltpu.SemaphoreType.DMA((3, buffers)), pltpu.SemaphoreType.DMA((2,)), pltpu.SemaphoreType.DMA((3,)),
            pltpu.SemaphoreType.DMA((2,)),
        ],
        compiler_params=pltpu.CompilerParams(vmem_limit_bytes=58 * 1024 * 1024),
    )(n2, dy, *weights, gate)


def forward_layer(nz, x, upstream, marks, weights, out_weight, small, shared, groups, name):
    rows, width = x.shape[0] // 2, x.shape[1]
    seq = nz * 2 * rows
    cols = weights[0].shape[1] // nz
    heads = cols // HD
    full = 2 * rows
    strip = 32
    scale = HD ** (-0.5)
    ffn = shared[0].shape[1] // nz
    held = window_width(ffn, nz)
    block = width // groups
    lane = min(block, TILE)
    per = TILE // lane
    slabs = width // TILE
    gate_row = small.shape[0] - 3

    def kernel(x_ref, up_ref, marks_ref, small_ref, wq_hbm, wk_hbm, wv_hbm, wo_hbm, wg_hbm, wu_hbm, wd_hbm,
               n1_hbm, dy_hbm, all_ref, qkv_hbm, p_hbm, o_hbm, n2_hbm, h_ref, inv_ref, logit_ref, grad_hbm, da_hbm, db_hbm,
               gu_hbm, dgate_ref,
               n1_ref, dy_ref, qkv_ref, p_ref, o_ref, n2_ref, own, w, scores, seg_k, heads_in, acc, give, take_in,
               inv_own, wo, wg, wu, wd, da, db, gu, turned, slab,
               w_sem, m_send, m_recv, m_local, a_send, a_recv, e_send, e_recv, i_sems, out_sem, slab_sem, *sems):
        z, c = here()
        at = pl.ds(pl.multiple_of(z * cols, cols), cols)
        loads = [
            pltpu.make_async_copy(src.at[:, at], w.at[:, pl.ds(i * cols, cols)], w_sem.at[i])
            for i, src in enumerate((wq_hbm, wk_hbm, wv_hbm))
        ]
        loads.append(pltpu.make_async_copy(wo_hbm, wo, w_sem.at[3]))
        first = pl.multiple_of(z * ffn // LANES * LANES, LANES)
        skip = z * ffn - first
        for i, (src, dst) in enumerate(((wg_hbm, wg), (wu_hbm, wu), (wd_hbm, wd))):
            loads.append(pltpu.make_async_copy(src.at[:, pl.ds(first, held)], dst, w_sem.at[4 + i]))
        saves = []

        def save(src, dst):
            saves.append(pltpu.make_async_copy(src, dst, out_sem.at[len(saves)]))
            saves[-1].start()

        for load in loads:
            load.start()

        def step(strip_at):
            normed, _ = norm_rows(x_ref[pl.ds(pl.multiple_of(c * rows + strip_at.start, STRIP), STRIP), :].astype(f32), small_ref[gate_row + 1 : gate_row + 2, :].astype(f32))
            own[strip_at, :] = normed.astype(bf16)

        strips(rows, step)
        greet(nz)
        n1 = Gather(nz, own, n1_ref, *sems[:5])
        dy = Gather(nz, up_ref.at[pl.ds(pl.multiple_of(c * rows, rows), rows)], dy_ref, *sems[5:10])
        n2 = Gather(nz, own, n2_ref, *sems[10:])
        n1.start_along(UP)
        n1.start_along(DOWN)
        n1.start_across()
        keep = pltpu.make_async_copy(marks_ref, all_ref.at[z], m_local)
        keep.start()

        def send(way, d):
            to = z + d if way == UP else z - d
            return remote(marks_ref, all_ref.at[z], m_send.at[way, d], m_recv.at[way, d], {"expert": to})

        def take(way, d):
            dst = all_ref.at[z - d if way == UP else z + d]
            remote(dst, dst, m_send.at[way, d], m_recv.at[way, d], {"tensor": 1 - c}).wait_recv()

        for d in range(1, nz):
            for way in (UP, DOWN):
                pl.when(z + d < nz if way == UP else z >= d)(lambda way=way, d=d: send(way, d).start())

        def follow(d):
            pl.when(z == d)(lambda: dy.start_along(UP))
            pl.when(nz - 1 - z == d)(lambda: dy.start_along(DOWN))

        follow(0)
        for d in range(1, nz):
            for p in range(PIECES):
                n1.event(d, p)
            follow(d)
        dy.start_across()
        keep.wait()
        for d in range(1, nz):
            for way in (UP, DOWN):
                pl.when(z + d < nz if way == UP else z >= d)(lambda way=way, d=d: send(way, d).wait_send())
                pl.when(z >= d if way == UP else z + d < nz)(lambda way=way, d=d: take(way, d))
        n1.settle_all()
        n1.finish()
        save(n1_ref, n1_hbm)
        for load in loads:
            load.wait()

        def project(first, last):
            def one(i, carry):
                to = pl.ds(pl.multiple_of(i * full, full), full)
                qkv_ref[to, :] = jnp.dot(n1_ref[to, :], w[...], preferred_element_type=f32).astype(bf16)
                return carry

            lax.fori_loop(first, last, one, 0)

        def label():
            for b in range(nz):
                some = all_ref[b].astype(f32)
                dgate_ref[b * full : (b + 1) * full, :1] = some.T[:, :1]
                seg_k[:, b * full : (b + 1) * full] = some[:1, :]

        def head(i):
            length = (i + 1) * full

            def one(h, carry):
                def part(k):
                    return pl.ds(pl.multiple_of(k * cols + h * HD, HD), HD)

                base = i * full
                scores[:, :length] = lax.dot_general(
                    qkv_ref[base : base + full, part(0)], qkv_ref[:length, part(1)], (((1,), (1,)), ((), ())),
                    preferred_element_type=f32,
                )

                def soften(j, inner):
                    local = pl.ds(pl.multiple_of(j * strip, strip), strip)
                    row = pl.ds(pl.multiple_of(base + j * strip, strip), strip)
                    place_q = base + j * strip + lax.broadcasted_iota(jnp.int32, (strip, length), 0)
                    place_k = lax.broadcasted_iota(jnp.int32, (strip, length), 1)
                    allowed = jnp.logical_and(place_k <= place_q, seg_k[:, :length] == dgate_ref[row, :1])
                    value = jnp.where(allowed, scores[local, :length] * scale, -jnp.inf)
                    value = jnp.exp(value - jnp.max(value, axis=-1, keepdims=True))
                    share = 1.0 / jnp.sum(value, axis=-1, keepdims=True)
                    p_ref[h, row, :length] = (value * share).astype(bf16)
                    return inner

                lax.fori_loop(0, full // strip, soften, 0)
                if length < seq:
                    p_ref[h, base : base + full, length:] = jnp.zeros((full, seq - length), bf16)
                o_ref[base : base + full, pl.ds(pl.multiple_of(h * HD, HD), HD)] = jnp.dot(
                    p_ref[h, base : base + full, :length], qkv_ref[:length, part(2)], preferred_element_type=f32
                ).astype(bf16)
                return carry

            lax.fori_loop(0, heads, one, 0)

        works = [label] + [functools.partial(head, i) for i in range(nz)]
        left_events = [(d, p) for d in range(1, nz) for p in range(PIECES)]

        def events(count=None):
            for _ in range(len(left_events) if count is None else count):
                dy.event(*left_events.pop(0))

        project(0, 2)
        events(1)
        project(2, nz)
        events(1)
        for work in works:
            work()
            if len(left_events) > 2:
                events(1)

        def inside(way, d):
            return z + d < nz if way == UP else z >= d

        def send_heads(way, d):
            to = z + d if way == UP else z - d
            src = o_ref.at[pl.ds(pl.multiple_of(to * full, full), full)]
            return remote(src, heads_in.at[way, d], a_send.at[way, d], a_recv.at[way, d], {"expert": to})

        for d in range(nz - 1, 0, -1):
            for way in (UP, DOWN):
                pl.when(inside(way, d))(lambda way=way, d=d: send_heads(way, d).start())

        save(qkv_ref, qkv_hbm)
        save(p_ref, p_hbm)
        save(o_ref, o_hbm)
        tile = 512 if width % 512 == 0 else width

        def put(block, left, fresh):
            at = pl.ds(pl.multiple_of(block * cols, cols), cols)

            def one(i, carry):
                to = pl.ds(pl.multiple_of(i * tile, tile), tile)
                value = lax.dot_general(
                    left(), wo[to, at], (((1,), (1,)), ((), ())), preferred_element_type=f32
                )
                acc[:, to] = value if fresh else acc[:, to] + value
                return carry

            lax.fori_loop(0, width // tile, one, 0)

        put(z, lambda: o_ref[pl.ds(pl.multiple_of(z * full, full), full), :], True)
        events()
        for d in range(1, nz):
            for way in (UP, DOWN):
                @pl.when(z >= d if way == UP else z + d < nz)
                def _(way=way, d=d):
                    remote(
                        heads_in.at[way, d], heads_in.at[way, d], a_send.at[way, d], a_recv.at[way, d], {"tensor": 1 - c}
                    ).wait_recv()
                    put(z - d if way == UP else z + d, lambda: heads_in[way, d], False)

        def pack(at):
            give[at, :] = acc[pl.ds(pl.multiple_of((1 - c) * rows + at.start, STRIP), STRIP), :].astype(bf16)

        strips(rows, pack)
        swap = remote(give, take_in, e_send, e_recv, {"tensor": 1 - c})
        swap.start()
        swap.wait_recv()

        def norm_two(at):
            mixed = acc[pl.ds(pl.multiple_of(c * rows + at.start, STRIP), STRIP), :] + take_in[at, :].astype(f32)
            h = x_ref[pl.ds(pl.multiple_of(c * rows + at.start, STRIP), STRIP), :].astype(f32) + mixed
            normed, inverse = norm_rows(h, small_ref[gate_row + 2 : gate_row + 3, :].astype(f32))
            h_ref[at, :] = h
            own[at, :] = normed.astype(bf16)
            inv_own[at, :] = jnp.broadcast_to(inverse, (STRIP, 128))

        strips(rows, norm_two)
        spot = inv_ref.at[pl.ds(pl.multiple_of(c * rows, rows), rows)]
        keep_inv = pltpu.make_async_copy(inv_own, spot, i_sems.at[0])
        pass_on = remote(inv_own, spot, i_sems.at[1], i_sems.at[2], {"tensor": 1 - c})
        keep_inv.start()
        pass_on.start()
        n2.start_along(UP)
        n2.start_along(DOWN)
        n2.start_across()
        dy.settle_all()
        dy.finish()
        save(dy_ref, dy_hbm)
        a, b, back = acc.at[:, pl.ds(0, held)], acc.at[:, pl.ds(held, held)], scores.at[:, pl.ds(0, held)]

        def hidden(index):
            at = pl.ds(pl.multiple_of(index * full, full), full)
            logit_ref[at, :] = nt_dot(n2_ref[at, :], small_ref[...])
            a[...] = nn_dot(n2_ref[at, :], wg[...])
            b[...] = nn_dot(n2_ref[at, :], wu[...])
            back[...] = nn_dot(dy_ref[at, :], wd[...])

            def point(j, carry):
                row = pl.ds(pl.multiple_of(index * full + j * strip, strip), strip)
                local = pl.ds(pl.multiple_of(j * strip, strip), strip)
                column = lax.broadcasted_iota(jnp.int32, (strip, held), 1)
                valid = jnp.logical_and(column >= skip, column < skip + ffn)
                av, bv = a[local, :], b[local, :]
                kv = jnp.where(valid, back[local, :], 0.0)
                gv = 1.0 / (1.0 + jnp.exp(-logit_ref[row, gate_row : gate_row + 1]))
                sig = 1.0 / (1.0 + jnp.exp(-av))
                act = av * sig
                u = jnp.where(valid, act * bv, 0.0)
                last = lax.broadcasted_iota(jnp.int32, (strip, small.shape[0]), 1) == gate_row
                dgate_ref[row, :] = jnp.where(last, jnp.sum(u * kv, axis=-1, keepdims=True), 0.0)
                gu[row, :] = (gv * u).astype(bf16)
                du = gv * kv
                da[row, :] = (du * bv * (sig + act * (1.0 - sig))).astype(bf16)
                db[row, :] = (du * act).astype(bf16)
                return carry

            lax.fori_loop(0, full // strip, point, 0)
            for k, ref in enumerate((da, db, gu)):
                turned[k, :, at] = ref[at, :].T

        def arrivals(d):
            for way in (UP, DOWN):

                @pl.when(n2.inside(way, d))
                def _(way=way):
                    n2.settle(way, d)

        def pair(d):
            def one(k, carry):
                index = z + (2 * k - 1) * d
                pl.when(jnp.logical_and(index >= 0, index < nz))(lambda: hidden(index))
                return carry

            arrivals(d)
            lax.fori_loop(0, 2, one, 0)

        n2.settle(UP, 0)
        hidden(z)
        for d in range(1, nz):
            for p in range(PIECES):
                n2.event(d, p)
            if d > 1:
                pair(d - 1)
        pair(nz - 1)
        n2.finish()
        save(n2_ref, n2_hbm)
        save(da, da_hbm.at[0])
        save(db, db_hbm.at[0])
        save(gu, gu_hbm.at[0])

        def leave(i):
            slot = lax.rem(i, 2)
            if per > 1:
                dst = grad_hbm.at[pl.ds(i * per, per)]
            else:
                many = block // TILE
                to = pl.ds(pl.multiple_of(lax.rem(i, many) * TILE, TILE), TILE)
                dst = grad_hbm.at[pl.ds(i // many, 1), :, to]
            return pltpu.make_async_copy(slab.at[slot], dst, slab_sem.at[slot])

        def four(i, at):
            slot = lax.rem(i, 2)
            pl.when(i >= 2)(lambda: leave(i).wait())
            for k, right in enumerate((n2_ref, n2_ref, dy_ref)):
                value = nn_dot(turned[k, pl.ds(pl.multiple_of(skip, 16), ffn), :], right[:, at]).astype(bf16)
                for j in range(per):
                    slab[slot, j, k * ffn : (k + 1) * ffn, :] = value[:, j * lane : (j + 1) * lane]
            leave(i).start()

        tiles(slabs, four)
        leave(slabs - 2).wait()
        leave(slabs - 1).wait()
        keep_inv.wait()
        pass_on.wait()
        swap.wait_send()
        for d in range(1, nz):
            for way in (UP, DOWN):
                pl.when(inside(way, d))(lambda way=way, d=d: send_heads(way, d).wait_send())
        for copy in saves:
            copy.wait()

    hidden_shape = jax.ShapeDtypeStruct((1, seq, held), bf16)
    return pl.pallas_call(
        kernel,
        out_shape=[
            jax.ShapeDtypeStruct((seq, width), bf16),
            jax.ShapeDtypeStruct((seq, width), bf16),
            jax.ShapeDtypeStruct((nz,) + marks.shape, jnp.int32),
            jax.ShapeDtypeStruct((seq, 3 * cols), bf16),
            jax.ShapeDtypeStruct((heads, seq, seq), bf16),
            jax.ShapeDtypeStruct((seq, cols), bf16),
            jax.ShapeDtypeStruct((seq, width), bf16),
            jax.ShapeDtypeStruct((rows, width), f32),
            jax.ShapeDtypeStruct((full, 128), f32),
            jax.ShapeDtypeStruct((seq, small.shape[0]), f32),
            jax.ShapeDtypeStruct((groups, 3 * ffn, block), bf16),
            hidden_shape, hidden_shape, hidden_shape,
            jax.ShapeDtypeStruct((seq, small.shape[0]), f32),
        ],
        in_specs=[VMEM] * 4 + [ANY] * 7,
        out_specs=[ANY, ANY, VMEM, ANY, ANY, ANY, ANY, VMEM, ANY, VMEM, ANY, ANY, ANY, ANY, VMEM],
        scratch_shapes=[
            pltpu.VMEM((seq, width), bf16), pltpu.VMEM((seq, width), bf16), pltpu.VMEM((seq, 3 * cols), bf16),
            pltpu.VMEM((heads, seq, seq), bf16), pltpu.VMEM((seq, cols), bf16), pltpu.VMEM((seq, width), bf16),
            pltpu.VMEM((rows, width), bf16), pltpu.VMEM((width, 3 * cols), bf16), pltpu.VMEM((full, seq), f32),
            pltpu.VMEM((1, seq), f32),
            pltpu.VMEM((2, nz, full, cols), bf16),
            pltpu.VMEM((full, width), f32),
            pltpu.VMEM((rows, width), bf16), pltpu.VMEM((rows, width), bf16),
            pltpu.VMEM((rows, 128), f32), pltpu.VMEM(out_weight.shape, bf16),
            pltpu.VMEM((width, held), bf16), pltpu.VMEM((width, held), bf16), pltpu.VMEM((width, held), bf16),
            pltpu.VMEM((seq, held), bf16), pltpu.VMEM((seq, held), bf16), pltpu.VMEM((seq, held), bf16),
            pltpu.VMEM((3, held, seq), bf16), pltpu.VMEM((2, per, 3 * ffn, lane), bf16),
            pltpu.SemaphoreType.DMA((7,)),
            pltpu.SemaphoreType.DMA((2, nz)), pltpu.SemaphoreType.DMA((2, nz)), pltpu.SemaphoreType.DMA,
            pltpu.SemaphoreType.DMA((2, nz)), pltpu.SemaphoreType.DMA((2, nz)),
            pltpu.SemaphoreType.DMA, pltpu.SemaphoreType.DMA, pltpu.SemaphoreType.DMA((3,)),
            pltpu.SemaphoreType.DMA((9,)), pltpu.SemaphoreType.DMA((2,)),
        ]
        + gather_sems(nz) * 3,
        compiler_params=pltpu.CompilerParams(
            collective_id=name, has_side_effects=True, vmem_limit_bytes=63 * 1024 * 1024
        ),
    )(x, upstream, marks, small, *weights, out_weight, *shared)


def attention_back(nz, d_h, n1, qkv, probs, o, out_weight, groups, part, n2, small, name):
    seq, width = d_h.shape
    heads = probs.shape[0]
    cols = o.shape[1]
    full = seq // nz
    block = width // groups
    lane = min(block, TILE)
    per = TILE // lane
    slabs = width // TILE
    strip = 32
    scale = HD ** (-0.5)

    def kernel(dh_hbm, n1_hbm, qkv_ref, p_ref, o_ref, wo_hbm, part_hbm, n2_hbm, small_ref, heads_ref, grad_hbm, box_hbm,
               sum_ref, n2_ref, s_turned, b_send, b_recv, b_local, dh_ref, n1_ref, wo, d_o, scores, ds, dk, dv, turned, o_turned, slab, in_sem, slab_sem):
        z, c = here()
        at = pl.ds(pl.multiple_of(z * cols, cols), cols)
        loads = [
            pltpu.make_async_copy(wo_hbm.at[:, at], wo, in_sem.at[0]),
            pltpu.make_async_copy(dh_hbm, dh_ref, in_sem.at[1]),
            pltpu.make_async_copy(n1_hbm, n1_ref, in_sem.at[2]),
            pltpu.make_async_copy(n2_hbm, n2_ref, in_sem.at[3]),
        ]
        for load in loads:
            load.start()
        greet(nz)
        keep = pltpu.make_async_copy(part_hbm.at[z], box_hbm.at[z], b_local)
        keep.start()

        def send(way, d):
            to = z + d if way == UP else z - d
            return remote(part_hbm.at[to], box_hbm.at[z], b_send.at[way, d], b_recv.at[way, d], {"expert": to})

        def take(way, d):
            dst = box_hbm.at[z - d if way == UP else z + d]
            remote(dst, dst, b_send.at[way, d], b_recv.at[way, d], {"tensor": 1 - c}).wait_recv()

        for d in range(nz - 1, 0, -1):
            for way in (UP, DOWN):
                pl.when(z + d < nz if way == UP else z >= d)(lambda way=way, d=d: send(way, d).start())
        o_turned[...] = o_ref[...].T
        s_turned[...] = small_ref[...].T
        loads[0].wait()
        loads[1].wait()

        def project(i, to):
            d_o[to, :] = nn_dot(dh_ref[to, :], wo[...]).astype(bf16)

        tiles(seq // TILE, project)

        def head(h, carry):
            def part(k):
                return pl.ds(pl.multiple_of(k * cols + h * HD, HD), HD)

            mine = part(0)
            for i in reversed(range(nz)):
                length = (i + 1) * full
                row = pl.ds(i * full, full)
                scores[:, :length] = nt_dot(d_o[row, mine], qkv_ref[:length, part(2)])

                def harden(j, inner, i=i, length=length):
                    local = pl.ds(pl.multiple_of(j * strip, strip), strip)
                    to = pl.ds(pl.multiple_of(i * full + j * strip, strip), strip)
                    mean = jnp.sum(
                        d_o[to, mine].astype(f32) * o_ref[to, mine].astype(f32), axis=-1, keepdims=True
                    )
                    value = p_ref[h, to, :length].astype(f32) * (scores[local, :length] - mean)
                    ds[local, :length] = value.astype(bf16)
                    return inner

                lax.fori_loop(0, full // strip, harden, 0)
                d_s = ds[:, :length]
                heads_ref[row, mine] = (nn_dot(d_s, qkv_ref[:length, part(1)]) * scale).astype(bf16)
                d_k = tn_dot(d_s, qkv_ref[row, mine])
                d_v = tn_dot(p_ref[h, row, :length], d_o[row, mine])
                if i == nz - 1:
                    dk[...], dv[...] = d_k, d_v
                else:
                    dk[:length, :] += d_k
                    dv[:length, :] += d_v
            heads_ref[:, part(1)] = (dk[...] * scale).astype(bf16)
            heads_ref[:, part(2)] = dv[...].astype(bf16)
            return carry

        lax.fori_loop(0, heads, head, 0)

        def turn(i, to):
            turned[:, to] = heads_ref[to, :].T

        tiles(seq // TILE, turn)
        loads[2].wait()
        loads[3].wait()

        def leave(i):
            slot = lax.rem(i, 2)
            if per > 1:
                dst = grad_hbm.at[pl.ds(i * per, per)]
            else:
                many = block // TILE
                to = pl.ds(pl.multiple_of(lax.rem(i, many) * TILE, TILE), TILE)
                dst = grad_hbm.at[pl.ds(i // many, 1), :, to]
            return pltpu.make_async_copy(slab.at[slot], dst, slab_sem.at[slot])

        def write(i, to):
            slot = lax.rem(i, 2)
            pl.when(i >= 2)(lambda: leave(i).wait())
            inner = nn_dot(turned[...], n1_ref[:, to]).astype(bf16)
            outer = nn_dot(o_turned[...], dh_ref[:, to]).astype(bf16)
            both = nn_dot(s_turned[:32, :], n2_ref[:, to])
            sum_ref[:, to] = both[:16, :] + both[16:, :]
            for j in range(per):
                slab[slot, j, : 3 * cols, :] = inner[:, j * lane : (j + 1) * lane]
                slab[slot, j, 3 * cols :, :] = outer[:, j * lane : (j + 1) * lane]
            leave(i).start()

        tiles(slabs, write)
        leave(slabs - 2).wait()
        leave(slabs - 1).wait()
        keep.wait()
        for d in range(1, nz):
            for way in (UP, DOWN):
                pl.when(z + d < nz if way == UP else z >= d)(lambda way=way, d=d: send(way, d).wait_send())
                pl.when(z >= d if way == UP else z + d < nz)(lambda way=way, d=d: take(way, d))

    return pl.pallas_call(
        kernel,
        out_shape=[
            jax.ShapeDtypeStruct((seq, 3 * cols), bf16),
            jax.ShapeDtypeStruct((groups, 4 * cols, block), bf16),
            jax.ShapeDtypeStruct(part.shape, bf16),
            jax.ShapeDtypeStruct((16, width), f32),
        ],
        in_specs=[ANY, ANY, VMEM, VMEM, VMEM, ANY, ANY, ANY, VMEM],
        out_specs=[VMEM, ANY, ANY, VMEM],
        scratch_shapes=[
            pltpu.VMEM((seq, width), bf16), pltpu.VMEM((small.shape[1], seq), bf16),
            pltpu.SemaphoreType.DMA((2, nz)), pltpu.SemaphoreType.DMA((2, nz)), pltpu.SemaphoreType.DMA,
            pltpu.VMEM((seq, width), bf16), pltpu.VMEM((seq, width), bf16), pltpu.VMEM((width, cols), bf16),
            pltpu.VMEM((seq, cols), bf16), pltpu.VMEM((full, seq), f32), pltpu.VMEM((full, seq), bf16),
            pltpu.VMEM((seq, HD), f32), pltpu.VMEM((seq, HD), f32),
            pltpu.VMEM((3 * cols, seq), bf16), pltpu.VMEM((cols, seq), bf16), pltpu.VMEM((2, per, 4 * cols, lane), bf16),
            pltpu.SemaphoreType.DMA((4,)), pltpu.SemaphoreType.DMA((2,)),
        ],
        compiler_params=params(name),
    )(d_h, n1, qkv, probs, o, out_weight, part, n2, small)


def spread_turned(nz, part, splits, name):
    _, columns, block = part.shape
    cols = columns // splits

    def kernel(in_ref, *rest):
        outs, (box, send_sem, recv_sem) = rest[:splits], rest[splits:]
        z, c = here()
        greet(nz)

        def send(way, d):
            to = z + d if way == UP else z - d
            return remote(in_ref.at[to], box.at[z], send_sem.at[way, d], recv_sem.at[way, d], {"expert": to})

        def take(way, d):
            dst = box.at[z - d if way == UP else z + d]
            remote(dst, dst, send_sem.at[way, d], recv_sem.at[way, d], {"tensor": 1 - c}).wait_recv()

        for d in range(nz - 1, 0, -1):
            for way in (UP, DOWN):
                pl.when(z + d < nz if way == UP else z >= d)(lambda way=way, d=d: send(way, d).start())
        box[z] = in_ref[z]
        for d in range(1, nz):
            for way in (UP, DOWN):
                pl.when(z + d < nz if way == UP else z >= d)(lambda way=way, d=d: send(way, d).wait_send())
                pl.when(z >= d if way == UP else z + d < nz)(lambda way=way, d=d: take(way, d))
        for j in range(splits):
            for b in range(nz):
                value = box[b, j * cols : (j + 1) * cols, :].astype(f32).T
                outs[j][:, b * cols : (b + 1) * cols] = value

    return pl.pallas_call(
        kernel,
        out_shape=[jax.ShapeDtypeStruct((block, nz * cols), f32)] * splits,
        in_specs=[VMEM],
        out_specs=[VMEM] * splits,
        scratch_shapes=[
            pltpu.VMEM(part.shape, bf16), pltpu.SemaphoreType.DMA((2, nz)), pltpu.SemaphoreType.DMA((2, nz)),
        ],
        compiler_params=params(name),
    )(part)


PART = 512


class Products:
    def __init__(self, nz, experts, shared, extra):
        self.nz, self.experts, self.shared = nz, experts, shared
        _, self.seq, self.kept = experts[0][0][0].shape
        _, self.ffn, self.width = experts[0][1][0].shape
        self.held = shared[0][0][0].shape[2]
        self.own = shared[0][1].shape[1] // nz
        self.more = [] if extra is None else list(extra)
        self.inputs = (
            [left[0] for left, _ in experts] + [right[0] for _, right in experts] + [left[0] for left, _ in shared]
            + [right for _, right in shared] + self.more
        )
        ne, ns = len(experts), len(shared)
        self.specs = [ANY] * (2 * (ne + ns)) + [VMEM] * len(self.more)
        self.scratch = [
            pltpu.VMEM((self.seq, ne * self.kept), bf16), pltpu.VMEM((ne * self.kept, self.width), bf16),
            pltpu.VMEM((self.seq, ns * self.held), bf16), pltpu.VMEM((self.width, ns * self.held), bf16),
            pltpu.SemaphoreType.DMA((self.width // PART, ne + ns)), pltpu.SemaphoreType.DMA((nz, ne + ns)),
        ]

    def bind(self, refs, scratch):
        ne, ns = len(self.experts), len(self.shared)
        self.left, self.right, self.sleft, self.sright, self.r_sem, self.l_sem = scratch
        self.e_left, self.e_right = refs[:ne], refs[ne : 2 * ne]
        self.s_left, self.s_right = refs[2 * ne : 2 * ne + ns], refs[2 * ne + ns : 2 * (ne + ns)]
        self.small = refs[2 * (ne + ns) :]
        self.first = pl.multiple_of(lax.axis_index("expert") * self.own // LANES * LANES, LANES)

    def rights(self, j):
        to = pl.ds(pl.multiple_of(j * PART, PART), PART)
        for i, (_, (_, index)) in enumerate(self.experts):
            dst = self.right.at[pl.ds(i * self.kept, self.ffn), to]
            yield pltpu.make_async_copy(self.e_right[i].at[index, :, to], dst, self.r_sem.at[j, i])
        for i in range(len(self.shared)):
            src = self.s_right[i].at[to, pl.ds(self.first, self.held)]
            dst = self.sright.at[to, pl.ds(i * self.held, self.held)]
            yield pltpu.make_async_copy(src, dst, self.r_sem.at[j, len(self.experts) + i])

    def lefts(self, b):
        rows = self.seq // self.nz
        at = pl.ds(pl.multiple_of(b * rows, rows), rows)
        for i, ((_, index), _) in enumerate(self.experts):
            dst = self.left.at[at, pl.ds(i * self.kept, self.kept)]
            yield pltpu.make_async_copy(self.e_left[i].at[index, at], dst, self.l_sem.at[b, i])
        for i, ((_, index), _) in enumerate(self.shared):
            dst = self.sleft.at[at, pl.ds(i * self.held, self.held)]
            yield pltpu.make_async_copy(self.s_left[i].at[index, at], dst, self.l_sem.at[b, len(self.experts) + i])

    def fetch(self, order):
        for copy in self.lefts(order(0)):
            copy.start()
        for j in range(self.width // PART):
            for copy in self.rights(j):
                copy.start()
        for k in range(1, self.nz):
            for copy in self.lefts(order(k)):
                copy.start()
        if self.kept > self.ffn:
            for i in range(len(self.experts)):
                self.right[i * self.kept + self.ffn : (i + 1) * self.kept, :] = jnp.zeros(
                    (self.kept - self.ffn, self.width), bf16
                )

    def block(self, k, b, out, start, end):
        rows = self.seq // self.nz
        at = pl.ds(pl.multiple_of(b * rows, rows), rows)
        if start == 0:
            for copy in self.lefts(b):
                copy.wait()

        def one(j, carry):
            @pl.when(k == 0)
            def _():
                for copy in self.rights(j):
                    copy.wait()

            to = pl.ds(pl.multiple_of(j * PART, PART), PART)
            value = nn_dot(self.left[at, :], self.right[:, to]) + nt_dot(self.sleft[at, :], self.sright[to, :])
            if self.more:
                value += nt_dot(self.small[0][at, :], self.small[1][to, :])
            out[at, to] = value.astype(bf16)
            return carry

        lax.fori_loop(start, end, one, 0)


def reduce_and_gather(nz, products, h, gains, upstream, name):
    rows, width = h.shape
    n_in, n_scratch = len(products.inputs), len(products.scratch)

    def kernel(*refs):
        p_refs, (h_ref, gain_ref, up_ref, out_ref, dh_ref, gg_ref) = refs[:n_in], refs[n_in : n_in + 6]
        rest = refs[n_in + 6 :]
        p_scratch, (part, own), rest = rest[:n_scratch], rest[n_scratch : n_scratch + 2], rest[n_scratch + 2 :]
        scratch, sems = rest[:REDUCE_SCRATCH], rest[REDUCE_SCRATCH:]
        total = scratch[3]
        products.bind(p_refs, p_scratch)
        reducer = Reducer(nz, part, *scratch)
        products.fetch(reducer.block)
        greet(nz)
        z, c = here()
        ends = reducer.ends()

        def one(s, carry):
            products.block(s, reducer.block(s), part, 0, 1)
            pl.when(jnp.logical_and(ends, s >= 1))(lambda: reducer.forward(s - 1))
            products.block(s, reducer.block(s), part, 1, width // PART)
            reducer.begin(s)
            pl.when(jnp.logical_and(jnp.logical_not(ends), s >= 2))(lambda: reducer.forward(s - 2))
            return carry

        lax.fori_loop(0, nz, one, 0)
        pl.when(jnp.logical_not(ends))(lambda: reducer.forward(nz - 2))
        reducer.finish()
        gg_ref[...] = jnp.zeros_like(gg_ref)

        def step(at):
            change, along = norm_back(h_ref[at, :], gain_ref[gains.shape[0] - 1 :, :].astype(f32), total[at, :])
            dh = up_ref[pl.ds(pl.multiple_of(c * rows + at.start, STRIP), STRIP), :].astype(f32) + change
            dh_ref[at, :] = dh
            own[at, :] = dh.astype(bf16)
            gg_ref[...] += along

        strips(rows, step)
        gather_rows(nz, own, out_ref, *sems)
        reducer.drain()

    return pl.pallas_call(
        kernel,
        out_shape=[
            jax.ShapeDtypeStruct((nz * 2 * rows, width), bf16),
            jax.ShapeDtypeStruct((rows, width), f32),
            jax.ShapeDtypeStruct((STRIP, width), f32),
        ],
        in_specs=products.specs + [VMEM] * 3,
        out_specs=[ANY, VMEM, VMEM],
        scratch_shapes=products.scratch
        + [pltpu.VMEM((nz * 2 * rows, width), bf16), pltpu.VMEM((rows, width), bf16)]
        + reduce_scratch(nz, rows, width)
        + gather_sems(nz),
        compiler_params=params(name),
    )(*products.inputs, h, gains, upstream)


def reduce_last(nz, d_heads, weights, x, gains, dh, products, h, small, box, name):
    rows, width = dh.shape
    cols = d_heads.shape[1] // 3
    n, small_rows, lanes = small.shape
    box_rows, block = box.shape[1] // 3, box.shape[2]
    n_in, n_scratch = len(products.inputs), len(products.scratch)

    def kernel(*refs):
        p_refs, (
            d_ref, wq_hbm, wk_hbm, wv_hbm, x_ref, gain_ref, dh_ref, h_ref, small_ref, box_ref, in_ref, out_ref, sum_ref, *turned,
        ) = refs[:n_in], refs[n_in : n_in + 16]
        gg_ref, s_out, s_box, s_total, s_other, s_send, s_recv, swap_sem = refs[n_in + 16 : n_in + 24]
        rest = refs[n_in + 24 :]
        p_scratch, (d_part, b_part, own, sems, w_ref, w_sem), rest = (
            rest[:n_scratch], rest[n_scratch : n_scratch + 6], rest[n_scratch + 6 :],
        )
        mine = pl.ds(pl.multiple_of(lax.axis_index("expert") * cols, cols), cols)
        loads = [
            pltpu.make_async_copy(src.at[:, mine], w_ref.at[:, pl.ds(i * cols, cols)], w_sem.at[i])
            for i, src in enumerate((wq_hbm, wk_hbm, wv_hbm))
        ]
        for load in loads:
            load.start()
        d_scratch, b_scratch = rest[:REDUCE_SCRATCH], rest[REDUCE_SCRATCH:]
        d_total, b_total = d_scratch[3], b_scratch[3]
        products.bind(p_refs, p_scratch)
        first, second = Reducer(nz, d_part, *d_scratch), Reducer(nz, b_part, *b_scratch)
        z, c = here()
        me = lax.axis_index("dp") * nz + z
        barrier = pltpu.get_barrier_semaphore()

        def peer(q):
            to = lax.rem(me + q, n)
            return to, {"dp": to // nz, "expert": lax.rem(to, nz)}

        pl.semaphore_signal(barrier, inc=1, device_id={"tensor": 1 - c}, device_id_type=MESH)
        for q in range(1, n):
            pl.semaphore_signal(barrier, inc=1, device_id=peer(q)[1], device_id_type=MESH)
        pl.semaphore_wait(barrier, n)

        def send_small(q):
            to, device = peer(q)
            return remote(s_out.at[to], s_box.at[q], s_send.at[q], s_recv.at[q], device)

        ends = first.ends()
        middle = jnp.logical_not(ends)

        def inner(block):
            at = pl.ds(pl.multiple_of(block * 2 * rows, 2 * rows), 2 * rows)

            def one(j, carry):
                to = pl.ds(pl.multiple_of(j * PART, PART), PART)
                d_part[at, to] = nt_dot(d_ref[at, :], w_ref[to, :]).astype(bf16)
                return carry

            lax.fori_loop(0, width // PART, one, 0)

        def one(s, carry):
            inner(first.block(s))
            first.begin(s)
            pl.when(jnp.logical_and(ends, s >= 1))(lambda: first.forward(s - 1))
            return carry

        def two(s, carry):
            products.block(s, second.block(s), b_part, 0, width // PART)
            second.begin(s)

            @pl.when(s >= 1)
            def _():
                pl.when(ends)(lambda: second.forward(s - 1))
                pl.when(middle)(lambda: first.forward(s - 1))

            return carry

        def three(s, carry):
            pl.when(middle)(lambda: second.forward(s))
            return carry

        for load in loads:
            load.wait()
        products.fetch(second.block)
        lax.fori_loop(0, nz, one, 0)
        lax.fori_loop(0, nz, two, 0)
        lax.fori_loop(0, nz - 1, three, 0)
        for i in range(3):
            for b in range(nz):
                value = box_ref[b, i * box_rows : (i + 1) * box_rows, :].astype(f32).T
                turned[i][:, b * box_rows : (b + 1) * box_rows] = value
        first.finish()
        gg_ref[...] = jnp.zeros_like(gg_ref)

        def step(at):
            change, along = norm_back(x_ref[pl.ds(pl.multiple_of(c * rows + at.start, STRIP), STRIP), :].astype(f32), gain_ref[gains.shape[0] - 2 : gains.shape[0] - 1, :].astype(f32), d_total[at, :])
            own[0, at, :] = dh_ref[at, :] + change
            gg_ref[...] += along

        strips(rows, step)

        def leave(i, ref):
            spot = ref.at[pl.ds(pl.multiple_of(c * rows, rows), rows)]
            return (
                pltpu.make_async_copy(own.at[i], spot, sems.at[i, 0]),
                remote(own.at[i], spot, sems.at[i, 1], sems.at[i, 2], {"tensor": 1 - c}),
            )

        for copy in leave(0, in_ref):
            copy.start()
        first_row = jnp.sum(gg_ref[...], axis=0, keepdims=True)
        for q in range(n):
            s_out[q] = small_ref[q]
            s_out[q, :1, :] = first_row[:, q * lanes : (q + 1) * lanes]
        for q in range(1, n):
            send_small(q).start()
        s_total[...] = s_out[me]
        for q in range(1, n):
            send_small(q).wait_recv()
            s_total[...] += s_box[q]
        swap = remote(s_total, s_other, swap_sem.at[0], swap_sem.at[1], {"tensor": 1 - c})
        swap.start()
        second.finish()

        def last(at):
            own[1, at, :] = h_ref[at, :] + b_total[at, :]

        strips(rows, last)
        for copy in leave(1, out_ref):
            copy.start()
        first.drain()
        second.drain()
        swap.wait_recv()
        sum_ref[...] = s_total[...] + s_other[...]
        swap.wait_send()
        for q in range(1, n):
            send_small(q).wait_send()
        for copy in (*leave(0, in_ref), *leave(1, out_ref)):
            copy.wait()

    return pl.pallas_call(
        kernel,
        out_shape=[
            jax.ShapeDtypeStruct((2 * rows, width), f32),
            jax.ShapeDtypeStruct((2 * rows, width), f32),
            jax.ShapeDtypeStruct((small_rows, lanes), f32),
        ]
        + [jax.ShapeDtypeStruct((block, nz * box_rows), f32)] * 3,
        in_specs=products.specs + [VMEM] + [ANY] * 3 + [VMEM] * 6,
        out_specs=[ANY, ANY] + [VMEM] * 4,
        scratch_shapes=[
            pltpu.VMEM((STRIP, width), f32), pltpu.VMEM(small.shape, f32), pltpu.VMEM(small.shape, f32),
            pltpu.VMEM((small_rows, lanes), f32), pltpu.VMEM((small_rows, lanes), f32),
            pltpu.SemaphoreType.DMA((n,)), pltpu.SemaphoreType.DMA((n,)), pltpu.SemaphoreType.DMA((2,)),
        ]
        + products.scratch
        + [
            pltpu.VMEM((nz * 2 * rows, width), bf16), pltpu.VMEM((nz * 2 * rows, width), bf16),
            pltpu.VMEM((2, rows, width), f32), pltpu.SemaphoreType.DMA((2, 3)),
            pltpu.VMEM((width, 3 * cols), bf16), pltpu.SemaphoreType.DMA((3,)),
        ]
        + reduce_scratch(nz, rows, width) * 2,
        compiler_params=params(name, 60),
    )(*products.inputs, d_heads, *weights, x, gains, dh, h, small, box)


def cross_rows(left, right):
    return lax.dot_general(left, right, (((0,), (0,)), ((), ())), preferred_element_type=f32)


def cross_cols(left, right):
    return lax.dot_general(left, right, (((1,), (1,)), ((), ())), preferred_element_type=f32)


def dot(left, right):
    return jnp.dot(left, right, preferred_element_type=f32)


def two_parts(values):
    high = values.astype(bf16)
    return high, (values - high.astype(f32)).astype(bf16)


def body(
    tokens, segments, routes, norm1_gain, q_weight, k_weight, v_weight, o_weight, norm2_gain,
    router_weight, shared_gate_vector, shared_gate_weight, shared_up_weight, shared_down_weight,
    expert_gate_weight, expert_up_weight, expert_down_weight, out_grad,
):
    nz = lax.axis_size("expert")
    nc = lax.axis_size("tensor")
    z = lax.axis_index("expert")
    c = lax.axis_index("tensor")
    rows, width = tokens.shape
    own_rows = rows // nc
    local_count, _, ffn = expert_gate_weight.shape
    expert_count = local_count * nz
    head_cols = q_weight.shape[1] // nz
    shared_cols = shared_gate_weight.shape[1] // nz
    heads = head_cols // HD
    seq = rows * nz
    scale = HD ** (-0.5)

    def head_slice(values):
        return lax.dynamic_slice_in_dim(values, z * head_cols, head_cols, 1)

    x_all_rows = tokens.astype(f32)
    inverse_one_rows = lax.rsqrt(jnp.mean(x_all_rows * x_all_rows, axis=-1) + epsilon)
    marks = jnp.concatenate([segments, routes.T, jnp.zeros((7 - routes.shape[1], rows), jnp.int32)], axis=0)
    ndp = lax.axis_size("dp")
    small_rows_weight = jnp.concatenate(
        [router_weight.T, shared_gate_vector[None], norm1_gain[None], norm2_gain[None]], axis=0
    )
    shared_weights = (shared_gate_weight, shared_up_weight, shared_down_weight)
    (
        n1, dy, all_marks, qkv, p_low, o, n2, h, inverse_two, logits, grad_s, da_s, db_s, gu_s, dgate_s,
    ) = forward_layer(
        nz, tokens, out_grad, marks, (q_weight, k_weight, v_weight), o_weight, small_rows_weight, shared_weights,
        ndp * nz, 0,
    )
    all_routes = jnp.transpose(all_marks[:, 1 : 1 + routes.shape[1]], (0, 2, 1)).reshape(seq, routes.shape[1])

    probs = jax.nn.softmax(logits[:, :expert_count], axis=-1)
    chosen = jnp.any(all_routes[:, :, None] == jnp.arange(expert_count)[None, None, :], axis=1)
    gates = jnp.where(chosen, probs, 0.0)
    sigma = jax.nn.sigmoid(logits[:, expert_count : expert_count + 1])

    turned = [jnp.swapaxes(w, 1, 2) for w in (expert_gate_weight, expert_up_weight, expert_down_weight)]
    grad_e, da_e, db_e, gu_e, dgate_e = hidden_layer(nz, n2, dy, gates, turned, ndp)

    d_probs = jnp.where(chosen, dgate_e, 0.0)
    d_logits = probs * (d_probs - jnp.sum(probs * d_probs, axis=-1, keepdims=True))
    d_vector = dgate_s[:, expert_count : expert_count + 1] * (sigma * (1.0 - sigma))
    small = jnp.concatenate([d_logits, d_vector], axis=1)
    small_high, small_low = two_parts(small)
    small_weights = jnp.concatenate([router_weight, shared_gate_vector[:, None]], axis=1)
    fill = ((0, 0), (0, 128 - small.shape[1]))
    experts = range(local_count)
    d_n2 = Products(
        nz,
        [((da_e, i), (turned[0], i)) for i in experts] + [((db_e, i), (turned[1], i)) for i in experts],
        [((da_s, 0), shared_gate_weight), ((db_s, 0), shared_up_weight)],
        (jnp.pad(small_high, fill), jnp.pad(small_weights, fill)),
    )
    few = small.shape[1]
    mixed = jnp.pad(small_high, ((0, 0), (2, 126 - few))) + jnp.pad(small_low, ((0, 0), (18, 110 - few)))


    def over_dp(grad):
        rows = grad.reshape(-1, grad.shape[-1])
        return lax.psum_scatter(rows, "dp", scatter_dimension=0, tiled=True)

    shared_part = over_dp(grad_s).reshape((nz,) + grad_s.shape[1:])
    expert_part = over_dp(grad_e).reshape(local_count, 3, ffn, -1)
    dhr, dh, grad_two = reduce_and_gather(nz, d_n2, h, small_rows_weight, out_grad, 2)
    d_heads, grad_attention, shared_box, small_grad = attention_back(
        nz, dhr, n1, qkv, p_low, o, o_weight, ndp * nz, shared_part, n2, mixed, 1
    )
    attention_part = over_dp(grad_attention).reshape((nz,) + grad_attention.shape[1:])
    branch = Products(
        nz,
        [((gu_e, i), (turned[2], i)) for i in experts],
        [((gu_s, 0), shared_down_weight)],
        None,
    )
    dh_now, _ = lax.optimization_barrier((dh, grad_attention))
    small_rows = small_grad + jnp.pad(jnp.sum(grad_two, axis=0)[None], ((1, 14), (0, 0)))
    count = ndp * nz
    small_blocks = jnp.swapaxes(small_rows.reshape(16, count, width // count), 0, 1)
    input_grad, layer_out, small_all, s_gate, s_up, s_down = reduce_last(
        nz, d_heads, (q_weight, k_weight, v_weight), tokens, small_rows_weight, dh_now, branch, h, small_blocks, shared_box, 3
    )
    stats = jnp.stack([inverse_one_rows, inverse_two[:, 0]])

    e_gate, e_up, e_down = (jnp.swapaxes(expert_part[:, k].astype(f32), 1, 2) for k in range(3))
    attention_part, e_gate, e_up, e_down, small_all = lax.optimization_barrier(
        (attention_part, e_gate, e_up, e_down, small_all)
    )
    g_q, g_k, g_v, g_o = spread_turned(nz, attention_part, 4, 6)
    g_one, g_two, g_router, g_vector = small_all[0], small_all[1], small_all[2 : 2 + expert_count].T, small_all[2 + expert_count]
    return (
        layer_out, input_grad, stats, g_one, g_q, g_k, g_v, g_o, g_two, g_router, g_vector,
        s_gate, s_up, s_down, e_gate, e_up, e_down,
    )


def solution(mesh):
    both = ("dp", "expert")
    cols = P(None, "tensor")
    placed = (
        P(both, None), P("dp", "expert"), P(both, None), P(), cols, cols, cols, cols, P(), P(), P(),
        cols, cols, cols, P("expert", None, "tensor"), P("expert", None, "tensor"),
        P("expert", None, "tensor"), P(both, None),
    )
    split = P(both, "tensor")
    experts = P("expert", "dp", "tensor")
    return jax.shard_map(
        body,
        mesh=mesh,
        in_specs=placed,
        out_specs=(
            P(both, None), P(both, None), P(None, both), P(both), split, split, split, split, P(both),
            P(both, None), P(both), split, split, split, experts, experts, experts,
        ),
        check_vma=False,
    )
```

```python
import functools

import jax
import jax.numpy as jnp
from jax import lax
from jax.experimental import pallas as pl
from jax.experimental.pallas import tpu as pltpu
from jax.sharding import PartitionSpec as P

HD = 128
MESH = pl.DeviceIdType.MESH
PIECES = 2
STRIP = 16
epsilon = 1e-06
f32 = jnp.float32
bf16 = jnp.bfloat16
UP, DOWN = 0, 1


def here():
    return lax.axis_index("expert"), lax.axis_index("tensor")


def greet(nz):
    z, c = here()
    barrier = pltpu.get_barrier_semaphore()

    def tell(device):
        pl.semaphore_signal(barrier, inc=1, device_id=device, device_id_type=MESH)

    tell({"tensor": 1 - c})
    for d in range(1, nz):
        tell({"expert": lax.rem(z + d, nz)})
    pl.semaphore_wait(barrier, nz)


def remote(src, dst, send, recv, device):
    return pltpu.make_async_remote_copy(
        src_ref=src, dst_ref=dst, send_sem=send, recv_sem=recv, device_id=device, device_id_type=MESH
    )


def strips(rows, step):
    def one(i, carry):
        step(pl.ds(pl.multiple_of(i * STRIP, STRIP), STRIP))
        return carry

    lax.fori_loop(0, rows // STRIP, one, 0)


GATHER_SEMS = 4


def gather_sems(nz):
    return [pltpu.SemaphoreType.DMA((2, nz, PIECES))] * GATHER_SEMS + [pltpu.SemaphoreType.DMA]


class Gather:
    def __init__(self, nz, own, out, z_send, z_recv, s_send, s_recv, local_sem):
        self.nz, self.own, self.out = nz, own, out
        self.z_send, self.z_recv, self.s_send, self.s_recv, self.local_sem = z_send, z_recv, s_send, s_recv, local_sem
        self.z, self.c = here()
        self.rows = own.shape[0]
        self.piece = self.rows // PIECES

    def origin(self, way, d):
        return self.z - d if way == UP else self.z + d

    def inside(self, way, d):
        return self.z >= d if way == UP else self.z + d < self.nz

    def onward(self, way):
        return self.z < self.nz - 1 if way == UP else self.z > 0

    def place(self, block, core, p):
        start = (block * 2 + core) * self.rows + p * self.piece
        return self.out.at[pl.ds(pl.multiple_of(start, self.piece), self.piece)]

    def source(self, way, d, p):
        if d == 0:
            return self.own.at[pl.ds(p * self.piece, self.piece)]
        return self.place(self.origin(way, d), self.c, p)

    def along(self, way, d, p):
        device = {"expert": self.z + 1 if way == UP else self.z - 1}
        dst = self.place(self.origin(way, d), self.c, p)
        return remote(self.source(way, d, p), dst, self.z_send.at[way, d, p], self.z_recv.at[way, d, p], device)

    def across(self, way, d, p):
        dst = self.place(self.origin(way, d), self.c, p)
        return remote(
            self.source(way, d, p), dst, self.s_send.at[way, d, p], self.s_recv.at[way, d, p], {"tensor": 1 - self.c}
        )

    def arrived(self, way, d, p):
        dst = self.place(self.origin(way, d), self.c, p)
        remote(dst, dst, self.z_send.at[way, d - 1, p], self.z_recv.at[way, d - 1, p], {"tensor": 1 - self.c}).wait_recv()

    def crossed(self, way, d, p):
        dst = self.place(self.origin(way, d), 1 - self.c, p)
        remote(dst, dst, self.s_send.at[way, d, p], self.s_recv.at[way, d, p], {"tensor": 1 - self.c}).wait_recv()

    def mine(self):
        dst = self.out.at[pl.ds(pl.multiple_of((self.z * 2 + self.c) * self.rows, self.rows), self.rows)]
        return pltpu.make_async_copy(self.own, dst, self.local_sem)

    def start_along(self, way):
        @pl.when(self.onward(way))
        def _():
            for p in range(PIECES):
                self.along(way, 0, p).start()

    def start_across(self):
        for p in range(PIECES):
            self.across(UP, 0, p).start()
        self.mine().start()

    def event(self, d, p):
        for way in (UP, DOWN):

            @pl.when(self.inside(way, d))
            def _(way=way):
                self.arrived(way, d, p)
                pl.when(self.onward(way))(lambda: self.along(way, d, p).start())
                self.across(way, d, p).start()

    def settle(self, way, d):
        for p in range(PIECES):
            self.crossed(way, d, p)
        if d == 0:
            self.mine().wait()

    def settle_all(self):
        self.settle(UP, 0)
        for d in range(1, self.nz):
            for way in (UP, DOWN):
                pl.when(self.inside(way, d))(functools.partial(self.settle, way, d))

    def finish(self):
        for p in range(PIECES):
            self.across(UP, 0, p).wait_send()
            for way in (UP, DOWN):
                pl.when(self.onward(way))(lambda way=way, p=p: self.along(way, 0, p).wait_send())
                for d in range(1, self.nz):

                    @pl.when(self.inside(way, d))
                    def _(way=way, d=d, p=p):
                        self.across(way, d, p).wait_send()
                        pl.when(self.onward(way))(lambda: self.along(way, d, p).wait_send())


def gather_rows(nz, own, out, *sems):
    gather = Gather(nz, own, out, *sems)
    gather.start_along(UP)
    gather.start_along(DOWN)
    gather.start_across()
    for d in range(1, nz):
        for p in range(PIECES):
            gather.event(d, p)
    gather.settle_all()
    gather.finish()


REDUCE_SCRATCH = 8


def reduce_scratch(nz, rows, width):
    return [
        pltpu.VMEM((nz, rows, width), bf16),
        pltpu.VMEM((nz + 1, rows, width), bf16),
        pltpu.VMEM((nz, rows, width), bf16),
        pltpu.VMEM((rows, width), f32),
        pltpu.SemaphoreType.DMA((nz, PIECES)),
        pltpu.SemaphoreType.DMA((nz, PIECES)),
        pltpu.SemaphoreType.DMA((nz, PIECES)),
        pltpu.SemaphoreType.DMA((nz + 1, PIECES)),
    ]


def block_order(nz, z, s):
    down = 2 * z // nz
    far = jnp.maximum(z, nz - 1 - z)
    near = nz - 1 - far
    late = s - (far - near)
    distance = jnp.where(late < 0, far - s, near - late // 2)
    sign = (1 - 2 * down) * jnp.where(late < 0, 1, 1 - 2 * lax.rem(late + nz * 2, 2))
    return z + sign * distance


class Reducer:
    def __init__(self, nz, part, side, inbox, outbox, total, s_send, s_recv, z_send, z_recv):
        self.nz, self.part, self.side, self.inbox, self.outbox, self.total = nz, part, side, inbox, outbox, total
        self.s_send, self.s_recv, self.z_send, self.z_recv = s_send, s_recv, z_send, z_recv
        self.z, self.c = here()
        self.rows = total.shape[0]
        self.piece = self.rows // PIECES

    def block(self, s):
        return block_order(self.nz, self.z, s)

    def cut(self, p):
        return pl.ds(p * self.piece, self.piece)

    def across(self, block, p):
        start = (block * 2 + 1 - self.c) * self.rows + p * self.piece
        src = self.part.at[pl.ds(pl.multiple_of(start, self.piece), self.piece)]
        return remote(
            src, self.side.at[block, self.cut(p)], self.s_send.at[block, p], self.s_recv.at[block, p],
            {"tensor": 1 - self.c},
        )

    def along(self, block, p):
        up = block > self.z
        slot = jnp.where(block == self.z - 1, self.nz, block)
        return remote(
            self.outbox.at[block, self.cut(p)], self.inbox.at[slot, self.cut(p)], self.z_send.at[block, p],
            self.z_recv.at[slot, p], {"expert": self.z + jnp.where(up, 1, -1)},
        )

    def arrived(self, slot, p):
        dst = self.inbox.at[slot, self.cut(p)]
        remote(dst, dst, self.z_send.at[0, p], self.z_recv.at[slot, p], {"tensor": 1 - self.c}).wait_recv()

    def mine(self, block, at):
        base = (block * 2 + self.c) * self.rows
        own = self.part[pl.ds(pl.multiple_of(base + at.start, STRIP), STRIP), :].astype(f32)
        return own + self.side[block, at, :].astype(f32)

    def strips(self, p, step):
        def one(i, carry):
            step(pl.ds(pl.multiple_of(p * self.piece + i * STRIP, STRIP), STRIP))
            return carry

        lax.fori_loop(0, self.piece // STRIP, one, 0)

    def ends(self):
        return jnp.logical_or(self.z == 0, self.z == self.nz - 1)

    def begin(self, s):
        for p in range(PIECES):
            self.across(self.block(s), p).start()

    def forward(self, s):
        block = self.block(s)
        behind = jnp.where(block > self.z, self.z, self.nz - 1 - self.z) > 0
        for p in range(PIECES):
            self.across(block, p).wait_recv()

            @pl.when(behind)
            def _(p=p):
                self.arrived(block, p)

                def add(at):
                    self.outbox[block, at, :] = (self.mine(block, at) + self.inbox[block, at, :].astype(f32)).astype(bf16)

                self.strips(p, add)

            @pl.when(jnp.logical_not(behind))
            def _(p=p):
                def keep(at):
                    self.outbox[block, at, :] = self.mine(block, at).astype(bf16)

                self.strips(p, keep)

            self.along(block, p).start()

    def finish(self):
        z, nz = self.z, self.nz
        for p in range(PIECES):
            self.across(z, p).wait_recv()

            def first(at):
                self.total[at, :] = self.mine(z, at)

            self.strips(p, first)
            for slot, some in ((z, z > 0), (nz, z < nz - 1)):

                @pl.when(some)
                def _(slot=slot, p=p):
                    self.arrived(slot, p)

                    def add(at):
                        self.total[at, :] += self.inbox[slot, at, :].astype(f32)

                    self.strips(p, add)

    def drain(self):
        def one(s, carry):
            block = self.block(s)
            for p in range(PIECES):
                self.across(block, p).wait_send()
                pl.when(s < self.nz - 1)(lambda p=p: self.along(block, p).wait_send())
            return carry

        lax.fori_loop(0, self.nz, one, 0)


def params(name, room=56):
    return pltpu.CompilerParams(collective_id=name, has_side_effects=True, vmem_limit_bytes=room * 1024 * 1024)


VMEM = pl.BlockSpec(memory_space=pltpu.VMEM)
ANY = pl.BlockSpec(memory_space=pl.ANY)


def norm_rows(values, gain):
    inverse = lax.rsqrt(jnp.mean(values * values, axis=-1, keepdims=True) + epsilon)
    return values * inverse * gain, inverse


def norm_back(values, gain, upstream):
    inverse = lax.rsqrt(jnp.mean(values * values, axis=-1, keepdims=True) + epsilon)
    scaled = upstream * gain
    inner = jnp.mean(scaled * values, axis=-1, keepdims=True)
    change = inverse * scaled - values * inverse * inverse * inverse * inner
    return change, upstream * values * inverse


def swap_rows(nz, own, out_ref, sems):
    z, c = here()
    rows = own.shape[0]
    spot = out_ref.at[pl.ds(pl.multiple_of(c * rows, rows), rows)]
    keep = pltpu.make_async_copy(own, spot, sems.at[0])
    pass_on = remote(own, spot, sems.at[1], sems.at[2], {"tensor": 1 - c})
    keep.start()
    pass_on.start()
    keep.wait()
    pass_on.wait()


TILE = 256
TALL = 512
LANES = 128


def nt_dot(left, right):
    return lax.dot_general(left, right, (((1,), (1,)), ((), ())), preferred_element_type=f32)


def tn_dot(left, right):
    return lax.dot_general(left, right, (((0,), (0,)), ((), ())), preferred_element_type=f32)


def nn_dot(left, right):
    return jnp.dot(left, right, preferred_element_type=f32)


def tiles(count, step, size=TILE):
    def one(i, carry):
        step(i, pl.ds(pl.multiple_of(i * size, size), size))
        return carry

    lax.fori_loop(0, count, one, 0)


def padded(columns):
    return -(-columns // LANES) * LANES


def window(columns, place):
    first = place * columns // LANES * LANES
    return first, place * columns - first


def window_width(columns, places):
    return max(padded(window(columns, i)[1] + columns) for i in range(places))


def hidden_layer(nz, n2, dy, gate, weights, groups):
    seq, width = n2.shape
    experts = weights[0].shape[0]
    buffers = min(experts, 2)
    held = weights[0].shape[1]
    ffn, kept = held, padded(held)
    block = width // groups
    lane = min(block, TILE)
    per = TILE // lane
    count, slabs = seq // TILE, width // TILE
    strip = 32
    w_shape = (held, width)

    def kernel(n2_hbm, dy_hbm, wg_hbm, wu_hbm, wd_hbm, gate_ref, grad_hbm, da_hbm, db_hbm, gu_hbm, dgate_ref,
               n2_ref, dy_ref, wg, wu, wd, a, b, back, da, db, gu, turned, slab, in_sem, row_sem, out_sem, slab_sem):
        z = lax.axis_index("expert")
        def weight(i, e):
            slot = lax.rem(e, buffers)
            src, dst = ((wg_hbm, wg), (wu_hbm, wu), (wd_hbm, wd))[i]
            return pltpu.make_async_copy(src.at[e], dst.at[slot], in_sem.at[i, slot])

        rows_in = [
            pltpu.make_async_copy(n2_hbm, n2_ref, row_sem.at[0]), pltpu.make_async_copy(dy_hbm, dy_ref, row_sem.at[1])
        ]
        weight(0, 0).start()
        rows_in[0].start()
        weight(1, 0).start()
        weight(2, 0).start()
        rows_in[1].start()
        if kept > held:
            for ref in (da, db, gu):
                ref[:, held:] = jnp.zeros((seq, kept - held), bf16)

        def expert(e, carry):
            slot = lax.rem(e, buffers)
            weight(0, e).wait()
            pl.when(e == 0)(rows_in[0].wait)

            def one(i, at):
                a[at, :] = nt_dot(n2_ref[at, :], wg[slot])

            tiles(seq // TALL, one, TALL)
            weight(1, e).wait()

            def two(i, at):
                b[at, :] = nt_dot(n2_ref[at, :], wu[slot])

            tiles(seq // TALL, two, TALL)
            weight(2, e).wait()
            pl.when(e == 0)(rows_in[1].wait)
            if experts > 1:

                @pl.when(e + 1 < experts)
                def _():
                    for i in range(3):
                        weight(i, e + 1).start()

            def three(i, at):
                back[...] = nt_dot(dy_ref[at, :], wd[slot])

                def point(j, carry):
                    row = pl.ds(pl.multiple_of(i * TILE + j * strip, strip), strip)
                    local = pl.ds(pl.multiple_of(j * strip, strip), strip)
                    av, bv, kv = a[row, :], b[row, :], back[local, :]
                    here_now = lax.broadcasted_iota(jnp.int32, (strip, gate.shape[1]), 1) == z * experts + e
                    gv = jnp.sum(jnp.where(here_now, gate_ref[row, :], 0.0), axis=-1, keepdims=True)
                    sig = 1.0 / (1.0 + jnp.exp(-av))
                    act = av * sig
                    u = act * bv
                    dgate_ref[row, :] += jnp.where(here_now, jnp.sum(u * kv, axis=-1, keepdims=True), 0.0)
                    gu[row, :held] = (gv * u).astype(bf16)
                    du = gv * kv
                    da[row, :held] = (du * bv * (sig + act * (1.0 - sig))).astype(bf16)
                    db[row, :held] = (du * act).astype(bf16)
                    return carry

                lax.fori_loop(0, TILE // strip, point, 0)
                for k, ref in enumerate((da, db, gu)):
                    turned[k, :, at] = ref[at, :held].T

            tiles(count, three)
            saves = [
                pltpu.make_async_copy(src, dst.at[e], out_sem.at[i])
                for i, (src, dst) in enumerate(((da, da_hbm), (db, db_hbm), (gu, gu_hbm)))
            ]
            for save in saves:
                save.start()

            def leave(i):
                slot = lax.rem(i, 2)
                below = pl.ds(pl.multiple_of(e * 3 * ffn, 16), 3 * ffn)
                if per > 1:
                    dst = grad_hbm.at[pl.ds(i * per, per), below]
                else:
                    many = block // TILE
                    to = pl.ds(pl.multiple_of(lax.rem(i, many) * TILE, TILE), TILE)
                    dst = grad_hbm.at[pl.ds(i // many, 1), below, to]
                return pltpu.make_async_copy(slab.at[slot], dst, slab_sem.at[slot])

            def four(i, at):
                slot = lax.rem(i, 2)
                pl.when(i >= 2)(lambda: leave(i).wait())
                for k, right in enumerate((n2_ref, n2_ref, dy_ref)):
                    value = nn_dot(turned[k], right[:, at]).astype(bf16)
                    for j in range(per):
                        slab[slot, j, k * ffn : (k + 1) * ffn, :] = value[:, j * lane : (j + 1) * lane]
                leave(i).start()

            tiles(slabs, four)
            leave(slabs - 2).wait()
            leave(slabs - 1).wait()
            for save in saves:
                save.wait()
            return carry

        dgate_ref[...] = jnp.zeros_like(dgate_ref)
        lax.fori_loop(0, experts, expert, 0)

    hidden = jax.ShapeDtypeStruct((experts, seq, kept), bf16)
    return pl.pallas_call(
        kernel,
        out_shape=[
            jax.ShapeDtypeStruct((groups, experts * 3 * ffn, block), bf16), hidden, hidden, hidden,
            jax.ShapeDtypeStruct(gate.shape, f32),
        ],
        in_specs=[ANY] * 5 + [VMEM],
        out_specs=[ANY] * 4 + [VMEM],
        scratch_shapes=[
            pltpu.VMEM((seq, width), bf16), pltpu.VMEM((seq, width), bf16),
            pltpu.VMEM((buffers,) + w_shape, bf16), pltpu.VMEM((buffers,) + w_shape, bf16), pltpu.VMEM((buffers,) + w_shape, bf16),
            pltpu.VMEM((seq, held), f32), pltpu.VMEM((seq, held), f32), pltpu.VMEM((TILE, held), f32),
            pltpu.VMEM((seq, kept), bf16), pltpu.VMEM((seq, kept), bf16), pltpu.VMEM((seq, kept), bf16),
            pltpu.VMEM((3, held, seq), bf16),
            pltpu.VMEM((2, per, 3 * ffn, lane), bf16),
            pltpu.SemaphoreType.DMA((3, buffers)), pltpu.SemaphoreType.DMA((2,)), pltpu.SemaphoreType.DMA((3,)),
            pltpu.SemaphoreType.DMA((2,)),
        ],
        compiler_params=pltpu.CompilerParams(vmem_limit_bytes=58 * 1024 * 1024),
    )(n2, dy, *weights, gate)


def forward_layer(nz, x, upstream, marks, weights, out_weight, small, shared, groups, name):
    rows, width = x.shape[0] // 2, x.shape[1]
    seq = nz * 2 * rows
    cols = weights[0].shape[1] // nz
    heads = cols // HD
    full = 2 * rows
    strip = 32
    scale = HD ** (-0.5)
    ffn = shared[0].shape[1] // nz
    held = window_width(ffn, nz)
    block = width // groups
    lane = min(block, TILE)
    per = TILE // lane
    slabs = width // TILE
    gate_row = small.shape[0] - 3

    def kernel(x_ref, up_ref, marks_ref, small_ref, wq_hbm, wk_hbm, wv_hbm, wo_hbm, wg_hbm, wu_hbm, wd_hbm,
               n1_hbm, dy_hbm, all_ref, qkv_hbm, p_hbm, o_hbm, n2_hbm, h_ref, inv_ref, logit_ref, grad_hbm, da_hbm, db_hbm,
               gu_hbm, dgate_ref,
               n1_ref, dy_ref, qkv_ref, p_ref, o_ref, n2_ref, own, w, scores, seg_k, heads_in, acc, give, take_in,
               inv_own, wo, wg, wu, wd, da, db, gu, turned, slab,
               w_sem, m_send, m_recv, m_local, a_send, a_recv, e_send, e_recv, i_sems, out_sem, slab_sem, *sems):
        z, c = here()
        at = pl.ds(pl.multiple_of(z * cols, cols), cols)
        loads = [
            pltpu.make_async_copy(src.at[:, at], w.at[:, pl.ds(i * cols, cols)], w_sem.at[i])
            for i, src in enumerate((wq_hbm, wk_hbm, wv_hbm))
        ]
        loads.append(pltpu.make_async_copy(wo_hbm, wo, w_sem.at[3]))
        first = pl.multiple_of(z * ffn // LANES * LANES, LANES)
        skip = z * ffn - first
        for i, (src, dst) in enumerate(((wg_hbm, wg), (wu_hbm, wu), (wd_hbm, wd))):
            loads.append(pltpu.make_async_copy(src.at[:, pl.ds(first, held)], dst, w_sem.at[4 + i]))
        saves = []

        def save(src, dst):
            saves.append(pltpu.make_async_copy(src, dst, out_sem.at[len(saves)]))
            saves[-1].start()

        for load in loads:
            load.start()

        def step(strip_at):
            normed, _ = norm_rows(x_ref[pl.ds(pl.multiple_of(c * rows + strip_at.start, STRIP), STRIP), :].astype(f32), small_ref[gate_row + 1 : gate_row + 2, :].astype(f32))
            own[strip_at, :] = normed.astype(bf16)

        strips(rows, step)
        greet(nz)
        n1 = Gather(nz, own, n1_ref, *sems[:5])
        dy = Gather(nz, up_ref.at[pl.ds(pl.multiple_of(c * rows, rows), rows)], dy_ref, *sems[5:10])
        n2 = Gather(nz, own, n2_ref, *sems[10:])
        n1.start_along(UP)
        n1.start_along(DOWN)
        n1.start_across()
        keep = pltpu.make_async_copy(marks_ref, all_ref.at[z], m_local)
        keep.start()

        def send(way, d):
            to = z + d if way == UP else z - d
            return remote(marks_ref, all_ref.at[z], m_send.at[way, d], m_recv.at[way, d], {"expert": to})

        def take(way, d):
            dst = all_ref.at[z - d if way == UP else z + d]
            remote(dst, dst, m_send.at[way, d], m_recv.at[way, d], {"tensor": 1 - c}).wait_recv()

        for d in range(1, nz):
            for way in (UP, DOWN):
                pl.when(z + d < nz if way == UP else z >= d)(lambda way=way, d=d: send(way, d).start())

        def follow(d):
            pl.when(z == d)(lambda: dy.start_along(UP))
            pl.when(nz - 1 - z == d)(lambda: dy.start_along(DOWN))

        follow(0)
        for d in range(1, nz):
            for p in range(PIECES):
                n1.event(d, p)
            follow(d)
        dy.start_across()
        keep.wait()
        for d in range(1, nz):
            for way in (UP, DOWN):
                pl.when(z + d < nz if way == UP else z >= d)(lambda way=way, d=d: send(way, d).wait_send())
                pl.when(z >= d if way == UP else z + d < nz)(lambda way=way, d=d: take(way, d))
        n1.settle_all()
        n1.finish()
        save(n1_ref, n1_hbm)
        for load in loads:
            load.wait()

        def project(first, last):
            def one(i, carry):
                to = pl.ds(pl.multiple_of(i * full, full), full)
                qkv_ref[to, :] = jnp.dot(n1_ref[to, :], w[...], preferred_element_type=f32).astype(bf16)
                return carry

            lax.fori_loop(first, last, one, 0)

        def label():
            for b in range(nz):
                some = all_ref[b].astype(f32)
                dgate_ref[b * full : (b + 1) * full, :1] = some.T[:, :1]
                seg_k[:, b * full : (b + 1) * full] = some[:1, :]

        def head(i):
            length = (i + 1) * full

            def one(h, carry):
                def part(k):
                    return pl.ds(pl.multiple_of(k * cols + h * HD, HD), HD)

                base = i * full
                scores[:, :length] = lax.dot_general(
                    qkv_ref[base : base + full, part(0)], qkv_ref[:length, part(1)], (((1,), (1,)), ((), ())),
                    preferred_element_type=f32,
                )

                def soften(j, inner):
                    local = pl.ds(pl.multiple_of(j * strip, strip), strip)
                    row = pl.ds(pl.multiple_of(base + j * strip, strip), strip)
                    place_q = base + j * strip + lax.broadcasted_iota(jnp.int32, (strip, length), 0)
                    place_k = lax.broadcasted_iota(jnp.int32, (strip, length), 1)
                    allowed = jnp.logical_and(place_k <= place_q, seg_k[:, :length] == dgate_ref[row, :1])
                    value = jnp.where(allowed, scores[local, :length] * scale, -jnp.inf)
                    value = jnp.exp(value - jnp.max(value, axis=-1, keepdims=True))
                    share = 1.0 / jnp.sum(value, axis=-1, keepdims=True)
                    p_ref[h, row, :length] = (value * share).astype(bf16)
                    return inner

                lax.fori_loop(0, full // strip, soften, 0)
                if length < seq:
                    p_ref[h, base : base + full, length:] = jnp.zeros((full, seq - length), bf16)
                o_ref[base : base + full, pl.ds(pl.multiple_of(h * HD, HD), HD)] = jnp.dot(
                    p_ref[h, base : base + full, :length], qkv_ref[:length, part(2)], preferred_element_type=f32
                ).astype(bf16)
                return carry

            lax.fori_loop(0, heads, one, 0)

        works = [label] + [functools.partial(head, i) for i in range(nz)]
        left_events = [(d, p) for d in range(1, nz) for p in range(PIECES)]

        def events(count=None):
            for _ in range(len(left_events) if count is None else count):
                dy.event(*left_events.pop(0))

        project(0, 2)
        events(1)
        project(2, nz)
        events(1)
        for work in works:
            work()
            if len(left_events) > 2:
                events(1)

        def inside(way, d):
            return z + d < nz if way == UP else z >= d

        def send_heads(way, d):
            to = z + d if way == UP else z - d
            src = o_ref.at[pl.ds(pl.multiple_of(to * full, full), full)]
            return remote(src, heads_in.at[way, d], a_send.at[way, d], a_recv.at[way, d], {"expert": to})

        for d in range(nz - 1, 0, -1):
            for way in (UP, DOWN):
                pl.when(inside(way, d))(lambda way=way, d=d: send_heads(way, d).start())

        save(qkv_ref, qkv_hbm)
        save(p_ref, p_hbm)
        save(o_ref, o_hbm)
        tile = 512 if width % 512 == 0 else width

        def put(block, left, fresh):
            at = pl.ds(pl.multiple_of(block * cols, cols), cols)

            def one(i, carry):
                to = pl.ds(pl.multiple_of(i * tile, tile), tile)
                value = lax.dot_general(
                    left(), wo[to, at], (((1,), (1,)), ((), ())), preferred_element_type=f32
                )
                acc[:, to] = value if fresh else acc[:, to] + value
                return carry

            lax.fori_loop(0, width // tile, one, 0)

        put(z, lambda: o_ref[pl.ds(pl.multiple_of(z * full, full), full), :], True)
        events()
        for d in range(1, nz):
            for way in (UP, DOWN):
                @pl.when(z >= d if way == UP else z + d < nz)
                def _(way=way, d=d):
                    remote(
                        heads_in.at[way, d], heads_in.at[way, d], a_send.at[way, d], a_recv.at[way, d], {"tensor": 1 - c}
                    ).wait_recv()
                    put(z - d if way == UP else z + d, lambda: heads_in[way, d], False)

        def pack(at):
            give[at, :] = acc[pl.ds(pl.multiple_of((1 - c) * rows + at.start, STRIP), STRIP), :].astype(bf16)

        strips(rows, pack)
        swap = remote(give, take_in, e_send, e_recv, {"tensor": 1 - c})
        swap.start()
        swap.wait_recv()

        def norm_two(at):
            mixed = acc[pl.ds(pl.multiple_of(c * rows + at.start, STRIP), STRIP), :] + take_in[at, :].astype(f32)
            h = x_ref[pl.ds(pl.multiple_of(c * rows + at.start, STRIP), STRIP), :].astype(f32) + mixed
            normed, inverse = norm_rows(h, small_ref[gate_row + 2 : gate_row + 3, :].astype(f32))
            h_ref[at, :] = h
            own[at, :] = normed.astype(bf16)
            inv_own[at, :] = jnp.broadcast_to(inverse, (STRIP, 128))

        strips(rows, norm_two)
        spot = inv_ref.at[pl.ds(pl.multiple_of(c * rows, rows), rows)]
        keep_inv = pltpu.make_async_copy(inv_own, spot, i_sems.at[0])
        pass_on = remote(inv_own, spot, i_sems.at[1], i_sems.at[2], {"tensor": 1 - c})
        keep_inv.start()
        pass_on.start()
        n2.start_along(UP)
        n2.start_along(DOWN)
        n2.start_across()
        dy.settle_all()
        dy.finish()
        save(dy_ref, dy_hbm)
        a, b, back = acc.at[:, pl.ds(0, held)], acc.at[:, pl.ds(held, held)], scores.at[:, pl.ds(0, held)]

        def hidden(index):
            at = pl.ds(pl.multiple_of(index * full, full), full)
            logit_ref[at, :] = nt_dot(n2_ref[at, :], small_ref[...])
            a[...] = nn_dot(n2_ref[at, :], wg[...])
            b[...] = nn_dot(n2_ref[at, :], wu[...])
            back[...] = nn_dot(dy_ref[at, :], wd[...])

            def point(j, carry):
                row = pl.ds(pl.multiple_of(index * full + j * strip, strip), strip)
                local = pl.ds(pl.multiple_of(j * strip, strip), strip)
                column = lax.broadcasted_iota(jnp.int32, (strip, held), 1)
                valid = jnp.logical_and(column >= skip, column < skip + ffn)
                av, bv = a[local, :], b[local, :]
                kv = jnp.where(valid, back[local, :], 0.0)
                gv = 1.0 / (1.0 + jnp.exp(-logit_ref[row, gate_row : gate_row + 1]))
                sig = 1.0 / (1.0 + jnp.exp(-av))
                act = av * sig
                u = jnp.where(valid, act * bv, 0.0)
                last = lax.broadcasted_iota(jnp.int32, (strip, small.shape[0]), 1) == gate_row
                dgate_ref[row, :] = jnp.where(last, jnp.sum(u * kv, axis=-1, keepdims=True), 0.0)
                gu[row, :] = (gv * u).astype(bf16)
                du = gv * kv
                da[row, :] = (du * bv * (sig + act * (1.0 - sig))).astype(bf16)
                db[row, :] = (du * act).astype(bf16)
                return carry

            lax.fori_loop(0, full // strip, point, 0)
            for k, ref in enumerate((da, db, gu)):
                turned[k, :, at] = ref[at, :].T

        def arrivals(d):
            for way in (UP, DOWN):

                @pl.when(n2.inside(way, d))
                def _(way=way):
                    n2.settle(way, d)

        def pair(d):
            def one(k, carry):
                index = z + (2 * k - 1) * d
                pl.when(jnp.logical_and(index >= 0, index < nz))(lambda: hidden(index))
                return carry

            arrivals(d)
            lax.fori_loop(0, 2, one, 0)

        n2.settle(UP, 0)
        hidden(z)
        for d in range(1, nz):
            for p in range(PIECES):
                n2.event(d, p)
            if d > 1:
                pair(d - 1)
        pair(nz - 1)
        n2.finish()
        save(n2_ref, n2_hbm)
        save(da, da_hbm.at[0])
        save(db, db_hbm.at[0])
        save(gu, gu_hbm.at[0])

        def leave(i):
            slot = lax.rem(i, 2)
            if per > 1:
                dst = grad_hbm.at[pl.ds(i * per, per)]
            else:
                many = block // TILE
                to = pl.ds(pl.multiple_of(lax.rem(i, many) * TILE, TILE), TILE)
                dst = grad_hbm.at[pl.ds(i // many, 1), :, to]
            return pltpu.make_async_copy(slab.at[slot], dst, slab_sem.at[slot])

        def four(i, at):
            slot = lax.rem(i, 2)
            pl.when(i >= 2)(lambda: leave(i).wait())
            for k, right in enumerate((n2_ref, n2_ref, dy_ref)):
                value = nn_dot(turned[k, pl.ds(pl.multiple_of(skip, 16), ffn), :], right[:, at]).astype(bf16)
                for j in range(per):
                    slab[slot, j, k * ffn : (k + 1) * ffn, :] = value[:, j * lane : (j + 1) * lane]
            leave(i).start()

        tiles(slabs, four)
        leave(slabs - 2).wait()
        leave(slabs - 1).wait()
        keep_inv.wait()
        pass_on.wait()
        swap.wait_send()
        for d in range(1, nz):
            for way in (UP, DOWN):
                pl.when(inside(way, d))(lambda way=way, d=d: send_heads(way, d).wait_send())
        for copy in saves:
            copy.wait()

    hidden_shape = jax.ShapeDtypeStruct((1, seq, held), bf16)
    return pl.pallas_call(
        kernel,
        out_shape=[
            jax.ShapeDtypeStruct((seq, width), bf16),
            jax.ShapeDtypeStruct((seq, width), bf16),
            jax.ShapeDtypeStruct((nz,) + marks.shape, jnp.int32),
            jax.ShapeDtypeStruct((seq, 3 * cols), bf16),
            jax.ShapeDtypeStruct((heads, seq, seq), bf16),
            jax.ShapeDtypeStruct((seq, cols), bf16),
            jax.ShapeDtypeStruct((seq, width), bf16),
            jax.ShapeDtypeStruct((rows, width), f32),
            jax.ShapeDtypeStruct((full, 128), f32),
            jax.ShapeDtypeStruct((seq, small.shape[0]), f32),
            jax.ShapeDtypeStruct((groups, 3 * ffn, block), bf16),
            hidden_shape, hidden_shape, hidden_shape,
            jax.ShapeDtypeStruct((seq, small.shape[0]), f32),
        ],
        in_specs=[VMEM] * 4 + [ANY] * 7,
        out_specs=[ANY, ANY, VMEM, ANY, ANY, ANY, ANY, VMEM, ANY, VMEM, ANY, ANY, ANY, ANY, VMEM],
        scratch_shapes=[
            pltpu.VMEM((seq, width), bf16), pltpu.VMEM((seq, width), bf16), pltpu.VMEM((seq, 3 * cols), bf16),
            pltpu.VMEM((heads, seq, seq), bf16), pltpu.VMEM((seq, cols), bf16), pltpu.VMEM((seq, width), bf16),
            pltpu.VMEM((rows, width), bf16), pltpu.VMEM((width, 3 * cols), bf16), pltpu.VMEM((full, seq), f32),
            pltpu.VMEM((1, seq), f32),
            pltpu.VMEM((2, nz, full, cols), bf16),
            pltpu.VMEM((full, width), f32),
            pltpu.VMEM((rows, width), bf16), pltpu.VMEM((rows, width), bf16),
            pltpu.VMEM((rows, 128), f32), pltpu.VMEM(out_weight.shape, bf16),
            pltpu.VMEM((width, held), bf16), pltpu.VMEM((width, held), bf16), pltpu.VMEM((width, held), bf16),
            pltpu.VMEM((seq, held), bf16), pltpu.VMEM((seq, held), bf16), pltpu.VMEM((seq, held), bf16),
            pltpu.VMEM((3, held, seq), bf16), pltpu.VMEM((2, per, 3 * ffn, lane), bf16),
            pltpu.SemaphoreType.DMA((7,)),
            pltpu.SemaphoreType.DMA((2, nz)), pltpu.SemaphoreType.DMA((2, nz)), pltpu.SemaphoreType.DMA,
            pltpu.SemaphoreType.DMA((2, nz)), pltpu.SemaphoreType.DMA((2, nz)),
            pltpu.SemaphoreType.DMA, pltpu.SemaphoreType.DMA, pltpu.SemaphoreType.DMA((3,)),
            pltpu.SemaphoreType.DMA((9,)), pltpu.SemaphoreType.DMA((2,)),
        ]
        + gather_sems(nz) * 3,
        compiler_params=pltpu.CompilerParams(
            collective_id=name, has_side_effects=True, vmem_limit_bytes=63 * 1024 * 1024
        ),
    )(x, upstream, marks, small, *weights, out_weight, *shared)


def attention_back(nz, d_h, n1, qkv, probs, o, out_weight, groups, part, n2, small, name):
    seq, width = d_h.shape
    heads = probs.shape[0]
    cols = o.shape[1]
    full = seq // nz
    block = width // groups
    lane = min(block, TILE)
    per = TILE // lane
    slabs = width // TILE
    strip = 32
    scale = HD ** (-0.5)

    def kernel(dh_hbm, n1_hbm, qkv_ref, p_ref, o_ref, wo_hbm, part_hbm, n2_hbm, small_ref, heads_ref, grad_hbm, box_hbm,
               sum_ref, n2_ref, s_turned, b_send, b_recv, b_local, dh_ref, n1_ref, wo, d_o, scores, ds, dk, dv, turned, o_turned, slab, in_sem, slab_sem):
        z, c = here()
        at = pl.ds(pl.multiple_of(z * cols, cols), cols)
        loads = [
            pltpu.make_async_copy(wo_hbm.at[:, at], wo, in_sem.at[0]),
            pltpu.make_async_copy(dh_hbm, dh_ref, in_sem.at[1]),
            pltpu.make_async_copy(n1_hbm, n1_ref, in_sem.at[2]),
            pltpu.make_async_copy(n2_hbm, n2_ref, in_sem.at[3]),
        ]
        for load in loads:
            load.start()
        greet(nz)
        keep = pltpu.make_async_copy(part_hbm.at[z], box_hbm.at[z], b_local)
        keep.start()

        def send(way, d):
            to = z + d if way == UP else z - d
            return remote(part_hbm.at[to], box_hbm.at[z], b_send.at[way, d], b_recv.at[way, d], {"expert": to})

        def take(way, d):
            dst = box_hbm.at[z - d if way == UP else z + d]
            remote(dst, dst, b_send.at[way, d], b_recv.at[way, d], {"tensor": 1 - c}).wait_recv()

        for d in range(1, nz):
            for way in (UP, DOWN):
                pl.when(z + d < nz if way == UP else z >= d)(lambda way=way, d=d: send(way, d).start())
        o_turned[...] = o_ref[...].T
        s_turned[...] = small_ref[...].T
        loads[0].wait()
        loads[1].wait()

        def project(i, to):
            d_o[to, :] = nn_dot(dh_ref[to, :], wo[...]).astype(bf16)

        tiles(seq // TILE, project)

        def head(h, carry):
            def part(k):
                return pl.ds(pl.multiple_of(k * cols + h * HD, HD), HD)

            mine = part(0)
            for i in reversed(range(nz)):
                length = (i + 1) * full
                row = pl.ds(i * full, full)
                scores[:, :length] = nt_dot(d_o[row, mine], qkv_ref[:length, part(2)])

                def harden(j, inner, i=i, length=length):
                    local = pl.ds(pl.multiple_of(j * strip, strip), strip)
                    to = pl.ds(pl.multiple_of(i * full + j * strip, strip), strip)
                    mean = jnp.sum(
                        d_o[to, mine].astype(f32) * o_ref[to, mine].astype(f32), axis=-1, keepdims=True
                    )
                    value = p_ref[h, to, :length].astype(f32) * (scores[local, :length] - mean)
                    ds[local, :length] = value.astype(bf16)
                    return inner

                lax.fori_loop(0, full // strip, harden, 0)
                d_s = ds[:, :length]
                heads_ref[row, mine] = (nn_dot(d_s, qkv_ref[:length, part(1)]) * scale).astype(bf16)
                d_k = tn_dot(d_s, qkv_ref[row, mine])
                d_v = tn_dot(p_ref[h, row, :length], d_o[row, mine])
                if i == nz - 1:
                    dk[...], dv[...] = d_k, d_v
                else:
                    dk[:length, :] += d_k
                    dv[:length, :] += d_v
            heads_ref[:, part(1)] = (dk[...] * scale).astype(bf16)
            heads_ref[:, part(2)] = dv[...].astype(bf16)
            return carry

        lax.fori_loop(0, heads, head, 0)

        def turn(i, to):
            turned[:, to] = heads_ref[to, :].T

        tiles(seq // TILE, turn)
        loads[2].wait()
        loads[3].wait()

        def leave(i):
            slot = lax.rem(i, 2)
            if per > 1:
                dst = grad_hbm.at[pl.ds(i * per, per)]
            else:
                many = block // TILE
                to = pl.ds(pl.multiple_of(lax.rem(i, many) * TILE, TILE), TILE)
                dst = grad_hbm.at[pl.ds(i // many, 1), :, to]
            return pltpu.make_async_copy(slab.at[slot], dst, slab_sem.at[slot])

        def write(i, to):
            slot = lax.rem(i, 2)
            pl.when(i >= 2)(lambda: leave(i).wait())
            inner = nn_dot(turned[...], n1_ref[:, to]).astype(bf16)
            outer = nn_dot(o_turned[...], dh_ref[:, to]).astype(bf16)
            both = nn_dot(s_turned[:32, :], n2_ref[:, to])
            sum_ref[:, to] = both[:16, :] + both[16:, :]
            for j in range(per):
                slab[slot, j, : 3 * cols, :] = inner[:, j * lane : (j + 1) * lane]
                slab[slot, j, 3 * cols :, :] = outer[:, j * lane : (j + 1) * lane]
            leave(i).start()

        tiles(slabs, write)
        leave(slabs - 2).wait()
        leave(slabs - 1).wait()
        keep.wait()
        for d in range(1, nz):
            for way in (UP, DOWN):
                pl.when(z + d < nz if way == UP else z >= d)(lambda way=way, d=d: send(way, d).wait_send())
                pl.when(z >= d if way == UP else z + d < nz)(lambda way=way, d=d: take(way, d))

    return pl.pallas_call(
        kernel,
        out_shape=[
            jax.ShapeDtypeStruct((seq, 3 * cols), bf16),
            jax.ShapeDtypeStruct((groups, 4 * cols, block), bf16),
            jax.ShapeDtypeStruct(part.shape, bf16),
            jax.ShapeDtypeStruct((16, width), f32),
        ],
        in_specs=[ANY, ANY, VMEM, VMEM, VMEM, ANY, ANY, ANY, VMEM],
        out_specs=[VMEM, ANY, ANY, VMEM],
        scratch_shapes=[
            pltpu.VMEM((seq, width), bf16), pltpu.VMEM((small.shape[1], seq), bf16),
            pltpu.SemaphoreType.DMA((2, nz)), pltpu.SemaphoreType.DMA((2, nz)), pltpu.SemaphoreType.DMA,
            pltpu.VMEM((seq, width), bf16), pltpu.VMEM((seq, width), bf16), pltpu.VMEM((width, cols), bf16),
            pltpu.VMEM((seq, cols), bf16), pltpu.VMEM((full, seq), f32), pltpu.VMEM((full, seq), bf16),
            pltpu.VMEM((seq, HD), f32), pltpu.VMEM((seq, HD), f32),
            pltpu.VMEM((3 * cols, seq), bf16), pltpu.VMEM((cols, seq), bf16), pltpu.VMEM((2, per, 4 * cols, lane), bf16),
            pltpu.SemaphoreType.DMA((4,)), pltpu.SemaphoreType.DMA((2,)),
        ],
        compiler_params=params(name),
    )(d_h, n1, qkv, probs, o, out_weight, part, n2, small)


def spread_turned(nz, part, splits, name):
    _, columns, block = part.shape
    cols = columns // splits

    def kernel(in_ref, *rest):
        outs, (box, send_sem, recv_sem) = rest[:splits], rest[splits:]
        z, c = here()
        greet(nz)

        def send(way, d):
            to = z + d if way == UP else z - d
            return remote(in_ref.at[to], box.at[z], send_sem.at[way, d], recv_sem.at[way, d], {"expert": to})

        def take(way, d):
            dst = box.at[z - d if way == UP else z + d]
            remote(dst, dst, send_sem.at[way, d], recv_sem.at[way, d], {"tensor": 1 - c}).wait_recv()

        for d in range(nz - 1, 0, -1):
            for way in (UP, DOWN):
                pl.when(z + d < nz if way == UP else z >= d)(lambda way=way, d=d: send(way, d).start())
        box[z] = in_ref[z]
        for d in range(1, nz):
            for way in (UP, DOWN):
                pl.when(z + d < nz if way == UP else z >= d)(lambda way=way, d=d: send(way, d).wait_send())
                pl.when(z >= d if way == UP else z + d < nz)(lambda way=way, d=d: take(way, d))
        for j in range(splits):
            for b in range(nz):
                value = box[b, j * cols : (j + 1) * cols, :].astype(f32).T
                outs[j][:, b * cols : (b + 1) * cols] = value

    return pl.pallas_call(
        kernel,
        out_shape=[jax.ShapeDtypeStruct((block, nz * cols), f32)] * splits,
        in_specs=[VMEM],
        out_specs=[VMEM] * splits,
        scratch_shapes=[
            pltpu.VMEM(part.shape, bf16), pltpu.SemaphoreType.DMA((2, nz)), pltpu.SemaphoreType.DMA((2, nz)),
        ],
        compiler_params=params(name),
    )(part)


PART = 512


class Products:
    def __init__(self, nz, experts, shared, extra):
        self.nz, self.experts, self.shared = nz, experts, shared
        _, self.seq, self.kept = experts[0][0][0].shape
        _, self.ffn, self.width = experts[0][1][0].shape
        self.held = shared[0][0][0].shape[2]
        self.own = shared[0][1].shape[1] // nz
        self.more = [] if extra is None else list(extra)
        self.inputs = (
            [left[0] for left, _ in experts] + [right[0] for _, right in experts] + [left[0] for left, _ in shared]
            + [right for _, right in shared] + self.more
        )
        ne, ns = len(experts), len(shared)
        self.specs = [ANY] * (2 * (ne + ns)) + [VMEM] * len(self.more)
        self.scratch = [
            pltpu.VMEM((self.seq, ne * self.kept), bf16), pltpu.VMEM((ne * self.kept, self.width), bf16),
            pltpu.VMEM((self.seq, ns * self.held), bf16), pltpu.VMEM((self.width, ns * self.held), bf16),
            pltpu.SemaphoreType.DMA((self.width // PART, ne + ns)), pltpu.SemaphoreType.DMA((nz, ne + ns)),
        ]

    def bind(self, refs, scratch):
        ne, ns = len(self.experts), len(self.shared)
        self.left, self.right, self.sleft, self.sright, self.r_sem, self.l_sem = scratch
        self.e_left, self.e_right = refs[:ne], refs[ne : 2 * ne]
        self.s_left, self.s_right = refs[2 * ne : 2 * ne + ns], refs[2 * ne + ns : 2 * (ne + ns)]
        self.small = refs[2 * (ne + ns) :]
        self.first = pl.multiple_of(lax.axis_index("expert") * self.own // LANES * LANES, LANES)

    def rights(self, j):
        to = pl.ds(pl.multiple_of(j * PART, PART), PART)
        for i, (_, (_, index)) in enumerate(self.experts):
            dst = self.right.at[pl.ds(i * self.kept, self.ffn), to]
            yield pltpu.make_async_copy(self.e_right[i].at[index, :, to], dst, self.r_sem.at[j, i])
        for i in range(len(self.shared)):
            src = self.s_right[i].at[to, pl.ds(self.first, self.held)]
            dst = self.sright.at[to, pl.ds(i * self.held, self.held)]
            yield pltpu.make_async_copy(src, dst, self.r_sem.at[j, len(self.experts) + i])

    def lefts(self, b):
        rows = self.seq // self.nz
        at = pl.ds(pl.multiple_of(b * rows, rows), rows)
        for i, ((_, index), _) in enumerate(self.experts):
            dst = self.left.at[at, pl.ds(i * self.kept, self.kept)]
            yield pltpu.make_async_copy(self.e_left[i].at[index, at], dst, self.l_sem.at[b, i])
        for i, ((_, index), _) in enumerate(self.shared):
            dst = self.sleft.at[at, pl.ds(i * self.held, self.held)]
            yield pltpu.make_async_copy(self.s_left[i].at[index, at], dst, self.l_sem.at[b, len(self.experts) + i])

    def fetch(self, order):
        for copy in self.lefts(order(0)):
            copy.start()
        for j in range(self.width // PART):
            for copy in self.rights(j):
                copy.start()
        for k in range(1, self.nz):
            for copy in self.lefts(order(k)):
                copy.start()
        if self.kept > self.ffn:
            for i in range(len(self.experts)):
                self.right[i * self.kept + self.ffn : (i + 1) * self.kept, :] = jnp.zeros(
                    (self.kept - self.ffn, self.width), bf16
                )

    def block(self, k, b, out, start, end):
        rows = self.seq // self.nz
        at = pl.ds(pl.multiple_of(b * rows, rows), rows)
        if start == 0:
            for copy in self.lefts(b):
                copy.wait()

        def one(j, carry):
            @pl.when(k == 0)
            def _():
                for copy in self.rights(j):
                    copy.wait()

            to = pl.ds(pl.multiple_of(j * PART, PART), PART)
            value = nn_dot(self.left[at, :], self.right[:, to]) + nt_dot(self.sleft[at, :], self.sright[to, :])
            if self.more:
                value += nt_dot(self.small[0][at, :], self.small[1][to, :])
            out[at, to] = value.astype(bf16)
            return carry

        lax.fori_loop(start, end, one, 0)


def reduce_and_gather(nz, products, h, gains, upstream, name):
    rows, width = h.shape
    n_in, n_scratch = len(products.inputs), len(products.scratch)

    def kernel(*refs):
        p_refs, (h_ref, gain_ref, up_ref, out_ref, dh_ref, gg_ref) = refs[:n_in], refs[n_in : n_in + 6]
        rest = refs[n_in + 6 :]
        p_scratch, (part, own), rest = rest[:n_scratch], rest[n_scratch : n_scratch + 2], rest[n_scratch + 2 :]
        scratch, sems = rest[:REDUCE_SCRATCH], rest[REDUCE_SCRATCH:]
        total = scratch[3]
        products.bind(p_refs, p_scratch)
        reducer = Reducer(nz, part, *scratch)
        products.fetch(reducer.block)
        greet(nz)
        z, c = here()
        ends = reducer.ends()

        def one(s, carry):
            products.block(s, reducer.block(s), part, 0, 1)
            pl.when(jnp.logical_and(ends, s >= 1))(lambda: reducer.forward(s - 1))
            products.block(s, reducer.block(s), part, 1, width // PART)
            reducer.begin(s)
            pl.when(jnp.logical_and(jnp.logical_not(ends), s >= 2))(lambda: reducer.forward(s - 2))
            return carry

        lax.fori_loop(0, nz, one, 0)
        pl.when(jnp.logical_not(ends))(lambda: reducer.forward(nz - 2))
        reducer.finish()
        gg_ref[...] = jnp.zeros_like(gg_ref)

        def step(at):
            change, along = norm_back(h_ref[at, :], gain_ref[gains.shape[0] - 1 :, :].astype(f32), total[at, :])
            dh = up_ref[pl.ds(pl.multiple_of(c * rows + at.start, STRIP), STRIP), :].astype(f32) + change
            dh_ref[at, :] = dh
            own[at, :] = dh.astype(bf16)
            gg_ref[...] += along

        strips(rows, step)
        gather_rows(nz, own, out_ref, *sems)
        reducer.drain()

    return pl.pallas_call(
        kernel,
        out_shape=[
            jax.ShapeDtypeStruct((nz * 2 * rows, width), bf16),
            jax.ShapeDtypeStruct((rows, width), f32),
            jax.ShapeDtypeStruct((STRIP, width), f32),
        ],
        in_specs=products.specs + [VMEM] * 3,
        out_specs=[ANY, VMEM, VMEM],
        scratch_shapes=products.scratch
        + [pltpu.VMEM((nz * 2 * rows, width), bf16), pltpu.VMEM((rows, width), bf16)]
        + reduce_scratch(nz, rows, width)
        + gather_sems(nz),
        compiler_params=params(name),
    )(*products.inputs, h, gains, upstream)


def reduce_last(nz, d_heads, weights, x, gains, dh, products, h, small, box, name):
    rows, width = dh.shape
    cols = d_heads.shape[1] // 3
    n, small_rows, lanes = small.shape
    box_rows, block = box.shape[1] // 3, box.shape[2]
    n_in, n_scratch = len(products.inputs), len(products.scratch)

    def kernel(*refs):
        p_refs, (
            d_ref, wq_hbm, wk_hbm, wv_hbm, x_ref, gain_ref, dh_ref, h_ref, small_ref, box_ref, in_ref, out_ref, sum_ref, *turned,
        ) = refs[:n_in], refs[n_in : n_in + 16]
        gg_ref, s_out, s_box, s_total, s_other, s_send, s_recv, swap_sem = refs[n_in + 16 : n_in + 24]
        rest = refs[n_in + 24 :]
        p_scratch, (d_part, b_part, own, sems, w_ref, w_sem), rest = (
            rest[:n_scratch], rest[n_scratch : n_scratch + 6], rest[n_scratch + 6 :],
        )
        mine = pl.ds(pl.multiple_of(lax.axis_index("expert") * cols, cols), cols)
        loads = [
            pltpu.make_async_copy(src.at[:, mine], w_ref.at[:, pl.ds(i * cols, cols)], w_sem.at[i])
            for i, src in enumerate((wq_hbm, wk_hbm, wv_hbm))
        ]
        for load in loads:
            load.start()
        d_scratch, b_scratch = rest[:REDUCE_SCRATCH], rest[REDUCE_SCRATCH:]
        d_total, b_total = d_scratch[3], b_scratch[3]
        products.bind(p_refs, p_scratch)
        first, second = Reducer(nz, d_part, *d_scratch), Reducer(nz, b_part, *b_scratch)
        z, c = here()
        me = lax.axis_index("dp") * nz + z
        barrier = pltpu.get_barrier_semaphore()

        def peer(q):
            to = lax.rem(me + q, n)
            return to, {"dp": to // nz, "expert": lax.rem(to, nz)}

        pl.semaphore_signal(barrier, inc=1, device_id={"tensor": 1 - c}, device_id_type=MESH)
        for q in range(1, n):
            pl.semaphore_signal(barrier, inc=1, device_id=peer(q)[1], device_id_type=MESH)
        pl.semaphore_wait(barrier, n)

        def send_small(q):
            to, device = peer(q)
            return remote(s_out.at[to], s_box.at[q], s_send.at[q], s_recv.at[q], device)

        ends = first.ends()
        middle = jnp.logical_not(ends)

        def inner(block):
            at = pl.ds(pl.multiple_of(block * 2 * rows, 2 * rows), 2 * rows)

            def one(j, carry):
                to = pl.ds(pl.multiple_of(j * PART, PART), PART)
                d_part[at, to] = nt_dot(d_ref[at, :], w_ref[to, :]).astype(bf16)
                return carry

            lax.fori_loop(0, width // PART, one, 0)

        def one(s, carry):
            inner(first.block(s))
            first.begin(s)
            pl.when(jnp.logical_and(ends, s >= 1))(lambda: first.forward(s - 1))
            return carry

        def two(s, carry):
            products.block(s, second.block(s), b_part, 0, width // PART)
            second.begin(s)

            @pl.when(s >= 1)
            def _():
                pl.when(ends)(lambda: second.forward(s - 1))
                pl.when(middle)(lambda: first.forward(s - 1))

            return carry

        def three(s, carry):
            pl.when(middle)(lambda: second.forward(s))
            return carry

        for load in loads:
            load.wait()
        products.fetch(second.block)
        lax.fori_loop(0, nz, one, 0)
        lax.fori_loop(0, nz, two, 0)
        lax.fori_loop(0, nz - 1, three, 0)
        for i in range(3):
            for b in range(nz):
                value = box_ref[b, i * box_rows : (i + 1) * box_rows, :].astype(f32).T
                turned[i][:, b * box_rows : (b + 1) * box_rows] = value
        first.finish()
        gg_ref[...] = jnp.zeros_like(gg_ref)

        def step(at):
            change, along = norm_back(x_ref[pl.ds(pl.multiple_of(c * rows + at.start, STRIP), STRIP), :].astype(f32), gain_ref[gains.shape[0] - 2 : gains.shape[0] - 1, :].astype(f32), d_total[at, :])
            own[0, at, :] = dh_ref[at, :] + change
            gg_ref[...] += along

        strips(rows, step)

        def leave(i, ref):
            spot = ref.at[pl.ds(pl.multiple_of(c * rows, rows), rows)]
            return (
                pltpu.make_async_copy(own.at[i], spot, sems.at[i, 0]),
                remote(own.at[i], spot, sems.at[i, 1], sems.at[i, 2], {"tensor": 1 - c}),
            )

        for copy in leave(0, in_ref):
            copy.start()
        first_row = jnp.sum(gg_ref[...], axis=0, keepdims=True)
        for q in range(n):
            s_out[q] = small_ref[q]
            s_out[q, :1, :] = first_row[:, q * lanes : (q + 1) * lanes]
        for q in range(1, n):
            send_small(q).start()
        s_total[...] = s_out[me]
        for q in range(1, n):
            send_small(q).wait_recv()
            s_total[...] += s_box[q]
        swap = remote(s_total, s_other, swap_sem.at[0], swap_sem.at[1], {"tensor": 1 - c})
        swap.start()
        second.finish()

        def last(at):
            own[1, at, :] = h_ref[at, :] + b_total[at, :]

        strips(rows, last)
        for copy in leave(1, out_ref):
            copy.start()
        first.drain()
        second.drain()
        swap.wait_recv()
        sum_ref[...] = s_total[...] + s_other[...]
        swap.wait_send()
        for q in range(1, n):
            send_small(q).wait_send()
        for copy in (*leave(0, in_ref), *leave(1, out_ref)):
            copy.wait()

    return pl.pallas_call(
        kernel,
        out_shape=[
            jax.ShapeDtypeStruct((2 * rows, width), f32),
            jax.ShapeDtypeStruct((2 * rows, width), f32),
            jax.ShapeDtypeStruct((small_rows, lanes), f32),
        ]
        + [jax.ShapeDtypeStruct((block, nz * box_rows), f32)] * 3,
        in_specs=products.specs + [VMEM] + [ANY] * 3 + [VMEM] * 6,
        out_specs=[ANY, ANY] + [VMEM] * 4,
        scratch_shapes=[
            pltpu.VMEM((STRIP, width), f32), pltpu.VMEM(small.shape, f32), pltpu.VMEM(small.shape, f32),
            pltpu.VMEM((small_rows, lanes), f32), pltpu.VMEM((small_rows, lanes), f32),
            pltpu.SemaphoreType.DMA((n,)), pltpu.SemaphoreType.DMA((n,)), pltpu.SemaphoreType.DMA((2,)),
        ]
        + products.scratch
        + [
            pltpu.VMEM((nz * 2 * rows, width), bf16), pltpu.VMEM((nz * 2 * rows, width), bf16),
            pltpu.VMEM((2, rows, width), f32), pltpu.SemaphoreType.DMA((2, 3)),
            pltpu.VMEM((width, 3 * cols), bf16), pltpu.SemaphoreType.DMA((3,)),
        ]
        + reduce_scratch(nz, rows, width) * 2,
        compiler_params=params(name, 60),
    )(*products.inputs, d_heads, *weights, x, gains, dh, h, small, box)


def cross_rows(left, right):
    return lax.dot_general(left, right, (((0,), (0,)), ((), ())), preferred_element_type=f32)


def cross_cols(left, right):
    return lax.dot_general(left, right, (((1,), (1,)), ((), ())), preferred_element_type=f32)


def dot(left, right):
    return jnp.dot(left, right, preferred_element_type=f32)


def two_parts(values):
    high = values.astype(bf16)
    return high, (values - high.astype(f32)).astype(bf16)


def body(
    tokens, segments, routes, norm1_gain, q_weight, k_weight, v_weight, o_weight, norm2_gain,
    router_weight, shared_gate_vector, shared_gate_weight, shared_up_weight, shared_down_weight,
    expert_gate_weight, expert_up_weight, expert_down_weight, out_grad,
):
    nz = lax.axis_size("expert")
    nc = lax.axis_size("tensor")
    z = lax.axis_index("expert")
    c = lax.axis_index("tensor")
    rows, width = tokens.shape
    own_rows = rows // nc
    local_count, _, ffn = expert_gate_weight.shape
    expert_count = local_count * nz
    head_cols = q_weight.shape[1] // nz
    shared_cols = shared_gate_weight.shape[1] // nz
    heads = head_cols // HD
    seq = rows * nz
    scale = HD ** (-0.5)

    def head_slice(values):
        return lax.dynamic_slice_in_dim(values, z * head_cols, head_cols, 1)

    x_all_rows = tokens.astype(f32)
    inverse_one_rows = lax.rsqrt(jnp.mean(x_all_rows * x_all_rows, axis=-1) + epsilon)
    marks = jnp.concatenate([segments, routes.T, jnp.zeros((7 - routes.shape[1], rows), jnp.int32)], axis=0)
    ndp = lax.axis_size("dp")
    small_rows_weight = jnp.concatenate(
        [router_weight.T, shared_gate_vector[None], norm1_gain[None], norm2_gain[None]], axis=0
    )
    shared_weights = (shared_gate_weight, shared_up_weight, shared_down_weight)
    (
        n1, dy, all_marks, qkv, p_low, o, n2, h, inverse_two, logits, grad_s, da_s, db_s, gu_s, dgate_s,
    ) = forward_layer(
        nz, tokens, out_grad, marks, (q_weight, k_weight, v_weight), o_weight, small_rows_weight, shared_weights,
        ndp * nz, 0,
    )
    all_routes = jnp.transpose(all_marks[:, 1 : 1 + routes.shape[1]], (0, 2, 1)).reshape(seq, routes.shape[1])

    probs = jax.nn.softmax(logits[:, :expert_count], axis=-1)
    chosen = jnp.any(all_routes[:, :, None] == jnp.arange(expert_count)[None, None, :], axis=1)
    gates = jnp.where(chosen, probs, 0.0)
    sigma = jax.nn.sigmoid(logits[:, expert_count : expert_count + 1])

    turned = [jnp.swapaxes(w, 1, 2) for w in (expert_gate_weight, expert_up_weight, expert_down_weight)]
    grad_e, da_e, db_e, gu_e, dgate_e = hidden_layer(nz, n2, dy, gates, turned, ndp)

    d_probs = jnp.where(chosen, dgate_e, 0.0)
    d_logits = probs * (d_probs - jnp.sum(probs * d_probs, axis=-1, keepdims=True))
    d_vector = dgate_s[:, expert_count : expert_count + 1] * (sigma * (1.0 - sigma))
    small = jnp.concatenate([d_logits, d_vector], axis=1)
    small_high, small_low = two_parts(small)
    small_weights = jnp.concatenate([router_weight, shared_gate_vector[:, None]], axis=1)
    fill = ((0, 0), (0, 128 - small.shape[1]))
    experts = range(local_count)
    d_n2 = Products(
        nz,
        [((da_e, i), (turned[0], i)) for i in experts] + [((db_e, i), (turned[1], i)) for i in experts],
        [((da_s, 0), shared_gate_weight), ((db_s, 0), shared_up_weight)],
        (jnp.pad(small_high, fill), jnp.pad(small_weights, fill)),
    )
    few = small.shape[1]
    mixed = jnp.pad(small_high, ((0, 0), (2, 126 - few))) + jnp.pad(small_low, ((0, 0), (18, 110 - few)))


    def over_dp(grad):
        rows = grad.reshape(-1, grad.shape[-1])
        return lax.psum_scatter(rows, "dp", scatter_dimension=0, tiled=True)

    shared_part = over_dp(grad_s).reshape((nz,) + grad_s.shape[1:])
    expert_part = over_dp(grad_e).reshape(local_count, 3, ffn, -1)
    dhr, dh, grad_two = reduce_and_gather(nz, d_n2, h, small_rows_weight, out_grad, 2)
    d_heads, grad_attention, shared_box, small_grad = attention_back(
        nz, dhr, n1, qkv, p_low, o, o_weight, ndp * nz, shared_part, n2, mixed, 1
    )
    attention_part = over_dp(grad_attention).reshape((nz,) + grad_attention.shape[1:])
    branch = Products(
        nz,
        [((gu_e, i), (turned[2], i)) for i in experts],
        [((gu_s, 0), shared_down_weight)],
        None,
    )
    dh_now, _ = lax.optimization_barrier((dh, grad_attention))
    small_rows = small_grad + jnp.pad(jnp.sum(grad_two, axis=0)[None], ((1, 14), (0, 0)))
    count = ndp * nz
    small_blocks = jnp.swapaxes(small_rows.reshape(16, count, width // count), 0, 1)
    input_grad, layer_out, small_all, s_gate, s_up, s_down = reduce_last(
        nz, d_heads, (q_weight, k_weight, v_weight), tokens, small_rows_weight, dh_now, branch, h, small_blocks, shared_box, 3
    )
    stats = jnp.stack([inverse_one_rows, inverse_two[:, 0]])

    e_gate, e_up, e_down = (jnp.swapaxes(expert_part[:, k].astype(f32), 1, 2) for k in range(3))
    attention_part, e_gate, e_up, e_down, small_all = lax.optimization_barrier(
        (attention_part, e_gate, e_up, e_down, small_all)
    )
    g_q, g_k, g_v, g_o = spread_turned(nz, attention_part, 4, 6)
    g_one, g_two, g_router, g_vector = small_all[0], small_all[1], small_all[2 : 2 + expert_count].T, small_all[2 + expert_count]
    return (
        layer_out, input_grad, stats, g_one, g_q, g_k, g_v, g_o, g_two, g_router, g_vector,
        s_gate, s_up, s_down, e_gate, e_up, e_down,
    )


def solution(mesh):
    both = ("dp", "expert")
    cols = P(None, "tensor")
    placed = (
        P(both, None), P("dp", "expert"), P(both, None), P(), cols, cols, cols, cols, P(), P(), P(),
        cols, cols, cols, P("expert", None, "tensor"), P("expert", None, "tensor"),
        P("expert", None, "tensor"), P(both, None),
    )
    split = P(both, "tensor")
    experts = P("expert", "dp", "tensor")
    return jax.shard_map(
        body,
        mesh=mesh,
        in_specs=placed,
        out_specs=(
            P(both, None), P(both, None), P(None, both), P(both), split, split, split, split, P(both),
            P(both, None), P(both), split, split, split, experts, experts, experts,
        ),
        check_vma=False,
    )
```
